32 devices in a mesh: dp: 2 (over x), ctx: 4 (over y, core), head: 4 (over z).
Axes of the slice: x: 2, y: 2, z: 4, core: 2. Of those that a mesh axis runs over, the one named last changes fastest.
Arguments:
- tokens: bfloat16 [4, 2048, 768], P('dp', ('ctx', 'head')), may hold values from -6 to 6
- cotangent: bfloat16 [4, 2048, 768], P('dp', ('ctx', 'head')), may hold values from -6 to 6
- lengths: int32 [4], P('dp'), may hold values from 513 to 2048, as said below
- attention_gain: bfloat16 [768], P(('dp', 'ctx', 'head')), may hold values from 0.25 to 1.75
- attention_shift: bfloat16 [768], P(('dp', 'ctx', 'head')), may hold values from -3 to 3
- packed_weight: bfloat16 [768, 2304], P(('dp', 'ctx', 'head')), may hold values from -0.21875 to 0.21875
- query_bias: bfloat16 [768], P(('dp', 'ctx', 'head')), may hold values from -3 to 3
- value_bias: bfloat16 [768], P(('dp', 'ctx', 'head')), may hold values from -0.59765625 to 0.59765625
- mixer_weight: bfloat16 [768, 768], P(('dp', 'ctx', 'head')), may hold values from -1.75 to 1.75
- mixer_bias: bfloat16 [768], P(('dp', 'ctx', 'head')), may hold values from -3 to 3
- feedforward_gain: bfloat16 [768], P(('dp', 'ctx', 'head')), may hold values from 0.25 to 1.75
- feedforward_shift: bfloat16 [768], P(('dp', 'ctx', 'head')), may hold values from -3 to 3
- expand_weight: bfloat16 [768, 3072], P(('dp', 'ctx', 'head')), may hold values from -0.21875 to 0.21875
- expand_bias: bfloat16 [3072], P(('dp', 'ctx', 'head')), may hold values from -3 to 3
- shrink_weight: bfloat16 [3072, 768], P(('dp', 'ctx', 'head')), may hold values from -0.109375 to 0.109375
- shrink_bias: bfloat16 [768], P(('dp', 'ctx', 'head')), may hold values from -3 to 3
Outputs:
- block_output: bfloat16 [4, 2048, 768], P('dp', ('ctx', 'head'))
- input_grad: bfloat16 [4, 2048, 768], P('dp', ('ctx', 'head'))
- grad_attention_gain: float32 [768], P(('dp', 'ctx', 'head'))
- grad_attention_shift: float32 [768], P(('dp', 'ctx', 'head'))
- grad_packed_weight: float32 [768, 2304], P(('dp', 'ctx', 'head'))
- grad_query_bias: float32 [768], P(('dp', 'ctx', 'head'))
- grad_value_bias: float32 [768], P(('dp', 'ctx', 'head'))
- grad_mixer_weight: float32 [768, 768], P(('dp', 'ctx', 'head'))
- grad_mixer_bias: float32 [768], P(('dp', 'ctx', 'head'))
- grad_feedforward_gain: float32 [768], P(('dp', 'ctx', 'head'))
- grad_feedforward_shift: float32 [768], P(('dp', 'ctx', 'head'))
- grad_expand_weight: float32 [768, 3072], P(('dp', 'ctx', 'head'))
- grad_expand_bias: float32 [3072], P(('dp', 'ctx', 'head'))
- grad_shrink_weight: float32 [3072, 768], P(('dp', 'ctx', 'head'))
- grad_shrink_bias: float32 [768], P(('dp', 'ctx', 'head'))
The draws below stay inside these ranges and needn't reach their ends.
Inputs may be any that keep to these rules, and one draw needn't show every extreme that they name: `lengths`: the number of leading positions of each image that hold real patches; keys at later positions are hidden from every query.
All inputs are finite; a program needn't handle non-finite values.
Results may differ from the reference program's by a relative error of at most 0.035.
Values may be sent and summed in bfloat16 or wider, within the bound.
A program may use at most 128 MiB of HBM per device.

```python
import math
import jax
import jax.numpy as jnp
from jax import lax

D = 768
HEADS = 12
FF = 3072
HEAD_DIM = 64
L = 2048
IMAGES = 4


def draw_lengths(key, part):
    values = jax.random.randint(jax.random.fold_in(key, 7), (IMAGES,), L // 4 + 1, L + 1)
    longest = jax.random.randint(jax.random.fold_in(key, 8), (), 0, IMAGES)
    image_ids = jnp.arange(IMAGES)
    values = jnp.where(image_ids == longest, L, values)
    return values.astype(jnp.int32)


def shard_levels(key, shape, cuts, low, largest):
    level, own = 1.0, jax.random.fold_in(key, 6)
    for position, blocks in cuts:
        heights = jnp.exp(jax.random.uniform(jax.random.fold_in(own, position), (blocks,), jnp.float32, low / len(cuts), largest / len(cuts)))
        level = level * jnp.repeat(heights, shape[position] // blocks).reshape([-1 if axis == position else 1 for axis in range(len(shape))])
    return level


def gaussian(own_key, extent, scale, bound, cuts=(), kind=jnp.bfloat16):
    loudness = shard_levels(own_key, extent, cuts, -0.22, 0.18) if cuts else 1.0
    values = jax.random.normal(own_key, extent, jnp.float32) * scale * loudness
    return jnp.minimum(jnp.maximum(values, -bound), bound).astype(kind)


def setup_inputs(seed: int = 0) -> dict:
    arg_keys = jax.random.split(jax.random.key(seed), 17)
    tokens = gaussian(arg_keys[0], (IMAGES, L, D), 1.0, 6.0, ((0, 2), (1, 16)))
    cotangent = gaussian(arg_keys[1], (IMAGES, L, D), 1.0, 6.0, ((0, 2), (1, 16)))
    lengths = draw_lengths(jax.random.fold_in(arg_keys[16], 71), 0)
    attention_gain = jnp.clip(1.0 + 0.15 * jax.random.normal(arg_keys[3], (D,), jnp.float32), 0.25, 1.75).astype(jnp.bfloat16)
    attention_shift = gaussian(arg_keys[4], (D,), 0.5, 3.0, ((0, 32),))
    packed_weight = gaussian(arg_keys[5], (D, 3 * D), D ** -0.5, 0.21875, ((0, 32),))
    query_bias = gaussian(arg_keys[6], (D,), 0.5, 3.0, ((0, 32),))
    value_bias = gaussian(arg_keys[7], (D,), 0.1, 0.59765625, ((0, 32),))
    mixer_weight = gaussian(arg_keys[8], (D, D), (D // 64) ** -0.5, 1.75, ((0, 32),))
    mixer_bias = gaussian(arg_keys[9], (D,), 0.5, 3.0, ((0, 32),))
    feedforward_gain = jnp.clip(1.0 + 0.15 * jax.random.normal(arg_keys[10], (D,), jnp.float32), 0.25, 1.75).astype(jnp.bfloat16)
    feedforward_shift = gaussian(arg_keys[11], (D,), 0.5, 3.0, ((0, 32),))
    expand_weight = gaussian(arg_keys[12], (D, FF), D ** -0.5, 0.21875, ((0, 32),))
    expand_bias = gaussian(arg_keys[13], (FF,), 0.5, 3.0, ((0, 32),))
    shrink_weight = gaussian(arg_keys[14], (FF, D), FF ** -0.5, 0.109375, ((0, 32),))
    shrink_bias = gaussian(arg_keys[15], (D,), 0.5, 3.0, ((0, 32),))
    return dict(tokens=tokens, cotangent=cotangent, lengths=lengths, attention_gain=attention_gain, attention_shift=attention_shift, packed_weight=packed_weight, query_bias=query_bias, value_bias=value_bias, mixer_weight=mixer_weight, mixer_bias=mixer_bias, feedforward_gain=feedforward_gain, feedforward_shift=feedforward_shift, expand_weight=expand_weight, expand_bias=expand_bias, shrink_weight=shrink_weight, shrink_bias=shrink_bias)


NORM_EPS = 1e-06
MASKED_SCORE = -1e+30

def layer_norm(token_rows, norm_gain, norm_shift):
    row_mean = lax.optimization_barrier(jnp.mean(token_rows, axis=-1, keepdims=True))
    centred = token_rows - row_mean
    row_var = lax.optimization_barrier(jnp.mean(centred * centred, axis=-1, keepdims=True))
    inv_std = lax.rsqrt(row_var + NORM_EPS)
    normed = centred * inv_std
    return (normed * norm_gain + norm_shift, normed, inv_std)

def norm_backward(grad_out, normed, inv_std, norm_gain):
    scaled = grad_out * norm_gain
    first_mean = lax.optimization_barrier(jnp.mean(scaled, axis=-1, keepdims=True))
    second_mean = lax.optimization_barrier(jnp.mean(scaled * normed, axis=-1, keepdims=True))
    return inv_std * (scaled - first_mean - normed * second_mean)

def gelu_value(pre_act):
    return 0.5 * pre_act * (1.0 + jax.scipy.special.erf(pre_act * (1.0 / math.sqrt(2.0))))

def gelu_slope(pre_act):
    cumulative = 0.5 * (1.0 + jax.scipy.special.erf(pre_act * (1.0 / math.sqrt(2.0))))
    density = jnp.exp(-0.5 * pre_act * pre_act) * (1.0 / math.sqrt(2.0 * math.pi))
    return cumulative + pre_act * density

def masked_scores(query_item, key_item, length, score_scale):
    scores = jnp.einsum('qd,kd->qk', query_item, key_item, preferred_element_type=jnp.float32) * score_scale
    key_pos = jnp.arange(key_item.shape[0], dtype=jnp.int32)
    return jnp.where(key_pos[None, :] < length, scores, MASKED_SCORE)

def reference(tokens, cotangent, lengths, attention_gain, attention_shift, packed_weight, query_bias, value_bias, mixer_weight, mixer_bias, feedforward_gain, feedforward_shift, expand_weight, expand_bias, shrink_weight, shrink_bias):
    seq_len = tokens.shape[1]
    width = tokens.shape[2]
    score_scale = 1.0 / math.sqrt(HEAD_DIM)
    gain_one = attention_gain.astype(jnp.float32)
    shift_one = attention_shift.astype(jnp.float32)
    gain_two = feedforward_gain.astype(jnp.float32)
    shift_two = feedforward_shift.astype(jnp.float32)
    packed_bias = jnp.concatenate([query_bias.astype(jnp.float32), jnp.zeros((width,), jnp.float32), value_bias.astype(jnp.float32)])

    def attend(item_args):
        query_item, key_item, value_item, length = item_args
        scores = masked_scores(query_item, key_item, length, score_scale)
        row_max = lax.optimization_barrier(jnp.max(scores, axis=1, keepdims=True))
        log_total = row_max + jnp.log(lax.optimization_barrier(jnp.sum(jnp.exp(scores - row_max), axis=1, keepdims=True)))
        attn_weight = jnp.exp(scores - log_total)
        mixed = jnp.einsum('qk,kd->qd', attn_weight, value_item.astype(jnp.float32), precision=lax.Precision.HIGHEST)
        return (mixed.astype(jnp.bfloat16), log_total[:, 0])

    def attend_back(item_args):
        query_item, key_item, value_item, mixed_item, grad_item, log_total, length = item_args
        scores = masked_scores(query_item, key_item, length, score_scale)
        attn_weight = jnp.exp(scores - log_total[:, None])
        grad_prob = jnp.einsum('qd,kd->qk', grad_item, value_item, preferred_element_type=jnp.float32)
        row_delta = lax.optimization_barrier(jnp.sum(grad_item.astype(jnp.float32) * mixed_item.astype(jnp.float32), axis=1))
        grad_score = (attn_weight * (grad_prob - row_delta[:, None]) * score_scale).astype(jnp.bfloat16)
        grad_query = jnp.dot(grad_score, key_item, preferred_element_type=jnp.float32).astype(jnp.bfloat16)
        grad_key = jnp.einsum('qk,qd->kd', grad_score, query_item, preferred_element_type=jnp.float32).astype(jnp.bfloat16)
        grad_value = jnp.einsum('qk,qd->kd', attn_weight.astype(jnp.bfloat16), grad_item, preferred_element_type=jnp.float32).astype(jnp.bfloat16)
        return (grad_query, grad_key, grad_value)

    def image_step(totals, inputs):
        image_tokens, image_grad, length = inputs
        token_rows = image_tokens.astype(jnp.float32)
        first_out, first_normed, first_inv = layer_norm(token_rows, gain_one, shift_one)
        first_input = first_out.astype(jnp.bfloat16)
        projected = (jnp.dot(first_input, packed_weight, preferred_element_type=jnp.float32) + packed_bias).astype(jnp.bfloat16)
        head_view = jnp.transpose(projected.reshape(seq_len, 3, HEADS, HEAD_DIM), (1, 2, 0, 3))
        head_lengths = jnp.full((HEADS,), length, jnp.int32)
        mixed_heads, log_totals = lax.map(attend, (head_view[0], head_view[1], head_view[2], head_lengths))
        mixed_rows = jnp.transpose(mixed_heads, (1, 0, 2)).reshape(seq_len, width)
        residual = token_rows + jnp.dot(mixed_rows, mixer_weight, preferred_element_type=jnp.float32) + mixer_bias.astype(jnp.float32)
        second_out, second_normed, second_inv = layer_norm(residual, gain_two, shift_two)
        second_input = second_out.astype(jnp.bfloat16)
        pre_act = jnp.dot(second_input, expand_weight, preferred_element_type=jnp.float32) + expand_bias.astype(jnp.float32)
        activated = gelu_value(pre_act).astype(jnp.bfloat16)
        block_out = (residual + jnp.dot(activated, shrink_weight, preferred_element_type=jnp.float32) + shrink_bias.astype(jnp.float32)).astype(jnp.bfloat16)
        grad_rows = image_grad.astype(jnp.float32)
        grad_shrink = jnp.einsum('rf,rd->fd', activated, image_grad, preferred_element_type=jnp.float32)
        grad_shrink_b = lax.optimization_barrier(jnp.sum(grad_rows, axis=0))
        grad_pre = jnp.einsum('rd,fd->rf', image_grad, shrink_weight, preferred_element_type=jnp.float32) * gelu_slope(pre_act)
        grad_pre_bf = grad_pre.astype(jnp.bfloat16)
        grad_expand = jnp.einsum('rd,rf->df', second_input, grad_pre_bf, preferred_element_type=jnp.float32)
        grad_expand_b = lax.optimization_barrier(jnp.sum(grad_pre, axis=0))
        grad_second = jnp.einsum('rf,df->rd', grad_pre_bf, expand_weight, preferred_element_type=jnp.float32)
        grad_gain_two = lax.optimization_barrier(jnp.sum(grad_second * second_normed, axis=0))
        grad_shift_two = lax.optimization_barrier(jnp.sum(grad_second, axis=0))
        grad_residual = grad_rows + norm_backward(grad_second, second_normed, second_inv, gain_two)
        grad_residual_bf = grad_residual.astype(jnp.bfloat16)
        grad_mixer = jnp.einsum('rd,re->de', mixed_rows, grad_residual_bf, preferred_element_type=jnp.float32)
        grad_mixer_b = lax.optimization_barrier(jnp.sum(grad_residual, axis=0))
        grad_mixed = jnp.einsum('re,de->rd', grad_residual_bf, mixer_weight, preferred_element_type=jnp.float32).astype(jnp.bfloat16)
        grad_mixed_heads = jnp.transpose(grad_mixed.reshape(seq_len, HEADS, HEAD_DIM), (1, 0, 2))
        grad_q, grad_k, grad_v = lax.map(attend_back, (head_view[0], head_view[1], head_view[2], mixed_heads, grad_mixed_heads, log_totals, head_lengths))
        grad_packed = jnp.transpose(jnp.stack([grad_q, grad_k, grad_v]), (2, 0, 1, 3)).reshape(seq_len, 3 * width)
        grad_packed_w = jnp.einsum('rd,re->de', first_input, grad_packed, preferred_element_type=jnp.float32)
        grad_packed_f = grad_packed.astype(jnp.float32)
        grad_query_b = lax.optimization_barrier(jnp.sum(grad_packed_f[:, :width], axis=0))
        grad_value_b = lax.optimization_barrier(jnp.sum(grad_packed_f[:, 2 * width:], axis=0))
        grad_first = jnp.einsum('re,de->rd', grad_packed, packed_weight, preferred_element_type=jnp.float32)
        grad_gain_one = lax.optimization_barrier(jnp.sum(grad_first * first_normed, axis=0))
        grad_shift_one = lax.optimization_barrier(jnp.sum(grad_first, axis=0))
        input_grad = (grad_residual + norm_backward(grad_first, first_normed, first_inv, gain_one)).astype(jnp.bfloat16)
        terms = (grad_gain_one, grad_shift_one, grad_packed_w, grad_query_b, grad_value_b, grad_mixer, grad_mixer_b, grad_gain_two, grad_shift_two, grad_expand, grad_expand_b, grad_shrink, grad_shrink_b)
        new_totals = tuple((total + term for total, term in zip(totals, terms)))
        return (new_totals, (block_out, input_grad))
    start_totals = (jnp.zeros((width,), jnp.float32), jnp.zeros((width,), jnp.float32), jnp.zeros((width, 3 * width), jnp.float32), jnp.zeros((width,), jnp.float32), jnp.zeros((width,), jnp.float32), jnp.zeros((width, width), jnp.float32), jnp.zeros((width,), jnp.float32), jnp.zeros((width,), jnp.float32), jnp.zeros((width,), jnp.float32), jnp.zeros((width, FF), jnp.float32), jnp.zeros((FF,), jnp.float32), jnp.zeros((FF, width), jnp.float32), jnp.zeros((width,), jnp.float32))
    totals, (block_output, input_grad) = lax.scan(image_step, start_totals, (tokens, cotangent, lengths))
    return (block_output, input_grad, totals[0], totals[1], totals[2], totals[3], totals[4], totals[5], totals[6], totals[7], totals[8], totals[9], totals[10], totals[11], totals[12])
```

```python
import functools
import math

import jax
import jax.numpy as jnp
from jax import lax
from jax.experimental import pallas as pl
from jax.experimental.pallas import tpu as pltpu
from jax.sharding import PartitionSpec as P

HEADS = 12
HEAD_DIM = 64
NORM_EPS = 1e-06
MASKED = -1e30
LOG2E = 1.4426950408889634
MESH = pl.DeviceIdType.MESH
ANY = pl.BlockSpec(memory_space=pl.ANY)
VM = pl.BlockSpec(memory_space=pltpu.VMEM)
SM = pl.BlockSpec(memory_space=pltpu.SMEM)
BF = jnp.bfloat16
F32 = jnp.float32
SPLIT = 2


def coords():
    ctx = lax.axis_index("ctx")
    return lax.axis_index("dp"), ctx // SPLIT, ctx % SPLIT, lax.axis_index("head")


def device(x, y, c, z):
    return (x, y * SPLIT + c, z)


def enter(targets):
    sem = pltpu.get_barrier_semaphore()
    for t in targets:
        pl.semaphore_signal(sem, inc=1, device_id=t, device_id_type=MESH)
    pl.semaphore_wait(sem, len(targets))


def rcopy(src, dst, ss, rs, to):
    return pltpu.make_async_remote_copy(src, dst, ss, rs, device_id=to, device_id_type=MESH)


def run_events(events):
    for _, fn in sorted(events, key=lambda e: e[0]):
        fn()


def partners(x, y, c, z):
    return dict(
        core=device(x, y, 1 - c, z),
        x=device(1 - x, y, c, z),
        y=device(x, 1 - y, c, z),
        z1=device(x, y, c, z ^ 1),
        z2=device(x, y, c, z ^ 2),
        z3=device(x, y, c, z ^ 3),
    )


def line_gather(events, z, inner, own, at, ss, rs, near, far, start, pace, arrived):
    def first():
        rcopy(own, at(z), ss.at[0], rs.at[z], near).start()

        @pl.when(inner)
        def _():
            rcopy(own, at(z), ss.at[1], rs.at[z], far).start()

    events.append((start, first))
    blocks = (z ^ 1, jnp.where(inner, z ^ 3, z ^ 2), jnp.where(inner, z ^ 2, z ^ 3))
    for k, b in enumerate(blocks):

        def land(k=k, b=b):
            rcopy(own, at(b), ss.at[0], rs.at[b], near).wait_recv()

            @pl.when(inner)
            def _():
                rcopy(at(b), at(b), ss.at[2 + k], rs.at[b], far if k == 0 else near).start()

            arrived(k, b)

        events.append((start + pace * (k + 1), land))

    def last():
        rcopy(own, at(z), ss.at[0], rs.at[z], near).wait_send()

        @pl.when(inner)
        def _():
            for k in range(4):
                rcopy(own, at(z), ss.at[1 + k], rs.at[z], near).wait_send()

    events.append((1000, last))


def weight_gather(events, co, to, w_in, w_out, local_sem, zss, zrs, ass, ars, bss, brs, css, crs, order, start, pace):
    x, y, c, z = co
    inner = jnp.logical_or(z == 1, z == 2)
    a, b = order

    def spot(fa, fb):
        px = jnp.where(fa, 1 - x, x) if a == "x" else jnp.where(fb, 1 - x, x)
        py = jnp.where(fa, 1 - y, y) if a == "y" else jnp.where(fb, 1 - y, y)
        return px, py

    def at(fa, fb, zz):
        px, py = spot(fa, fb)
        return w_out.at[px, py, c, zz]

    def group(fa, fb, cc):
        px, py = spot(fa, fb)
        return w_out.at[px, py, cc]

    F, T = False, True

    def begin():
        pltpu.make_async_copy(w_in, at(F, F, z), local_sem).start()
        rcopy(w_in, at(F, F, z), ass.at[0], ars.at[z], to[a]).start()
        rcopy(w_in, at(F, F, z), bss.at[0], brs.at[0, z], to[b]).start()

    events.append((start - 0.1, begin))
    order4 = (z, z ^ 1, jnp.where(inner, z ^ 3, z ^ 2), jnp.where(inner, z ^ 2, z ^ 3))

    def arrived(k, blk):
        rcopy(at(F, F, blk), at(F, F, blk), ass.at[k + 1], ars.at[blk], to[a]).start()
        rcopy(at(F, F, blk), at(F, F, blk), bss.at[k + 1], brs.at[0, blk], to[b]).start()

    line_gather(events, z, inner, w_in, lambda zz: at(F, F, zz), zss, zrs, to["z1"], to["z3"], start, pace, arrived)

    def core_send(k, fa, fb):
        g = group(fa, fb, c)
        rcopy(g, g, css.at[k], crs.at[k], to["core"]).start()

    def own_done():
        pltpu.make_async_copy(w_in, at(F, F, z), local_sem).wait()
        core_send(0, F, F)

    events.append((start + 3 * pace + 0.1, own_done))
    for k, blk in enumerate(order4):

        def a_land(k=k, blk=blk):
            d = at(T, F, blk)
            rcopy(d, d, ass.at[k], ars.at[blk], to[a]).wait_recv()
            rcopy(d, d, bss.at[4 + k], brs.at[1, blk], to[b]).start()

        events.append((start + (k + 1) * pace + 0.2, a_land))
    events.append((start + 4 * pace + 0.3, lambda: core_send(1, T, F)))
    for g in range(2):

        def b_land(g=g):
            for blk in order4:
                d = at(g == 1, T, blk)
                rcopy(d, d, bss.at[0], brs.at[g, blk], to[b]).wait_recv()
            core_send(2 + g, g == 1, T)

        events.append((start + (5 + 4 * g) * pace, b_land))

    def last():
        d = at(F, F, z)
        for k in range(4):
            rcopy(d, d, ass.at[k], ars.at[0], to[a]).wait_send()
        for k in range(8):
            rcopy(d, d, bss.at[k], brs.at[0, 0], to[b]).wait_send()
        for k, (fa, fb) in enumerate(((F, F), (T, F), (F, T), (T, T))):
            g = group(fa, fb, 1 - c)
            rcopy(g, g, css.at[k], crs.at[k], to["core"]).wait()

    events.append((1001, last))


def small_gather(events, co, to, src, out, ls, ss, rs, start, pace, spread):
    x, y, c, z = co
    own = src.at[z] if spread else src

    def begin():
        pltpu.make_async_copy(own, out.at[x, y, c, z], ls).start()
        for k in (1, 2, 3):
            rcopy(src.at[z ^ k] if spread else src, out.at[x, y, c, z], ss.at[k - 1], rs.at[k - 1], to["z%d" % k]).start()

    def step_y():
        pltpu.make_async_copy(own, out.at[x, y, c, z], ls).wait()
        for k in (1, 2, 3):
            d = out.at[x, y, c, z ^ k]
            rcopy(d, d, ss.at[k - 1], rs.at[k - 1], to["z1"]).wait()
        g = out.at[x, y, c]
        rcopy(g, g, ss.at[3], rs.at[3], to["y"]).start()

    def step_x():
        g = out.at[x, 1 - y, c]
        rcopy(g, g, ss.at[3], rs.at[3], to["y"]).wait()
        for yy in range(2):
            g = out.at[x, yy, c]
            rcopy(g, g, ss.at[4 + yy], rs.at[4 + yy], to["x"]).start()

    def step_c():
        for yy in range(2):
            g = out.at[1 - x, yy, c]
            rcopy(g, g, ss.at[4 + yy], rs.at[4 + yy], to["x"]).wait()
        for xx in range(2):
            for yy in range(2):
                g = out.at[xx, yy, c]
                rcopy(g, g, ss.at[6 + 2 * xx + yy], rs.at[6 + 2 * xx + yy], to["core"]).start()

    def last():
        for xx in range(2):
            for yy in range(2):
                g = out.at[xx, yy, 1 - c]
                rcopy(g, g, ss.at[6 + 2 * xx + yy], rs.at[6 + 2 * xx + yy], to["core"]).wait()

    for i, fn in enumerate((begin, step_y, step_x, step_c, last)):
        events.append((start + pace * i, fn))


def token_gather(events, co, to, tok, img, ls, yss, yrs, zss, zrs, css, crs, start, pace):
    x, y, c, z = co
    inner = jnp.logical_or(z == 1, z == 2)

    def begin():
        rcopy(tok.at[1 - y], img.at[y, c, z], yss, yrs, to["y"]).start()
        pltpu.make_async_copy(tok.at[y], img.at[y, c, z], ls).start()
        rcopy(tok.at[y], img.at[y, c, z], css.at[0, 0], crs.at[0, z], to["core"]).start()

    events.append((start - 0.1, begin))

    def other():
        d = img.at[1 - y, c, z]
        rcopy(d, d, yss, yrs, to["y"]).wait()
        rcopy(d, d, css.at[1, 0], crs.at[1, z], to["core"]).start()

    events.append((start + pace * 0.9, other))
    for r in range(2):
        row = y if r == 0 else 1 - y

        def arrived(k, blk, r=r, row=row):
            d = img.at[row, c, blk]
            rcopy(d, d, css.at[r, k + 1], crs.at[r, blk], to["core"]).start()

        own = tok.at[y] if r == 0 else img.at[1 - y, c, z]
        line_gather(
            events, z, inner, own, lambda zz, row=row: img.at[row, c, zz], zss.at[r], zrs.at[r], to["z1"], to["z3"], start + pace * r, 2 * pace, arrived
        )

    def last():
        pltpu.make_async_copy(tok.at[y], img.at[y, c, z], ls).wait()
        for r in range(2):
            for k in range(4):
                d = img.at[y if r == 0 else 1 - y, 1 - c, k]
                rcopy(d, d, css.at[r, k], crs.at[r, k], to["core"]).wait()

    events.append((start + 7.5 * pace, last))


def gather_kernel(tok, pk, mx, ex, sh, sv, img, pko, mxo, exo, sho, svo, ls, tys, tzs, tzr, tcs, tcr, ps, pr, vs, vr, *wsems):
    co = coords()
    to = partners(*co)
    enter(list(to.values()))
    ev = []
    token_gather(ev, co, to, tok, img, ls.at[0], tys.at[0], tys.at[1], tzs, tzr, tcs, tcr, 0.5, 4.0)
    small_gather(ev, co, to, sv, svo, ls.at[1], vs, vr, 0.0, 3.0, False)
    small_gather(ev, co, to, pk, pko, ls.at[2], ps, pr, 0.1, 5.0, True)
    per = len(wsems) // 3
    for i, (src, dst, order, start, pace) in enumerate(
        ((mx, mxo, "yx", 1.0, 3.0), (ex, exo, "xy", 2.0, 5.5), (sh, sho, "yx", 3.0, 5.5))
    ):
        weight_gather(ev, co, to, src, dst, ls.at[3 + i], *wsems[i * per : (i + 1) * per], order, start, pace)
    run_events(ev)


def gather_all(tok, pk, mx, ex, sh, sv):
    lead = (2, SPLIT, SPLIT, 4)
    D = pltpu.SemaphoreType.DMA
    wsem = [D((5,)), D((4,)), D((4,)), D((4,)), D((8,)), D((2, 4)), D((4,)), D((4,))]
    outs = [
        jax.ShapeDtypeStruct((2, 2, 4) + tok.shape[1:], BF),
        jax.ShapeDtypeStruct(lead + pk.shape[1:], BF),
        jax.ShapeDtypeStruct(lead + mx.shape, BF),
        jax.ShapeDtypeStruct(lead + ex.shape, BF),
        jax.ShapeDtypeStruct(lead + sh.shape, BF),
        jax.ShapeDtypeStruct(lead + sv.shape, BF),
    ]
    return pl.pallas_call(
        gather_kernel,
        out_shape=outs,
        in_specs=[ANY] * 6,
        out_specs=[ANY] * 6,
        scratch_shapes=[D((6,)), D((2,)), D((2, 5)), D((2, 4)), D((2, 4)), D((2, 4)), D((10,)), D((10,)), D((10,)), D((10,))] + wsem * 3,
        compiler_params=pltpu.CompilerParams(collective_id=0, has_side_effects=True),
        name="gather_tokens_weights",
    )(tok, pk, mx, ex, sh, sv)


def gather_generic(tok, pk, mx, ex, sh, sv):
    every = ("dp", "ctx", "head")
    images = lax.all_gather(tok, ("ctx", "head"), axis=1, tiled=True)
    img = lax.dynamic_index_in_dim(images, coords()[1], 0, keepdims=False)
    spread = lax.all_gather(pk, every, axis=1, tiled=True)
    pko = lax.dynamic_index_in_dim(spread, lax.axis_index("head"), 0, keepdims=False)
    return [img, pko] + [lax.all_gather(t, every, axis=0, tiled=True) for t in (mx, ex, sh, sv)]


def exchange_kernel(src, dst, ls, ss, rs):
    x, y, c, z = coords()
    others = [(dy, dz) for dy in range(2) for dz in range(4) if dy or dz]
    enter([device(x, y ^ dy, c, z ^ dz) for dy, dz in others])
    me = y * 4 + z
    mine = pltpu.make_async_copy(src.at[me], dst.at[me], ls)
    mine.start()
    copies = []
    for i, (dy, dz) in enumerate(others):
        ty, tz = y ^ dy, z ^ dz
        cp = rcopy(src.at[ty * 4 + tz], dst.at[me], ss.at[i], rs.at[i], device(x, ty, c, tz))
        cp.start()
        copies.append(cp)
    mine.wait()
    for cp in copies:
        cp.wait()


def exchange(src, cid):
    D = pltpu.SemaphoreType.DMA
    return pl.pallas_call(
        exchange_kernel,
        out_shape=jax.ShapeDtypeStruct(src.shape, src.dtype),
        in_specs=[ANY],
        out_specs=ANY,
        scratch_shapes=[D, D((7,)), D((7,))],
        compiler_params=pltpu.CompilerParams(collective_id=cid, has_side_effects=True),
        name="exchange_heads_%d" % cid,
    )(src)


def dot(a, b):
    return jnp.dot(a, b, preferred_element_type=F32)


def dot_nt(a, b):
    return lax.dot_general(a, b, (((1,), (1,)), ((), ())), preferred_element_type=F32)


def row_norm(rows):
    mean = jnp.mean(rows, axis=-1, keepdims=True)
    centred = rows - mean
    inv = lax.rsqrt(jnp.mean(centred * centred, axis=-1, keepdims=True) + NORM_EPS)
    return centred * inv, inv


def forward_kernel(lens, img, pw, gain, shift, bias, mixed, lse, fi, qt, q, k, kt, v, vt):
    x, y, c, z = coords()
    heads = k.shape[0]
    length = lens[y]
    keys = k.shape[1]
    hd = HEAD_DIM
    step = 256

    def project(g, carry):
        rows = img[pl.ds(2 * g, 2)].reshape(step, img.shape[2]).astype(F32)
        normed, _ = row_norm(rows)
        first = (normed * gain[...] + shift[...]).astype(BF)
        off = pl.multiple_of(g * step, step)
        fi[pl.ds(off, step), :] = first
        qkv = dot(first, pw[...]) + bias[...]
        qkv = qkv.astype(BF).astype(F32)
        width = heads * hd
        qv = qkv[:, :width] * (1.0 / math.sqrt(hd))
        kv = qkv[:, width : 2 * width]
        vv = qkv[:, 2 * width :]
        qt[g] = qv.T.astype(BF)
        kt[g] = kv.T.astype(BF)
        vt[g] = vv.T.astype(BF)
        pos = off + lax.broadcasted_iota(jnp.int32, (step, hd), 0)
        lane = lax.broadcasted_iota(jnp.int32, (step, hd), 1)
        hide = jnp.where(lane == 0, jnp.where(pos < length, 0.0, MASKED), jnp.where(lane < 4, 1.0, 0.0))
        ones = jnp.where(jnp.logical_and(lane > 0, lane < 4), 1.0, 0.0)
        for h in range(heads):
            k[h, pl.ds(off, step), :] = jnp.concatenate([kv[:, h * hd : (h + 1) * hd], hide], axis=1).astype(BF)
            v[h, pl.ds(off, step), :] = jnp.concatenate([vv[:, h * hd : (h + 1) * hd], ones], axis=1).astype(BF)
            q[g, h] = qv[:, h * hd : (h + 1) * hd].astype(BF)
        return carry

    lax.fori_loop(0, keys // step, project, 0)
    chunk = 512
    row = lax.broadcasted_iota(jnp.int32, (hd, step), 0)
    extra = jnp.where(row == 0, 1.0, 0.0).astype(BF)

    def attend(j, carry):
        g = (j // 2) * 4 + c * 2 + j % 2
        for h in range(heads):
            qa = jnp.concatenate([qt[g, h * hd : (h + 1) * hd, :], extra], axis=0)
            top = jnp.full((1, step), MASKED, F32)
            total = jnp.zeros((1, step), F32)
            acc = jnp.zeros((hd, step), F32)
            for kc in range(keys // chunk):
                s = dot(k[h, kc * chunk : (kc + 1) * chunk, :], qa)
                new = jnp.maximum(top, jnp.max(s, axis=0, keepdims=True))
                p = jnp.exp2((s - new) * LOG2E)
                scale = jnp.exp2((top - new) * LOG2E)
                total = total * scale + jnp.sum(p, axis=0, keepdims=True)
                part = None
                pb = p.astype(BF)
                for i in range(chunk // step):
                    t = dot(vt[kc * (chunk // step) + i, h * hd : (h + 1) * hd, :], pb[i * step : (i + 1) * step])
                    part = t if part is None else part + t
                acc = acc * scale + part
                top = new
            out = acc / total
            lse[j, h] = top + jnp.log(total)
            for i in range(2):
                mixed[2 * j + i, h * hd : (h + 1) * hd, :] = out[:, i * 128 : (i + 1) * 128].astype(BF)
        return carry

    lax.fori_loop(0, 4, attend, 0)


def attention_forward(lens, img, pw, gain, shift, bias):
    heads = pw.shape[1] // (3 * HEAD_DIM)
    keys = img.shape[0] * img.shape[1]
    width = heads * HEAD_DIM
    n = keys // 256
    outs = [
        jax.ShapeDtypeStruct((8, width, 128), BF),
        jax.ShapeDtypeStruct((4, heads, 1, 256), F32),
        jax.ShapeDtypeStruct((keys, img.shape[2]), BF),
        jax.ShapeDtypeStruct((n, width, 256), BF),
        jax.ShapeDtypeStruct((n, heads, 256, HEAD_DIM), BF),
        jax.ShapeDtypeStruct((heads, keys, 2 * HEAD_DIM), BF),
        jax.ShapeDtypeStruct((n, width, 256), BF),
        jax.ShapeDtypeStruct((heads, keys, 2 * HEAD_DIM), BF),
    ]
    return pl.pallas_call(
        forward_kernel,
        out_shape=outs,
        in_specs=[SM] + [VM] * 5,
        out_specs=[VM] * 8,
        scratch_shapes=[pltpu.VMEM((n, width, 256), BF)],
        compiler_params=pltpu.CompilerParams(vmem_limit_bytes=50 << 20),
        name="attention_forward",
    )(lens, img, pw, gain, shift, bias)


def split3(value):
    hi = value.astype(BF)
    rest = value - hi.astype(F32)
    mid = rest.astype(BF)
    low = (rest - mid.astype(F32)).astype(BF)
    return hi, mid, low


def backward_kernel(grad, mixed, lse, qt, q, k, kt, v, out, dk, dv):
    x, y, c, z = coords()
    heads, keys = k.shape[0], k.shape[1]
    hd = HEAD_DIM
    width = heads * hd
    step = 256
    chunk = 512
    scale = 1.0 / math.sqrt(hd)
    row = lax.broadcasted_iota(jnp.int32, (hd, step), 0)
    dk[...] = jnp.zeros_like(dk)
    dv[...] = jnp.zeros_like(dv)

    def clear(i, carry):
        out[pl.ds(pl.multiple_of(i * step, step), step), :] = jnp.zeros((step, 3 * width), BF)
        return carry

    lax.fori_loop(0, keys // step, clear, 0)

    def one(j, carry):
        g = (j // 2) * 4 + c * 2 + j % 2
        off = pl.multiple_of(g * step, step)
        for h in range(heads):
            sl = slice(h * hd, (h + 1) * hd)
            do = jnp.concatenate([grad[2 * j, sl, :], grad[2 * j + 1, sl, :]], axis=1)
            mx = jnp.concatenate([mixed[2 * j, sl, :], mixed[2 * j + 1, sl, :]], axis=1)
            dof = do.astype(F32)
            delta = jnp.sum(dof * mx.astype(F32), axis=0, keepdims=True)
            a, b, d = split3(-lse[j, h])
            e0, e1, e2 = split3(-delta)
            qx = jnp.where(row == 0, 1.0, 0.0) + jnp.where(row == 1, a.astype(F32), 0.0) + jnp.where(row == 2, b.astype(F32), 0.0) + jnp.where(row == 3, d.astype(F32), 0.0)
            dx = jnp.where(row == 1, e0.astype(F32), 0.0) + jnp.where(row == 2, e1.astype(F32), 0.0) + jnp.where(row == 3, e2.astype(F32), 0.0)
            qa = jnp.concatenate([qt[g, sl, :], qx.astype(BF)], axis=0)
            da = jnp.concatenate([do, dx.astype(BF)], axis=0)
            dor = dof.T.astype(BF)
            qr = q[g, h]
            dq = jnp.zeros((hd, step), F32)
            for kc in range(keys // chunk):
                rows = slice(kc * chunk, (kc + 1) * chunk)
                p = jnp.exp2(dot(k[h, rows, :], qa) * LOG2E)
                dp = dot(v[h, rows, :], da)
                ds = (p * dp).astype(BF)
                pb = p.astype(BF)
                dk[h, rows, :] += dot(ds, qr)
                dv[h, rows, :] += dot(pb, dor)
                for i in range(chunk // step):
                    dq += dot(kt[kc * (chunk // step) + i, sl, :], ds[i * step : (i + 1) * step])
            out[pl.ds(off, step), sl] = (dq.T * scale).astype(BF)
        return carry

    lax.fori_loop(0, 4, one, 0)
    for h in range(heads):
        for r in range(keys // step):
            rows = slice(r * step, (r + 1) * step)
            out[rows, width + h * hd : width + (h + 1) * hd] = dk[h, rows, :].astype(BF)
            out[rows, 2 * width + h * hd : 2 * width + (h + 1) * hd] = dv[h, rows, :].astype(BF)


def attention_backward(grad, mixed, lse, qt, q, k, kt, v):
    heads, keys = k.shape[0], k.shape[1]
    return pl.pallas_call(
        backward_kernel,
        out_shape=jax.ShapeDtypeStruct((keys, 3 * heads * HEAD_DIM), BF),
        in_specs=[VM] * 8,
        out_specs=VM,
        scratch_shapes=[pltpu.VMEM((heads, keys, HEAD_DIM), F32)] * 2,
        compiler_params=pltpu.CompilerParams(vmem_limit_bytes=50 << 20),
        name="attention_backward",
    )(grad, mixed, lse, qt, q, k, kt, v)


def reduce_rows(events, co, to, g, out, acc, r0, r1, r2, r3, cs, cr, as_, ar, bs, br, zs, zr, order, start, pace, sum_z):
    x, y, c, z = co
    a, b = order

    def spot(fa, fb):
        px = (1 - x if fa else x) if a == "x" else (1 - x if fb else x)
        py = (1 - y if fa else y) if a == "y" else (1 - y if fb else y)
        return px, py

    seq = ((True, True), (True, False), (False, True), (False, False))

    def begin():
        for i, (fa, fb) in enumerate(seq):
            px, py = spot(fa, fb)
            rcopy(g.at[px, py, 1 - c], r0.at[px, py], cs.at[i], cr.at[i], to["core"]).start()

    events.append((start, begin))

    def add(dst, one, two, pick):
        def body(i, carry):
            dst[pick + (i,)] = (one(i).astype(F32) + two(i).astype(F32)).astype(dst.dtype)
            return carry

        lax.fori_loop(0, 4, body, 0)

    for i, (fa, fb) in enumerate(seq):

        def core_land(i=i, fa=fa, fb=fb):
            px, py = spot(fa, fb)
            rcopy(g.at[px, py, 1 - c], r0.at[px, py], cs.at[i], cr.at[i], to["core"]).wait_recv()
            add(acc, lambda j: g[px, py, c, j], lambda j: r0[px, py, j], (px, py))
            if fa:
                n = 0 if fb else 1
                rcopy(acc.at[px, py], r1.at[n], as_.at[n], ar.at[n], to[a]).start()

        events.append((start + pace * 0.5 * (i + 1), core_land))
    for n, fb in enumerate((True, False)):

        def a_land(n=n, fb=fb):
            px, py = spot(False, fb)
            rcopy(r1.at[n], r1.at[n], as_.at[n], ar.at[n], to[a]).wait_recv()
            add(acc, lambda j: acc[px, py, j], lambda j: r1[n, j], (px, py))
            if fb:
                rcopy(acc.at[px, py], r2, bs, br, to[b]).start()

        events.append((start + pace * (3 + 2 * n), a_land))

    def b_land():
        rcopy(r2, r2, bs, br, to[b]).wait_recv()
        add(acc, lambda j: acc[x, y, j], lambda j: r2[j], (x, y))
        for kk in (1, 2, 3):
            rcopy(acc.at[x, y, z ^ kk], r3.at[kk - 1], zs.at[kk - 1], zr.at[kk - 1], to["z%d" % kk]).start()

    events.append((start + pace * 6, b_land))

    def last():
        for kk in range(3):
            rcopy(r3.at[kk], r3.at[kk], zs.at[kk], zr.at[kk], to["z1"]).wait()
        if sum_z:
            out[...] = acc[x, y, z].astype(F32) + r3[0].astype(F32) + r3[1].astype(F32) + r3[2].astype(F32)
        else:
            out[z] = acc[x, y, z].astype(F32)
            for kk in (1, 2, 3):
                out[z ^ kk] = r3[kk - 1].astype(F32)
        for i, (fa, fb) in enumerate(seq):
            px, py = spot(fa, fb)
            rcopy(g.at[px, py, 1 - c], r0.at[px, py], cs.at[i], cr.at[i], to["core"]).wait_send()
        for n in range(2):
            rcopy(r1.at[n], r1.at[n], as_.at[n], ar.at[n], to[a]).wait_send()
        rcopy(r2, r2, bs, br, to[b]).wait_send()

    events.append((start + pace * 9, last))


def reduce_tokens(events, co, to, g, out, acc, r0, rz, ry, sy, cs, cr, zs, zr, ys, yr, start, pace):
    x, y, c, z = co

    def begin():
        for yy in range(2):
            rcopy(g.at[yy, 1 - c], r0.at[yy], cs.at[yy], cr.at[yy], to["core"]).start()

    events.append((start, begin))
    for r in range(2):
        row = 1 - y if r == 0 else y

        def core_land(r=r, row=row):
            rcopy(g.at[row, 1 - c], r0.at[row], cs.at[row], cr.at[row], to["core"]).wait()

            def body(i, carry):
                acc[row, i] = (g[row, c, i].astype(F32) + r0[row, i].astype(F32)).astype(BF)
                return carry

            lax.fori_loop(0, 4, body, 0)
            for kk in (1, 2, 3):
                rcopy(acc.at[row, z ^ kk], rz.at[r, kk - 1], zs.at[r, kk - 1], zr.at[r, kk - 1], to["z%d" % kk]).start()

        events.append((start + 0.4 * pace + 0.3 * pace * r, core_land))

        def z_land(r=r, row=row):
            for kk in range(3):
                rcopy(rz.at[r, kk], rz.at[r, kk], zs.at[r, kk], zr.at[r, kk], to["z1"]).wait()
            total = acc[row, z].astype(F32) + rz[r, 0].astype(F32) + rz[r, 1].astype(F32) + rz[r, 2].astype(F32)
            if r == 0:
                sy[...] = total.astype(BF)
                rcopy(sy, ry, ys, yr, to["y"]).start()
            else:
                out[y] = total

        events.append((start + pace * (2 + r), z_land))

    def last():
        rcopy(sy, ry, ys, yr, to["y"]).wait()
        out[1 - y] = ry[...].astype(F32)

    events.append((start + pace * 3.5, last))


def reduce_kernel(gf, gp, gm, ge, gs, gv, of, op, om, oe, os_, ov, *rest):
    co = coords()
    to = partners(*co)
    enter(list(to.values()))
    ev = []
    tok = rest[:11]
    reduce_tokens(ev, co, to, gf, of, *tok[:5], *tok[5:11], 0.5, 8.0)
    rest = rest[11:]
    per = 13
    for i, (g, o, order, start, pace, sum_z) in enumerate(
        (
            (gs, os_, "xy", 1.0, 6.0, True),
            (ge, oe, "yx", 1.1, 6.0, True),
            (gm, om, "yx", 1.2, 6.1, True),
            (gp, op, "xy", 1.3, 6.2, False),
            (gv, ov, "yx", 1.4, 6.3, True),
        )
    ):
        reduce_rows(ev, co, to, g, o, *rest[i * per : (i + 1) * per], order, start, pace, sum_z)
    run_events(ev)


def reduce_all(gf, gp, gm, ge, gs, gv):
    D = pltpu.SemaphoreType.DMA
    tail = gf.shape[3:]
    scr = [
        pltpu.VMEM((2, 4) + tail, BF),
        pltpu.VMEM((2, 4) + tail, BF),
        pltpu.VMEM((2, 3) + tail, BF),
        pltpu.VMEM(tail, BF),
        pltpu.VMEM(tail, BF),
        D((2,)),
        D((2,)),
        D((2, 3)),
        D((2, 3)),
        D,
        D,
    ]
    outs = [jax.ShapeDtypeStruct((2,) + tail, F32)]
    for g, spread in ((gp, True), (gm, False), (ge, False), (gs, False), (gv, False)):
        blk = g.shape[4:]
        outs.append(jax.ShapeDtypeStruct(((4,) if spread else ()) + blk, F32))
    for g in (gs, ge, gm, gp, gv):
        blk = g.shape[4:]
        dt = g.dtype
        scr += [
            pltpu.VMEM((2, 2, 4) + blk, dt),
            pltpu.VMEM((2, 2, 4) + blk, dt),
            pltpu.VMEM((2, 4) + blk, dt),
            pltpu.VMEM((4,) + blk, dt),
            pltpu.VMEM((3,) + blk, dt),
            D((4,)),
            D((4,)),
            D((2,)),
            D((2,)),
            D,
            D,
            D((3,)),
            D((3,)),
        ]
    return pl.pallas_call(
        reduce_kernel,
        out_shape=outs,
        in_specs=[VM] * 6,
        out_specs=[VM] * 6,
        scratch_shapes=scr,
        compiler_params=pltpu.CompilerParams(collective_id=3, has_side_effects=True, vmem_limit_bytes=60 << 20),
        name="reduce_gradients",
    )(gf, gp, gm, ge, gs, gv)


def reduce_generic(gf, gp, gm, ge, gs, gv, n_dev):
    every = ("dp", "ctx", "head")
    x, y, c, z = coords()
    flat = gf.reshape((1, -1) + gf.shape[-1:])
    both = jnp.concatenate([jnp.where(y == i, flat, jnp.zeros_like(flat)) for i in range(2)], axis=0)
    of = lax.psum_scatter(both.astype(F32), ("ctx", "head"), scatter_dimension=1, tiled=True)
    cols = gp.shape[-1]
    rows = gp.size // cols
    spread = lax.dynamic_update_slice_in_dim(jnp.zeros((rows, 4, cols), F32), gp.reshape(rows, 1, cols).astype(F32), z, 1)
    op = jnp.swapaxes(lax.psum_scatter(spread, every, scatter_dimension=0, tiled=True), 0, 1)
    rest = [
        lax.psum_scatter(g.reshape((n_dev, -1) + g.shape[-1:]).astype(F32), every, scatter_dimension=0, tiled=True)[0] for g in (gm, ge, gs, gv)
    ]
    return [of, op] + rest


def layer_norm(token_rows, norm_gain, norm_shift):
    normed, inv_std = row_norm(token_rows)
    return (normed * norm_gain + norm_shift, normed, inv_std)


def norm_backward(grad_out, normed, inv_std, norm_gain):
    scaled = grad_out * norm_gain
    first_mean = jnp.mean(scaled, axis=-1, keepdims=True)
    second_mean = jnp.mean(scaled * normed, axis=-1, keepdims=True)
    return inv_std * (scaled - first_mean - normed * second_mean)


def gelu_parts(pre_act):
    cumulative = 0.5 * (1.0 + jax.scipy.special.erf(pre_act * (1.0 / math.sqrt(2.0))))
    density = jnp.exp(-0.5 * pre_act * pre_act) * (1.0 / math.sqrt(2.0 * math.pi))
    return pre_act * cumulative, cumulative + pre_act * density


def on_device(
    tokens,
    cotangent,
    lengths,
    attention_gain,
    attention_shift,
    packed_weight,
    query_bias,
    value_bias,
    mixer_weight,
    mixer_bias,
    feedforward_gain,
    feedforward_shift,
    expand_weight,
    expand_bias,
    shrink_weight,
    shrink_bias,
):
    images, shard_len, width = tokens.shape
    groups = lax.axis_size("head")
    heads = HEADS // groups
    part = heads * HEAD_DIM
    hidden = expand_weight.shape[1]
    rows = images * shard_len
    n_dev = lax.axis_size("dp") * lax.axis_size("ctx") * groups
    z = lax.axis_index("head")
    wr = packed_weight.shape[0]
    fr = shrink_weight.shape[0]

    tiled = wr % 8 == 0 and fr % 8 == 0 and lax.axis_size("dp") == 2
    slab = (lambda r, n: (r // 8, 8, n)) if tiled else (lambda r, n: (r, n))
    pk = jnp.transpose(packed_weight.reshape(wr, 3, groups, part), (2, 0, 1, 3)).reshape((groups,) + slab(wr, 3 * part))
    vecs = [attention_gain, attention_shift, query_bias, value_bias, mixer_bias, feedforward_gain, feedforward_shift, shrink_bias, expand_bias]
    sv = jnp.stack([jnp.pad(v, (0, 128 - v.shape[0])) for v in vecs] + [jnp.zeros((128,), BF)] * 7)
    img, pko, mxo, exo, sho, svo = (gather_all if tiled else gather_generic)(
        tokens,
        pk,
        mixer_weight.reshape(slab(wr, width)),
        expand_weight.reshape(slab(wr, hidden)),
        shrink_weight.reshape(slab(fr, width)),
        sv,
    )
    full_packed = pko.reshape(width, 3 * part)
    full_mixer = mxo.reshape(width, width)
    full_expand = exo.reshape(width, hidden)
    full_shrink = sho.reshape(hidden, width)
    svo = svo.reshape(n_dev, 16, 128).astype(F32)
    gain_one, shift_one, qb, vb, mb, gain_two, shift_two, sb = [svo[:, i, :wr].reshape(width) for i in range(8)]
    eb = svo[:, 8, :fr].reshape(hidden)
    own = lambda v: lax.dynamic_slice_in_dim(v, z * part, part)
    bias = jnp.concatenate([own(qb), jnp.zeros((part,), F32), own(vb)])
    img = img.reshape(16, shard_len, width)
    mixed_t, lse, fi, qt, q, k, kt, v = attention_forward(lengths, img, full_packed, gain_one[None], shift_one[None], bias[None])
    mix = exchange(mixed_t, 1).reshape(images, width, shard_len)

    token_rows = tokens.reshape(rows, width).astype(F32)
    mixed_rows = jnp.swapaxes(mix, 1, 2).reshape(rows, width)
    residual = token_rows + dot(mixed_rows, full_mixer) + mb
    second_out, second_normed, second_inv = layer_norm(residual, gain_two, shift_two)
    second_input = second_out.astype(BF)
    pre_act = dot(second_input, full_expand) + eb
    value, slope = gelu_parts(pre_act)
    activated = value.astype(BF)
    block_output = (residual + dot(activated, full_shrink) + sb).astype(BF)
    grad_in = cotangent.reshape(rows, width)
    grad_rows = grad_in.astype(F32)
    grad_shrink = jnp.einsum("rf,rd->fd", activated, grad_in, preferred_element_type=F32).astype(BF)
    grad_shrink_b = jnp.sum(grad_rows, axis=0)
    grad_pre = jnp.einsum("rd,fd->rf", grad_in, full_shrink, preferred_element_type=F32) * slope
    grad_pre_bf = grad_pre.astype(BF)
    grad_expand = jnp.einsum("rd,rf->df", second_input, grad_pre_bf, preferred_element_type=F32).astype(BF)
    grad_expand_b = jnp.sum(grad_pre, axis=0)
    grad_second = jnp.einsum("rf,df->rd", grad_pre_bf, full_expand, preferred_element_type=F32)
    grad_gain_two = jnp.sum(grad_second * second_normed, axis=0)
    grad_shift_two = jnp.sum(grad_second, axis=0)
    grad_residual = grad_rows + norm_backward(grad_second, second_normed, second_inv, gain_two)
    grad_residual_bf = grad_residual.astype(BF)
    grad_mixer = jnp.einsum("rd,re->de", mixed_rows, grad_residual_bf, preferred_element_type=F32).astype(BF)
    grad_mixer_b = jnp.sum(grad_residual, axis=0)
    grad_mixed = jnp.einsum("de,ire->idr", full_mixer, grad_residual_bf.reshape(images, shard_len, width), preferred_element_type=F32).astype(BF)
    grad_t = exchange(grad_mixed.reshape(images * groups, part, shard_len), 2)

    dqkv = attention_backward(grad_t, mixed_t, lse, qt, q, k, kt, v)
    grad_packed_w = jnp.einsum("rd,re->de", fi, dqkv, preferred_element_type=F32).astype(BF)
    grad_first_part = jnp.einsum("re,de->rd", dqkv, full_packed, preferred_element_type=F32)
    img_rows = img.reshape(16 * shard_len, width).astype(F32)
    img_normed, _ = row_norm(img_rows)
    grad_gain_one = jnp.sum(grad_first_part * img_normed, axis=0)
    grad_shift_one = jnp.sum(grad_first_part, axis=0)
    dsum = jnp.sum(dqkv.astype(F32), axis=0)
    place = lambda v: lax.dynamic_update_slice_in_dim(jnp.zeros((width,), F32), v, z * part, 0)
    grad_query_b = place(dsum[:part])
    grad_value_b = place(dsum[2 * part :])

    vec_grads = [grad_gain_one, grad_shift_one, grad_query_b, grad_value_b, grad_mixer_b, grad_gain_two, grad_shift_two, grad_shrink_b, grad_expand_b]
    gv = jnp.stack(
        [jnp.pad(g.reshape(n_dev, -1), ((0, 0), (0, 128 - g.shape[0] // n_dev))) for g in vec_grads] + [jnp.zeros((n_dev, 128), F32)] * 7, axis=1
    )
    lead = (2, SPLIT, SPLIT, groups) if tiled else (n_dev,)
    of, op, om, oe, os_, ov = (reduce_all if tiled else functools.partial(reduce_generic, n_dev=n_dev))(
        grad_first_part.astype(BF).reshape(2, 2, groups, shard_len, width),
        grad_packed_w.reshape(lead + slab(wr, 3 * part)),
        grad_mixer.reshape(lead + slab(wr, width)),
        grad_expand.reshape(lead + slab(wr, hidden)),
        grad_shrink.reshape(lead + slab(fr, width)),
        gv.reshape(lead + (16, 128)),
    )
    grad_first = of.reshape(rows, width)
    _, first_normed, first_inv = layer_norm(token_rows, gain_one, shift_one)
    input_grad = (grad_residual + norm_backward(grad_first, first_normed, first_inv, gain_one)).astype(BF)
    out_packed = jnp.transpose(op.reshape(groups, wr, 3, part), (1, 2, 0, 3)).reshape(wr, 3 * width)
    vec = [ov[i, :wr] for i in range(8)]
    return (
        block_output.reshape(images, shard_len, width),
        input_grad.reshape(images, shard_len, width),
        vec[0],
        vec[1],
        out_packed,
        vec[2],
        vec[3],
        om.reshape(wr, width),
        vec[4],
        vec[5],
        vec[6],
        oe.reshape(wr, hidden),
        ov[8, :fr],
        os_.reshape(fr, width),
        vec[7],
    )


def solution(mesh):
    every = ("dp", "ctx", "head")
    tok, vec, mat = P("dp", ("ctx", "head"), None), P(every), P(every, None)
    in_specs = (tok, tok, P("dp"), vec, vec, mat, vec, vec, mat, vec, vec, vec, mat, vec, mat, vec)
    out_specs = (tok, tok, vec, vec, mat, vec, vec, mat, vec, vec, vec, mat, vec, mat, vec)
    return jax.shard_map(on_device, mesh=mesh, in_specs=in_specs, out_specs=out_specs, check_vma=False)
```

```python
import functools
import math

import jax
import jax.numpy as jnp
from jax import lax
from jax.experimental import pallas as pl
from jax.experimental.pallas import tpu as pltpu
from jax.sharding import PartitionSpec as P

HEADS = 12
HEAD_DIM = 64
NORM_EPS = 1e-06
MASKED = -1e30
LOG2E = 1.4426950408889634
MESH = pl.DeviceIdType.MESH
ANY = pl.BlockSpec(memory_space=pl.ANY)
VM = pl.BlockSpec(memory_space=pltpu.VMEM)
SM = pl.BlockSpec(memory_space=pltpu.SMEM)
BF = jnp.bfloat16
F32 = jnp.float32
SPLIT = 2


def coords():
    ctx = lax.axis_index("ctx")
    return lax.axis_index("dp"), ctx // SPLIT, ctx % SPLIT, lax.axis_index("head")


def device(x, y, c, z):
    return (x, y * SPLIT + c, z)


def enter(targets):
    sem = pltpu.get_barrier_semaphore()
    for t in targets:
        pl.semaphore_signal(sem, inc=1, device_id=t, device_id_type=MESH)
    pl.semaphore_wait(sem, len(targets))


def rcopy(src, dst, ss, rs, to):
    return pltpu.make_async_remote_copy(src, dst, ss, rs, device_id=to, device_id_type=MESH)


def run_events(events):
    for _, fn in sorted(events, key=lambda e: e[0]):
        fn()


def partners(x, y, c, z):
    return dict(
        core=device(x, y, 1 - c, z),
        x=device(1 - x, y, c, z),
        y=device(x, 1 - y, c, z),
        z1=device(x, y, c, z ^ 1),
        z2=device(x, y, c, z ^ 2),
        z3=device(x, y, c, z ^ 3),
    )


def weight_gather(ev, co, to, src, out, sems, order, times):
    x, y, c, z = co
    lsem, zss, zrs, ass, ars, bss, brs, css, crs = sems
    a, b = order

    def spot(fa, fb):
        px = (1 - x if fa else x) if a == "x" else (1 - x if fb else x)
        py = (1 - y if fa else y) if a == "y" else (1 - y if fb else y)
        return px, py

    def at(fa, fb, k):
        return out(*spot(fa, fb), c, z ^ k)

    def group(fa, fb, cc):
        return out(*spot(fa, fb), cc, slice(None))

    F, T = False, True
    zsend = lambda i, k, ref, dst, name: rcopy(ref, dst, zss.at[i], zrs.at[k], to[name])
    asend = lambda k, ref: rcopy(ref, at(F, F, k), ass.at[k], ars.at[k], to[a])
    bsend = lambda fa, k, ref: rcopy(ref, at(fa, F, k), bss.at[int(fa), k], brs.at[int(fa), k], to[b])
    csend = lambda i, g: rcopy(g, g, css.at[i], crs.at[i], to["core"])
    local = lambda: pltpu.make_async_copy(src, at(F, F, 0), lsem)

    def begin():
        local().start()
        asend(0, src).start()
        bsend(F, 0, src).start()

    def z_begin():
        zsend(0, 0, src, at(F, F, 0), "z1").start()
        zsend(1, 1, src, at(F, F, 0), "z2").start()

    def z_land(k):
        d = at(F, F, k)
        zsend(k - 1, k - 1, d, d, "z1").wait_recv()
        if k == 2:
            zsend(2, 2, d, d, "z1").start()
        asend(k, d).start()
        bsend(F, k, d).start()

    def own_done():
        local().wait()
        csend(0, group(F, F, c)).start()

    def a_land(k):
        d = at(T, F, k)
        asend(k, d).wait_recv()
        bsend(T, k, d).start()
        if k == 3:
            csend(1, group(T, F, c)).start()

    def b_land(fa):
        for k in range(4):
            bsend(fa, k, at(fa, T, k)).wait_recv()
        csend(2 + int(fa), group(fa, T, c)).start()

    def last():
        d = at(F, F, 0)
        for i in range(3):
            zsend(i, 0, d, d, "z1").wait_send()
        for k in range(4):
            asend(k, d).wait_send()
            bsend(F, k, d).wait_send()
            bsend(T, k, d).wait_send()
        for i, (fa, fb) in enumerate(((F, F), (T, F), (F, T), (T, T))):
            csend(i, group(fa, fb, 1 - c)).wait()

    t_begin, t_z, t_zl, t_al, t_bl = times
    ev.append((t_begin, begin))
    ev.append((t_z, z_begin))
    for k in range(1, 4):
        ev.append((t_zl[k - 1], functools.partial(z_land, k)))
    ev.append((t_zl[2] + 0.3, own_done))
    for k in range(4):
        ev.append((t_al[k], functools.partial(a_land, k)))
    ev.append((t_bl[0], functools.partial(b_land, F)))
    ev.append((t_bl[1], functools.partial(b_land, T)))
    ev.append((1000.0, last))


def small_gather(co, to, src, out, ls, ss, rs, spread):
    x, y, c, z = co
    own = src.at[z] if spread else src

    def begin():
        pltpu.make_async_copy(own, out.at[x, y, c, z], ls).start()
        for k in (1, 2, 3):
            rcopy(src.at[z ^ k] if spread else src, out.at[x, y, c, z], ss.at[k - 1], rs.at[k - 1], to["z%d" % k]).start()

    def step_y():
        pltpu.make_async_copy(own, out.at[x, y, c, z], ls).wait()
        for k in (1, 2, 3):
            d = out.at[x, y, c, z ^ k]
            rcopy(d, d, ss.at[k - 1], rs.at[k - 1], to["z1"]).wait()
        g = out.at[x, y, c]
        rcopy(g, g, ss.at[3], rs.at[3], to["y"]).start()

    def step_x():
        g = out.at[x, 1 - y, c]
        rcopy(g, g, ss.at[3], rs.at[3], to["y"]).wait()
        for yy in range(2):
            g = out.at[x, yy, c]
            rcopy(g, g, ss.at[4 + yy], rs.at[4 + yy], to["x"]).start()

    def step_c():
        for yy in range(2):
            g = out.at[1 - x, yy, c]
            rcopy(g, g, ss.at[4 + yy], rs.at[4 + yy], to["x"]).wait()
        for xx in range(2):
            for yy in range(2):
                g = out.at[xx, yy, c]
                rcopy(g, g, ss.at[6 + 2 * xx + yy], rs.at[6 + 2 * xx + yy], to["core"]).start()

    def last():
        for xx in range(2):
            for yy in range(2):
                g = out.at[xx, yy, 1 - c]
                rcopy(g, g, ss.at[6 + 2 * xx + yy], rs.at[6 + 2 * xx + yy], to["core"]).wait()

    return begin, step_y, step_x, step_c, last


def gather_generic(tok, pk, mx, ex, sh, sv):
    every = ("dp", "ctx", "head")
    images = lax.all_gather(tok, ("ctx", "head"), axis=1, tiled=True)
    img = lax.dynamic_index_in_dim(images, coords()[1], 0, keepdims=False)
    spread = lax.all_gather(pk, every, axis=1, tiled=True)
    pko = lax.dynamic_index_in_dim(spread, lax.axis_index("head"), 0, keepdims=False)
    return [img, pko] + [lax.all_gather(t, every, axis=0, tiled=True) for t in (mx, ex, sh, sv)]


def exchange_kernel(src, dst, ls, ss, rs):
    x, y, c, z = coords()
    others = [(dy, dz) for dy in range(2) for dz in range(4) if dy or dz]
    enter([device(x, y ^ dy, c, z ^ dz) for dy, dz in others])
    me = y * 4 + z
    mine = pltpu.make_async_copy(src.at[me], dst.at[me], ls)
    mine.start()
    copies = []
    for i, (dy, dz) in enumerate(others):
        ty, tz = y ^ dy, z ^ dz
        cp = rcopy(src.at[ty * 4 + tz], dst.at[me], ss.at[i], rs.at[i], device(x, ty, c, tz))
        cp.start()
        copies.append(cp)
    mine.wait()
    for cp in copies:
        cp.wait()


def exchange(src, cid):
    D = pltpu.SemaphoreType.DMA
    return pl.pallas_call(
        exchange_kernel,
        out_shape=jax.ShapeDtypeStruct(src.shape, src.dtype),
        in_specs=[ANY],
        out_specs=ANY,
        scratch_shapes=[D, D((7,)), D((7,))],
        compiler_params=pltpu.CompilerParams(collective_id=cid, has_side_effects=True),
        name="exchange_heads_%d" % cid,
    )(src)


def dot(a, b):
    return jnp.dot(a, b, preferred_element_type=F32)


def dot_nt(a, b):
    return lax.dot_general(a, b, (((1,), (1,)), ((), ())), preferred_element_type=F32)


def row_norm(rows):
    mean = jnp.mean(rows, axis=-1, keepdims=True)
    centred = rows - mean
    inv = lax.rsqrt(jnp.mean(centred * centred, axis=-1, keepdims=True) + NORM_EPS)
    return centred * inv, inv


def project(g, rows, length, gain, shift, bias, pw, fi, nrm, qt, kv, kt, vt):
    heads = kv.shape[0]
    hd, step = HEAD_DIM, 256
    wide = 2 * hd * heads
    normed, _ = row_norm(rows.astype(F32))
    first = (normed * gain + shift).astype(BF)
    off = pl.multiple_of(g * step, step)
    fi[pl.ds(off, step), :] = first
    nrm[pl.ds(off, step), :] = normed.astype(BF)
    kvq = (dot(first, pw[...]) + bias).astype(BF).astype(F32)
    flip = kvq.T
    pos = off + lax.broadcasted_iota(jnp.int32, (step, 2 * hd), 0)
    lane = lax.broadcasted_iota(jnp.int32, (step, 2 * hd), 1)
    extra = jnp.where(lane == 0, jnp.where(pos < length, 0.0, MASKED), jnp.where(lane < 4, 1.0, 0.0)).astype(BF)
    for h in range(heads):
        kt[h, g] = flip[2 * h * hd : (2 * h + 1) * hd].astype(BF)
        vt[h, g] = flip[(2 * h + 1) * hd : (2 * h + 2) * hd].astype(BF)
        qt[g, h] = (flip[wide + h * hd : wide + (h + 1) * hd] * (1.0 / math.sqrt(hd))).astype(BF)
        kv[h, pl.ds(off, step), : 2 * hd] = kvq[:, 2 * h * hd : (2 * h + 2) * hd].astype(BF)
        kv[h, pl.ds(off, step), 2 * hd :] = extra


def attend(h, j, c, qt, kv, vt, mixed, lse):
    keys = kv.shape[1]
    hd, step, chunk = HEAD_DIM, 256, 512
    per = chunk // step
    row = lax.broadcasted_iota(jnp.int32, (16, step), 0)
    unit = jnp.where(row == 0, 1.0, 0.0).astype(BF)
    g = (j // 2) * 4 + c * 2 + j % 2
    sl = pl.ds(pl.multiple_of(h * hd, hd), hd)
    qa = jnp.concatenate([qt[g, h], jnp.zeros((hd, step), BF), unit, jnp.zeros((2 * hd - 16, step), BF)], axis=0)
    top = jnp.full((1, step), MASKED, F32)
    total = jnp.zeros((1, step), F32)
    acc = jnp.zeros((hd, step), F32)
    for kc in range(keys // chunk):
        s = dot(kv[h, kc * chunk : (kc + 1) * chunk, :], qa)
        new = jnp.maximum(top, jnp.max(s, axis=0, keepdims=True))
        p = jnp.exp2((s - new) * LOG2E)
        scale = jnp.exp2((top - new) * LOG2E)
        total = total * scale + jnp.sum(p, axis=0, keepdims=True)
        pb = p.astype(BF)
        part = dot(vt[h, kc * per], pb[:step])
        for i in range(1, per):
            part += dot(vt[h, kc * per + i], pb[i * step : (i + 1) * step])
        acc = acc * scale + part
        top = new
    out = acc / total
    lse[j, h] = top + jnp.log(total)
    for i in range(2):
        mixed[2 * j + i, sl, :] = out[:, i * 128 : (i + 1) * 128].astype(BF)


def forward_kernel(lens, img, pw, gain, shift, bias, mixed, lse, fi, nrm, qt, kv, kt, vt):
    x, y, c, z = coords()
    heads, keys = kv.shape[0], kv.shape[1]
    length = lens[y]

    def rows_of(g, carry):
        rows = img[pl.ds(2 * g, 2)].reshape(256, img.shape[2])
        project(g, rows, length, gain[...], shift[...], bias[...], pw, fi, nrm, qt, kv, kt, vt)
        return carry

    def step(s, carry):
        attend(s % heads, s // heads, c, qt, kv, vt, mixed, lse)
        return carry

    lax.fori_loop(0, keys // 256, rows_of, 0)
    lax.fori_loop(0, 4 * heads, step, 0)


FT = dict(
    small=(0.0, 2.5, 5.0, 7.5, 9.5),
    tok=((0.1, 5.5, 14.0, 26.0), (4.0, 9.0, 20.0, 33.0)),
    mx=(0.5, 0.5, (7.0, 11.0, 15.0), (4.0, 8.0, 12.0, 17.0), (19.0, 21.0)),
    ex=(0.6, 0.6, (7.1, 11.1, 15.1), (4.1, 9.0, 13.0, 18.0), (24.0, 34.0)),
    s0=(0.7, 20.5, (27.0, 33.1, 38.0), (5.0, 30.0, 36.0, 41.0), (45.0, 50.0)),
    s1=(0.8, 20.6, (27.1, 33.2, 38.1), (5.1, 30.1, 36.1, 41.1), (45.1, 50.1)),
    att=(36.0, 1.25),
)


def own_columns(rows, g, part):
    width = rows.shape[1] // 3
    at = lambda t, h: rows[:, t * width + g * part + h * HEAD_DIM : t * width + g * part + (h + 1) * HEAD_DIM]
    heads = part // HEAD_DIM
    return jnp.concatenate([at(t, h) for h in range(heads) for t in (1, 2)] + [at(0, h) for h in range(heads)], axis=1)


def forward_all_kernel(
    lens, tok, pkw, mx, ex, sh, v0, v1, v2, v3, v4, v5, v6, v7, v8,
    mix, mixed_o, lse_o, fi_o, nrm_o, qt_o, kv_o, kt_o, pw_o, vec, hid, mxo, exo, sho,
    pk, sv, img, pwg, svg, mixed, lse, fi, nrm, qt, kv, kt, vt, pw, bias,
    ls, tys, tzs, tzr, tcs, tcr, ps, pr, vs, vr, xs, xr, xl, osem, *wsems,
):
    co = coords()
    x, y, c, z = co
    to = partners(*co)
    zh = z // 2
    heads, keys = kv.shape[0], kv.shape[1]
    width = img.shape[4]
    n_dev = 32
    others = [(dy, dz) for dy in range(2) for dz in range(4) if dy or dz]
    part = heads * HEAD_DIM
    raw = pkw[...].astype(F32).reshape(3 * 8, pkw.shape[2])
    for g in range(4):
        pk[g] = own_columns(raw, g, part).astype(BF).reshape(3, 8, 3 * part)
    lines = [jnp.concatenate([v[...].astype(F32).reshape(1, -1), jnp.zeros((1, 128 - v.shape[-1]), F32)], axis=1) for v in (v0, v1, v2, v3, v4, v5, v6, v7, v8)]
    sv[...] = jnp.concatenate(lines + [jnp.zeros((7, 128), F32)], axis=0).astype(BF)
    enter([to["core"], to["x"]] + [device(x, y ^ dy, c, z ^ dz) for dy, dz in others])
    length = lens[y]
    ev = []

    row = lambda r: y if r == 0 else 1 - y

    def tz(r, i, k, ref, dst, name):
        return rcopy(ref, dst, tzs.at[r, i], tzr.at[r, k], to[name])

    def tcore(r, k, ref):
        return rcopy(ref, img.at[row(r), c, z ^ k], tcs.at[r, k], tcr.at[r, k], to["core"])

    spread = lambda: rcopy(tok.at[1 - y], img.at[y, c, z], tys.at[0], tys.at[1], to["y"])
    keep = lambda: pltpu.make_async_copy(tok.at[y], img.at[y, c, z], ls.at[0])

    def t_begin(r):
        d = img.at[row(r), c, z]
        if r == 0:
            spread().start()
            keep().start()
            own = tok.at[y]
        else:
            rcopy(d, d, tys.at[0], tys.at[1], to["y"]).wait()
            own = d
        tz(r, 0, 0, own, d, "z1").start()
        tz(r, 1, 1, own, d, "z2").start()
        tcore(r, 0, own).start()

    def t_land(r, k):
        d = img.at[row(r), c, z ^ k]
        tz(r, k - 1, k - 1, d, d, "z1").wait_recv()
        if k == 2:
            tz(r, 2, 2, d, d, "z1").start()
        tcore(r, k, d).start()

    for r in range(2):
        t = FT["tok"][r]
        ev.append((t[0], functools.partial(t_begin, r)))
        for k in range(1, 4):
            ev.append((t[k], functools.partial(t_land, r, k)))

    def t_last():
        for r in range(2):
            d = img.at[row(r), c, z]
            for i in range(3):
                tz(r, i, 0, d, d, "z1").wait_send()
            for k in range(4):
                tcore(r, k, d).wait_send()

    ev.append((1001.0, t_last))

    steps_v = small_gather(co, to, sv, svg, ls.at[1], vs, vr, False)
    steps_p = small_gather(co, to, pk, pwg, ls.at[2], ps, pr, True)
    for t, fv, fp in zip(FT["small"], steps_v, steps_p):
        ev.append((t, fv))
        ev.append((t + 0.05, fp))

    def unpack():
        small = width // n_dev
        part = heads * HEAD_DIM
        col = lax.broadcasted_iota(jnp.int32, (128, width), 1)
        lane = lax.broadcasted_iota(jnp.int32, (128, width), 0)
        spread_ = jnp.where(col % small == lane, 1.0, 0.0).astype(BF)
        every = svg[...].reshape(n_dev * 16, 128)
        val = dot(every, spread_)
        line = lax.broadcasted_iota(jnp.int32, (n_dev * 16, width), 0) // 16
        own = lax.broadcasted_iota(jnp.int32, (n_dev * 16, width), 1) // small
        val = jnp.sum(jnp.where(line == own, val, 0.0).reshape(n_dev, 16, width), axis=0)
        vec[...] = val
        big = hid.shape[1] // n_dev
        col = lax.broadcasted_iota(jnp.int32, (128, hid.shape[1]), 1)
        lane = lax.broadcasted_iota(jnp.int32, (128, hid.shape[1]), 0)
        wide_ = jnp.where(col % big == lane, 1.0, 0.0).astype(BF)
        line = lax.broadcasted_iota(jnp.int32, (n_dev, hid.shape[1]), 0)
        own = lax.broadcasted_iota(jnp.int32, (n_dev, hid.shape[1]), 1) // big
        eight = svg[...].astype(F32).reshape(n_dev, 16, 128)[:, 8, :].astype(BF)
        hid[...] = jnp.sum(jnp.where(line == own, dot(eight, wide_), 0.0), axis=0, keepdims=True)
        src = lax.broadcasted_iota(jnp.int32, (width, 3 * part), 0)
        dst = lax.broadcasted_iota(jnp.int32, (width, 3 * part), 1)
        head, off = dst // (2 * HEAD_DIM), dst % (2 * HEAD_DIM)
        hv = jnp.logical_and(jnp.logical_and(dst < 2 * part, off >= HEAD_DIM), src == z * part + head * HEAD_DIM + off - HEAD_DIM)
        hq = jnp.logical_and(dst >= 2 * part, src == z * part + dst - 2 * part)
        rows = val.astype(BF)
        bq = dot(rows, jnp.where(hq, 1.0, 0.0).astype(BF))
        bv = dot(rows, jnp.where(hv, 1.0, 0.0).astype(BF))
        bias[...] = bq[2:3] + bv[3:4]

    def flatten():
        def body(i, carry):
            blk = pwg[i // 4, (i // 2) % 2, i % 2].astype(F32)
            n = blk.shape[0] * blk.shape[1] * blk.shape[2]
            pw[pl.ds(pl.multiple_of(i * n, n), n), :] = blk.reshape(n, blk.shape[3]).astype(BF)
            return carry

        lax.fori_loop(0, 8, body, 0)

    ev.append((FT["small"][4] + 0.1, unpack))
    ev.append((FT["small"][4] + 0.2, flatten))

    def project_group(r, mine, p):
        cc = c if mine else 1 - c
        zz = zh if p == 0 else 1 - zh
        if r == 0 and mine and p == 0:
            keep().wait()
        if not mine:
            for k in (2 * p, 2 * p + 1):
                d = img.at[row(r), cc, z ^ k]
                rcopy(d, d, tcs.at[r, k], tcr.at[r, k], to["core"]).wait_recv()
        g = row(r) * 4 + cc * 2 + zz
        rows = img[row(r), cc, pl.ds(2 * zz, 2)].reshape(256, width)
        project(g, rows, length, vec[0:1, :], vec[1:2, :], bias[...], pw, fi, nrm, qt, kv, kt, vt)

    t_ready = FT["small"][4] + 0.3
    for p in range(2):
        for r in range(2):
            for mine in (True, False):
                t = max(FT["tok"][r][1 if p == 0 else 3] + (0.3 if mine else 0.6), t_ready + 0.01 * (r * 2 + (not mine)))
                ev.append((t, functools.partial(project_group, r, mine, p)))

    per = len(wsems) // 4
    half = sh.shape[0] // 2
    full = lambda o: (lambda px, py, cc, zz: o.at[px, py, cc, zz])
    weights = (
        ("mx", mx, full(mxo), "yx"),
        ("ex", ex, full(exo), "xy"),
        ("s0", sh.at[:half], lambda px, py, cc, zz: sho.at[px, py, cc, zz, :half], "yx"),
        ("s1", sh.at[half:], lambda px, py, cc, zz: sho.at[px, py, cc, zz, half:], "xy"),
    )
    for i, (name, src, out, order) in enumerate(weights):
        weight_gather(ev, co, to, src, out, wsems[i * per : (i + 1) * per], order, FT[name])

    stored = [(fi, fi_o), (nrm, nrm_o), (qt, qt_o), (kv, kv_o), (kt, kt_o), (pw, pw_o), (mixed, mixed_o), (lse, lse_o)]
    store = lambda i: pltpu.make_async_copy(stored[i][0], stored[i][1], osem.at[i])

    def store_first():
        for i in range(6):
            store(i).start()

    t_att, t_step = FT["att"]
    steps = 4 * heads
    t_end = t_att + steps * t_step
    ev.append((t_att + 0.001, store_first))

    me = y * 4 + z

    def target(q):
        w = 3 - q
        return [(w // 2, 2 * (w % 2)), (w // 2, 2 * (w % 2) + 1)]

    def xcopy(dy, dz):
        i = dy * 4 + dz
        return rcopy(mixed.at[(y ^ dy) * 4 + (z ^ dz)], mix.at[me], xs.at[i], xr.at[i], device(x, y ^ dy, c, z ^ dz))

    mine_copy = lambda: pltpu.make_async_copy(mixed.at[me], mix.at[me], xl)

    def send_group(q):
        for dy, dz in target(q):
            if dy or dz:
                xcopy(dy, dz).start()
            else:
                mine_copy().start()

    for q in range(4):
        ev.append((t_att + (q + 1) * heads * t_step + 0.002, functools.partial(send_group, q)))

    def finish():
        store(6).start()
        store(7).start()
        for dy, dz in others:
            xcopy(dy, dz).wait()
        mine_copy().wait()

    ev.append((t_end + 0.5, finish))

    def drain():
        for i in range(8):
            store(i).wait()

    ev.append((1002.0, drain))

    ev.sort(key=lambda e: e[0])
    for t, fn in ev:
        if t < t_att:
            fn()

    def step(s, carry):
        for k in range(steps):
            here = [fn for t, fn in ev if t_att + k * t_step <= t < t_att + (k + 1) * t_step]
            if here:

                @pl.when(s == k)
                def _():
                    for fn in here:
                        fn()

        attend(s % heads, (3 - s // heads) ^ (2 * y + zh), c, qt, kv, vt, mixed, lse)
        return carry

    lax.fori_loop(0, steps, step, 0)
    for t, fn in ev:
        if t >= t_end:
            fn()


def forward_all(lens, tok, pkw, mx, ex, sh, vecs):
    D, V, S = pltpu.SemaphoreType.DMA, pltpu.VMEM, jax.ShapeDtypeStruct
    shard, width = tok.shape[1], tok.shape[2]
    cols = pkw.shape[2] // 4
    pk_shape = (3, 8, cols)
    heads = cols // (3 * HEAD_DIM)
    keys = 16 * shard
    n = keys // 256
    lead = (2, SPLIT, SPLIT, 4)
    part = heads * HEAD_DIM
    hidden = ex.shape[2]
    outs = [
        S((8, part, shard), BF),
        S((8, part, shard), BF),
        S((4, heads, 1, 256), F32),
        S((keys, width), BF),
        S((keys, width), BF),
        S((n, heads, HEAD_DIM, 256), BF),
        S((heads, keys, 4 * HEAD_DIM), BF),
        S((heads, n, HEAD_DIM, 256), BF),
        S((width, cols), BF),
        S((16, width), F32),
        S((1, hidden), F32),
        S(lead + mx.shape, BF),
        S(lead + ex.shape, BF),
        S(lead + sh.shape, BF),
    ]
    wsem = [D, D((3,)), D((3,)), D((4,)), D((4,)), D((2, 4)), D((2, 4)), D((4,)), D((4,))]
    scr = [V((4,) + pk_shape, BF), V((16, 128), BF)]
    scr += [V((2, 2, 4) + tok.shape[1:], BF), V(lead + pk_shape, BF), V(lead + (16, 128), BF), V((8, part, shard), BF), V((4, heads, 1, 256), F32)]
    scr += [V((keys, width), BF), V((keys, width), BF), V((n, heads, HEAD_DIM, 256), BF), V((heads, keys, 4 * HEAD_DIM), BF)]
    scr += [V((heads, n, HEAD_DIM, 256), BF), V((heads, n, HEAD_DIM, 256), BF), V((width, cols), BF), V((1, cols), F32)]
    scr += [D((3,)), D((2,)), D((2, 3)), D((2, 3)), D((2, 4)), D((2, 4)), D((10,)), D((10,)), D((10,)), D((10,)), D((8,)), D((8,)), D, D((8,))]
    return pl.pallas_call(
        forward_all_kernel,
        out_shape=outs,
        in_specs=[SM, ANY, VM, ANY, ANY, ANY] + [VM] * 9,
        out_specs=[ANY] * 9 + [VM] * 2 + [ANY] * 3,
        scratch_shapes=scr + wsem * 4,
        compiler_params=pltpu.CompilerParams(collective_id=0, has_side_effects=True, vmem_limit_bytes=62 << 20),
        name="gather_attention_forward",
    )(lens, tok, pkw, mx, ex, sh, *vecs)


def attention_forward(lens, img, pw, gain, shift, bias):
    heads = pw.shape[1] // (3 * HEAD_DIM)
    keys = img.shape[0] * img.shape[1]
    width = heads * HEAD_DIM
    n = keys // 256
    outs = [
        jax.ShapeDtypeStruct((8, width, 128), BF),
        jax.ShapeDtypeStruct((4, heads, 1, 256), F32),
        jax.ShapeDtypeStruct((keys, img.shape[2]), BF),
        jax.ShapeDtypeStruct((keys, img.shape[2]), BF),
        jax.ShapeDtypeStruct((n, heads, HEAD_DIM, 256), BF),
        jax.ShapeDtypeStruct((heads, keys, 4 * HEAD_DIM), BF),
        jax.ShapeDtypeStruct((heads, n, HEAD_DIM, 256), BF),
    ]
    return pl.pallas_call(
        forward_kernel,
        out_shape=outs,
        in_specs=[SM] + [VM] * 5,
        out_specs=[VM] * 7,
        scratch_shapes=[pltpu.VMEM((heads, n, HEAD_DIM, 256), BF)],
        compiler_params=pltpu.CompilerParams(vmem_limit_bytes=50 << 20),
        name="attention_forward",
    )(lens, img, pw, gain, shift, bias)


def dot_tn(a, b):
    return lax.dot_general(a, b, (((0,), (0,)), ((), ())), preferred_element_type=F32)


def dense_kernel(
    tok, cot, mix, vec, hid, mx_h, ex_h, sh_h,
    out, act, sin, gpre, gres, gresf, send, s4, s5, s6, s7, s8,
    mx, ex, sh, sems,
):
    images, shard, width = tok.shape
    rows = images * shard
    hidden = ex.shape[1]
    n = hidden // width
    load = [pltpu.make_async_copy(mx_h, mx, sems.at[0])]
    for i in range(n):
        cols = slice(i * width, (i + 1) * width)
        load.append(pltpu.make_async_copy(ex_h.at[:, cols], ex.at[:, cols], sems.at[1 + i]))
        load.append(pltpu.make_async_copy(sh_h.at[cols, :], sh.at[cols, :], sems.at[1 + n + i]))
    for cp in load:
        cp.start()
    cin = cot[...].reshape(rows, width)
    cf = cin.astype(F32)
    s7[...] = jnp.sum(cf, axis=0, keepdims=True)
    mixed_t = jnp.concatenate([mix[i] for i in range(images)], axis=1)
    load[0].wait()
    residual = tok[...].astype(F32).reshape(rows, width) + dot_tn(mixed_t, mx[...]) + vec[4:5, :]
    normed, inv = row_norm(residual)
    second = (normed * vec[5:6, :] + vec[6:7, :]).astype(BF)
    sin[...] = second
    up = jnp.zeros((rows, width), F32)
    down = jnp.zeros((rows, width), F32)
    for i in range(n):
        cols = slice(i * width, (i + 1) * width)
        load[1 + 2 * i].wait()
        load[2 + 2 * i].wait()
        pre = dot(second, ex[:, cols]) + hid[:, cols]
        cum = 0.5 * (1.0 + lax.erf(pre * (1.0 / math.sqrt(2.0))))
        slope = cum + pre * (jnp.exp(-0.5 * pre * pre) * (1.0 / math.sqrt(2.0 * math.pi)))
        a = (pre * cum).astype(BF)
        act[:, cols] = a
        g = dot_nt(cin, sh[cols, :]) * slope
        s8[:, cols] = jnp.sum(g, axis=0, keepdims=True)
        gb = g.astype(BF)
        gpre[:, cols] = gb
        up += dot(a, sh[cols, :])
        down += dot_nt(gb, ex[:, cols])
    out[...] = (residual + up + vec[7:8, :]).astype(BF).reshape(images, shard, width)
    s5[...] = jnp.sum(down * normed, axis=0, keepdims=True)
    s6[...] = jnp.sum(down, axis=0, keepdims=True)
    scaled = down * vec[5:6, :]
    m1 = jnp.mean(scaled, axis=-1, keepdims=True)
    m2 = jnp.mean(scaled * normed, axis=-1, keepdims=True)
    gr = cf + inv * (scaled - m1 - normed * m2)
    s4[...] = jnp.sum(gr, axis=0, keepdims=True)
    gresf[...] = gr.reshape(images, shard, width)
    gb = gr.astype(BF)
    gres[...] = gb
    for i in range(images):
        val = dot_nt(mx[...], gb[i * shard : (i + 1) * shard]).astype(BF)
        send[4 * i : 4 * (i + 1)] = val.reshape(4, width // 4, shard)


def dense_layers(tok, cot, mix, vec, hid, mx, ex, sh):
    S, V = jax.ShapeDtypeStruct, pltpu.VMEM
    images, shard, width = tok.shape
    rows, hidden = images * shard, ex.shape[1]
    line = S((1, width), F32)
    outs = [
        S(tok.shape, BF),
        S((rows, hidden), BF),
        S((rows, width), BF),
        S((rows, hidden), BF),
        S((rows, width), BF),
        S(tok.shape, F32),
        S((4 * images, width // 4, shard), BF),
    ] + [line] * 4 + [S((1, hidden), F32)]
    return pl.pallas_call(
        dense_kernel,
        out_shape=outs,
        in_specs=[VM] * 5 + [ANY] * 3,
        out_specs=[VM] * len(outs),
        scratch_shapes=[V(mx.shape, BF), V(ex.shape, BF), V(sh.shape, BF), pltpu.SemaphoreType.DMA((1 + 2 * (hidden // width),))],
        compiler_params=pltpu.CompilerParams(vmem_limit_bytes=62 << 20),
        name="dense_layers",
    )(tok, cot, mix, vec, hid, mx, ex, sh)


def hand_over_kernel(*refs):
    n = 5
    src, vec, dst, outs = refs[:n], refs[n], refs[n + 1 : 2 * n + 1], refs[2 * n + 1 :]
    for i in range(n):
        dst[i][...] = src[i][...]
    for i, o in enumerate(outs):
        line = 16 if i == 8 else i
        o[...] = vec[line : line + 1, : o.shape[0]].reshape(o.shape[0])


def hand_over(arrays, vec, small, big):
    S = jax.ShapeDtypeStruct
    outs = [S(t.shape, t.dtype) for t in arrays] + [S((small,), F32)] * 8 + [S((big,), F32)]
    return pl.pallas_call(
        hand_over_kernel,
        out_shape=outs,
        in_specs=[VM] * 6,
        out_specs=[VM] * 14,
        name="hand_over",
    )(*arrays, vec)


def split3(value):
    hi = value.astype(BF)
    rest = value - hi.astype(F32)
    mid = rest.astype(BF)
    low = (rest - mid.astype(F32)).astype(BF)
    return hi, mid, low


def pick(value, hot):
    a, b, d = split3(value)
    return dot(a, hot) + dot(b, hot) + dot(d, hot)


def stacked_extra(lead, value, row):
    a, b, d = (t.astype(F32) for t in split3(value))
    out = jnp.where(row == 1, a, 0.0) + jnp.where(row == 2, b, 0.0) + jnp.where(row == 3, d, 0.0)
    return (jnp.where(row == 0, lead, 0.0) + out).astype(BF)


def backward_step(h, j, c, grad, mixed, lse, qt, kv, kt, dkv, dqt):
    keys = kv.shape[1]
    hd, step, chunk = HEAD_DIM, 256, 512
    per = chunk // step
    g = (j // 2) * 4 + c * 2 + j % 2
    sl = pl.ds(pl.multiple_of(h * hd, hd), hd)
    do = jnp.concatenate([grad[2 * j, sl, :], grad[2 * j + 1, sl, :]], axis=1)
    mx = jnp.concatenate([mixed[2 * j, sl, :], mixed[2 * j + 1, sl, :]], axis=1)
    delta = jnp.sum(do.astype(F32) * mx.astype(F32), axis=0, keepdims=True)
    row = lax.broadcasted_iota(jnp.int32, (16, step), 0)
    none = jnp.zeros((hd, step), BF)
    rest = jnp.zeros((2 * hd - 16, step), BF)
    qh = qt[g, h]
    qa = jnp.concatenate([qh, none, stacked_extra(1.0, -lse[j, h], row), rest], axis=0)
    da = jnp.concatenate([none, do, stacked_extra(0.0, -delta, row), rest], axis=0)
    qr = jnp.concatenate([qh, none], axis=0).astype(F32).T.astype(BF)
    dr = jnp.concatenate([none, do], axis=0).astype(F32).T.astype(BF)
    dq = jnp.zeros((hd, step), F32)
    for kc in range(keys // chunk):
        rows = slice(kc * chunk, (kc + 1) * chunk)
        block = kv[h, rows, :]
        p = jnp.exp2(dot(block, qa) * LOG2E)
        dp = dot(block, da)
        ds = (p * dp).astype(BF)
        dkv[h, rows, :] += dot(ds, qr) + dot(p.astype(BF), dr)
        for i in range(per):
            dq += dot(kt[h, kc * per + i], ds[i * step : (i + 1) * step])
    dqt[j, sl, :] = (dq * (1.0 / math.sqrt(hd))).astype(BF)


def add_into(dst, src, lead, n):
    def body(i, carry):
        dst[lead + (i,)] = dst[lead + (i,)] + src[i]
        return carry

    lax.fori_loop(0, n, body, 0)


def halving(co, to, G, u, bufs, ss, rs, order, finish):
    x, y, c, z = co
    zh, zl = z // 2, z % 2
    r0, r1, r2, r3, r4 = bufs
    a, b = order
    first = (lambda n: G.at[u, 1 - x, n, c]) if a == "x" else (lambda n: G.at[u, n, 1 - y, c])
    keep = (lambda n: (u, x, n, c)) if a == "x" else (lambda n: (u, n, y, c))
    second = G.at[u, x, 1 - y, c] if b == "y" else G.at[u, 1 - x, y, c]

    def cp0(i):
        return rcopy(G.at[u, i // 2, i % 2, 1 - c], r0.at[u, i], ss.at[u, i], rs.at[u, i], to["core"])

    def cp1(n):
        return rcopy(first(n), r1.at[u, n], ss.at[u, 4 + n], rs.at[u, 4 + n], to[a])

    cp2 = lambda: rcopy(second, r2.at[u], ss.at[u, 6], rs.at[u, 6], to[b])
    cp3 = lambda n: rcopy(G.at[u, x, y, c, 2 * n + 1 - zl], r3.at[u, n], ss.at[u, 7 + n], rs.at[u, 7 + n], to["z1"])
    cp4 = lambda: rcopy(G.at[u, x, y, c, 2 * (1 - zh) + zl], r4.at[u], ss.at[u, 9], rs.at[u, 9], to["z2"])

    def core_send():
        for i in range(4):
            cp0(i).start()

    def core_land():
        for i in range(4):
            cp0(i).wait()
            add_into(G, r0.at[u, i], (u, i // 2, i % 2, c), 4)

    def a_send():
        for n in range(2):
            cp1(n).start()

    def a_wait():
        for n in range(2):
            cp1(n).wait()

    def a_add():
        for n in range(2):
            add_into(G, r1.at[u, n], keep(n), 4)
        cp2().start()

    def b_land():
        cp2().wait()
        add_into(G, r2.at[u], (u, x, y, c), 4)
        for n in range(2):
            cp3(n).start()

    def z1_land():
        for n in range(2):
            cp3(n).wait()
            here = (u, x, y, c, 2 * n + zl)
            G[here] = G[here] + r3[u, n]
        cp4().start()

    def z2_land():
        cp4().wait()
        finish(G[u, x, y, c, z].astype(F32) + r4[u].astype(F32))

    return dict(core_send=core_send, core_land=core_land, a_send=a_send, a_wait=a_wait, a_add=a_add, b_land=b_land, z1_land=z1_land, z2_land=z2_land)


TIMES = dict(
    core=(3, 4.8, 6.6, 8.4, 10.2),
    a=(12, 20, 28, 36, 42.4),
    b_land=(24, 32, 40, 48, 54.4),
    z1_land=(30, 38, 46, 54, 60.4),
    z2_land=(35, 43, 51, 59, 65.4),
)


def backward_kernel(
    send, cot, act, sin, gpre, mix, gres, gain, s4, s5, s6, s7, s8, mixed_h, lse_h, qt_h, kv_h, kt_h, fi_h, nrm_h, pw_h, gresf_h, tok_h,
    out_in, out_s, out_e, out_m, out_p, out_v,
    mixed, lse, qt, kv, kt, fi, nrm, pw, gresf, tok, lsem, grad, G, r0, r1, r2, r3, r4, dkv, dqt, dall, GF, q0, q1, q2, q3, sq, GP, p0, p1, p2, p3, V, vr,
    els, ess, ers, gss, grs, qss, qrs, pss, prs, vss, vrs,
):
    co = coords()
    x, y, c, z = co
    to = partners(*co)
    zh, zl = z // 2, z % 2
    heads, keys = kv.shape[0], kv.shape[1]
    rows, width = cot.shape
    late = [(mixed_h, mixed), (lse_h, lse), (qt_h, qt), (kv_h, kv), (kt_h, kt), (fi_h, fi), (nrm_h, nrm), (pw_h, pw), (gresf_h, gresf), (tok_h, tok)]

    def local(i):
        return pltpu.make_async_copy(late[i][0], late[i][1], lsem.at[i])

    for i in range(len(late)):
        local(i).start()
    others = [(dy, dz) for dy in range(2) for dz in range(4) if dy or dz]
    enter([to["core"], to["x"]] + [device(x, y ^ dy, c, z ^ dz) for dy, dz in others])
    me = y * 4 + z

    def exch(i):
        dy, dz = others[i]
        return rcopy(send.at[(y ^ dy) * 4 + (z ^ dz)], grad.at[me], ess.at[i], ers.at[i], device(x, y ^ dy, c, z ^ dz))

    mine = pltpu.make_async_copy(send.at[me], grad.at[me], els)
    mine.start()
    for i in range(7):
        exch(i).start()

    ev = []
    n_hid = act.shape[1] // width

    def shrink_all():
        span = act.shape[1] // 8

        def body(t, carry):
            val = dot_tn(act[:, pl.ds(pl.multiple_of(t * span, span), span)], cot[...]).astype(BF)
            val = val.reshape(4, n_hid, 3, 8, width)
            for zz in range(4):
                for i in range(n_hid):
                    G[i, t // 4, (t // 2) % 2, t % 2, zz] = val[zz, i]
            return carry

        lax.fori_loop(0, 8, body, 0)

    def expand_one(i):
        for t in range(2):
            val = dot_tn(sin[:, t * width // 2 : (t + 1) * width // 2], gpre[:, i * width : (i + 1) * width]).astype(BF)
            G[n_hid + i, t] = val.reshape(2, 2, 4, 3, 8, width)

    def mixer_one():
        half = rows // 2
        for t in range(2):
            sl = slice(t * width // 2, (t + 1) * width // 2)
            val = dot(mix[0, sl, :], gres[:half]) + dot(mix[1, sl, :], gres[half:])
            G[2 * n_hid, t] = val.astype(BF).reshape(2, 2, 4, 3, 8, width)

    bufs = (r0, r1, r2, r3, r4)
    ev.append((0.0, shrink_all))
    pairs = [[i, n_hid + i] for i in range(n_hid)] + [[2 * n_hid]]
    plan = []
    for p, us in enumerate(pairs):
        entry = []
        for u in us:
            if u < n_hid:
                fin = functools.partial(lambda u, val: out_s.__setitem__(u, val), u)
            elif u < 2 * n_hid:
                fin = functools.partial(lambda i, val: out_e.__setitem__((slice(None), slice(None), slice(i * width, (i + 1) * width)), val), u - n_hid)
                ev.append((0.6 + p, functools.partial(expand_one, u - n_hid)))
            else:
                fin = lambda val: out_m.__setitem__(Ellipsis, val)
                ev.append((0.6 + p, mixer_one))
            entry.append(halving(co, to, G, u, bufs, gss, grs, "yx" if n_hid <= u < 2 * n_hid else "xy", fin))
        plan.append(entry)

    def every(p, name):
        return [st[name] for st in plan[p]]

    def run(fns):
        for fn in fns:
            fn()

    def a_land(p):
        run(every(p, "a_wait"))
        if p + 2 < len(plan):
            run(every(p + 2, "a_send"))
        run(every(p, "a_add"))

    for p in range(len(plan)):
        ev.append((0.5 + (p if p else 0.0) + (0.2 if p else 0.0), functools.partial(run, every(p, "core_send")[:1])))
        ev.append((0.7 + p, functools.partial(run, every(p, "core_send")[1:])))
        ev.append((TIMES["core"][p], functools.partial(run, every(p, "core_land"))))
        if p < 2:
            ev.append((TIMES["core"][p] + 0.01, functools.partial(run, every(p, "a_send"))))
        ev.append((TIMES["a"][p], functools.partial(a_land, p)))
        for name in ("b_land", "z1_land", "z2_land"):
            ev.append((TIMES[name][p], functools.partial(run, every(p, name))))

    def zero():
        def body(i, carry):
            for h in range(heads):
                dkv[h, pl.ds(pl.multiple_of(i * 256, 256), 256), :] = jnp.zeros((256, 2 * HEAD_DIM), F32)
            return carry

        lax.fori_loop(0, keys // 256, body, 0)

    def arrive(q):
        if q == 0:
            mine.wait()
            for i in range(5):
                local(i).wait()
        for i in range(7):
            if 2 * others[i][0] + others[i][1] // 2 == q:
                exch(i).wait()

    ev.append((5.2, zero))
    steps = 4 * heads
    t_att, t_step = 6.5, 1.65
    t_end = t_att + t_step * steps
    for q in range(4):
        ev.append((t_att + heads * q * t_step + 0.001, functools.partial(arrive, q)))

    V[...] = jnp.zeros_like(V)
    for i, ref in ((4, s4), (5, s5), (6, s6), (7, s7)):
        V[i : i + 1, :] = ref[...]
    for i in range(n_hid):
        V[8 + i : 9 + i, :] = s8[:, i * width : (i + 1) * width]

    def group(slot, mine_rows):
        cc = c if mine_rows else 1 - c
        yy = slot // 2
        g = yy * 4 + cc * 2 + slot % 2
        off = pl.multiple_of(g * 256, 256)
        rs_ = pl.ds(off, 256)
        wide = 2 * HEAD_DIM * heads
        dk = jnp.concatenate([dkv[h, rs_, :].astype(BF) for h in range(heads)], axis=1)
        gf = dot_nt(dk, pw[:, :wide])
        dall[rs_, :wide] = dk
        sums = jnp.sum(dk.astype(F32), axis=0, keepdims=True)
        V[16:17, :wide] += sums
        if mine_rows:
            dq = dqt[slot].astype(F32).T.astype(BF)
            gf += dot_nt(dq, pw[:, wide:])
            dall[rs_, wide:] = dq
            V[17:18, : dq.shape[1]] += jnp.sum(dq.astype(F32), axis=0, keepdims=True)
        else:
            dall[rs_, wide:] = jnp.zeros((256, heads * HEAD_DIM), BF)
        V[0:1, :] += jnp.sum(gf * nrm[rs_, :].astype(F32), axis=0, keepdims=True)
        V[1:2, :] += jnp.sum(gf, axis=0, keepdims=True)
        GF[yy, cc, pl.ds(2 * (slot % 2), 2)] = gf.astype(BF).reshape(2, 2, 64, width)

    def q_core(r):
        yy = rowof(r)
        return rcopy(GF.at[yy, 1 - c], q0.at[r], qss.at[r], qrs.at[r], to["core"])

    def q_z1(r, f, n):
        i = 2 + 4 * r + 2 * f + n
        return rcopy(GF.at[rowof(r), c, 2 * n + 1 - zl, f], q1.at[r, f, n], qss.at[i], qrs.at[i], to["z1"])

    def q_z2(r, f):
        i = 10 + 2 * r + f
        return rcopy(GF.at[rowof(r), c, 2 * (1 - zh) + zl, f], q2.at[r, f], qss.at[i], qrs.at[i], to["z2"])

    def q_y(f):
        return rcopy(sq.at[f], q3.at[f], qss.at[14 + f], qrs.at[14 + f], to["y"])

    def rowof(r):
        return 1 - y if r == 0 else y

    def walk(mine_rows, r):
        def body(i, carry):
            group(2 * rowof(r) + i, mine_rows)
            return carry

        lax.fori_loop(0, 2, body, 0)
        if not mine_rows:
            q_core(r).start()

    def q_sum(r):
        q_core(r).wait()
        yy = rowof(r)

        def body(i, carry):
            GF[yy, c, i // 2, i % 2] = GF[yy, c, i // 2, i % 2] + q0[r, i // 2, i % 2]
            return carry

        lax.fori_loop(0, 8, body, 0)
        if r == 0:
            q_send(0, 0)
            q_send(0, 1)

    def q_send(r, f):
        for n in range(2):
            q_z1(r, f, n).start()

    chunks = [(r, f) for r in range(2) for f in range(2)]

    def q_half(i):
        r, f = chunks[i]
        for n in range(2):
            q_z1(r, f, n).wait()
        if i + 2 < 4:
            q_send(*chunks[i + 2])
        for n in range(2):
            here = (rowof(r), c, 2 * n + zl, f)
            GF[here] = GF[here] + q1[r, f, n]
        q_z2(r, f).start()

    def finish(img, f, total):
        rs_ = slice(64 * f, 64 * (f + 1))
        normed, inv = row_norm(tok[img, rs_].astype(F32))
        scaled = total * gain[0:1, :]
        m1 = jnp.mean(scaled, axis=-1, keepdims=True)
        m2 = jnp.mean(scaled * normed, axis=-1, keepdims=True)
        out_in[img, rs_] = (gresf[img, rs_] + inv * (scaled - m1 - normed * m2)).astype(BF)

    def q_full(i):
        r, f = chunks[i]
        q_z2(r, f).wait()
        total = GF[rowof(r), c, z, f].astype(F32) + q2[r, f].astype(F32)
        if r == 0:
            sq[f] = total.astype(BF)
            q_y(f).start()
        else:
            finish(y, f, total)

    def q_last(f):
        q_y(f).wait()
        finish(1 - y, f, q3[f].astype(F32))

    def late_rows():
        for i in range(5, 10):
            local(i).wait()

    ev.append((t_end + 0.05, late_rows))
    ev.append((t_end + 0.1, lambda: walk(False, 0)))
    ev.append((t_end + 2.0, lambda: walk(False, 1)))
    ev.append((t_end + 4.0, lambda: walk(True, 0)))
    ev.append((t_end + 6.0, lambda: q_sum(0)))
    ev.append((t_end + 6.1, lambda: walk(True, 1)))
    ev.append((t_end + 8.0, lambda: q_sum(1)))
    for i in range(4):
        ev.append((t_end + 15.0 + 6.0 * i, functools.partial(q_half, i)))
        ev.append((t_end + 20.5 + 6.0 * i, functools.partial(q_full, i)))
    for f in range(2):
        ev.append((t_end + 31.0 + 6.0 * f, functools.partial(q_last, f)))

    def packed():
        val = dot_tn(fi[...], dall[...]).astype(BF)
        GP[0] = val.reshape(2, 2, 2, 4, 3, 8, val.shape[1])
        for i in range(4):
            p_core(i).start()

    def p_core(i):
        return rcopy(GP.at[0, i // 2, i % 2, 1 - c], p0.at[i], pss.at[i], prs.at[i], to["core"])

    def p_a(n):
        return rcopy(GP.at[0, 1 - x, n, c], p1.at[n], pss.at[4 + n], prs.at[4 + n], to["x"])

    p_b = lambda: rcopy(GP.at[0, x, 1 - y, c], p2, pss.at[6], prs.at[6], to["y"])
    p_z = lambda k: rcopy(GP.at[0, x, y, c, z ^ k], p3.at[k - 1], pss.at[6 + k], prs.at[6 + k], to["z%d" % k])

    def packed_core():
        for i in range(4):
            p_core(i).wait()
            add_into(GP, p0.at[i], (0, i // 2, i % 2, c), 4)
        for n in range(2):
            p_a(n).start()

    def packed_a():
        for n in range(2):
            p_a(n).wait()
            add_into(GP, p1.at[n], (0, x, n, c), 4)
        p_b().start()

    def packed_b():
        p_b().wait()
        add_into(GP, p2, (0, x, y, c), 4)
        for k in (1, 2, 3):
            p_z(k).start()

    def packed_z():
        GP[0, 1 - x, y, c, z] = GP[0, x, y, c, z]
        for k in (1, 2, 3):
            p_z(k).wait()
            GP[0, 1 - x, y, c, z ^ k] = p3[k - 1]
        part = heads * HEAD_DIM
        for g in range(4):
            val = GP[0, 1 - x, y, c, g].astype(F32)
            for h in range(heads):
                spots = ((1, 2 * h), (2, 2 * h + 1), (0, 2 * heads + h))
                for t, i in spots:
                    lo = t * width + g * part + h * HEAD_DIM
                    out_p[:, :, lo : lo + HEAD_DIM] = val[:, :, i * HEAD_DIM : (i + 1) * HEAD_DIM]

    def v_copy(i):
        return rcopy(V.at[0:16], vr.at[i], vss.at[i], vrs.at[i], to[("core", "x", "y", "z1", "z2")[i]])

    def vec_start():
        part = heads * HEAD_DIM
        wide = 2 * part
        src = lax.broadcasted_iota(jnp.int32, (wide, width), 0)
        dst = lax.broadcasted_iota(jnp.int32, (wide, width), 1)
        head, lane = src // (2 * HEAD_DIM), src % (2 * HEAD_DIM)
        hot = jnp.logical_and(lane >= HEAD_DIM, dst == z * part + head * HEAD_DIM + lane - HEAD_DIM)
        V[3:4, :] = pick(V[16:17, :wide], jnp.where(hot, 1.0, 0.0).astype(BF))
        hot = dst == z * part + src
        V[2:3, :] = pick(V[17:18, :part], jnp.where(hot, 1.0, 0.0).astype(BF)[:part])
        v_copy(0).start()

    def vec_step(i):
        v_copy(i).wait()
        V[0:16, :] = V[0:16, :] + vr[i]
        if i < 4:
            v_copy(i + 1).start()
        else:
            n_dev = 32
            small = width // n_dev
            d = (x * 4 + y * 2 + c) * 4 + z
            src = lax.broadcasted_iota(jnp.int32, (width, 128), 0)
            dst = lax.broadcasted_iota(jnp.int32, (width, 128), 1)
            hot = jnp.logical_and(src == d * small + dst, dst < small)
            out_v[0:16, :] = pick(V[0:16, :], jnp.where(hot, 1.0, 0.0).astype(BF))
            big = n_hid * small
            hot = jnp.logical_and(src == (d % (n_dev // n_hid)) * big + dst, dst < big)
            line = lax.broadcasted_iota(jnp.int32, (16, 128), 0)
            val = pick(V[0:16, :], jnp.where(hot, 1.0, 0.0).astype(BF))
            val = jnp.where(line == 8 + d // (n_dev // n_hid), val, 0.0)
            out_v[16:17, :] = jnp.sum(val, axis=0, keepdims=True)

    ev.append((t_end + 8.2, packed))
    ev.append((t_end + 12.5, vec_start))
    ev.append((t_end + 14.0, packed_core))
    for i in range(5):
        ev.append((t_end + 15.0 + 2.2 * i, functools.partial(vec_step, i)))
    ev.append((t_end + 19.0, packed_a))
    ev.append((t_end + 23.0, packed_b))
    ev.append((t_end + 34.0, packed_z))

    ev.sort(key=lambda e: e[0])
    for t, fn in ev:
        if t < t_att:
            fn()

    def step(s, carry):
        for k in range(steps):
            here = [fn for t, fn in ev if t_att + k * t_step <= t < t_att + (k + 1) * t_step]
            if here:

                @pl.when(s == k)
                def _():
                    for fn in here:
                        fn()

        backward_step(s % heads, (s // heads) ^ (2 * y + zh), c, grad, mixed, lse, qt, kv, kt, dkv, dqt)
        return carry

    lax.fori_loop(0, steps, step, 0)
    for t, fn in ev:
        if t >= t_end:
            fn()


def backward_all(send, cot, act, sin, gpre, mix, gres, gresf, tok, gain, sums, mixed, lse, qt, kv, kt, fi, nrm, pw):
    D = pltpu.SemaphoreType.DMA
    heads, keys = kv.shape[0], kv.shape[1]
    rows, width = cot.shape
    n_hid = act.shape[1] // width
    units = 2 * n_hid + 1
    blk = (3, 8, width)
    cols = pw.shape[1]
    pb = (3, 8, cols)
    S = jax.ShapeDtypeStruct
    outs = [S(tok.shape, BF), S((n_hid,) + blk, F32), S((3, 8, n_hid * width), F32), S(blk, F32), S((3, 8, 4 * cols), F32), S((24, 128), F32)]
    V = pltpu.VMEM
    rowt = (64, width)
    scr = [V(t.shape, t.dtype) for t in (mixed, lse, qt, kv, kt, fi, nrm, pw, gresf, tok)] + [
        D((10,)),
        V(send.shape, BF),
        V((units, 2, 2, 2, 4) + blk, BF),
        V((units, 4, 4) + blk, BF),
        V((units, 2, 4) + blk, BF),
        V((units, 4) + blk, BF),
        V((units, 2) + blk, BF),
        V((units,) + blk, BF),
        V((heads, keys, 2 * HEAD_DIM), F32),
        V((4, heads * HEAD_DIM, 256), BF),
        V((keys, cols), BF),
        V((2, 2, 4, 2) + rowt, BF),
        V((2, 4, 2) + rowt, BF),
        V((2, 2, 2) + rowt, BF),
        V((2, 2) + rowt, BF),
        V((2,) + rowt, BF),
        V((2,) + rowt, BF),
        V((1, 2, 2, 2, 4) + pb, BF),
        V((4, 4) + pb, BF),
        V((2, 4) + pb, BF),
        V((4,) + pb, BF),
        V((3,) + pb, BF),
        V((24, width), F32),
        V((5, 16, width), F32),
        D,
        D((7,)),
        D((7,)),
        D((units, 10)),
        D((units, 10)),
        D((16,)),
        D((16,)),
        D((10,)),
        D((10,)),
        D((5,)),
        D((5,)),
    ]
    args = (send, cot, act, sin, gpre, mix, gres, gain, *sums, mixed, lse, qt, kv, kt, fi, nrm, pw, gresf, tok)
    return pl.pallas_call(
        backward_kernel,
        out_shape=outs,
        in_specs=[ANY] + [VM] * 12 + [ANY] * 10,
        out_specs=[VM] * len(outs),
        scratch_shapes=scr,
        compiler_params=pltpu.CompilerParams(collective_id=2, has_side_effects=True, vmem_limit_bytes=63 << 20),
        name="backward_reduce",
    )(*args)


def backward_local_kernel(grad, mixed, lse, qt, kv, kt, out, dkv, dqt):
    _, _, c, _ = coords()
    heads, keys = kv.shape[0], kv.shape[1]
    wide = 2 * HEAD_DIM * heads
    dkv[...] = jnp.zeros_like(dkv)

    def step(s, carry):
        backward_step(s % heads, s // heads, c, grad, mixed, lse, qt, kv, kt, dkv, dqt)
        return carry

    lax.fori_loop(0, 4 * heads, step, 0)
    for g in range(8):
        rs = slice(g * 256, (g + 1) * 256)
        for h in range(heads):
            out[rs, 2 * h * HEAD_DIM : 2 * (h + 1) * HEAD_DIM] = dkv[h, rs, :].astype(BF)
        dq = dqt[(g // 4) * 2 + g % 2].astype(F32).T
        out[rs, wide:] = jnp.where((g // 2) % 2 == c, dq, 0.0).astype(BF)


def backward_local(grad, mixed, lse, qt, kv, kt):
    heads, keys = kv.shape[0], kv.shape[1]
    return pl.pallas_call(
        backward_local_kernel,
        out_shape=jax.ShapeDtypeStruct((keys, 3 * heads * HEAD_DIM), BF),
        in_specs=[VM] * 6,
        out_specs=VM,
        scratch_shapes=[pltpu.VMEM((heads, keys, 2 * HEAD_DIM), F32), pltpu.VMEM((4, heads * HEAD_DIM, 256), BF)],
        compiler_params=pltpu.CompilerParams(vmem_limit_bytes=50 << 20),
        name="attention_backward",
    )(grad, mixed, lse, qt, kv, kt)


def reduce_generic(gf, gp, gm, ge, gs, n_dev):
    every = ("dp", "ctx", "head")
    x, y, c, z = coords()
    flat = gf.reshape((1, -1) + gf.shape[-1:])
    both = jnp.concatenate([jnp.where(y == i, flat, jnp.zeros_like(flat)) for i in range(2)], axis=0)
    of = lax.psum_scatter(both.astype(F32), ("ctx", "head"), scatter_dimension=1, tiled=True)
    cols = gp.shape[-1]
    rows = gp.size // cols
    spread = lax.dynamic_update_slice_in_dim(jnp.zeros((rows, 4, cols), F32), gp.reshape(rows, 1, cols).astype(F32), z, 1)
    op = jnp.swapaxes(lax.psum_scatter(spread, every, scatter_dimension=0, tiled=True), 0, 1)
    rest = [
        lax.psum_scatter(g.reshape((n_dev, -1) + g.shape[-1:]).astype(F32), every, scatter_dimension=0, tiled=True)[0] for g in (gm, ge, gs)
    ]
    return [of, op] + rest


def layer_norm(token_rows, norm_gain, norm_shift):
    normed, inv_std = row_norm(token_rows)
    return (normed * norm_gain + norm_shift, normed, inv_std)


def norm_backward(grad_out, normed, inv_std, norm_gain):
    scaled = grad_out * norm_gain
    first_mean = jnp.mean(scaled, axis=-1, keepdims=True)
    second_mean = jnp.mean(scaled * normed, axis=-1, keepdims=True)
    return inv_std * (scaled - first_mean - normed * second_mean)


def gelu_parts(pre_act):
    cumulative = 0.5 * (1.0 + jax.scipy.special.erf(pre_act * (1.0 / math.sqrt(2.0))))
    density = jnp.exp(-0.5 * pre_act * pre_act) * (1.0 / math.sqrt(2.0 * math.pi))
    return pre_act * cumulative, cumulative + pre_act * density


def on_device(
    tokens,
    cotangent,
    lengths,
    attention_gain,
    attention_shift,
    packed_weight,
    query_bias,
    value_bias,
    mixer_weight,
    mixer_bias,
    feedforward_gain,
    feedforward_shift,
    expand_weight,
    expand_bias,
    shrink_weight,
    shrink_bias,
):
    images, shard_len, width = tokens.shape
    groups = lax.axis_size("head")
    heads = HEADS // groups
    part = heads * HEAD_DIM
    hidden = expand_weight.shape[1]
    rows = images * shard_len
    n_dev = lax.axis_size("dp") * lax.axis_size("ctx") * groups
    z = lax.axis_index("head")
    wr = packed_weight.shape[0]
    fr = shrink_weight.shape[0]

    tiled = wr % 8 == 0 and fr % 8 == 0 and lax.axis_size("dp") == 2
    slab = (lambda r, n: (r // 8, 8, n)) if tiled else (lambda r, n: (r, n))
    vecs = [attention_gain, attention_shift, query_bias, value_bias, mixer_bias, feedforward_gain, feedforward_shift, shrink_bias, expand_bias]
    mx, ex, sh = mixer_weight.reshape(slab(wr, width)), expand_weight.reshape(slab(wr, hidden)), shrink_weight.reshape(slab(fr, width))
    if tiled:
        mix, mixed_t, lse, fi, nrm, qt, kv, kt, full_packed, full_vecs, eb, mxo, exo, sho = forward_all(lengths, tokens, packed_weight.reshape(slab(wr, 3 * width)), mx, ex, sh, vecs)
        hidden_bias = eb
    else:
        pk = jnp.stack([own_columns(packed_weight, g, part) for g in range(groups)])
        sv = jnp.stack([jnp.pad(v, (0, 128 - v.shape[0])) for v in vecs] + [jnp.zeros((128,), BF)] * 7)
        img, pko, mxo, exo, sho, svo = gather_generic(tokens, pk, mx, ex, sh, sv)
        full_packed = pko.reshape(width, 3 * part)
        svo = svo.reshape(n_dev, 16, 128).astype(F32)
        gain_one, shift_one, qb, vb, mb, gain_two, shift_two, sb = [svo[:, i, :wr].reshape(width) for i in range(8)]
        eb = svo[:, 8, :fr].reshape(hidden)
        own = lambda v: lax.dynamic_slice_in_dim(v, z * part, part)
        vb_own = own(vb).reshape(heads, 1, HEAD_DIM)
        bias = jnp.concatenate([jnp.concatenate([jnp.zeros_like(vb_own), vb_own], axis=1).reshape(2 * part), own(qb)])
        img = img.reshape(16, shard_len, width)
        mixed_t, lse, fi, nrm, qt, kv, kt = attention_forward(lengths, img, full_packed, gain_one[None], shift_one[None], bias[None])
        mix = exchange(mixed_t, 1)
    mix = mix.reshape(images, width, shard_len)
    full_mixer = mxo.reshape(width, width)
    full_expand = exo.reshape(width, hidden)
    full_shrink = sho.reshape(hidden, width)

    if tiled:
        block_output, activated, second_input, grad_pre_bf, grad_residual_bf, grad_residual, grad_mixed, *sums = dense_layers(
            tokens, cotangent, mix, full_vecs, hidden_bias, full_mixer, full_expand, full_shrink
        )
        ig, os_, oe, om, op, ov = backward_all(
            grad_mixed, cotangent.reshape(rows, width), activated, second_input, grad_pre_bf, mix, grad_residual_bf,
            grad_residual, tokens, full_vecs, sums, mixed_t, lse, qt, kv, kt, fi, nrm, full_packed,
        )
        ig, os_, oe, om, op, *vec = hand_over([ig, os_, oe, om, op], ov, wr, fr)
        op = op.reshape(wr, 3 * width)
    else:
        token_rows = tokens.reshape(rows, width).astype(F32)
        mixed_rows = jnp.swapaxes(mix, 1, 2).reshape(rows, width)
        residual = token_rows + dot(mixed_rows, full_mixer) + mb
        second_out, second_normed, second_inv = layer_norm(residual, gain_two, shift_two)
        second_input = second_out.astype(BF)
        pre_act = dot(second_input, full_expand) + eb
        value, slope = gelu_parts(pre_act)
        activated = value.astype(BF)
        block_output = (residual + dot(activated, full_shrink) + sb).astype(BF)
        grad_in = cotangent.reshape(rows, width)
        grad_rows = grad_in.astype(F32)
        grad_shrink_b = jnp.sum(grad_rows, axis=0)
        grad_pre = jnp.einsum("rd,fd->rf", grad_in, full_shrink, preferred_element_type=F32) * slope
        grad_pre_bf = grad_pre.astype(BF)
        grad_expand_b = jnp.sum(grad_pre, axis=0)
        grad_second = jnp.einsum("rf,df->rd", grad_pre_bf, full_expand, preferred_element_type=F32)
        grad_gain_two = jnp.sum(grad_second * second_normed, axis=0)
        grad_shift_two = jnp.sum(grad_second, axis=0)
        grad_residual = grad_rows + norm_backward(grad_second, second_normed, second_inv, gain_two)
        grad_residual_bf = grad_residual.astype(BF)
        grad_mixer_b = jnp.sum(grad_residual, axis=0)
        grad_mixed = jnp.einsum("de,ire->idr", full_mixer, grad_residual_bf.reshape(images, shard_len, width), preferred_element_type=F32).astype(BF)
        grad_mixed = grad_mixed.reshape(images * groups, part, shard_len)
        grad_t = exchange(grad_mixed, 2)
        dqkv = backward_local(grad_t, mixed_t, lse, qt, kv, kt)
        grad_packed_w = jnp.einsum("rd,re->de", fi, dqkv, preferred_element_type=F32)
        grad_first_part = jnp.einsum("re,de->rd", dqkv, full_packed, preferred_element_type=F32)
        img_normed, _ = row_norm(img.reshape(16 * shard_len, width).astype(F32))
        dsum = jnp.sum(dqkv.astype(F32), axis=0)
        place = lambda v: lax.dynamic_update_slice_in_dim(jnp.zeros((width,), F32), v, z * part, 0)
        sums = [
            jnp.sum(grad_first_part * img_normed, axis=0),
            jnp.sum(grad_first_part, axis=0),
            place(dsum[2 * part :]),
            place(dsum[: 2 * part].reshape(heads, 2, HEAD_DIM)[:, 1].reshape(part)),
            grad_mixer_b,
            grad_gain_two,
            grad_shift_two,
            grad_shrink_b,
            grad_expand_b,
        ]
        vec = [lax.psum_scatter(t, ("dp", "ctx", "head"), scatter_dimension=0, tiled=True) for t in sums]
        of, op, om, oe, os_ = reduce_generic(
            grad_first_part.reshape(2, 2, groups, shard_len, width),
            grad_packed_w,
            jnp.einsum("rd,re->de", mixed_rows, grad_residual_bf, preferred_element_type=F32),
            jnp.einsum("rd,rf->df", second_input, grad_pre_bf, preferred_element_type=F32),
            jnp.einsum("rf,rd->fd", activated, grad_in, preferred_element_type=F32),
            n_dev,
        )
        op = op.reshape(groups, wr, 3 * part)
        okv = jnp.transpose(op[:, :, : 2 * part].reshape(groups, wr, heads, 2, HEAD_DIM), (1, 3, 0, 2, 4)).reshape(wr, 2 * width)
        op = jnp.concatenate([jnp.transpose(op[:, :, 2 * part :], (1, 0, 2)).reshape(wr, width), okv], axis=1)
        _, first_normed, first_inv = layer_norm(token_rows, gain_one, shift_one)
        ig = (grad_residual + norm_backward(of.reshape(rows, width), first_normed, first_inv, gain_one)).astype(BF)
    return (
        block_output.reshape(images, shard_len, width),
        ig.reshape(images, shard_len, width),
        vec[0],
        vec[1],
        op,
        vec[2],
        vec[3],
        om.reshape(wr, width),
        vec[4],
        vec[5],
        vec[6],
        oe.reshape(wr, hidden),
        vec[8],
        os_.reshape(fr, width),
        vec[7],
    )


def solution(mesh):
    every = ("dp", "ctx", "head")
    tok, vec, mat = P("dp", ("ctx", "head"), None), P(every), P(every, None)
    in_specs = (tok, tok, P("dp"), vec, vec, mat, vec, vec, mat, vec, vec, vec, mat, vec, mat, vec)
    out_specs = (tok, tok, vec, vec, mat, vec, vec, mat, vec, vec, vec, mat, vec, mat, vec)
    return jax.shard_map(on_device, mesh=mesh, in_specs=in_specs, out_specs=out_specs, check_vma=False)
```

```python
import functools
import math

import jax
import jax.numpy as jnp
from jax import lax
from jax.experimental import pallas as pl
from jax.experimental.pallas import tpu as pltpu
from jax.sharding import PartitionSpec as P

HEADS = 12
HEAD_DIM = 64
NORM_EPS = 1e-06
MASKED = -1e30
LOG2E = 1.4426950408889634
MESH = pl.DeviceIdType.MESH
ANY = pl.BlockSpec(memory_space=pl.ANY)
VM = pl.BlockSpec(memory_space=pltpu.VMEM)
SM = pl.BlockSpec(memory_space=pltpu.SMEM)
BF = jnp.bfloat16
F32 = jnp.float32
SPLIT = 2


def coords():
    ctx = lax.axis_index("ctx")
    return lax.axis_index("dp"), ctx // SPLIT, ctx % SPLIT, lax.axis_index("head")


def device(x, y, c, z):
    return (x, y * SPLIT + c, z)


def enter(targets):
    sem = pltpu.get_barrier_semaphore()
    for t in targets:
        pl.semaphore_signal(sem, inc=1, device_id=t, device_id_type=MESH)
    pl.semaphore_wait(sem, len(targets))


def rcopy(src, dst, ss, rs, to):
    return pltpu.make_async_remote_copy(src, dst, ss, rs, device_id=to, device_id_type=MESH)


def run_events(events):
    for _, fn in sorted(events, key=lambda e: e[0]):
        fn()


def partners(x, y, c, z):
    return dict(
        core=device(x, y, 1 - c, z),
        x=device(1 - x, y, c, z),
        y=device(x, 1 - y, c, z),
        z1=device(x, y, c, z ^ 1),
        z2=device(x, y, c, z ^ 2),
        z3=device(x, y, c, z ^ 3),
    )


def weight_gather(ev, co, to, src, out, sems, order, times):
    x, y, c, z = co
    lsem, zss, zrs, ass, ars, bss, brs, css, crs = sems
    a, b = order

    def spot(fa, fb):
        px = (1 - x if fa else x) if a == "x" else (1 - x if fb else x)
        py = (1 - y if fa else y) if a == "y" else (1 - y if fb else y)
        return px, py

    def at(fa, fb, k):
        return out(*spot(fa, fb), c, z ^ k)

    def group(fa, fb, cc):
        return out(*spot(fa, fb), cc, slice(None))

    F, T = False, True
    zsend = lambda i, k, ref, dst, name: rcopy(ref, dst, zss.at[i], zrs.at[k], to[name])
    asend = lambda k, ref: rcopy(ref, at(F, F, k), ass.at[k], ars.at[k], to[a])
    bsend = lambda fa, k, ref: rcopy(ref, at(fa, F, k), bss.at[int(fa), k], brs.at[int(fa), k], to[b])
    csend = lambda i, g: rcopy(g, g, css.at[i], crs.at[i], to["core"])
    local = lambda: pltpu.make_async_copy(src, at(F, F, 0), lsem)

    def begin():
        local().start()
        asend(0, src).start()
        bsend(F, 0, src).start()

    def z_begin():
        zsend(0, 0, src, at(F, F, 0), "z1").start()
        zsend(1, 1, src, at(F, F, 0), "z2").start()

    def z_land(k):
        d = at(F, F, k)
        zsend(k - 1, k - 1, d, d, "z1").wait_recv()
        if k == 2:
            zsend(2, 2, d, d, "z1").start()
        asend(k, d).start()
        bsend(F, k, d).start()

    def own_done():
        local().wait()
        csend(0, group(F, F, c)).start()

    def a_land(k):
        d = at(T, F, k)
        asend(k, d).wait_recv()
        bsend(T, k, d).start()
        if k == 3:
            csend(1, group(T, F, c)).start()

    def b_land(fa):
        for k in range(4):
            bsend(fa, k, at(fa, T, k)).wait_recv()
        csend(2 + int(fa), group(fa, T, c)).start()

    def last():
        d = at(F, F, 0)
        for i in range(3):
            zsend(i, 0, d, d, "z1").wait_send()
        for k in range(4):
            asend(k, d).wait_send()
            bsend(F, k, d).wait_send()
            bsend(T, k, d).wait_send()
        for i, (fa, fb) in enumerate(((F, F), (T, F), (F, T), (T, T))):
            csend(i, group(fa, fb, 1 - c)).wait()

    t_begin, t_z, t_zl, t_al, t_bl = times
    ev.append((t_begin, begin))
    ev.append((t_z, z_begin))
    for k in range(1, 4):
        ev.append((t_zl[k - 1], functools.partial(z_land, k)))
    ev.append((t_zl[2] + 0.3, own_done))
    for k in range(4):
        ev.append((t_al[k], functools.partial(a_land, k)))
    ev.append((t_bl[0], functools.partial(b_land, F)))
    ev.append((t_bl[1], functools.partial(b_land, T)))
    ev.append((1000.0, last))


def half_gather(ev, co, to, prepare, settle, own, view, sems, times):
    x, y, c, z = co
    zss, zrs, yss, yrs, css, crs = sems
    at = lambda k: view(y, c, z ^ k)
    zsend = lambda i, k, ref, dst, name: rcopy(ref, dst, zss.at[i], zrs.at[k], to[name])
    ysend = lambda k, ref: rcopy(ref, at(k), yss.at[k], yrs.at[k], to["y"])

    def csend(i):
        g = view(y if i == 0 else 1 - y, c, slice(None))
        return rcopy(g, g, css.at[i], crs.at[i], to["core"])

    def begin():
        prepare()
        ysend(0, own).start()

    def z_begin():
        zsend(0, 0, own, at(0), "z1").start()
        zsend(1, 1, own, at(0), "z2").start()

    def z_land(k):
        d = at(k)
        zsend(k - 1, k - 1, d, d, "z1").wait_recv()
        if k == 2:
            zsend(2, 2, d, d, "z1").start()
        ysend(k, d).start()
        if k == 3:
            settle()
            csend(0).start()

    def y_land():
        for k in range(4):
            d = view(1 - y, c, z ^ k)
            rcopy(d, d, yss.at[k], yrs.at[k], to["y"]).wait_recv()
        csend(1).start()

    def last():
        d = at(0)
        for i in range(3):
            zsend(i, 0, d, d, "z1").wait_send()
        for k in range(4):
            ysend(k, d).wait_send()
        for i in range(2):
            csend(i).wait()

    t_begin, t_z, t_zl, t_y = times
    ev.append((t_begin, begin))
    ev.append((t_z, z_begin))
    for k in range(1, 4):
        ev.append((t_zl[k - 1], functools.partial(z_land, k)))
    ev.append((t_y, y_land))
    ev.append((1000.5, last))


def small_gather(co, to, src, out, ls, ss, rs, spread):
    x, y, c, z = co
    own = src.at[z] if spread else src

    def begin():
        pltpu.make_async_copy(own, out.at[x, y, c, z], ls).start()
        for k in (1, 2, 3):
            rcopy(src.at[z ^ k] if spread else src, out.at[x, y, c, z], ss.at[k - 1], rs.at[k - 1], to["z%d" % k]).start()

    def step_y():
        pltpu.make_async_copy(own, out.at[x, y, c, z], ls).wait()
        for k in (1, 2, 3):
            d = out.at[x, y, c, z ^ k]
            rcopy(d, d, ss.at[k - 1], rs.at[k - 1], to["z1"]).wait()
        g = out.at[x, y, c]
        rcopy(g, g, ss.at[3], rs.at[3], to["y"]).start()

    def step_x():
        g = out.at[x, 1 - y, c]
        rcopy(g, g, ss.at[3], rs.at[3], to["y"]).wait()
        for yy in range(2):
            g = out.at[x, yy, c]
            rcopy(g, g, ss.at[4 + yy], rs.at[4 + yy], to["x"]).start()

    def step_c():
        for yy in range(2):
            g = out.at[1 - x, yy, c]
            rcopy(g, g, ss.at[4 + yy], rs.at[4 + yy], to["x"]).wait()
        for xx in range(2):
            for yy in range(2):
                g = out.at[xx, yy, c]
                rcopy(g, g, ss.at[6 + 2 * xx + yy], rs.at[6 + 2 * xx + yy], to["core"]).start()

    def last():
        for xx in range(2):
            for yy in range(2):
                g = out.at[xx, yy, 1 - c]
                rcopy(g, g, ss.at[6 + 2 * xx + yy], rs.at[6 + 2 * xx + yy], to["core"]).wait()

    return begin, step_y, step_x, step_c, last


def gather_generic(tok, pk, mx, ex, sh, sv):
    every = ("dp", "ctx", "head")
    images = lax.all_gather(tok, ("ctx", "head"), axis=1, tiled=True)
    img = lax.dynamic_index_in_dim(images, coords()[1], 0, keepdims=False)
    spread = lax.all_gather(pk, every, axis=1, tiled=True)
    pko = lax.dynamic_index_in_dim(spread, lax.axis_index("head"), 0, keepdims=False)
    return [img, pko] + [lax.all_gather(t, every, axis=0, tiled=True) for t in (mx, ex, sh, sv)]


def exchange_kernel(src, dst, ls, ss, rs):
    x, y, c, z = coords()
    others = [(dy, dz) for dy in range(2) for dz in range(4) if dy or dz]
    enter([device(x, y ^ dy, c, z ^ dz) for dy, dz in others])
    me = y * 4 + z
    mine = pltpu.make_async_copy(src.at[me], dst.at[me], ls)
    mine.start()
    copies = []
    for i, (dy, dz) in enumerate(others):
        ty, tz = y ^ dy, z ^ dz
        cp = rcopy(src.at[ty * 4 + tz], dst.at[me], ss.at[i], rs.at[i], device(x, ty, c, tz))
        cp.start()
        copies.append(cp)
    mine.wait()
    for cp in copies:
        cp.wait()


def exchange(src, cid):
    D = pltpu.SemaphoreType.DMA
    return pl.pallas_call(
        exchange_kernel,
        out_shape=jax.ShapeDtypeStruct(src.shape, src.dtype),
        in_specs=[ANY],
        out_specs=ANY,
        scratch_shapes=[D, D((7,)), D((7,))],
        compiler_params=pltpu.CompilerParams(collective_id=cid, has_side_effects=True),
        name="exchange_heads_%d" % cid,
    )(src)


def dot(a, b):
    return jnp.dot(a, b, preferred_element_type=F32)


def dot_nt(a, b):
    return lax.dot_general(a, b, (((1,), (1,)), ((), ())), preferred_element_type=F32)


def row_norm(rows):
    mean = jnp.mean(rows, axis=-1, keepdims=True)
    centred = rows - mean
    inv = lax.rsqrt(jnp.mean(centred * centred, axis=-1, keepdims=True) + NORM_EPS)
    return centred * inv, inv


def project(g, rows, length, gain, shift, bias, pw, fi, nrm, qt, kv, kt, vt):
    heads = kv.shape[0]
    hd, step = HEAD_DIM, 256
    wide = 2 * hd * heads
    normed, _ = row_norm(rows.astype(F32))
    first = (normed * gain + shift).astype(BF)
    off = pl.multiple_of(g * step, step)
    fi[pl.ds(off, step), :] = first
    nrm[pl.ds(off, step), :] = normed.astype(BF)
    kvq = (dot(first, pw[...]) + bias).astype(BF).astype(F32)
    flip = kvq.T
    ones = jnp.where(lax.broadcasted_iota(jnp.int32, (16, step), 0) == 0, 1.0, 0.0)
    pos = off + lax.broadcasted_iota(jnp.int32, (step, 2 * hd), 0)
    lane = lax.broadcasted_iota(jnp.int32, (step, 2 * hd), 1)
    extra = jnp.where(lane == 0, jnp.where(pos < length, 0.0, MASKED), jnp.where(lane < 4, 1.0, 0.0)).astype(BF)
    for h in range(heads):
        kt[h, g] = flip[2 * h * hd : (2 * h + 1) * hd].astype(BF)
        vt[h, g] = jnp.concatenate([flip[(2 * h + 1) * hd : (2 * h + 2) * hd], ones], axis=0).astype(BF)
        qt[g, h] = (flip[wide + h * hd : wide + (h + 1) * hd] * (1.0 / math.sqrt(hd))).astype(BF)
        kv[h, pl.ds(off, step), : 2 * hd] = kvq[:, 2 * h * hd : (2 * h + 2) * hd].astype(BF)
        kv[h, pl.ds(off, step), 2 * hd :] = extra


def attend(h, j, c, qt, kv, vt, mixed, lse):
    keys = kv.shape[1]
    hd, step, chunk = HEAD_DIM, 256, 512
    per = chunk // step
    row = lax.broadcasted_iota(jnp.int32, (16, step), 0)
    unit = jnp.where(row == 0, 1.0, 0.0).astype(BF)
    g = (j // 2) * 4 + c * 2 + j % 2
    sl = pl.ds(pl.multiple_of(h * hd, hd), hd)
    qa = jnp.concatenate([qt[g, h], jnp.zeros((hd, step), BF), unit, jnp.zeros((2 * hd - 16, step), BF)], axis=0)
    top = jnp.full((1, step), MASKED, F32)
    acc = jnp.zeros((hd + 16, step), F32)
    for kc in range(keys // chunk):
        s = dot(kv[h, kc * chunk : (kc + 1) * chunk, :], qa)
        new = jnp.maximum(top, jnp.max(s, axis=0, keepdims=True))
        pb = jnp.exp2((s - new) * LOG2E).astype(BF)
        scale = jnp.exp2((top - new) * LOG2E)
        part = dot(vt[h, kc * per], pb[:step])
        for i in range(1, per):
            part += dot(vt[h, kc * per + i], pb[i * step : (i + 1) * step])
        acc = acc * scale + part
        top = new
    total = acc[hd : hd + 1]
    out = acc[:hd] / total
    lse[j, h] = top + jnp.log(total)
    for i in range(2):
        mixed[2 * j + i, sl, :] = out[:, i * 128 : (i + 1) * 128].astype(BF)


def forward_kernel(lens, img, pw, gain, shift, bias, mixed, lse, fi, nrm, qt, kv, kt, vt):
    x, y, c, z = coords()
    heads, keys = kv.shape[0], kv.shape[1]
    length = lens[y]

    def rows_of(g, carry):
        rows = img[pl.ds(2 * g, 2)].reshape(256, img.shape[2])
        project(g, rows, length, gain[...], shift[...], bias[...], pw, fi, nrm, qt, kv, kt, vt)
        return carry

    def step(s, carry):
        attend(s % heads, s // heads, c, qt, kv, vt, mixed, lse)
        return carry

    lax.fori_loop(0, keys // 256, rows_of, 0)
    lax.fori_loop(0, 4 * heads, step, 0)


FT = dict(
    small=(0.0, 4.6, 12.3, 15.5, 18.4),
    tok=((0.1, 12.0, 12.1, 22.5), (4.8, 18.3, 22.0, 28.5)),
    mx=(5.5, 25.95, (33.2, 33.8, 39.5), (18.35, 36.0, 37.0, 43.0), (45.0, 48.0)),
    ex=(5.4, 31.0, (41.0, 41.6, 47.0), 52.0),
    sh=(5.3, 25.9, (33.0, 33.6, 39.0), 44.0),
    att=(30.0, 2.0),
)


def own_columns(rows, g, part):
    width = rows.shape[1] // 3
    at = lambda t, h: rows[:, t * width + g * part + h * HEAD_DIM : t * width + g * part + (h + 1) * HEAD_DIM]
    heads = part // HEAD_DIM
    return jnp.concatenate([at(t, h) for h in range(heads) for t in (1, 2)] + [at(0, h) for h in range(heads)], axis=1)


def forward_all_kernel(
    lens, tok, cot, pkw, mx, ex, sh, v0, v1, v2, v3, v4, v5, v6, v7, v8,
    mix, mixed_o, lse_o, fi_o, nrm_o, qt_o, kv_o, kt_o, pw_o, vec, hid, mxo, exo, sho, cotx,
    pk, sv, img, pwg, svg, mixed, lse, fi, nrm, qt, kv, kt, vt, pw, bias,
    ls, tys, tzs, tzr, tcs, tcr, ps, pr, vs, vr, xs, xr, xl, osem, xps, xpr, *wsems,
):
    co = coords()
    x, y, c, z = co
    to = partners(*co)
    zh = z // 2
    heads, keys = kv.shape[0], kv.shape[1]
    width = img.shape[4]
    n_dev = 32
    others = [(dy, dz) for dy in range(2) for dz in range(4) if dy or dz]
    part = heads * HEAD_DIM
    raw = pkw[...].astype(F32).reshape(3 * 8, pkw.shape[2])
    for g in range(4):
        pk[g] = own_columns(raw, g, part).astype(BF).reshape(3, 8, 3 * part)
    lines = [jnp.concatenate([v[...].astype(F32).reshape(1, -1), jnp.zeros((1, 128 - v.shape[-1]), F32)], axis=1) for v in (v0, v1, v2, v3, v4, v5, v6, v7, v8)]
    sv[...] = jnp.concatenate(lines + [jnp.zeros((7, 128), F32)], axis=0).astype(BF)
    enter([to["core"], to["x"]] + [device(x, y ^ dy, c, z ^ dz) for dy, dz in others])
    length = lens[y]
    ev = []

    row = lambda r: y if r == 0 else 1 - y

    def tz(r, i, k, ref, dst, name):
        return rcopy(ref, dst, tzs.at[r, i], tzr.at[r, k], to[name])

    def tcore(r, k, ref):
        return rcopy(ref, img.at[row(r), c, z ^ k], tcs.at[r, k], tcr.at[r, k], to["core"])

    spread = lambda: rcopy(tok.at[1 - y], img.at[y, c, z], tys.at[0], tys.at[1], to["y"])
    keep = lambda: pltpu.make_async_copy(tok.at[y], img.at[y, c, z], ls.at[0])

    def t_begin(r):
        d = img.at[row(r), c, z]
        if r == 0:
            spread().start()
            keep().start()
            own = tok.at[y]
        else:
            rcopy(d, d, tys.at[0], tys.at[1], to["y"]).wait()
            own = d
        tz(r, 0, 0, own, d, "z1").start()
        tz(r, 1, 1, own, d, "z2").start()
        tcore(r, 0, own).start()

    def t_land(r, k):
        d = img.at[row(r), c, z ^ k]
        tz(r, k - 1, k - 1, d, d, "z1").wait_recv()
        if k == 2:
            tz(r, 2, 2, d, d, "z1").start()
        tcore(r, k, d).start()

    for r in range(2):
        t = FT["tok"][r]
        ev.append((t[0], functools.partial(t_begin, r)))
        for k in range(1, 4):
            ev.append((t[k], functools.partial(t_land, r, k)))

    def t_last():
        for r in range(2):
            d = img.at[row(r), c, z]
            for i in range(3):
                tz(r, i, 0, d, d, "z1").wait_send()
            for k in range(4):
                tcore(r, k, d).wait_send()

    ev.append((1001.0, t_last))

    steps_v = small_gather(co, to, sv, svg, ls.at[1], vs, vr, False)
    steps_p = small_gather(co, to, pk, pwg, ls.at[4], ps, pr, True)
    for t, fv, fp in zip(FT["small"], steps_v, steps_p):
        ev.append((t, fv))
        ev.append((t + 0.05, fp))

    def unpack():
        small = width // n_dev
        big = hid.shape[1] // n_dev
        part = heads * HEAD_DIM
        across = lambda n: lax.broadcasted_iota(jnp.int32, (1, n), 1)
        down = lambda n: lax.broadcasted_iota(jnp.int32, (n, 1), 0)
        hot = lambda m: jnp.where(m, 1.0, 0.0).astype(BF)
        col = across(width)
        val = dot(svg[...].reshape(n_dev * 16, 128), hot(col % small == down(128)))
        val = jnp.where(col // small == down(n_dev * 16) // 16, val, 0.0)
        val = jnp.sum(val.reshape(n_dev, 16, width), axis=0)
        vec[...] = val
        col = across(hid.shape[1])
        eight = svg[...].astype(F32).reshape(n_dev, 16, 128)[:, 8, :].astype(BF)
        line = dot(eight, hot(col % big == down(128)))
        hid[...] = jnp.sum(jnp.where(col // big == down(n_dev), line, 0.0), axis=0, keepdims=True)
        dst = across(3 * part)
        head, off = dst // (2 * HEAD_DIM), dst % (2 * HEAD_DIM)
        hv = jnp.where(jnp.logical_and(dst < 2 * part, off >= HEAD_DIM), z * part + head * HEAD_DIM + off - HEAD_DIM, -1)
        hq = jnp.where(dst >= 2 * part, z * part + dst - 2 * part, -1)
        rows = val.astype(BF)
        bq = dot(rows, hot(hq == down(width)))
        bv = dot(rows, hot(hv == down(width)))
        bias[...] = bq[2:3] + bv[3:4]

    def flatten():
        def body(i, carry):
            blk = pwg[i // 4, (i // 2) % 2, i % 2].astype(F32)
            n = blk.shape[0] * blk.shape[1] * blk.shape[2]
            pw[pl.ds(pl.multiple_of(i * n, n), n), :] = blk.reshape(n, blk.shape[3]).astype(BF)
            return carry

        lax.fori_loop(0, 8, body, 0)

    ev.append((FT["small"][4] + 0.1, unpack))
    ev.append((FT["small"][4] + 0.2, flatten))

    def project_group(r, mine, p):
        cc = c if mine else 1 - c
        zz = zh if p == 0 else 1 - zh
        if r == 0 and mine and p == 0:
            keep().wait()
        if not mine:
            for k in (2 * p, 2 * p + 1):
                d = img.at[row(r), cc, z ^ k]
                rcopy(d, d, tcs.at[r, k], tcr.at[r, k], to["core"]).wait_recv()
        g = row(r) * 4 + cc * 2 + zz
        rows = img[row(r), cc, pl.ds(2 * zz, 2)].reshape(256, width)
        project(g, rows, length, vec[0:1, :], vec[1:2, :], bias[...], pw, fi, nrm, qt, kv, kt, vt)

    t_ready = FT["small"][4] + 0.3
    for p in range(2):
        for r in range(2):
            for mine in (True, False):
                t = max(FT["tok"][r][1 if p == 0 else 3] + (0.3 if mine else 0.6), t_ready + 0.01 * (r * 2 + (not mine)))
                ev.append((t, functools.partial(project_group, r, mine, p)))

    weight_gather(ev, co, to, mx, lambda px, py, cc, zz: mxo.at[px, py, cc, zz], wsems[:9], "yx", FT["mx"])
    half = ex.shape[2] // 2
    cols = lambda xx: pl.ds(pl.multiple_of(xx * half, half), half)
    ex_view = lambda yy, cc, zz: exo.at[:, yy, cc, zz]
    sh_view = lambda yy, cc, zz: sho.at[yy, cc, zz]
    ex_own = lambda: pltpu.make_async_copy(ex.at[:, :, cols(x)], exo.at[x, y, c, z], ls.at[2])
    ex_swap = lambda: rcopy(ex.at[:, :, cols(1 - x)], exo.at[x, y, c, z], xps.at[0], xpr.at[0], to["x"])
    sh_own = lambda: pltpu.make_async_copy(sh, sho.at[y, c, z], ls.at[3])
    cot_swap = lambda: rcopy(cot, cotx, xps.at[1], xpr.at[1], to["x"])

    def swap():
        ex_own().start()
        ex_swap().start()
        cot_swap().start()

    def ex_ready():
        ex_own().wait()
        ex_swap().wait()

    ev.append((0.6, swap))
    ev.append((1003.0, lambda: cot_swap().wait()))
    half_gather(ev, co, to, ex_ready, lambda: None, ex_view(y, c, z), ex_view, wsems[9:15], FT["ex"])
    half_gather(ev, co, to, lambda: sh_own().start(), lambda: sh_own().wait(), sh, sh_view, wsems[15:21], FT["sh"])

    stored = [(fi, fi_o), (nrm, nrm_o), (qt, qt_o), (kv, kv_o), (kt, kt_o), (pw, pw_o), (mixed, mixed_o), (lse, lse_o)]
    store = lambda i: pltpu.make_async_copy(stored[i][0], stored[i][1], osem.at[i])

    def store_first():
        for i in range(6):
            store(i).start()

    t_att, t_step = FT["att"]
    steps = 4 * heads
    t_end = t_att + steps * t_step
    ev.append((t_att + 0.001, store_first))

    me = y * 4 + z

    def target(q):
        w = 3 - q
        return [(w // 2, 2 * (w % 2)), (w // 2, 2 * (w % 2) + 1)]

    def xcopy(dy, dz):
        i = dy * 4 + dz
        return rcopy(mixed.at[(y ^ dy) * 4 + (z ^ dz)], mix.at[me], xs.at[i], xr.at[i], device(x, y ^ dy, c, z ^ dz))

    mine_copy = lambda: pltpu.make_async_copy(mixed.at[me], mix.at[me], xl)

    def send_group(q):
        for dy, dz in target(q):
            if dy or dz:
                xcopy(dy, dz).start()
            else:
                mine_copy().start()

    for q in range(4):
        ev.append((t_att + (q + 1) * heads * t_step + 0.002, functools.partial(send_group, q)))

    def finish():
        store(6).start()
        store(7).start()
        for dy, dz in others:
            xcopy(dy, dz).wait()
        mine_copy().wait()

    ev.append((t_end + 0.5, finish))

    def drain():
        for i in range(8):
            store(i).wait()

    ev.append((1002.0, drain))

    ev.sort(key=lambda e: e[0])
    for t, fn in ev:
        if t < t_att:
            fn()

    def step(s, carry):
        for k in range(steps):
            here = [fn for t, fn in ev if t_att + k * t_step <= t < t_att + (k + 1) * t_step]
            if here:

                @pl.when(s == k)
                def _():
                    for fn in here:
                        fn()

        attend(s % heads, (3 - s // heads) ^ (2 * y + zh), c, qt, kv, vt, mixed, lse)
        return carry

    lax.fori_loop(0, steps, step, 0)
    for t, fn in ev:
        if t >= t_end:
            fn()


def forward_all(lens, tok, cot, pkw, mx, ex, sh, vecs):
    D, V, S = pltpu.SemaphoreType.DMA, pltpu.VMEM, jax.ShapeDtypeStruct
    shard, width = tok.shape[1], tok.shape[2]
    cols = pkw.shape[2] // 4
    pk_shape = (3, 8, cols)
    heads = cols // (3 * HEAD_DIM)
    keys = 16 * shard
    n = keys // 256
    lead = (2, SPLIT, SPLIT, 4)
    part = heads * HEAD_DIM
    hidden = ex.shape[2]
    outs = [
        S((8, part, shard), BF),
        S((8, part, shard), BF),
        S((4, heads, 1, 256), F32),
        S((keys, width), BF),
        S((keys, width), BF),
        S((n, heads, HEAD_DIM, 256), BF),
        S((heads, keys, 4 * HEAD_DIM), BF),
        S((heads, n, HEAD_DIM, 256), BF),
        S((width, cols), BF),
        S((16, width), F32),
        S((1, hidden), F32),
        S(lead + mx.shape, BF),
        S(lead + (3, 8, hidden // 2), BF),
        S(lead[1:] + sh.shape, BF),
        S(cot.shape, BF),
    ]
    wsem = [D, D((3,)), D((3,)), D((4,)), D((4,)), D((2, 4)), D((2, 4)), D((4,)), D((4,))]
    wsem += [D((3,)), D((3,)), D((4,)), D((4,)), D((2,)), D((2,))] * 2
    scr = [V((4,) + pk_shape, BF), V((16, 128), BF)]
    scr += [V((2, 2, 4) + tok.shape[1:], BF), V(lead + pk_shape, BF), V(lead + (16, 128), BF), V((8, part, shard), BF), V((4, heads, 1, 256), F32)]
    scr += [V((keys, width), BF), V((keys, width), BF), V((n, heads, HEAD_DIM, 256), BF), V((heads, keys, 4 * HEAD_DIM), BF)]
    scr += [V((heads, n, HEAD_DIM, 256), BF), V((heads, n, HEAD_DIM + 16, 256), BF), V((width, cols), BF), V((1, cols), F32)]
    scr += [D((5,)), D((2,)), D((2, 3)), D((2, 3)), D((2, 4)), D((2, 4)), D((10,)), D((10,)), D((10,)), D((10,)), D((8,)), D((8,)), D, D((8,)), D((2,)), D((2,))]
    return pl.pallas_call(
        forward_all_kernel,
        out_shape=outs,
        in_specs=[SM, ANY, ANY, VM, ANY, ANY, ANY] + [VM] * 9,
        out_specs=[ANY] * 9 + [VM] * 2 + [ANY] * 4,
        scratch_shapes=scr + wsem,
        compiler_params=pltpu.CompilerParams(collective_id=0, has_side_effects=True, vmem_limit_bytes=62 << 20),
        name="gather_attention_forward",
    )(lens, tok, cot, pkw, mx, ex, sh, *vecs)


def attention_forward(lens, img, pw, gain, shift, bias):
    heads = pw.shape[1] // (3 * HEAD_DIM)
    keys = img.shape[0] * img.shape[1]
    width = heads * HEAD_DIM
    n = keys // 256
    outs = [
        jax.ShapeDtypeStruct((8, width, 128), BF),
        jax.ShapeDtypeStruct((4, heads, 1, 256), F32),
        jax.ShapeDtypeStruct((keys, img.shape[2]), BF),
        jax.ShapeDtypeStruct((keys, img.shape[2]), BF),
        jax.ShapeDtypeStruct((n, heads, HEAD_DIM, 256), BF),
        jax.ShapeDtypeStruct((heads, keys, 4 * HEAD_DIM), BF),
        jax.ShapeDtypeStruct((heads, n, HEAD_DIM, 256), BF),
    ]
    return pl.pallas_call(
        forward_kernel,
        out_shape=outs,
        in_specs=[SM] + [VM] * 5,
        out_specs=[VM] * 7,
        scratch_shapes=[pltpu.VMEM((heads, n, HEAD_DIM + 16, 256), BF)],
        compiler_params=pltpu.CompilerParams(vmem_limit_bytes=50 << 20),
        name="attention_forward",
    )(lens, img, pw, gain, shift, bias)


def dot_tn(a, b):
    return lax.dot_general(a, b, (((0,), (0,)), ((), ())), preferred_element_type=F32)


def dense_kernel(
    tok, cot, cotx, mix, vec, hid, mx_h, ex_h, sh_h,
    base, upx, act, sin, cot2, gpre, gres, gresf, send, s4, s5, s6, s7, s8,
    mx, ex, sh, down_out, down_in, sems, ss, rs,
):
    co = coords()
    x = co[0]
    to = partners(*co)["x"]
    images, shard, width = tok.shape
    rows = images * shard
    half = ex.shape[1]
    n = half // width
    load = [pltpu.make_async_copy(mx_h, mx, sems.at[0])]
    for i in range(n):
        cols = slice(i * width, (i + 1) * width)
        load.append(pltpu.make_async_copy(ex_h.at[:, cols], ex.at[:, cols], sems.at[1 + i]))
        load.append(pltpu.make_async_copy(sh_h.at[cols, :], sh.at[cols, :], sems.at[1 + n + i]))
    for cp in load:
        cp.start()
    cin = cot[...].reshape(rows, width)
    cf = cin.astype(F32)
    s7[...] = jnp.sum(cf, axis=0, keepdims=True)
    cot2[:rows, :] = cin
    cot2[rows:, :] = cotx[...].reshape(rows, width)
    enter([to])

    def sin_copy(i):
        return rcopy(sin.at[i * shard : (i + 1) * shard], sin.at[rows + i * shard : rows + (i + 1) * shard], ss.at[i], rs.at[i], to)

    def down_copy(i):
        return rcopy(down_out.at[i], down_in.at[i], ss.at[images + i], rs.at[images + i], to)

    load[0].wait()
    keep = []
    for i in range(images):
        res = tok[i].astype(F32) + dot_tn(mix[i], mx[...]) + vec[4:5, :]
        nr, iv = row_norm(res)
        sin[i * shard : (i + 1) * shard, :] = (nr * vec[5:6, :] + vec[6:7, :]).astype(BF)
        sin_copy(i).start()
        keep.append((res, nr, iv))
    residual, normed, inv = [jnp.concatenate(t, axis=0) for t in zip(*keep)]
    own = pl.ds(pl.multiple_of(x * half, half), half)
    s8[...] = jnp.zeros_like(s8)

    def chunks(lo, hi):
        up = jnp.zeros((hi - lo, width), F32)
        down = jnp.zeros((hi - lo, width), F32)
        second = sin[lo:hi, :]
        grad = cot2[lo:hi, :]
        for i in range(n):
            cols = slice(i * width, (i + 1) * width)
            if lo == 0:
                load[1 + 2 * i].wait()
                load[2 + 2 * i].wait()
            there = pl.ds(pl.multiple_of(x * half + i * width, width), width)
            pre = dot(second, ex[:, cols]) + hid[:, there]
            cum = 0.5 * (1.0 + lax.erf(pre * (1.0 / math.sqrt(2.0))))
            slope = cum + pre * (jnp.exp(-0.5 * pre * pre) * (1.0 / math.sqrt(2.0 * math.pi)))
            a = (pre * cum).astype(BF)
            act[lo:hi, cols] = a
            g = dot_nt(grad, sh[cols, :]) * slope
            s8[:, there] += jnp.sum(g, axis=0, keepdims=True)
            gb = g.astype(BF)
            gpre[lo:hi, cols] = gb
            up += dot(a, sh[cols, :])
            down += dot_nt(gb, ex[:, cols])
        return up, down

    up, down = chunks(0, rows)
    base[...] = (residual + up + vec[7:8, :]).reshape(images, shard, width)
    for i in range(images):
        sin_copy(i).wait()
        other_up, other_down = chunks(rows + i * shard, rows + (i + 1) * shard)
        down_out[i] = other_down.astype(BF)
        down_copy(i).start()
        upx[i] = other_up.astype(BF)
    rest = []
    for i in range(images):
        down_copy(i).wait()
        part = slice(i * shard, (i + 1) * shard)
        total = down[part] + down_in[i].astype(F32)
        nr = normed[part]
        scaled = total * vec[5:6, :]
        m1 = jnp.mean(scaled, axis=-1, keepdims=True)
        m2 = jnp.mean(scaled * nr, axis=-1, keepdims=True)
        gr = cf[part] + inv[part] * (scaled - m1 - nr * m2)
        gresf[i] = gr
        gb = gr.astype(BF)
        gres[part, :] = gb
        val = dot_nt(mx[...], gb).astype(BF)
        send[4 * i : 4 * (i + 1)] = val.reshape(4, width // 4, shard)
        sums = [jnp.sum(t, axis=0, keepdims=True) for t in (gr, total * nr, total)]
        rest.append(sums)
    for ref, a, b in zip((s4, s5, s6), *rest):
        ref[...] = a + b


def dense_layers(tok, cot, cotx, mix, vec, hid, mx, ex, sh):
    S, V, D = jax.ShapeDtypeStruct, pltpu.VMEM, pltpu.SemaphoreType.DMA
    images, shard, width = tok.shape
    rows, half = images * shard, ex.shape[1]
    line = S((1, width), F32)
    outs = [
        S(tok.shape, F32),
        S(tok.shape, BF),
        S((2 * rows, half), BF),
        S((2 * rows, width), BF),
        S((2 * rows, width), BF),
        S((2 * rows, half), BF),
        S((rows, width), BF),
        S(tok.shape, F32),
        S((4 * images, width // 4, shard), BF),
    ] + [line] * 4 + [S((1, 2 * half), F32)]
    return pl.pallas_call(
        dense_kernel,
        out_shape=outs,
        in_specs=[VM] * 6 + [ANY] * 3,
        out_specs=[VM] * len(outs),
        scratch_shapes=[
            V(mx.shape, BF),
            V(ex.shape, BF),
            V(sh.shape, BF),
            V(tok.shape, BF),
            V(tok.shape, BF),
            D((1 + 2 * (half // width),)),
            D((2 * images,)),
            D((2 * images,)),
        ],
        compiler_params=pltpu.CompilerParams(collective_id=5, has_side_effects=True, vmem_limit_bytes=62 << 20),
        name="dense_layers",
    )(tok, cot, cotx, mix, vec, hid, mx, ex, sh)


def hand_over_kernel(*refs):
    n = 6
    src, vec, dst, outs = refs[:n], refs[n], refs[n + 1 : 2 * n + 1], refs[2 * n + 1 :]
    for i in range(n):
        dst[i][...] = src[i][...]
    for i, o in enumerate(outs):
        line = 16 if i == 8 else i
        o[...] = vec[line : line + 1, : o.shape[0]].reshape(o.shape[0])


def hand_over(arrays, vec, small, big):
    S = jax.ShapeDtypeStruct
    outs = [S(t.shape, t.dtype) for t in arrays] + [S((small,), F32)] * 8 + [S((big,), F32)]
    return pl.pallas_call(
        hand_over_kernel,
        out_shape=outs,
        in_specs=[VM] * 7,
        out_specs=[VM] * 15,
        name="hand_over",
    )(*arrays, vec)


def split3(value):
    hi = value.astype(BF)
    rest = value - hi.astype(F32)
    mid = rest.astype(BF)
    low = (rest - mid.astype(F32)).astype(BF)
    return hi, mid, low


def pick(value, hot):
    a, b, d = split3(value)
    return dot(a, hot) + dot(b, hot) + dot(d, hot)


def stacked_extra(lead, value, row):
    a, b, d = (t.astype(F32) for t in split3(value))
    out = jnp.where(row == 1, a, 0.0) + jnp.where(row == 2, b, 0.0) + jnp.where(row == 3, d, 0.0)
    return (jnp.where(row == 0, lead, 0.0) + out).astype(BF)


def backward_step(h, j, c, grad, mixed, lse, qt, kv, kt, dkv, dqt):
    keys = kv.shape[1]
    hd, step, chunk = HEAD_DIM, 256, 512
    per = chunk // step
    g = (j // 2) * 4 + c * 2 + j % 2
    sl = pl.ds(pl.multiple_of(h * hd, hd), hd)
    do = jnp.concatenate([grad[2 * j, sl, :], grad[2 * j + 1, sl, :]], axis=1)
    mx = jnp.concatenate([mixed[2 * j, sl, :], mixed[2 * j + 1, sl, :]], axis=1)
    delta = jnp.sum(do.astype(F32) * mx.astype(F32), axis=0, keepdims=True)
    row = lax.broadcasted_iota(jnp.int32, (16, step), 0)
    none = jnp.zeros((hd, step), BF)
    rest = jnp.zeros((2 * hd - 16, step), BF)
    qh = qt[g, h]
    qa = jnp.concatenate([qh, none, stacked_extra(1.0, -lse[j, h], row), rest], axis=0)
    da = jnp.concatenate([none, do, stacked_extra(0.0, -delta, row), rest], axis=0)
    qr = jnp.concatenate([qh, none], axis=0).astype(F32).T.astype(BF)
    dr = jnp.concatenate([none, do], axis=0).astype(F32).T.astype(BF)
    dq = jnp.zeros((hd, step), F32)
    for kc in range(keys // chunk):
        rows = slice(kc * chunk, (kc + 1) * chunk)
        block = kv[h, rows, :]
        p = jnp.exp2(dot(block, qa) * LOG2E)
        dp = dot(block, da)
        ds = (p * dp).astype(BF)
        dkv[h, rows, :] += dot(ds, qr) + dot(p.astype(BF), dr)
        for i in range(per):
            dq += dot(kt[h, kc * per + i], ds[i * step : (i + 1) * step])
    dqt[j, sl, :] = (dq * (1.0 / math.sqrt(hd))).astype(BF)


def add_into(dst, src, lead, n):
    def body(i, carry):
        dst[lead + (i,)] = dst[lead + (i,)] + src[i]
        return carry

    lax.fori_loop(0, n, body, 0)


def halving(co, to, G, u, bufs, ss, rs, order, finish):
    x, y, c, z = co
    zh, zl = z // 2, z % 2
    r0, r1, r2, r3, r4 = bufs
    a, b = order
    first = (lambda n: G.at[u, 1 - x, n, c]) if a == "x" else (lambda n: G.at[u, n, 1 - y, c])
    keep = (lambda n: (u, x, n, c)) if a == "x" else (lambda n: (u, n, y, c))
    second = G.at[u, x, 1 - y, c] if b == "y" else G.at[u, 1 - x, y, c]

    def cp0(i):
        return rcopy(G.at[u, i // 2, i % 2, 1 - c], r0.at[u, i], ss.at[u, i], rs.at[u, i], to["core"])

    def cp1(n):
        return rcopy(first(n), r1.at[u, n], ss.at[u, 4 + n], rs.at[u, 4 + n], to[a])

    cp2 = lambda: rcopy(second, r2.at[u], ss.at[u, 6], rs.at[u, 6], to[b])
    cp3 = lambda n: rcopy(G.at[u, x, y, c, 2 * n + 1 - zl], r3.at[u, n], ss.at[u, 7 + n], rs.at[u, 7 + n], to["z1"])
    cp4 = lambda: rcopy(G.at[u, x, y, c, 2 * (1 - zh) + zl], r4.at[u], ss.at[u, 9], rs.at[u, 9], to["z2"])

    def core_send():
        for i in range(4):
            cp0(i).start()

    def core_land():
        for i in range(4):
            cp0(i).wait()
            add_into(G, r0.at[u, i], (u, i // 2, i % 2, c), 4)

    def a_send():
        for n in range(2):
            cp1(n).start()

    def a_wait():
        for n in range(2):
            cp1(n).wait()

    def a_add():
        for n in range(2):
            add_into(G, r1.at[u, n], keep(n), 4)
        cp2().start()

    def b_land():
        cp2().wait()
        add_into(G, r2.at[u], (u, x, y, c), 4)
        for n in range(2):
            cp3(n).start()

    def z1_land():
        for n in range(2):
            cp3(n).wait()
            here = (u, x, y, c, 2 * n + zl)
            G[here] = G[here] + r3[u, n]
        cp4().start()

    def z2_land():
        cp4().wait()
        finish(G[u, x, y, c, z].astype(F32) + r4[u].astype(F32))

    return dict(core_send=core_send, core_land=core_land, a_send=a_send, a_wait=a_wait, a_add=a_add, b_land=b_land, z1_land=z1_land, z2_land=z2_land)


def half_sum(co, to, H, b, r0, r1, r3, r4, ss, rs, finish):
    x, y, c, z = co
    zh, zl = z // 2, z % 2
    cp0 = lambda i: rcopy(H.at[b, i, 1 - c], r0.at[b, i], ss.at[b, i], rs.at[b, i], to["core"])
    cp1 = lambda: rcopy(H.at[b, 1 - y, c], r1.at[b], ss.at[b, 2], rs.at[b, 2], to["y"])
    cp3 = lambda n: rcopy(H.at[b, y, c, 2 * n + 1 - zl], r3.at[b, n], ss.at[b, 3 + n], rs.at[b, 3 + n], to["z1"])
    cp4 = lambda: rcopy(H.at[b, y, c, 2 * (1 - zh) + zl], r4.at[b], ss.at[b, 5], rs.at[b, 5], to["z2"])

    def core_send():
        for i in range(2):
            cp0(i).start()

    def core_land():
        for i in range(2):
            cp0(i).wait()
            add_into(H, r0.at[b, i], (b, i, c), 4)

    def y_send():
        cp1().start()

    def y_land():
        cp1().wait()
        add_into(H, r1.at[b], (b, y, c), 4)
        for n in range(2):
            cp3(n).start()

    def z1_land():
        for n in range(2):
            cp3(n).wait()
            here = (b, y, c, 2 * n + zl)
            H[here] = H[here] + r3[b, n]
        cp4().start()

    def z2_land():
        cp4().wait()
        finish(H[b, y, c, z].astype(F32) + r4[b].astype(F32))

    return core_send, core_land, y_send, y_land, z1_land, z2_land


def half_sum_line(co, to, H, b, r0, r1, r3, r4, ss, rs, finish):
    x, y, c, z = co
    zh, zl = z // 2, z % 2
    cp0 = lambda i: rcopy(H.at[b, i, 1 - c], r0.at[b, i], ss.at[b, i], rs.at[b, i], to["core"])
    cp3 = lambda i, n: rcopy(H.at[b, i, c, 2 * n + 1 - zl], r1.at[b, 2 * i + n], ss.at[b, 2 + 2 * i + n], rs.at[b, 2 + 2 * i + n], to["z1"])
    cp4 = lambda i: rcopy(H.at[b, i, c, 2 * (1 - zh) + zl], r3.at[b, i], ss.at[b, 6 + i], rs.at[b, 6 + i], to["z2"])
    cp1 = lambda: rcopy(H.at[b, 1 - y, c, z], r4.at[b], ss.at[b, 8], rs.at[b, 8], to["y"])

    def core_send():
        for i in range(2):
            cp0(i).start()

    def core_land():
        for i in range(2):
            cp0(i).wait()
            add_into(H, r0.at[b, i], (b, i, c), 4)

    def z1_send():
        for i in range(2):
            for n in range(2):
                cp3(i, n).start()

    def z1_land():
        for i in range(2):
            for n in range(2):
                cp3(i, n).wait()
                here = (b, i, c, 2 * n + zl)
                H[here] = H[here] + r1[b, 2 * i + n]
        for i in range(2):
            cp4(i).start()

    def z2_land():
        for i in range(2):
            cp4(i).wait()
            here = (b, i, c, z)
            H[here] = H[here] + r3[b, i]
        cp1().start()

    def y_land():
        cp1().wait()
        finish(H[b, y, c, z].astype(F32) + r4[b].astype(F32))

    return core_send, core_land, z1_send, z1_land, z2_land, y_land


TIMES = dict(
    core=(4.0, 5.0, 5.3, 5.6, 6.5),
    send=(4.01, 5.01, 17.25, 5.61),
    y=(17.2, 18.9, 25.8, 17.0),
    z1=(22.4, 24.1, 30.5, 24.0),
    z2=(27.5, 28.5, 36.0, 29.9),
    mixer=(20.6, 27.4, 31.9, 38.0),
    att=(7.2, 1.72),
    walk=(0.1, 0.95, 3.0, 3.9),
    fold=(2.2, 5.0),
    half=(8.6, 13.5, 19.5, 25.5),
    full=(14.5, 20.2, 26.2, 33.0),
    last=(20.6, 26.4),
    packed=(5.2, 10.0, 15.0, 20.3, 31.0),
    vec=(8.4, 10.1, 14.2, 18.2, 24.8, 32.5),
)


def backward_kernel(
    send, cot, act, sin, gpre, mix, gres, gain, s4, s5, s6, s7, s8, upx, base, mixed_h, lse_h, qt_h, kv_h, kt_h, fi_h, nrm_h, pw_h, gresf_h, tok_h,
    out_in, out_s, out_e, out_m, out_b, out_p, out_v,
    mixed, lse, qt, kv, kt, fi, nrm, pw, gresf, tok, lsem, grad, G, r0, r1, r2, r3, r4, H, h0, h1, h3, h4, F, xo, xe, ub, dkv, dqt, dall, GF, q0, q1, q2, q3, sq, GP, p0, p1, p2, p3, V, vr,
    els, ess, ers, gss, grs, hss, hrs, xss, xrs, qss, qrs, pss, prs, vss, vrs,
):
    co = coords()
    x, y, c, z = co
    to = partners(*co)
    zh, zl = z // 2, z % 2
    heads, keys = kv.shape[0], kv.shape[1]
    width = cot.shape[1]
    rows = gres.shape[0]
    late = [(mixed_h, mixed), (lse_h, lse), (qt_h, qt), (kv_h, kv), (kt_h, kt), (fi_h, fi), (nrm_h, nrm), (pw_h, pw), (gresf_h, gresf), (tok_h, tok)]

    def local(i):
        return pltpu.make_async_copy(late[i][0], late[i][1], lsem.at[i])

    for i in range(len(late)):
        local(i).start()
    others = [(dy, dz) for dy in range(2) for dz in range(4) if dy or dz]
    enter([to["core"], to["x"]] + [device(x, y ^ dy, c, z ^ dz) for dy, dz in others])
    me = y * 4 + z

    def exch(i):
        dy, dz = others[i]
        return rcopy(send.at[(y ^ dy) * 4 + (z ^ dz)], grad.at[me], ess.at[i], ers.at[i], device(x, y ^ dy, c, z ^ dz))

    mine = pltpu.make_async_copy(send.at[me], grad.at[me], els)
    mine.start()
    for i in range(7):
        exch(i).start()

    ev = []
    n_hid = 2 * act.shape[1] // width

    def shrink_all():
        span = act.shape[1] // 4

        def body(t, carry):
            val = dot_tn(act[:, pl.ds(pl.multiple_of(t * span, span), span)], cot[...]).astype(BF)
            val = val.reshape(4, 4, 3, 8, width)
            for zz in range(4):
                for i in range(4):
                    H[i // 2, t // 2, t % 2, zz, i % 2] = val[zz, i]
            return carry

        lax.fori_loop(0, 4, body, 0)

    def expand_one(q):
        for xx in range(2):
            val = dot_tn(sin[:, xx * width // 2 : (xx + 1) * width // 2], gpre[:, q * width : (q + 1) * width]).astype(BF)
            val = val.reshape(2, 2, 4, 3, 8, width)
            for i in range(16):
                H[2 + q, i // 8, (i // 4) % 2, i % 4, xx] = val[i // 8, (i // 4) % 2, i % 4]

    def mixer_one():
        half = rows // 2
        for t in range(2):
            sl = slice(t * width // 2, (t + 1) * width // 2)
            val = dot(mix[0, sl, :], gres[:half]) + dot(mix[1, sl, :], gres[half:])
            G[0, t] = val.astype(BF).reshape(2, 2, 4, 3, 8, width)

    def run(fns):
        for fn in fns:
            fn()

    def lanes(xx, q):
        return pl.ds(pl.multiple_of((xx * (n_hid // 2) + q) * width, width), width)

    swap = lambda q: rcopy(xo.at[q], xe.at[q], xss.at[q], xrs.at[q], to["x"])
    up_copy = lambda: rcopy(upx, ub, xss.at[2], xrs.at[2], to["x"])

    def done_s(b, val):
        for i in range(2):
            out_s[2 * b + i] = val[i]

    def done_e(q, val):
        F[...] = val
        out_e[:, :, lanes(x, q)] = F[x]
        xo[q] = F[1 - x].astype(BF)
        swap(q).start()

    def landed_e(q):
        swap(q).wait()
        out_e[:, :, lanes(1 - x, q)] = xe[q].astype(F32)

    def landed_up():
        up_copy().wait()
        for i in range(2):
            out_b[i] = (base[i] + ub[i].astype(F32)).astype(BF)

    ev.append((0.0, shrink_all))
    ev.append((0.6, functools.partial(expand_one, 0)))
    ev.append((0.8, functools.partial(expand_one, 1)))
    ev.append((1.0, mixer_one))
    ev.append((1.2, lambda: up_copy().start()))
    for b in range(4):
        fin = functools.partial(done_s, b) if b < 2 else functools.partial(done_e, b - 2)
        st = (half_sum if b < 3 else half_sum_line)(co, to, H, b, h0, h1, h3, h4, hss, hrs, fin)
        for t, fn in zip(((0.5, 0.51, 0.7, 0.9)[b], TIMES["core"][b], TIMES["send"][b], TIMES["y"][b], TIMES["z1"][b], TIMES["z2"][b]), st):
            ev.append((t, fn))
        if b >= 2:
            ev.append((TIMES["z2"][b] + 4.0, functools.partial(landed_e, b - 2)))
    ev.append((TIMES["z2"][3] + 4.1, landed_up))
    st = halving(co, to, G, 0, (r0, r1, r2, r3, r4), gss, grs, "xy", lambda val: out_m.__setitem__(Ellipsis, val))
    ev.append((1.1, st["core_send"]))
    ev.append((TIMES["core"][4], lambda: run([st["core_land"], st["a_send"]])))
    for t, names in zip(TIMES["mixer"], (("a_wait", "a_add"), ("b_land",), ("z1_land",), ("z2_land",))):
        ev.append((t, functools.partial(run, [st[k] for k in names])))

    def zero():
        def body(i, carry):
            for h in range(heads):
                dkv[h, pl.ds(pl.multiple_of(i * 256, 256), 256), :] = jnp.zeros((256, 2 * HEAD_DIM), F32)
            return carry

        lax.fori_loop(0, keys // 256, body, 0)

    def arrive(q):
        if q == 0:
            mine.wait()
            for i in range(5):
                local(i).wait()
        for i in range(7):
            if 2 * others[i][0] + others[i][1] // 2 == q:
                exch(i).wait()

    ev.append((5.2, zero))
    steps = 4 * heads
    t_att, t_step = TIMES["att"]
    t_end = t_att + t_step * steps
    for q in range(4):
        ev.append((t_att + heads * q * t_step + 0.001, functools.partial(arrive, q)))

    V[...] = jnp.zeros_like(V)
    for i, ref in ((4, s4), (5, s5), (6, s6), (7, s7)):
        V[i : i + 1, :] = ref[...]
    for i in range(n_hid):
        V[8 + i : 9 + i, :] = s8[:, i * width : (i + 1) * width]

    def group(slot, mine_rows):
        cc = c if mine_rows else 1 - c
        yy = slot // 2
        g = yy * 4 + cc * 2 + slot % 2
        off = pl.multiple_of(g * 256, 256)
        rs_ = pl.ds(off, 256)
        wide = 2 * HEAD_DIM * heads
        dk = jnp.concatenate([dkv[h, rs_, :].astype(BF) for h in range(heads)], axis=1)
        gf = dot_nt(dk, pw[:, :wide])
        dall[rs_, :wide] = dk
        sums = jnp.sum(dk.astype(F32), axis=0, keepdims=True)
        V[16:17, :wide] += sums
        if mine_rows:
            dq = dqt[slot].astype(F32).T.astype(BF)
            gf += dot_nt(dq, pw[:, wide:])
            dall[rs_, wide:] = dq
            V[17:18, : dq.shape[1]] += jnp.sum(dq.astype(F32), axis=0, keepdims=True)
        else:
            dall[rs_, wide:] = jnp.zeros((256, heads * HEAD_DIM), BF)
        V[0:1, :] += jnp.sum(gf * nrm[rs_, :].astype(F32), axis=0, keepdims=True)
        V[1:2, :] += jnp.sum(gf, axis=0, keepdims=True)
        GF[yy, cc, pl.ds(2 * (slot % 2), 2)] = gf.astype(BF).reshape(2, 2, 64, width)

    def q_core(r):
        yy = rowof(r)
        return rcopy(GF.at[yy, 1 - c], q0.at[r], qss.at[r], qrs.at[r], to["core"])

    def q_z1(r, f, n):
        i = 2 + 4 * r + 2 * f + n
        return rcopy(GF.at[rowof(r), c, 2 * n + 1 - zl, f], q1.at[r, f, n], qss.at[i], qrs.at[i], to["z1"])

    def q_z2(r, f):
        i = 10 + 2 * r + f
        return rcopy(GF.at[rowof(r), c, 2 * (1 - zh) + zl, f], q2.at[r, f], qss.at[i], qrs.at[i], to["z2"])

    def q_y(f):
        return rcopy(sq.at[f], q3.at[f], qss.at[14 + f], qrs.at[14 + f], to["y"])

    def rowof(r):
        return 1 - y if r == 0 else y

    def walk(mine_rows, r):
        def body(i, carry):
            group(2 * rowof(r) + i, mine_rows)
            return carry

        lax.fori_loop(0, 2, body, 0)
        if not mine_rows:
            q_core(r).start()

    def q_sum(r):
        q_core(r).wait()
        yy = rowof(r)

        def body(i, carry):
            GF[yy, c, i // 2, i % 2] = GF[yy, c, i // 2, i % 2] + q0[r, i // 2, i % 2]
            return carry

        lax.fori_loop(0, 8, body, 0)
        if r == 0:
            q_send(0, 0)

    def q_send(r, f):
        for n in range(2):
            q_z1(r, f, n).start()

    chunks = [(r, f) for r in range(2) for f in range(2)]

    def q_half(i):
        r, f = chunks[i]
        for n in range(2):
            q_z1(r, f, n).wait()
        if i + 2 < 4:
            q_send(*chunks[i + 2])
        for n in range(2):
            here = (rowof(r), c, 2 * n + zl, f)
            GF[here] = GF[here] + q1[r, f, n]
        q_z2(r, f).start()

    def finish(img, f, total):
        rs_ = slice(64 * f, 64 * (f + 1))
        normed, inv = row_norm(tok[img, rs_].astype(F32))
        scaled = total * gain[0:1, :]
        m1 = jnp.mean(scaled, axis=-1, keepdims=True)
        m2 = jnp.mean(scaled * normed, axis=-1, keepdims=True)
        out_in[img, rs_] = (gresf[img, rs_] + inv * (scaled - m1 - normed * m2)).astype(BF)

    def q_full(i):
        r, f = chunks[i]
        q_z2(r, f).wait()
        total = GF[rowof(r), c, z, f].astype(F32) + q2[r, f].astype(F32)
        if r == 0:
            sq[f] = total.astype(BF)
            q_y(f).start()
        else:
            finish(y, f, total)

    def q_last(f):
        q_y(f).wait()
        finish(1 - y, f, q3[f].astype(F32))

    def late_rows():
        for i in range(5, 10):
            local(i).wait()

    ev.append((t_end + 0.05, late_rows))
    for i in range(4):
        ev.append((t_end + TIMES["walk"][i], functools.partial(walk, i % 2 == 1, i // 2)))
        ev.append((t_end + TIMES["half"][i], functools.partial(q_half, i)))
        ev.append((t_end + TIMES["full"][i], functools.partial(q_full, i)))
    for f in range(2):
        ev.append((t_end + TIMES["fold"][f], functools.partial(q_sum, f)))
        if f == 0:
            ev.append((t_end + TIMES["walk"][3] + 0.1, functools.partial(q_send, 0, 1)))
        ev.append((t_end + TIMES["last"][f], functools.partial(q_last, f)))

    def packed():
        val = dot_tn(fi[...], dall[...]).astype(BF)
        GP[0] = val.reshape(2, 2, 2, 4, 3, 8, val.shape[1])
        for i in range(4):
            p_core(i).start()

    def p_core(i):
        return rcopy(GP.at[0, i // 2, i % 2, 1 - c], p0.at[i], pss.at[i], prs.at[i], to["core"])

    def p_a(n):
        return rcopy(GP.at[0, 1 - x, n, c], p1.at[n], pss.at[4 + n], prs.at[4 + n], to["x"])

    p_b = lambda: rcopy(GP.at[0, x, 1 - y, c], p2, pss.at[6], prs.at[6], to["y"])
    p_z = lambda k: rcopy(GP.at[0, x, y, c, z ^ k], p3.at[k - 1], pss.at[6 + k], prs.at[6 + k], to["z%d" % k])

    def packed_core():
        for i in range(4):
            p_core(i).wait()
            add_into(GP, p0.at[i], (0, i // 2, i % 2, c), 4)
        for n in range(2):
            p_a(n).start()

    def packed_a():
        for n in range(2):
            p_a(n).wait()
            add_into(GP, p1.at[n], (0, x, n, c), 4)
        p_b().start()

    def packed_b():
        p_b().wait()
        add_into(GP, p2, (0, x, y, c), 4)
        for k in (1, 2, 3):
            p_z(k).start()

    def packed_z():
        GP[0, 1 - x, y, c, z] = GP[0, x, y, c, z]
        for k in (1, 2, 3):
            p_z(k).wait()
            GP[0, 1 - x, y, c, z ^ k] = p3[k - 1]
        part = heads * HEAD_DIM
        for g in range(4):
            val = GP[0, 1 - x, y, c, g].astype(F32)
            for h in range(heads):
                spots = ((1, 2 * h), (2, 2 * h + 1), (0, 2 * heads + h))
                for t, i in spots:
                    lo = t * width + g * part + h * HEAD_DIM
                    out_p[:, :, lo : lo + HEAD_DIM] = val[:, :, i * HEAD_DIM : (i + 1) * HEAD_DIM]

    def v_copy(i):
        return rcopy(V.at[0:16], vr.at[i], vss.at[i], vrs.at[i], to[("core", "x", "y", "z1", "z2")[i]])

    def vec_start():
        part = heads * HEAD_DIM
        wide = 2 * part
        src = lax.broadcasted_iota(jnp.int32, (wide, 1), 0)
        dst = lax.broadcasted_iota(jnp.int32, (1, width), 1)
        head, lane = src // (2 * HEAD_DIM), src % (2 * HEAD_DIM)
        to_v = jnp.where(lane >= HEAD_DIM, z * part + head * HEAD_DIM + lane - HEAD_DIM, -1)
        V[3:4, :] = pick(V[16:17, :wide], jnp.where(to_v == dst, 1.0, 0.0).astype(BF))
        V[2:3, :] = pick(V[17:18, :part], jnp.where(z * part + src[:part] == dst, 1.0, 0.0).astype(BF))
        v_copy(0).start()

    def vec_step(i):
        v_copy(i).wait()
        V[0:16, :] = V[0:16, :] + vr[i]
        if i < 4:
            v_copy(i + 1).start()
        else:
            n_dev = 32
            small = width // n_dev
            d = (x * 4 + y * 2 + c) * 4 + z
            src = lax.broadcasted_iota(jnp.int32, (width, 1), 0)
            dst = lax.broadcasted_iota(jnp.int32, (1, 128), 1)
            hot = jnp.where(dst < small, d * small + dst, -1) == src
            out_v[0:16, :] = pick(V[0:16, :], jnp.where(hot, 1.0, 0.0).astype(BF))
            big = n_hid * small
            hot = jnp.where(dst < big, (d % (n_dev // n_hid)) * big + dst, -1) == src
            line = lax.broadcasted_iota(jnp.int32, (16, 128), 0)
            val = pick(V[0:16, :], jnp.where(hot, 1.0, 0.0).astype(BF))
            val = jnp.where(line == 8 + d // (n_dev // n_hid), val, 0.0)
            out_v[16:17, :] = jnp.sum(val, axis=0, keepdims=True)

    for t, fn in zip(TIMES["packed"], (packed, packed_core, packed_a, packed_b, packed_z)):
        ev.append((t_end + t, fn))
    for t, fn in zip(TIMES["vec"], [vec_start] + [functools.partial(vec_step, i) for i in range(5)]):
        ev.append((t_end + t, fn))

    ev.sort(key=lambda e: e[0])
    for t, fn in ev:
        if t < t_att:
            fn()

    def step(s, carry):
        for k in range(steps):
            here = [fn for t, fn in ev if t_att + k * t_step <= t < t_att + (k + 1) * t_step]
            if here:

                @pl.when(s == k)
                def _():
                    for fn in here:
                        fn()

        backward_step(s % heads, (s // heads) ^ (2 * y + zh), c, grad, mixed, lse, qt, kv, kt, dkv, dqt)
        return carry

    lax.fori_loop(0, steps, step, 0)
    for t, fn in ev:
        if t >= t_end:
            fn()


def backward_all(send, cot, act, sin, gpre, mix, gres, gresf, tok, gain, sums, upx, base, mixed, lse, qt, kv, kt, fi, nrm, pw):
    D = pltpu.SemaphoreType.DMA
    heads, keys = kv.shape[0], kv.shape[1]
    width = cot.shape[1]
    n_hid = 2 * act.shape[1] // width
    units = 1
    blk = (3, 8, width)
    cols = pw.shape[1]
    pb = (3, 8, cols)
    S = jax.ShapeDtypeStruct
    outs = [S(tok.shape, BF), S((n_hid,) + blk, F32), S((3, 8, n_hid * width), F32), S(blk, F32), S(tok.shape, BF), S((3, 8, 4 * cols), F32), S((24, 128), F32)]
    V = pltpu.VMEM
    rowt = (64, width)
    scr = [V(t.shape, t.dtype) for t in (mixed, lse, qt, kv, kt, fi, nrm, pw, gresf, tok)] + [
        D((10,)),
        V(send.shape, BF),
        V((units, 2, 2, 2, 4) + blk, BF),
        V((units, 4, 4) + blk, BF),
        V((units, 2, 4) + blk, BF),
        V((units, 4) + blk, BF),
        V((units, 2) + blk, BF),
        V((units,) + blk, BF),
        V((4, 2, 2, 4, 2) + blk, BF),
        V((4, 2, 4, 2) + blk, BF),
        V((4, 4, 2) + blk, BF),
        V((4, 2, 2) + blk, BF),
        V((4, 2) + blk, BF),
        V((2,) + blk, F32),
        V((2,) + blk, BF),
        V((2,) + blk, BF),
        V(tok.shape, BF),
        V((heads, keys, 2 * HEAD_DIM), F32),
        V((4, heads * HEAD_DIM, 256), BF),
        V((keys, cols), BF),
        V((2, 2, 4, 2) + rowt, BF),
        V((2, 4, 2) + rowt, BF),
        V((2, 2, 2) + rowt, BF),
        V((2, 2) + rowt, BF),
        V((2,) + rowt, BF),
        V((2,) + rowt, BF),
        V((1, 2, 2, 2, 4) + pb, BF),
        V((4, 4) + pb, BF),
        V((2, 4) + pb, BF),
        V((4,) + pb, BF),
        V((3,) + pb, BF),
        V((24, width), F32),
        V((5, 16, width), F32),
        D,
        D((7,)),
        D((7,)),
        D((units, 10)),
        D((units, 10)),
        D((4, 9)),
        D((4, 9)),
        D((3,)),
        D((3,)),
        D((16,)),
        D((16,)),
        D((10,)),
        D((10,)),
        D((5,)),
        D((5,)),
    ]
    args = (send, cot, act, sin, gpre, mix, gres, gain, *sums, upx, base, mixed, lse, qt, kv, kt, fi, nrm, pw, gresf, tok)
    return pl.pallas_call(
        backward_kernel,
        out_shape=outs,
        in_specs=[ANY] + [VM] * 12 + [ANY, VM] + [ANY] * 10,
        out_specs=[VM] * len(outs),
        scratch_shapes=scr,
        compiler_params=pltpu.CompilerParams(collective_id=2, has_side_effects=True, vmem_limit_bytes=63 << 20),
        name="backward_reduce",
    )(*args)


def backward_local_kernel(grad, mixed, lse, qt, kv, kt, out, dkv, dqt):
    _, _, c, _ = coords()
    heads, keys = kv.shape[0], kv.shape[1]
    wide = 2 * HEAD_DIM * heads
    dkv[...] = jnp.zeros_like(dkv)

    def step(s, carry):
        backward_step(s % heads, s // heads, c, grad, mixed, lse, qt, kv, kt, dkv, dqt)
        return carry

    lax.fori_loop(0, 4 * heads, step, 0)
    for g in range(8):
        rs = slice(g * 256, (g + 1) * 256)
        for h in range(heads):
            out[rs, 2 * h * HEAD_DIM : 2 * (h + 1) * HEAD_DIM] = dkv[h, rs, :].astype(BF)
        dq = dqt[(g // 4) * 2 + g % 2].astype(F32).T
        out[rs, wide:] = jnp.where((g // 2) % 2 == c, dq, 0.0).astype(BF)


def backward_local(grad, mixed, lse, qt, kv, kt):
    heads, keys = kv.shape[0], kv.shape[1]
    return pl.pallas_call(
        backward_local_kernel,
        out_shape=jax.ShapeDtypeStruct((keys, 3 * heads * HEAD_DIM), BF),
        in_specs=[VM] * 6,
        out_specs=VM,
        scratch_shapes=[pltpu.VMEM((heads, keys, 2 * HEAD_DIM), F32), pltpu.VMEM((4, heads * HEAD_DIM, 256), BF)],
        compiler_params=pltpu.CompilerParams(vmem_limit_bytes=50 << 20),
        name="attention_backward",
    )(grad, mixed, lse, qt, kv, kt)


def reduce_generic(gf, gp, gm, ge, gs, n_dev):
    every = ("dp", "ctx", "head")
    x, y, c, z = coords()
    flat = gf.reshape((1, -1) + gf.shape[-1:])
    both = jnp.concatenate([jnp.where(y == i, flat, jnp.zeros_like(flat)) for i in range(2)], axis=0)
    of = lax.psum_scatter(both.astype(F32), ("ctx", "head"), scatter_dimension=1, tiled=True)
    cols = gp.shape[-1]
    rows = gp.size // cols
    spread = lax.dynamic_update_slice_in_dim(jnp.zeros((rows, 4, cols), F32), gp.reshape(rows, 1, cols).astype(F32), z, 1)
    op = jnp.swapaxes(lax.psum_scatter(spread, every, scatter_dimension=0, tiled=True), 0, 1)
    rest = [
        lax.psum_scatter(g.reshape((n_dev, -1) + g.shape[-1:]).astype(F32), every, scatter_dimension=0, tiled=True)[0] for g in (gm, ge, gs)
    ]
    return [of, op] + rest


def layer_norm(token_rows, norm_gain, norm_shift):
    normed, inv_std = row_norm(token_rows)
    return (normed * norm_gain + norm_shift, normed, inv_std)


def norm_backward(grad_out, normed, inv_std, norm_gain):
    scaled = grad_out * norm_gain
    first_mean = jnp.mean(scaled, axis=-1, keepdims=True)
    second_mean = jnp.mean(scaled * normed, axis=-1, keepdims=True)
    return inv_std * (scaled - first_mean - normed * second_mean)


def gelu_parts(pre_act):
    cumulative = 0.5 * (1.0 + jax.scipy.special.erf(pre_act * (1.0 / math.sqrt(2.0))))
    density = jnp.exp(-0.5 * pre_act * pre_act) * (1.0 / math.sqrt(2.0 * math.pi))
    return pre_act * cumulative, cumulative + pre_act * density


def on_device(
    tokens,
    cotangent,
    lengths,
    attention_gain,
    attention_shift,
    packed_weight,
    query_bias,
    value_bias,
    mixer_weight,
    mixer_bias,
    feedforward_gain,
    feedforward_shift,
    expand_weight,
    expand_bias,
    shrink_weight,
    shrink_bias,
):
    images, shard_len, width = tokens.shape
    groups = lax.axis_size("head")
    heads = HEADS // groups
    part = heads * HEAD_DIM
    hidden = expand_weight.shape[1]
    rows = images * shard_len
    n_dev = lax.axis_size("dp") * lax.axis_size("ctx") * groups
    z = lax.axis_index("head")
    wr = packed_weight.shape[0]
    fr = shrink_weight.shape[0]

    tiled = wr % 8 == 0 and fr % 8 == 0 and lax.axis_size("dp") == 2
    slab = (lambda r, n: (r // 8, 8, n)) if tiled else (lambda r, n: (r, n))
    vecs = [attention_gain, attention_shift, query_bias, value_bias, mixer_bias, feedforward_gain, feedforward_shift, shrink_bias, expand_bias]
    mx, ex, sh = mixer_weight.reshape(slab(wr, width)), expand_weight.reshape(slab(wr, hidden)), shrink_weight.reshape(slab(fr, width))
    if tiled:
        mix, mixed_t, lse, fi, nrm, qt, kv, kt, full_packed, full_vecs, eb, mxo, exo, sho, cotx = forward_all(lengths, tokens, cotangent, packed_weight.reshape(slab(wr, 3 * width)), mx, ex, sh, vecs)
        hidden_bias = eb
    else:
        pk = jnp.stack([own_columns(packed_weight, g, part) for g in range(groups)])
        sv = jnp.stack([jnp.pad(v, (0, 128 - v.shape[0])) for v in vecs] + [jnp.zeros((128,), BF)] * 7)
        img, pko, mxo, exo, sho, svo = gather_generic(tokens, pk, mx, ex, sh, sv)
        full_packed = pko.reshape(width, 3 * part)
        svo = svo.reshape(n_dev, 16, 128).astype(F32)
        gain_one, shift_one, qb, vb, mb, gain_two, shift_two, sb = [svo[:, i, :wr].reshape(width) for i in range(8)]
        eb = svo[:, 8, :fr].reshape(hidden)
        own = lambda v: lax.dynamic_slice_in_dim(v, z * part, part)
        vb_own = own(vb).reshape(heads, 1, HEAD_DIM)
        bias = jnp.concatenate([jnp.concatenate([jnp.zeros_like(vb_own), vb_own], axis=1).reshape(2 * part), own(qb)])
        img = img.reshape(16, shard_len, width)
        mixed_t, lse, fi, nrm, qt, kv, kt = attention_forward(lengths, img, full_packed, gain_one[None], shift_one[None], bias[None])
        mix = exchange(mixed_t, 1)
    mix = mix.reshape(images, width, shard_len)
    full_mixer = mxo.reshape(width, width)
    full_expand = exo.reshape(width, -1)
    full_shrink = sho.reshape(-1, width)

    if tiled:
        base, upx, activated, second_input, cot2, grad_pre_bf, grad_residual_bf, grad_residual, grad_mixed, *sums = dense_layers(
            tokens, cotangent, cotx, mix, full_vecs, hidden_bias, full_mixer, full_expand, full_shrink
        )
        ig, os_, oe, om, block_output, op, ov = backward_all(
            grad_mixed, cot2, activated, second_input, grad_pre_bf, mix, grad_residual_bf,
            grad_residual, tokens, full_vecs, sums, upx, base, mixed_t, lse, qt, kv, kt, fi, nrm, full_packed,
        )
        ig, os_, oe, om, block_output, op, *vec = hand_over([ig, os_, oe, om, block_output, op], ov, wr, fr)
        op = op.reshape(wr, 3 * width)
    else:
        token_rows = tokens.reshape(rows, width).astype(F32)
        mixed_rows = jnp.swapaxes(mix, 1, 2).reshape(rows, width)
        residual = token_rows + dot(mixed_rows, full_mixer) + mb
        second_out, second_normed, second_inv = layer_norm(residual, gain_two, shift_two)
        second_input = second_out.astype(BF)
        pre_act = dot(second_input, full_expand) + eb
        value, slope = gelu_parts(pre_act)
        activated = value.astype(BF)
        block_output = (residual + dot(activated, full_shrink) + sb).astype(BF)
        grad_in = cotangent.reshape(rows, width)
        grad_rows = grad_in.astype(F32)
        grad_shrink_b = jnp.sum(grad_rows, axis=0)
        grad_pre = jnp.einsum("rd,fd->rf", grad_in, full_shrink, preferred_element_type=F32) * slope
        grad_pre_bf = grad_pre.astype(BF)
        grad_expand_b = jnp.sum(grad_pre, axis=0)
        grad_second = jnp.einsum("rf,df->rd", grad_pre_bf, full_expand, preferred_element_type=F32)
        grad_gain_two = jnp.sum(grad_second * second_normed, axis=0)
        grad_shift_two = jnp.sum(grad_second, axis=0)
        grad_residual = grad_rows + norm_backward(grad_second, second_normed, second_inv, gain_two)
        grad_residual_bf = grad_residual.astype(BF)
        grad_mixer_b = jnp.sum(grad_residual, axis=0)
        grad_mixed = jnp.einsum("de,ire->idr", full_mixer, grad_residual_bf.reshape(images, shard_len, width), preferred_element_type=F32).astype(BF)
        grad_mixed = grad_mixed.reshape(images * groups, part, shard_len)
        grad_t = exchange(grad_mixed, 2)
        dqkv = backward_local(grad_t, mixed_t, lse, qt, kv, kt)
        grad_packed_w = jnp.einsum("rd,re->de", fi, dqkv, preferred_element_type=F32)
        grad_first_part = jnp.einsum("re,de->rd", dqkv, full_packed, preferred_element_type=F32)
        img_normed, _ = row_norm(img.reshape(16 * shard_len, width).astype(F32))
        dsum = jnp.sum(dqkv.astype(F32), axis=0)
        place = lambda v: lax.dynamic_update_slice_in_dim(jnp.zeros((width,), F32), v, z * part, 0)
        sums = [
            jnp.sum(grad_first_part * img_normed, axis=0),
            jnp.sum(grad_first_part, axis=0),
            place(dsum[2 * part :]),
            place(dsum[: 2 * part].reshape(heads, 2, HEAD_DIM)[:, 1].reshape(part)),
            grad_mixer_b,
            grad_gain_two,
            grad_shift_two,
            grad_shrink_b,
            grad_expand_b,
        ]
        vec = [lax.psum_scatter(t, ("dp", "ctx", "head"), scatter_dimension=0, tiled=True) for t in sums]
        of, op, om, oe, os_ = reduce_generic(
            grad_first_part.reshape(2, 2, groups, shard_len, width),
            grad_packed_w,
            jnp.einsum("rd,re->de", mixed_rows, grad_residual_bf, preferred_element_type=F32),
            jnp.einsum("rd,rf->df", second_input, grad_pre_bf, preferred_element_type=F32),
            jnp.einsum("rf,rd->fd", activated, grad_in, preferred_element_type=F32),
            n_dev,
        )
        op = op.reshape(groups, wr, 3 * part)
        okv = jnp.transpose(op[:, :, : 2 * part].reshape(groups, wr, heads, 2, HEAD_DIM), (1, 3, 0, 2, 4)).reshape(wr, 2 * width)
        op = jnp.concatenate([jnp.transpose(op[:, :, 2 * part :], (1, 0, 2)).reshape(wr, width), okv], axis=1)
        _, first_normed, first_inv = layer_norm(token_rows, gain_one, shift_one)
        ig = (grad_residual + norm_backward(of.reshape(rows, width), first_normed, first_inv, gain_one)).astype(BF)
    return (
        block_output.reshape(images, shard_len, width),
        ig.reshape(images, shard_len, width),
        vec[0],
        vec[1],
        op,
        vec[2],
        vec[3],
        om.reshape(wr, width),
        vec[4],
        vec[5],
        vec[6],
        oe.reshape(wr, hidden),
        vec[8],
        os_.reshape(fr, width),
        vec[7],
    )


def solution(mesh):
    every = ("dp", "ctx", "head")
    tok, vec, mat = P("dp", ("ctx", "head"), None), P(every), P(every, None)
    in_specs = (tok, tok, P("dp"), vec, vec, mat, vec, vec, mat, vec, vec, vec, mat, vec, mat, vec)
    out_specs = (tok, tok, vec, vec, mat, vec, vec, mat, vec, vec, vec, mat, vec, mat, vec)
    return jax.shard_map(on_device, mesh=mesh, in_specs=in_specs, out_specs=out_specs, check_vma=False)
```

```python
import functools
import math

import jax
import jax.numpy as jnp
from jax import lax
from jax.experimental import pallas as pl
from jax.experimental.pallas import tpu as pltpu
from jax.sharding import PartitionSpec as P

HEADS = 12
HEAD_DIM = 64
NORM_EPS = 1e-06
MASKED = -1e30
LOG2E = 1.4426950408889634
MESH = pl.DeviceIdType.MESH
ANY = pl.BlockSpec(memory_space=pl.ANY)
VM = pl.BlockSpec(memory_space=pltpu.VMEM)
SM = pl.BlockSpec(memory_space=pltpu.SMEM)
BF = jnp.bfloat16
F32 = jnp.float32
SPLIT = 2


def coords():
    ctx = lax.axis_index("ctx")
    return lax.axis_index("dp"), ctx // SPLIT, ctx % SPLIT, lax.axis_index("head")


def device(x, y, c, z):
    return (x, y * SPLIT + c, z)


def enter(targets):
    sem = pltpu.get_barrier_semaphore()
    for t in targets:
        pl.semaphore_signal(sem, inc=1, device_id=t, device_id_type=MESH)
    pl.semaphore_wait(sem, len(targets))


def rcopy(src, dst, ss, rs, to):
    return pltpu.make_async_remote_copy(src, dst, ss, rs, device_id=to, device_id_type=MESH)


def run_events(events):
    for _, fn in sorted(events, key=lambda e: e[0]):
        fn()


def partners(x, y, c, z):
    return dict(
        core=device(x, y, 1 - c, z),
        x=device(1 - x, y, c, z),
        y=device(x, 1 - y, c, z),
        z1=device(x, y, c, z ^ 1),
        z2=device(x, y, c, z ^ 2),
        z3=device(x, y, c, z ^ 3),
    )


def weight_gather(ev, co, to, src, out, sems, order, times):
    x, y, c, z = co
    lsem, zss, zrs, ass, ars, bss, brs, css, crs = sems
    a, b = order

    def spot(fa, fb):
        px = (1 - x if fa else x) if a == "x" else (1 - x if fb else x)
        py = (1 - y if fa else y) if a == "y" else (1 - y if fb else y)
        return px, py

    def at(fa, fb, k):
        return out(*spot(fa, fb), c, z ^ k)

    def group(fa, fb, cc):
        return out(*spot(fa, fb), cc, slice(None))

    F, T = False, True
    zsend = lambda i, k, ref, dst, name: rcopy(ref, dst, zss.at[i], zrs.at[k], to[name])
    asend = lambda k, ref: rcopy(ref, at(F, F, k), ass.at[k], ars.at[k], to[a])
    bsend = lambda fa, k, ref: rcopy(ref, at(fa, F, k), bss.at[int(fa), k], brs.at[int(fa), k], to[b])
    csend = lambda i, g: rcopy(g, g, css.at[i], crs.at[i], to["core"])
    local = lambda: pltpu.make_async_copy(src, at(F, F, 0), lsem)

    def begin():
        local().start()
        asend(0, src).start()
        bsend(F, 0, src).start()

    def z_begin():
        zsend(0, 0, src, at(F, F, 0), "z1").start()
        zsend(1, 1, src, at(F, F, 0), "z2").start()

    def z_land(k):
        d = at(F, F, k)
        zsend(k - 1, k - 1, d, d, "z1").wait_recv()
        if k == 2:
            zsend(2, 2, d, d, "z1").start()
        asend(k, d).start()
        bsend(F, k, d).start()

    def own_done():
        local().wait()
        csend(0, group(F, F, c)).start()

    def a_land(k):
        d = at(T, F, k)
        asend(k, d).wait_recv()
        bsend(T, k, d).start()
        if k == 3:
            csend(1, group(T, F, c)).start()

    def b_land(fa):
        for k in range(4):
            bsend(fa, k, at(fa, T, k)).wait_recv()
        csend(2 + int(fa), group(fa, T, c)).start()

    def last():
        d = at(F, F, 0)
        for i in range(3):
            zsend(i, 0, d, d, "z1").wait_send()
        for k in range(4):
            asend(k, d).wait_send()
            bsend(F, k, d).wait_send()
            bsend(T, k, d).wait_send()
        for i, (fa, fb) in enumerate(((F, F), (T, F), (F, T), (T, T))):
            csend(i, group(fa, fb, 1 - c)).wait()

    t_begin, t_z, t_zl, t_al, t_bl = times
    ev.append((t_begin, begin))
    ev.append((t_z, z_begin))
    for k in range(1, 4):
        ev.append((t_zl[k - 1], functools.partial(z_land, k)))
    ev.append((t_zl[2] + 0.3, own_done))
    for k in range(4):
        ev.append((t_al[k], functools.partial(a_land, k)))
    ev.append((t_bl[0], functools.partial(b_land, F)))
    ev.append((t_bl[1], functools.partial(b_land, T)))
    ev.append((1000.0, last))


def half_gather(ev, co, to, prepare, settle, own, view, sems, times):
    x, y, c, z = co
    zss, zrs, yss, yrs, css, crs = sems
    at = lambda k: view(y, c, z ^ k)
    zsend = lambda i, k, ref, dst, name: rcopy(ref, dst, zss.at[i], zrs.at[k], to[name])
    ysend = lambda k, ref: rcopy(ref, at(k), yss.at[k], yrs.at[k], to["y"])

    def csend(i):
        g = view(y if i == 0 else 1 - y, c, slice(None))
        return rcopy(g, g, css.at[i], crs.at[i], to["core"])

    def begin():
        prepare()
        ysend(0, own).start()

    def z_begin():
        zsend(0, 0, own, at(0), "z1").start()
        zsend(1, 1, own, at(0), "z2").start()

    def z_land(k):
        d = at(k)
        zsend(k - 1, k - 1, d, d, "z1").wait_recv()
        if k == 2:
            zsend(2, 2, d, d, "z1").start()
        ysend(k, d).start()
        if k == 3:
            settle()
            csend(0).start()

    def y_land():
        for k in range(4):
            d = view(1 - y, c, z ^ k)
            rcopy(d, d, yss.at[k], yrs.at[k], to["y"]).wait_recv()
        csend(1).start()

    def last():
        d = at(0)
        for i in range(3):
            zsend(i, 0, d, d, "z1").wait_send()
        for k in range(4):
            ysend(k, d).wait_send()
        for i in range(2):
            csend(i).wait()

    t_begin, t_z, t_zl, t_y = times
    ev.append((t_begin, begin))
    ev.append((t_z, z_begin))
    for k in range(1, 4):
        ev.append((t_zl[k - 1], functools.partial(z_land, k)))
    ev.append((t_y, y_land))
    ev.append((1000.5, last))


def small_gather(co, to, src, out, ls, ss, rs, spread):
    x, y, c, z = co
    own = src.at[z] if spread else src

    def begin():
        pltpu.make_async_copy(own, out.at[x, y, c, z], ls).start()
        for k in (1, 2, 3):
            rcopy(src.at[z ^ k] if spread else src, out.at[x, y, c, z], ss.at[k - 1], rs.at[k - 1], to["z%d" % k]).start()

    def step_y():
        pltpu.make_async_copy(own, out.at[x, y, c, z], ls).wait()
        for k in (1, 2, 3):
            d = out.at[x, y, c, z ^ k]
            rcopy(d, d, ss.at[k - 1], rs.at[k - 1], to["z1"]).wait()
        g = out.at[x, y, c]
        rcopy(g, g, ss.at[3], rs.at[3], to["y"]).start()

    def step_x():
        g = out.at[x, 1 - y, c]
        rcopy(g, g, ss.at[3], rs.at[3], to["y"]).wait()
        for yy in range(2):
            g = out.at[x, yy, c]
            rcopy(g, g, ss.at[4 + yy], rs.at[4 + yy], to["x"]).start()

    def step_c():
        for yy in range(2):
            g = out.at[1 - x, yy, c]
            rcopy(g, g, ss.at[4 + yy], rs.at[4 + yy], to["x"]).wait()
        for xx in range(2):
            for yy in range(2):
                g = out.at[xx, yy, c]
                rcopy(g, g, ss.at[6 + 2 * xx + yy], rs.at[6 + 2 * xx + yy], to["core"]).start()

    def last():
        for xx in range(2):
            for yy in range(2):
                g = out.at[xx, yy, 1 - c]
                rcopy(g, g, ss.at[6 + 2 * xx + yy], rs.at[6 + 2 * xx + yy], to["core"]).wait()

    return begin, step_y, step_x, step_c, last


def gather_generic(tok, pk, mx, ex, sh, sv):
    every = ("dp", "ctx", "head")
    images = lax.all_gather(tok, ("ctx", "head"), axis=1, tiled=True)
    img = lax.dynamic_index_in_dim(images, coords()[1], 0, keepdims=False)
    spread = lax.all_gather(pk, every, axis=1, tiled=True)
    pko = lax.dynamic_index_in_dim(spread, lax.axis_index("head"), 0, keepdims=False)
    return [img, pko] + [lax.all_gather(t, every, axis=0, tiled=True) for t in (mx, ex, sh, sv)]


def exchange_kernel(src, dst, ls, ss, rs):
    x, y, c, z = coords()
    others = [(dy, dz) for dy in range(2) for dz in range(4) if dy or dz]
    enter([device(x, y ^ dy, c, z ^ dz) for dy, dz in others])
    me = y * 4 + z
    mine = pltpu.make_async_copy(src.at[me], dst.at[me], ls)
    mine.start()
    copies = []
    for i, (dy, dz) in enumerate(others):
        ty, tz = y ^ dy, z ^ dz
        cp = rcopy(src.at[ty * 4 + tz], dst.at[me], ss.at[i], rs.at[i], device(x, ty, c, tz))
        cp.start()
        copies.append(cp)
    mine.wait()
    for cp in copies:
        cp.wait()


def exchange(src, cid):
    D = pltpu.SemaphoreType.DMA
    return pl.pallas_call(
        exchange_kernel,
        out_shape=jax.ShapeDtypeStruct(src.shape, src.dtype),
        in_specs=[ANY],
        out_specs=ANY,
        scratch_shapes=[D, D((7,)), D((7,))],
        compiler_params=pltpu.CompilerParams(collective_id=cid, has_side_effects=True),
        name="exchange_heads_%d" % cid,
    )(src)


def dot(a, b):
    return jnp.dot(a, b, preferred_element_type=F32)


def dot_nt(a, b):
    return lax.dot_general(a, b, (((1,), (1,)), ((), ())), preferred_element_type=F32)


def row_norm(rows):
    mean = jnp.mean(rows, axis=-1, keepdims=True)
    centred = rows - mean
    inv = lax.rsqrt(jnp.mean(centred * centred, axis=-1, keepdims=True) + NORM_EPS)
    return centred * inv, inv


def project(g, rows, length, gain, shift, bias, pw, fi, nrm, qt, kv, kt, vt):
    heads = kv.shape[0]
    hd, step = HEAD_DIM, 256
    wide = 2 * hd * heads
    normed, _ = row_norm(rows.astype(F32))
    first = (normed * gain + shift).astype(BF)
    off = pl.multiple_of(g * step, step)
    fi[pl.ds(off, step), :] = first
    nrm[pl.ds(off, step), :] = normed.astype(BF)
    kvq = (dot(first, pw[...]) + bias).astype(BF).astype(F32)
    flip = kvq.T
    ones = jnp.where(lax.broadcasted_iota(jnp.int32, (16, step), 0) == 0, 1.0, 0.0)
    pos = off + lax.broadcasted_iota(jnp.int32, (step, 2 * hd), 0)
    lane = lax.broadcasted_iota(jnp.int32, (step, 2 * hd), 1)
    extra = jnp.where(lane == 0, jnp.where(pos < length, 0.0, MASKED), jnp.where(lane < 4, 1.0, 0.0)).astype(BF)
    for h in range(heads):
        kt[h, g] = flip[2 * h * hd : (2 * h + 1) * hd].astype(BF)
        vt[h, g] = jnp.concatenate([flip[(2 * h + 1) * hd : (2 * h + 2) * hd], ones], axis=0).astype(BF)
        qt[g, h] = (flip[wide + h * hd : wide + (h + 1) * hd] * (1.0 / math.sqrt(hd))).astype(BF)
        kv[h, pl.ds(off, step), : 2 * hd] = kvq[:, 2 * h * hd : (2 * h + 2) * hd].astype(BF)
        kv[h, pl.ds(off, step), 2 * hd :] = extra


def attend(h, j, c, qt, kv, vt, mixed, lse):
    keys = kv.shape[1]
    hd, step, chunk = HEAD_DIM, 256, 512
    per = chunk // step
    row = lax.broadcasted_iota(jnp.int32, (16, step), 0)
    unit = jnp.where(row == 0, 1.0, 0.0).astype(BF)
    g = (j // 2) * 4 + c * 2 + j % 2
    sl = pl.ds(pl.multiple_of(h * hd, hd), hd)
    qa = jnp.concatenate([qt[g, h], jnp.zeros((hd, step), BF), unit, jnp.zeros((2 * hd - 16, step), BF)], axis=0)
    top = jnp.full((1, step), MASKED, F32)
    acc = jnp.zeros((hd + 16, step), F32)
    for kc in range(keys // chunk):
        s = dot(kv[h, kc * chunk : (kc + 1) * chunk, :], qa)
        new = jnp.maximum(top, jnp.max(s, axis=0, keepdims=True))
        pb = jnp.exp2((s - new) * LOG2E).astype(BF)
        scale = jnp.exp2((top - new) * LOG2E)
        part = dot(vt[h, kc * per], pb[:step])
        for i in range(1, per):
            part += dot(vt[h, kc * per + i], pb[i * step : (i + 1) * step])
        acc = acc * scale + part
        top = new
    total = acc[hd : hd + 1]
    out = acc[:hd] / total
    lse[j, h] = top + jnp.log(total)
    for i in range(2):
        mixed[2 * j + i, sl, :] = out[:, i * 128 : (i + 1) * 128].astype(BF)


def forward_kernel(lens, img, pw, gain, shift, bias, mixed, lse, fi, nrm, qt, kv, kt, vt):
    x, y, c, z = coords()
    heads, keys = kv.shape[0], kv.shape[1]
    length = lens[y]

    def rows_of(g, carry):
        rows = img[pl.ds(2 * g, 2)].reshape(256, img.shape[2])
        project(g, rows, length, gain[...], shift[...], bias[...], pw, fi, nrm, qt, kv, kt, vt)
        return carry

    def step(s, carry):
        attend(s % heads, s // heads, c, qt, kv, vt, mixed, lse)
        return carry

    lax.fori_loop(0, keys // 256, rows_of, 0)
    lax.fori_loop(0, 4 * heads, step, 0)


FT = dict(
    small=(0.0, 4.6, 12.3, 15.5, 18.4),
    tok=((0.1, 12.0, 12.1, 24.0), (4.8, 18.9, 19.0, 27.0)),
    mx=(5.5, 12.2, (24.2, 24.3, 29.0), (18.8, 33.0, 36.0, 40.0), (46.0, 50.5)),
    ex=(5.4, 34.0, (47.5, 47.6, 51.7), 57.0),
    sh=(5.3, 28.01, (42.6, 42.7, 49.7), 54.5),
    att=(30.0, 1.95),
)


def own_columns(rows, g, part):
    width = rows.shape[1] // 3
    at = lambda t, h: rows[:, t * width + g * part + h * HEAD_DIM : t * width + g * part + (h + 1) * HEAD_DIM]
    heads = part // HEAD_DIM
    return jnp.concatenate([at(t, h) for h in range(heads) for t in (1, 2)] + [at(0, h) for h in range(heads)], axis=1)


def forward_all_kernel(
    lens, tok, cot, pkw, mx, ex, sh, v0, v1, v2, v3, v4, v5, v6, v7, v8,
    mix, mixed_o, lse_o, fi_o, nrm_o, qt_o, kv_o, kt_o, pw_o, vec, hid, mxo, exo, sho, cotx,
    pk, sv, img, pwg, svg, mixed, lse, fi, nrm, qt, kv, kt, vt, pw, bias,
    ls, tys, tzs, tzr, tcs, tcr, ps, pr, vs, vr, xs, xr, xl, osem, xps, xpr, *wsems,
):
    co = coords()
    x, y, c, z = co
    to = partners(*co)
    zh = z // 2
    heads, keys = kv.shape[0], kv.shape[1]
    width = img.shape[4]
    n_dev = 32
    others = [(dy, dz) for dy in range(2) for dz in range(4) if dy or dz]
    part = heads * HEAD_DIM
    enter([to["core"], to["x"]] + [device(x, y ^ dy, c, z ^ dz) for dy, dz in others])
    length = lens[y]
    ev = []

    def arrange():
        raw = pkw[...].astype(F32).reshape(3 * 8, pkw.shape[2])
        for g in range(4):
            pk[g] = own_columns(raw, g, part).astype(BF).reshape(3, 8, 3 * part)
        vs_ = (v0, v1, v2, v3, v4, v5, v6, v7, v8)
        lines = [jnp.concatenate([v[...].astype(F32).reshape(1, -1), jnp.zeros((1, 128 - v.shape[-1]), F32)], axis=1) for v in vs_]
        sv[...] = jnp.concatenate(lines + [jnp.zeros((7, 128), F32)], axis=0).astype(BF)

    ev.append((-0.1, arrange))

    row = lambda r: y if r == 0 else 1 - y

    def tz(r, i, k, ref, dst, name):
        return rcopy(ref, dst, tzs.at[r, i], tzr.at[r, k], to[name])

    def tcore(r, k, ref):
        return rcopy(ref, img.at[row(r), c, z ^ k], tcs.at[r, k], tcr.at[r, k], to["core"])

    spread = lambda: rcopy(tok.at[1 - y], img.at[y, c, z], tys.at[0], tys.at[1], to["y"])
    keep = lambda: pltpu.make_async_copy(tok.at[y], img.at[y, c, z], ls.at[0])

    def t_begin(r):
        d = img.at[row(r), c, z]
        if r == 0:
            spread().start()
            keep().start()
            own = tok.at[y]
        else:
            rcopy(d, d, tys.at[0], tys.at[1], to["y"]).wait()
            own = d
        tz(r, 0, 0, own, d, "z1").start()
        tz(r, 1, 1, own, d, "z2").start()
        tcore(r, 0, own).start()

    def t_land(r, k):
        d = img.at[row(r), c, z ^ k]
        tz(r, k - 1, k - 1, d, d, "z1").wait_recv()
        if k == 2:
            tz(r, 2, 2, d, d, "z1").start()
        tcore(r, k, d).start()

    for r in range(2):
        t = FT["tok"][r]
        ev.append((t[0], functools.partial(t_begin, r)))
        for k in range(1, 4):
            ev.append((t[k], functools.partial(t_land, r, k)))

    def t_last():
        for r in range(2):
            d = img.at[row(r), c, z]
            for i in range(3):
                tz(r, i, 0, d, d, "z1").wait_send()
            for k in range(4):
                tcore(r, k, d).wait_send()

    ev.append((1001.0, t_last))

    steps_v = small_gather(co, to, sv, svg, ls.at[1], vs, vr, False)
    steps_p = small_gather(co, to, pk, pwg, ls.at[4], ps, pr, True)
    for t, fv, fp in zip(FT["small"], steps_v, steps_p):
        ev.append((t, fv))
        ev.append((t + 0.05, fp))

    def unpack():
        small = width // n_dev
        big = hid.shape[1] // n_dev
        part = heads * HEAD_DIM
        across = lambda n: lax.broadcasted_iota(jnp.int32, (1, n), 1)
        down = lambda n: lax.broadcasted_iota(jnp.int32, (n, 1), 0)
        hot = lambda m: jnp.where(m, 1.0, 0.0).astype(BF)
        col = across(width)
        val = dot(svg[...].reshape(n_dev * 16, 128), hot(col % small == down(128)))
        val = jnp.where(col // small == down(n_dev * 16) // 16, val, 0.0)
        val = jnp.sum(val.reshape(n_dev, 16, width), axis=0)
        vec[...] = val
        col = across(hid.shape[1])
        eight = svg[...].astype(F32).reshape(n_dev, 16, 128)[:, 8, :].astype(BF)
        line = dot(eight, hot(col % big == down(128)))
        hid[...] = jnp.sum(jnp.where(col // big == down(n_dev), line, 0.0), axis=0, keepdims=True)
        dst = across(3 * part)
        head, off = dst // (2 * HEAD_DIM), dst % (2 * HEAD_DIM)
        hv = jnp.where(jnp.logical_and(dst < 2 * part, off >= HEAD_DIM), z * part + head * HEAD_DIM + off - HEAD_DIM, -1)
        hq = jnp.where(dst >= 2 * part, z * part + dst - 2 * part, -1)
        rows = val.astype(BF)
        bq = dot(rows, hot(hq == down(width)))
        bv = dot(rows, hot(hv == down(width)))
        bias[...] = bq[2:3] + bv[3:4]

    def flatten():
        def body(i, carry):
            blk = pwg[i // 4, (i // 2) % 2, i % 2].astype(F32)
            n = blk.shape[0] * blk.shape[1] * blk.shape[2]
            pw[pl.ds(pl.multiple_of(i * n, n), n), :] = blk.reshape(n, blk.shape[3]).astype(BF)
            return carry

        lax.fori_loop(0, 8, body, 0)

    ev.append((FT["small"][4] + 0.1, unpack))
    ev.append((FT["small"][4] + 0.2, flatten))

    def project_group(r, mine, p):
        cc = c if mine else 1 - c
        zz = zh if p == 0 else 1 - zh
        if r == 0 and mine and p == 0:
            keep().wait()
        if not mine:
            for k in (2 * p, 2 * p + 1):
                d = img.at[row(r), cc, z ^ k]
                rcopy(d, d, tcs.at[r, k], tcr.at[r, k], to["core"]).wait_recv()
        g = row(r) * 4 + cc * 2 + zz
        rows = img[row(r), cc, pl.ds(2 * zz, 2)].reshape(256, width)
        project(g, rows, length, vec[0:1, :], vec[1:2, :], bias[...], pw, fi, nrm, qt, kv, kt, vt)

    t_ready = FT["small"][4] + 0.3
    for p in range(2):
        for r in range(2):
            for mine in (True, False):
                t = max(FT["tok"][r][1 if p == 0 else 3] + (0.3 if mine else 0.6), t_ready + 0.01 * (r * 2 + (not mine)))
                ev.append((t, functools.partial(project_group, r, mine, p)))

    weight_gather(ev, co, to, mx, lambda px, py, cc, zz: mxo.at[px, py, cc, zz], wsems[:9], "yx", FT["mx"])
    half = ex.shape[2] // 2
    cols = lambda xx: pl.ds(pl.multiple_of(xx * half, half), half)
    ex_view = lambda yy, cc, zz: exo.at[:, yy, cc, zz]
    sh_view = lambda yy, cc, zz: sho.at[yy, cc, zz]
    ex_own = lambda: pltpu.make_async_copy(ex.at[:, :, cols(x)], exo.at[x, y, c, z], ls.at[2])
    ex_swap = lambda: rcopy(ex.at[:, :, cols(1 - x)], exo.at[x, y, c, z], xps.at[0], xpr.at[0], to["x"])
    sh_own = lambda: pltpu.make_async_copy(sh, sho.at[y, c, z], ls.at[3])
    cot_swap = lambda: rcopy(cot, cotx, xps.at[1], xpr.at[1], to["x"])

    def swap():
        ex_own().start()
        ex_swap().start()
        cot_swap().start()

    def ex_ready():
        ex_own().wait()
        ex_swap().wait()

    ev.append((0.6, swap))
    ev.append((1003.0, lambda: cot_swap().wait()))
    half_gather(ev, co, to, ex_ready, lambda: None, ex_view(y, c, z), ex_view, wsems[9:15], FT["ex"])
    half_gather(ev, co, to, lambda: sh_own().start(), lambda: sh_own().wait(), sh, sh_view, wsems[15:21], FT["sh"])

    stored = [(fi, fi_o), (nrm, nrm_o), (qt, qt_o), (kv, kv_o), (kt, kt_o), (pw, pw_o), (mixed, mixed_o), (lse, lse_o)]
    store = lambda i: pltpu.make_async_copy(stored[i][0], stored[i][1], osem.at[i])

    def store_first():
        for i in range(6):
            store(i).start()

    t_att, t_step = FT["att"]
    steps = 4 * heads
    t_end = t_att + steps * t_step
    ev.append((t_att + 0.001, store_first))

    me = y * 4 + z

    def target(q):
        w = 3 - q
        return [(w // 2, 2 * (w % 2)), (w // 2, 2 * (w % 2) + 1)]

    def xcopy(dy, dz):
        i = dy * 4 + dz
        return rcopy(mixed.at[(y ^ dy) * 4 + (z ^ dz)], mix.at[me], xs.at[i], xr.at[i], device(x, y ^ dy, c, z ^ dz))

    mine_copy = lambda: pltpu.make_async_copy(mixed.at[me], mix.at[me], xl)

    def send_group(q):
        for dy, dz in target(q):
            if dy or dz:
                xcopy(dy, dz).start()
            else:
                mine_copy().start()

    for q in range(4):
        ev.append((t_att + (q + 1) * heads * t_step + 0.002, functools.partial(send_group, q)))

    def finish():
        store(6).start()
        store(7).start()
        for dy, dz in others:
            xcopy(dy, dz).wait()
        mine_copy().wait()

    ev.append((t_end + 3.8, finish))

    def drain():
        for i in range(8):
            store(i).wait()

    ev.append((1002.0, drain))

    ev.sort(key=lambda e: e[0])
    for t, fn in ev:
        if t < t_att:
            fn()

    def step(s, carry):
        for k in range(steps):
            here = [fn for t, fn in ev if t_att + k * t_step <= t < t_att + (k + 1) * t_step]
            if here:

                @pl.when(s == k)
                def _():
                    for fn in here:
                        fn()

        attend(s % heads, (3 - s // heads) ^ (2 * y + zh), c, qt, kv, vt, mixed, lse)
        return carry

    lax.fori_loop(0, steps, step, 0)
    for t, fn in ev:
        if t >= t_end:
            fn()


def forward_all(lens, tok, cot, pkw, mx, ex, sh, vecs):
    D, V, S = pltpu.SemaphoreType.DMA, pltpu.VMEM, jax.ShapeDtypeStruct
    shard, width = tok.shape[1], tok.shape[2]
    cols = pkw.shape[2] // 4
    pk_shape = (3, 8, cols)
    heads = cols // (3 * HEAD_DIM)
    keys = 16 * shard
    n = keys // 256
    lead = (2, SPLIT, SPLIT, 4)
    part = heads * HEAD_DIM
    hidden = ex.shape[2]
    outs = [
        S((8, part, shard), BF),
        S((8, part, shard), BF),
        S((4, heads, 1, 256), F32),
        S((keys, width), BF),
        S((keys, width), BF),
        S((n, heads, HEAD_DIM, 256), BF),
        S((heads, keys, 4 * HEAD_DIM), BF),
        S((heads, n, HEAD_DIM, 256), BF),
        S((width, cols), BF),
        S((16, width), F32),
        S((1, hidden), F32),
        S(lead + mx.shape, BF),
        S(lead + (3, 8, hidden // 2), BF),
        S(lead[1:] + sh.shape, BF),
        S(cot.shape, BF),
    ]
    wsem = [D, D((3,)), D((3,)), D((4,)), D((4,)), D((2, 4)), D((2, 4)), D((4,)), D((4,))]
    wsem += [D((3,)), D((3,)), D((4,)), D((4,)), D((2,)), D((2,))] * 2
    scr = [V((4,) + pk_shape, BF), V((16, 128), BF)]
    scr += [V((2, 2, 4) + tok.shape[1:], BF), V(lead + pk_shape, BF), V(lead + (16, 128), BF), V((8, part, shard), BF), V((4, heads, 1, 256), F32)]
    scr += [V((keys, width), BF), V((keys, width), BF), V((n, heads, HEAD_DIM, 256), BF), V((heads, keys, 4 * HEAD_DIM), BF)]
    scr += [V((heads, n, HEAD_DIM, 256), BF), V((heads, n, HEAD_DIM + 16, 256), BF), V((width, cols), BF), V((1, cols), F32)]
    scr += [D((5,)), D((2,)), D((2, 3)), D((2, 3)), D((2, 4)), D((2, 4)), D((10,)), D((10,)), D((10,)), D((10,)), D((8,)), D((8,)), D, D((8,)), D((2,)), D((2,))]
    return pl.pallas_call(
        forward_all_kernel,
        out_shape=outs,
        in_specs=[SM, ANY, ANY, VM, ANY, ANY, ANY] + [VM] * 9,
        out_specs=[ANY] * 9 + [VM] * 2 + [ANY] * 4,
        scratch_shapes=scr + wsem,
        compiler_params=pltpu.CompilerParams(collective_id=0, has_side_effects=True, vmem_limit_bytes=62 << 20),
        name="gather_attention_forward",
    )(lens, tok, cot, pkw, mx, ex, sh, *vecs)


def attention_forward(lens, img, pw, gain, shift, bias):
    heads = pw.shape[1] // (3 * HEAD_DIM)
    keys = img.shape[0] * img.shape[1]
    width = heads * HEAD_DIM
    n = keys // 256
    outs = [
        jax.ShapeDtypeStruct((8, width, 128), BF),
        jax.ShapeDtypeStruct((4, heads, 1, 256), F32),
        jax.ShapeDtypeStruct((keys, img.shape[2]), BF),
        jax.ShapeDtypeStruct((keys, img.shape[2]), BF),
        jax.ShapeDtypeStruct((n, heads, HEAD_DIM, 256), BF),
        jax.ShapeDtypeStruct((heads, keys, 4 * HEAD_DIM), BF),
        jax.ShapeDtypeStruct((heads, n, HEAD_DIM, 256), BF),
    ]
    return pl.pallas_call(
        forward_kernel,
        out_shape=outs,
        in_specs=[SM] + [VM] * 5,
        out_specs=[VM] * 7,
        scratch_shapes=[pltpu.VMEM((heads, n, HEAD_DIM + 16, 256), BF)],
        compiler_params=pltpu.CompilerParams(vmem_limit_bytes=50 << 20),
        name="attention_forward",
    )(lens, img, pw, gain, shift, bias)


def dot_tn(a, b):
    return lax.dot_general(a, b, (((0,), (0,)), ((), ())), preferred_element_type=F32)


def dense_body(
    tok, cot, cotx, mix, vec, hid, mx_h, ex_h, sh_h,
    base, upx, act, sin, cot2, gpre, gres, gresf, send, s4, s5, s6, s7, s8,
    mx, ex, sh, down_out, down_in, sems, ss, rs, then, early,
):
    co = coords()
    x = co[0]
    to = partners(*co)["x"]
    images, shard, width = tok.shape
    rows = images * shard
    half = ex.shape[1]
    n = half // width
    load = [pltpu.make_async_copy(mx_h, mx, sems.at[0])]
    for i in range(n):
        cols = slice(i * width, (i + 1) * width)
        load.append(pltpu.make_async_copy(ex_h.at[:, cols], ex.at[:, cols], sems.at[1 + i]))
        load.append(pltpu.make_async_copy(sh_h.at[cols, :], sh.at[cols, :], sems.at[1 + n + i]))
    for cp in load:
        cp.start()
    cin = cot[...].reshape(rows, width)
    cf = cin.astype(F32)
    s7[...] = jnp.sum(cf, axis=0, keepdims=True)
    cot2[:rows, :] = cin
    cot2[rows:, :] = cotx[...].reshape(rows, width)

    def sin_copy(i):
        return rcopy(sin.at[i * shard : (i + 1) * shard], sin.at[rows + i * shard : rows + (i + 1) * shard], ss.at[i], rs.at[i], to)

    def down_copy(i):
        return rcopy(down_out.at[i], down_in.at[i], ss.at[images + i], rs.at[images + i], to)

    load[0].wait()
    keep = []
    for i in range(images):
        res = tok[i].astype(F32) + dot_tn(mix[i], mx[...]) + vec[4:5, :]
        nr, iv = row_norm(res)
        sin[i * shard : (i + 1) * shard, :] = (nr * vec[5:6, :] + vec[6:7, :]).astype(BF)
        sin_copy(i).start()
        keep.append((res, nr, iv))
    residual, normed, inv = [jnp.concatenate(t, axis=0) for t in zip(*keep)]
    own = pl.ds(pl.multiple_of(x * half, half), half)
    s8[...] = jnp.zeros_like(s8)

    def chunks(lo, hi):
        up = jnp.zeros((hi - lo, width), F32)
        down = jnp.zeros((hi - lo, width), F32)
        second = sin[lo:hi, :]
        grad = cot2[lo:hi, :]
        for i in range(n):
            cols = slice(i * width, (i + 1) * width)
            if lo == 0:
                load[1 + 2 * i].wait()
                load[2 + 2 * i].wait()
            there = pl.ds(pl.multiple_of(x * half + i * width, width), width)
            pre = dot(second, ex[:, cols]) + hid[:, there]
            cum = 0.5 * (1.0 + lax.erf(pre * (1.0 / math.sqrt(2.0))))
            slope = cum + pre * (jnp.exp(-0.5 * pre * pre) * (1.0 / math.sqrt(2.0 * math.pi)))
            a = (pre * cum).astype(BF)
            act[lo:hi, cols] = a
            g = dot_nt(grad, sh[cols, :]) * slope
            s8[:, there] += jnp.sum(g, axis=0, keepdims=True)
            gb = g.astype(BF)
            gpre[lo:hi, cols] = gb
            up += dot(a, sh[cols, :])
            down += dot_nt(gb, ex[:, cols])
        return up, down

    up, down = chunks(0, rows)
    then()
    base[...] = (residual + up + vec[7:8, :]).reshape(images, shard, width)
    for i in range(images):
        sin_copy(i).wait()
        other_up, other_down = chunks(rows + i * shard, rows + (i + 1) * shard)
        down_out[i] = other_down.astype(BF)
        down_copy(i).start()
        upx[i] = other_up.astype(BF)
    early()
    rest = []
    for i in range(images):
        down_copy(i).wait()
        part = slice(i * shard, (i + 1) * shard)
        total = down[part] + down_in[i].astype(F32)
        nr = normed[part]
        scaled = total * vec[5:6, :]
        m1 = jnp.mean(scaled, axis=-1, keepdims=True)
        m2 = jnp.mean(scaled * nr, axis=-1, keepdims=True)
        gr = cf[part] + inv[part] * (scaled - m1 - nr * m2)
        gresf[i] = gr
        gb = gr.astype(BF)
        gres[part, :] = gb
        val = dot_nt(mx[...], gb).astype(BF)
        send[4 * i : 4 * (i + 1)] = val.reshape(4, width // 4, shard)
        sums = [jnp.sum(t, axis=0, keepdims=True) for t in (gr, total * nr, total)]
        rest.append(sums)
    for ref, a, b in zip((s4, s5, s6), *rest):
        ref[...] = a + b


def hand_over_kernel(*refs):
    n = 6
    src, vec, dst, outs = refs[:n], refs[n], refs[n + 1 : 2 * n + 1], refs[2 * n + 1 :]
    for i in range(n):
        dst[i][...] = src[i][...]
    for i, o in enumerate(outs):
        line = 16 if i == 8 else i
        o[...] = vec[line : line + 1, : o.shape[0]].reshape(o.shape[0])


def hand_over(arrays, vec, small, big):
    S = jax.ShapeDtypeStruct
    outs = [S(t.shape, t.dtype) for t in arrays] + [S((small,), F32)] * 8 + [S((big,), F32)]
    return pl.pallas_call(
        hand_over_kernel,
        out_shape=outs,
        in_specs=[VM] * 7,
        out_specs=[VM] * 15,
        name="hand_over",
    )(*arrays, vec)


def split3(value):
    hi = value.astype(BF)
    rest = value - hi.astype(F32)
    mid = rest.astype(BF)
    low = (rest - mid.astype(F32)).astype(BF)
    return hi, mid, low


def pick(value, hot):
    a, b, d = split3(value)
    return dot(a, hot) + dot(b, hot) + dot(d, hot)


def stacked_extra(lead, value, row):
    a, b, d = (t.astype(F32) for t in split3(value))
    out = jnp.where(row == 1, a, 0.0) + jnp.where(row == 2, b, 0.0) + jnp.where(row == 3, d, 0.0)
    return (jnp.where(row == 0, lead, 0.0) + out).astype(BF)


def backward_step(h, j, c, grad, mixed, lse, qt, kv, kt, dkv, dqt):
    keys = kv.shape[1]
    hd, step, chunk = HEAD_DIM, 256, 512
    per = chunk // step
    g = (j // 2) * 4 + c * 2 + j % 2
    sl = pl.ds(pl.multiple_of(h * hd, hd), hd)
    do = jnp.concatenate([grad[2 * j, sl, :], grad[2 * j + 1, sl, :]], axis=1)
    mx = jnp.concatenate([mixed[2 * j, sl, :], mixed[2 * j + 1, sl, :]], axis=1)
    delta = jnp.sum(do.astype(F32) * mx.astype(F32), axis=0, keepdims=True)
    row = lax.broadcasted_iota(jnp.int32, (16, step), 0)
    none = jnp.zeros((hd, step), BF)
    rest = jnp.zeros((2 * hd - 16, step), BF)
    qh = qt[g, h]
    qa = jnp.concatenate([qh, none, stacked_extra(1.0, -lse[j, h], row), rest], axis=0)
    da = jnp.concatenate([none, do, stacked_extra(0.0, -delta, row), rest], axis=0)
    qr = jnp.concatenate([qh, none], axis=0).astype(F32).T.astype(BF)
    dr = jnp.concatenate([none, do], axis=0).astype(F32).T.astype(BF)
    dq = jnp.zeros((hd, step), F32)
    for kc in range(keys // chunk):
        rows = slice(kc * chunk, (kc + 1) * chunk)
        block = kv[h, rows, :]
        p = jnp.exp2(dot(block, qa) * LOG2E)
        dp = dot(block, da)
        ds = (p * dp).astype(BF)
        dkv[h, rows, :] += dot(ds, qr) + dot(p.astype(BF), dr)
        for i in range(per):
            dq += dot(kt[h, kc * per + i], ds[i * step : (i + 1) * step])
    dqt[j, sl, :] = (dq * (1.0 / math.sqrt(hd))).astype(BF)


def add_into(dst, src, lead, n):
    def body(i, carry):
        dst[lead + (i,)] = dst[lead + (i,)] + src[i]
        return carry

    lax.fori_loop(0, n, body, 0)


def halving(co, to, G, u, bufs, ss, rs, order, finish):
    x, y, c, z = co
    zh, zl = z // 2, z % 2
    r0, r1, r2, r3, r4 = bufs
    a, b = order
    first = (lambda n: G.at[u, 1 - x, n, c]) if a == "x" else (lambda n: G.at[u, n, 1 - y, c])
    keep = (lambda n: (u, x, n, c)) if a == "x" else (lambda n: (u, n, y, c))
    second = G.at[u, x, 1 - y, c] if b == "y" else G.at[u, 1 - x, y, c]

    def cp0(i):
        return rcopy(G.at[u, i // 2, i % 2, 1 - c], r0.at[u, i], ss.at[u, i], rs.at[u, i], to["core"])

    def cp1(n):
        return rcopy(first(n), r1.at[u, n], ss.at[u, 4 + n], rs.at[u, 4 + n], to[a])

    cp2 = lambda: rcopy(second, r2.at[u], ss.at[u, 6], rs.at[u, 6], to[b])
    cp3 = lambda n: rcopy(G.at[u, x, y, c, 2 * n + 1 - zl], r3.at[u, n], ss.at[u, 7 + n], rs.at[u, 7 + n], to["z1"])
    cp4 = lambda: rcopy(G.at[u, x, y, c, 2 * (1 - zh) + zl], r4.at[u], ss.at[u, 9], rs.at[u, 9], to["z2"])

    def core_send():
        for i in range(4):
            cp0(i).start()

    def core_land():
        for i in range(4):
            cp0(i).wait()
            add_into(G, r0.at[u, i], (u, i // 2, i % 2, c), 4)

    def a_send():
        for n in range(2):
            cp1(n).start()

    def a_wait():
        for n in range(2):
            cp1(n).wait()

    def a_add():
        for n in range(2):
            add_into(G, r1.at[u, n], keep(n), 4)
        cp2().start()

    def b_land():
        cp2().wait()
        add_into(G, r2.at[u], (u, x, y, c), 4)
        for n in range(2):
            cp3(n).start()

    def z1_land():
        for n in range(2):
            cp3(n).wait()
            here = (u, x, y, c, 2 * n + zl)
            G[here] = G[here] + r3[u, n]
        cp4().start()

    def z2_land():
        cp4().wait()
        finish(G[u, x, y, c, z].astype(F32) + r4[u].astype(F32))

    return dict(core_send=core_send, core_land=core_land, a_send=a_send, a_wait=a_wait, a_add=a_add, b_land=b_land, z1_land=z1_land, z2_land=z2_land)


def half_sum(co, to, H, b, r0, r1, r3, r4, ss, rs, finish):
    x, y, c, z = co
    zh, zl = z // 2, z % 2
    cp0 = lambda i: rcopy(H.at[b, i, 1 - c], r0.at[b, i], ss.at[b, i], rs.at[b, i], to["core"])
    cp1 = lambda: rcopy(H.at[b, 1 - y, c], r1.at[b], ss.at[b, 2], rs.at[b, 2], to["y"])
    cp3 = lambda n: rcopy(H.at[b, y, c, 2 * n + 1 - zl], r3.at[b, n], ss.at[b, 3 + n], rs.at[b, 3 + n], to["z1"])
    cp4 = lambda: rcopy(H.at[b, y, c, 2 * (1 - zh) + zl], r4.at[b], ss.at[b, 5], rs.at[b, 5], to["z2"])

    def core_send():
        for i in range(2):
            cp0(i).start()

    def core_land():
        for i in range(2):
            cp0(i).wait()
            add_into(H, r0.at[b, i], (b, i, c), 4)

    def y_send():
        cp1().start()

    def y_land():
        cp1().wait()
        add_into(H, r1.at[b], (b, y, c), 4)
        for n in range(2):
            cp3(n).start()

    def z1_land():
        for n in range(2):
            cp3(n).wait()
            here = (b, y, c, 2 * n + zl)
            H[here] = H[here] + r3[b, n]
        cp4().start()

    def z2_land():
        cp4().wait()
        finish(H[b, y, c, z].astype(F32) + r4[b].astype(F32))

    return core_send, core_land, y_send, y_land, z1_land, z2_land


def half_sum_line(co, to, H, b, r0, r1, r3, r4, ss, rs, finish):
    x, y, c, z = co
    zh, zl = z // 2, z % 2
    cp0 = lambda i: rcopy(H.at[b, i, 1 - c], r0.at[b, i], ss.at[b, i], rs.at[b, i], to["core"])
    cp3 = lambda i, n: rcopy(H.at[b, i, c, 2 * n + 1 - zl], r1.at[b, 2 * i + n], ss.at[b, 2 + 2 * i + n], rs.at[b, 2 + 2 * i + n], to["z1"])
    cp4 = lambda i: rcopy(H.at[b, i, c, 2 * (1 - zh) + zl], r3.at[b, i], ss.at[b, 6 + i], rs.at[b, 6 + i], to["z2"])
    cp1 = lambda: rcopy(H.at[b, 1 - y, c, z], r4.at[b], ss.at[b, 8], rs.at[b, 8], to["y"])

    def core_send():
        for i in range(2):
            cp0(i).start()

    def core_land():
        for i in range(2):
            cp0(i).wait()
            add_into(H, r0.at[b, i], (b, i, c), 4)

    def z1_send():
        for i in range(2):
            for n in range(2):
                cp3(i, n).start()

    def z1_land():
        for i in range(2):
            for n in range(2):
                cp3(i, n).wait()
                here = (b, i, c, 2 * n + zl)
                H[here] = H[here] + r1[b, 2 * i + n]
        for i in range(2):
            cp4(i).start()

    def z2_land():
        for i in range(2):
            cp4(i).wait()
            here = (b, i, c, z)
            H[here] = H[here] + r3[b, i]
        cp1().start()

    def y_land():
        cp1().wait()
        finish(H[b, y, c, z].astype(F32) + r4[b].astype(F32))

    return core_send, core_land, z1_send, z1_land, z2_land, y_land


TIMES = dict(
    core=(0.95, 1.31, 1.4, 1.5, 2.6),
    send=(0.96, 1.32, 10.25, 1.51),
    y=(10.2, 16.0, 21.0, 15.5),
    z1=(19.5, 26.0, 29.0, 24.0),
    z2=(27.0, 31.5, 36.5, 30.0),
    mixer=(16.2, 24.5, 31.8, 38.0),
    att=(4.0, 1.6),
    walk=(0.1, 0.95, 3.0, 3.9),
    fold=(2.2, 5.0),
    half=(8.6, 13.5, 20.5, 26.5),
    full=(16.0, 21.5, 27.2, 35.0),
    last=(22.0, 27.4),
    packed=(5.2, 9.0, 14.5, 18.0, 33.0),
    vec=(8.4, 9.1, 14.6, 18.1, 26.0, 34.0),
)


def backward_kernel(
    tok, cot_in, cotx, mix, vec, hid, mx_h, ex_h, sh_h, mixed_h, lse_h, qt_h, kv_h, kt_h, fi_h, nrm_h, pw_h,
    out_in, out_s, out_e, out_m, out_b, out_p, out_v,
    mx, ex, sh, down_out, down_in, base, upx, act, sin, cot, gpre, gres, gresf, send, s4, s5, s6, s7, s8, wsem, dss, drs,
    mixed, lse, qt, kv, kt, fi, nrm, pw, lsem, grad, G, r0, r1, r2, r3, r4, H, h0, h1, h3, h4, F, xo, xe, ub,
    dkv, dqt, dall, GF, q0, q1, q2, q3, sq, GP, p0, p1, p2, p3, V, vr,
    els, ess, ers, gss, grs, hss, hrs, xss, xrs, qss, qrs, pss, prs, vss, vrs,
):
    co = coords()
    x, y, c, z = co
    to = partners(*co)
    zh, zl = z // 2, z % 2
    heads, keys = kv.shape[0], kv.shape[1]
    width = cot.shape[1]
    rows = gres.shape[0]
    gain = vec
    late = [(mixed_h, mixed), (lse_h, lse), (qt_h, qt), (kv_h, kv), (kt_h, kt), (fi_h, fi), (nrm_h, nrm), (pw_h, pw)]

    def local(i):
        return pltpu.make_async_copy(late[i][0], late[i][1], lsem.at[i])

    others = [(dy, dz) for dy in range(2) for dz in range(4) if dy or dz]
    enter([to["core"], to["x"]] + [device(x, y ^ dy, c, z ^ dz) for dy, dz in others])
    me = y * 4 + z

    def exch(i):
        dy, dz = others[i]
        return rcopy(send.at[(y ^ dy) * 4 + (z ^ dz)], grad.at[me], ess.at[i], ers.at[i], device(x, y ^ dy, c, z ^ dz))

    mine = pltpu.make_async_copy(send.at[me], grad.at[me], els)
    ev = []
    n_hid = 2 * act.shape[1] // width

    def shrink_all():
        span = act.shape[1] // 4

        def body(t, carry):
            val = dot_tn(act[:, pl.ds(pl.multiple_of(t * span, span), span)], cot[...]).astype(BF)
            val = val.reshape(4, 4, 3, 8, width)
            for zz in range(4):
                for i in range(4):
                    H[i // 2, t // 2, t % 2, zz, i % 2] = val[zz, i]
            return carry

        lax.fori_loop(0, 4, body, 0)

    def expand_one(q):
        for xx in range(2):
            val = dot_tn(sin[:, xx * width // 2 : (xx + 1) * width // 2], gpre[:, q * width : (q + 1) * width]).astype(BF)
            val = val.reshape(2, 2, 4, 3, 8, width)
            for i in range(16):
                H[2 + q, i // 8, (i // 4) % 2, i % 4, xx] = val[i // 8, (i // 4) % 2, i % 4]

    def mixer_one():
        half = rows // 2
        for t in range(2):
            sl = slice(t * width // 2, (t + 1) * width // 2)
            val = dot(mix[0, sl, :], gres[:half]) + dot(mix[1, sl, :], gres[half:])
            G[0, t] = val.astype(BF).reshape(2, 2, 4, 3, 8, width)

    def run(fns):
        for fn in fns:
            fn()

    def lanes(xx, q):
        return pl.ds(pl.multiple_of((xx * (n_hid // 2) + q) * width, width), width)

    swap = lambda q: rcopy(xo.at[q], xe.at[q], xss.at[q], xrs.at[q], to["x"])
    up_copy = lambda: rcopy(upx, ub, xss.at[2], xrs.at[2], to["x"])

    def done_s(b, val):
        for i in range(2):
            out_s[2 * b + i] = val[i]

    def done_e(q, val):
        F[...] = val
        out_e[:, :, lanes(x, q)] = F[x]
        xo[q] = F[1 - x].astype(BF)
        swap(q).start()

    def landed_e(q):
        swap(q).wait()
        out_e[:, :, lanes(1 - x, q)] = xe[q].astype(F32)

    def landed_up():
        up_copy().wait()
        for i in range(2):
            out_b[i] = (base[i] + ub[i].astype(F32)).astype(BF)

    ev.append((0.0, shrink_all))
    ev.append((0.6, functools.partial(expand_one, 0)))
    ev.append((0.8, functools.partial(expand_one, 1)))
    ev.append((1.05, mixer_one))
    ev.append((1.2, lambda: up_copy().start()))
    for b in range(4):
        fin = functools.partial(done_s, b) if b < 2 else functools.partial(done_e, b - 2)
        st = (half_sum if b < 3 else half_sum_line)(co, to, H, b, h0, h1, h3, h4, hss, hrs, fin)
        for t, fn in zip(((0.5, 0.51, 0.7, 0.9)[b], TIMES["core"][b], TIMES["send"][b], TIMES["y"][b], TIMES["z1"][b], TIMES["z2"][b]), st):
            ev.append((t, fn))
        if b >= 2:
            ev.append((TIMES["z2"][b] + 4.0, functools.partial(landed_e, b - 2)))
    ev.append((TIMES["z2"][3] + 4.1, landed_up))
    st = halving(co, to, G, 0, (r0, r1, r2, r3, r4), gss, grs, "xy", lambda val: out_m.__setitem__(Ellipsis, val))
    ev.append((1.1, st["core_send"]))
    ev.append((TIMES["core"][4], lambda: run([st["core_land"], st["a_send"]])))
    for t, names in zip(TIMES["mixer"], (("a_wait", "a_add"), ("b_land",), ("z1_land",), ("z2_land",))):
        ev.append((t, functools.partial(run, [st[k] for k in names])))

    def zero():
        def body(i, carry):
            for h in range(heads):
                dkv[h, pl.ds(pl.multiple_of(i * 256, 256), 256), :] = jnp.zeros((256, 2 * HEAD_DIM), F32)
            return carry

        lax.fori_loop(0, keys // 256, body, 0)

    def arrive(q):
        if q == 0:
            mine.wait()
            for i in range(5):
                local(i).wait()
        for i in range(7):
            if 2 * others[i][0] + others[i][1] // 2 == q:
                exch(i).wait()

    ev.append((1.3, zero))
    steps = 4 * heads
    t_att, t_step = TIMES["att"]
    t_end = t_att + t_step * steps
    for q in range(4):
        ev.append((t_att + heads * q * t_step + 0.001, functools.partial(arrive, q)))

    def begin():
        mine.start()
        for i in range(7):
            exch(i).start()
        V[...] = jnp.zeros_like(V)
        for i, ref in ((4, s4), (5, s5), (6, s6), (7, s7)):
            V[i : i + 1, :] = ref[...]
        for i in range(n_hid):
            V[8 + i : 9 + i, :] = s8[:, i * width : (i + 1) * width]

    ev.append((1.0, begin))

    def group(slot, mine_rows):
        cc = c if mine_rows else 1 - c
        yy = slot // 2
        g = yy * 4 + cc * 2 + slot % 2
        off = pl.multiple_of(g * 256, 256)
        rs_ = pl.ds(off, 256)
        wide = 2 * HEAD_DIM * heads
        dk = jnp.concatenate([dkv[h, rs_, :].astype(BF) for h in range(heads)], axis=1)
        gf = dot_nt(dk, pw[:, :wide])
        dall[rs_, :wide] = dk
        sums = jnp.sum(dk.astype(F32), axis=0, keepdims=True)
        V[16:17, :wide] += sums
        if mine_rows:
            dq = dqt[slot].astype(F32).T.astype(BF)
            gf += dot_nt(dq, pw[:, wide:])
            dall[rs_, wide:] = dq
            V[17:18, : dq.shape[1]] += jnp.sum(dq.astype(F32), axis=0, keepdims=True)
        else:
            dall[rs_, wide:] = jnp.zeros((256, heads * HEAD_DIM), BF)
        V[0:1, :] += jnp.sum(gf * nrm[rs_, :].astype(F32), axis=0, keepdims=True)
        V[1:2, :] += jnp.sum(gf, axis=0, keepdims=True)
        GF[yy, cc, pl.ds(2 * (slot % 2), 2)] = gf.astype(BF).reshape(2, 2, 64, width)

    def q_core(r):
        yy = rowof(r)
        return rcopy(GF.at[yy, 1 - c], q0.at[r], qss.at[r], qrs.at[r], to["core"])

    def q_z1(r, f, n):
        i = 2 + 4 * r + 2 * f + n
        return rcopy(GF.at[rowof(r), c, 2 * n + 1 - zl, f], q1.at[r, f, n], qss.at[i], qrs.at[i], to["z1"])

    def q_z2(r, f):
        i = 10 + 2 * r + f
        return rcopy(GF.at[rowof(r), c, 2 * (1 - zh) + zl, f], q2.at[r, f], qss.at[i], qrs.at[i], to["z2"])

    def q_y(f):
        return rcopy(sq.at[f], q3.at[f], qss.at[14 + f], qrs.at[14 + f], to["y"])

    def rowof(r):
        return 1 - y if r == 0 else y

    def walk(mine_rows, r):
        def body(i, carry):
            group(2 * rowof(r) + i, mine_rows)
            return carry

        lax.fori_loop(0, 2, body, 0)
        if not mine_rows:
            q_core(r).start()

    def q_sum(r):
        q_core(r).wait()
        yy = rowof(r)

        def body(i, carry):
            GF[yy, c, i // 2, i % 2] = GF[yy, c, i // 2, i % 2] + q0[r, i // 2, i % 2]
            return carry

        lax.fori_loop(0, 8, body, 0)
        if r == 0:
            q_send(0, 0)

    def q_send(r, f):
        for n in range(2):
            q_z1(r, f, n).start()

    chunks = [(r, f) for r in range(2) for f in range(2)]

    def q_half(i):
        r, f = chunks[i]
        for n in range(2):
            q_z1(r, f, n).wait()
        if i + 2 < 4:
            q_send(*chunks[i + 2])
        for n in range(2):
            here = (rowof(r), c, 2 * n + zl, f)
            GF[here] = GF[here] + q1[r, f, n]
        q_z2(r, f).start()

    def finish(img, f, total):
        rs_ = slice(64 * f, 64 * (f + 1))
        normed, inv = row_norm(tok[img, rs_].astype(F32))
        scaled = total * gain[0:1, :]
        m1 = jnp.mean(scaled, axis=-1, keepdims=True)
        m2 = jnp.mean(scaled * normed, axis=-1, keepdims=True)
        out_in[img, rs_] = (gresf[img, rs_] + inv * (scaled - m1 - normed * m2)).astype(BF)

    def q_full(i):
        r, f = chunks[i]
        q_z2(r, f).wait()
        total = GF[rowof(r), c, z, f].astype(F32) + q2[r, f].astype(F32)
        if r == 0:
            sq[f] = total.astype(BF)
            q_y(f).start()
        else:
            finish(y, f, total)

    def q_last(f):
        q_y(f).wait()
        finish(1 - y, f, q3[f].astype(F32))

    def late_rows():
        for i in range(5, 8):
            local(i).wait()

    ev.append((t_end + 0.05, late_rows))
    for i in range(4):
        ev.append((t_end + TIMES["walk"][i], functools.partial(walk, i % 2 == 1, i // 2)))
        ev.append((t_end + TIMES["half"][i], functools.partial(q_half, i)))
        ev.append((t_end + TIMES["full"][i], functools.partial(q_full, i)))
    for f in range(2):
        ev.append((t_end + TIMES["fold"][f], functools.partial(q_sum, f)))
        if f == 0:
            ev.append((t_end + TIMES["walk"][3] + 0.1, functools.partial(q_send, 0, 1)))
        ev.append((t_end + TIMES["last"][f], functools.partial(q_last, f)))

    def packed():
        val = dot_tn(fi[...], dall[...]).astype(BF)
        GP[0] = val.reshape(2, 2, 2, 4, 3, 8, val.shape[1])
        for i in range(4):
            p_core(i).start()

    def p_core(i):
        return rcopy(GP.at[0, i // 2, i % 2, 1 - c], p0.at[i], pss.at[i], prs.at[i], to["core"])

    def p_a(n):
        return rcopy(GP.at[0, 1 - x, n, c], p1.at[n], pss.at[4 + n], prs.at[4 + n], to["x"])

    p_b = lambda: rcopy(GP.at[0, x, 1 - y, c], p2, pss.at[6], prs.at[6], to["y"])
    p_z = lambda k: rcopy(GP.at[0, x, y, c, z ^ k], p3.at[k - 1], pss.at[6 + k], prs.at[6 + k], to["z%d" % k])

    def packed_core():
        for i in range(4):
            p_core(i).wait()
            add_into(GP, p0.at[i], (0, i // 2, i % 2, c), 4)
        for n in range(2):
            p_a(n).start()

    def packed_a():
        for n in range(2):
            p_a(n).wait()
            add_into(GP, p1.at[n], (0, x, n, c), 4)
        p_b().start()

    def packed_b():
        p_b().wait()
        add_into(GP, p2, (0, x, y, c), 4)
        for k in (1, 2, 3):
            p_z(k).start()

    def packed_z():
        GP[0, 1 - x, y, c, z] = GP[0, x, y, c, z]
        for k in (1, 2, 3):
            p_z(k).wait()
            GP[0, 1 - x, y, c, z ^ k] = p3[k - 1]
        part = heads * HEAD_DIM
        for g in range(4):
            val = GP[0, 1 - x, y, c, g].astype(F32)
            for h in range(heads):
                spots = ((1, 2 * h), (2, 2 * h + 1), (0, 2 * heads + h))
                for t, i in spots:
                    lo = t * width + g * part + h * HEAD_DIM
                    out_p[:, :, lo : lo + HEAD_DIM] = val[:, :, i * HEAD_DIM : (i + 1) * HEAD_DIM]

    def v_copy(i):
        return rcopy(V.at[0:16], vr.at[i], vss.at[i], vrs.at[i], to[("core", "x", "y", "z1", "z2")[i]])

    def vec_start():
        part = heads * HEAD_DIM
        wide = 2 * part
        src = lax.broadcasted_iota(jnp.int32, (wide, 1), 0)
        dst = lax.broadcasted_iota(jnp.int32, (1, width), 1)
        head, lane = src // (2 * HEAD_DIM), src % (2 * HEAD_DIM)
        to_v = jnp.where(lane >= HEAD_DIM, z * part + head * HEAD_DIM + lane - HEAD_DIM, -1)
        V[3:4, :] = pick(V[16:17, :wide], jnp.where(to_v == dst, 1.0, 0.0).astype(BF))
        V[2:3, :] = pick(V[17:18, :part], jnp.where(z * part + src[:part] == dst, 1.0, 0.0).astype(BF))
        v_copy(0).start()

    def vec_step(i):
        v_copy(i).wait()
        V[0:16, :] = V[0:16, :] + vr[i]
        if i < 4:
            v_copy(i + 1).start()
        else:
            n_dev = 32
            small = width // n_dev
            d = (x * 4 + y * 2 + c) * 4 + z
            src = lax.broadcasted_iota(jnp.int32, (width, 1), 0)
            dst = lax.broadcasted_iota(jnp.int32, (1, 128), 1)
            hot = jnp.where(dst < small, d * small + dst, -1) == src
            out_v[0:16, :] = pick(V[0:16, :], jnp.where(hot, 1.0, 0.0).astype(BF))
            big = n_hid * small
            hot = jnp.where(dst < big, (d % (n_dev // n_hid)) * big + dst, -1) == src
            line = lax.broadcasted_iota(jnp.int32, (16, 128), 0)
            val = pick(V[0:16, :], jnp.where(hot, 1.0, 0.0).astype(BF))
            val = jnp.where(line == 8 + d // (n_dev // n_hid), val, 0.0)
            out_v[16:17, :] = jnp.sum(val, axis=0, keepdims=True)

    for t, fn in zip(TIMES["packed"], (packed, packed_core, packed_a, packed_b, packed_z)):
        ev.append((t_end + t, fn))
    for t, fn in zip(TIMES["vec"], [vec_start] + [functools.partial(vec_step, i) for i in range(5)]):
        ev.append((t_end + t, fn))

    ev.sort(key=lambda e: e[0])
    dense_body(
        tok, cot_in, cotx, mix, vec, hid, mx_h, ex_h, sh_h,
        base, upx, act, sin, cot, gpre, gres, gresf, send, s4, s5, s6, s7, s8,
        mx, ex, sh, down_out, down_in, wsem, dss, drs,
        lambda: [local(i).start() for i in range(len(late))],
        lambda: [fn() for t, fn in ev if t < 1.0],
    )
    for t, fn in ev:
        if 1.0 <= t < t_att:
            fn()

    def step(s, carry):
        for k in range(steps):
            here = [fn for t, fn in ev if t_att + k * t_step <= t < t_att + (k + 1) * t_step]
            if here:

                @pl.when(s == k)
                def _():
                    for fn in here:
                        fn()

        backward_step(s % heads, (s // heads) ^ (2 * y + zh), c, grad, mixed, lse, qt, kv, kt, dkv, dqt)
        return carry

    lax.fori_loop(0, steps, step, 0)
    for t, fn in ev:
        if t >= t_end:
            fn()


def backward_all(tok, cot, cotx, mix, vec, hid, mx, ex, sh, mixed, lse, qt, kv, kt, fi, nrm, pw):
    D, V, S = pltpu.SemaphoreType.DMA, pltpu.VMEM, jax.ShapeDtypeStruct
    heads, keys = kv.shape[0], kv.shape[1]
    images, shard, width = tok.shape
    rows, half = images * shard, ex.shape[1]
    blk = (3, 8, width)
    cols = pw.shape[1]
    pb = (3, 8, cols)
    send = (4 * images, width // 4, shard)
    outs = [S(tok.shape, BF), S((4,) + blk, F32), S((3, 8, 2 * half), F32), S(blk, F32), S(tok.shape, BF), S((3, 8, 4 * cols), F32), S((24, 128), F32)]
    scr = [V(mx.shape, BF), V(ex.shape, BF), V(sh.shape, BF), V(tok.shape, BF), V(tok.shape, BF)]
    scr += [V(tok.shape, F32), V(tok.shape, BF), V((2 * rows, half), BF), V((2 * rows, width), BF), V((2 * rows, width), BF), V((2 * rows, half), BF)]
    scr += [V((rows, width), BF), V(tok.shape, F32), V(send, BF)] + [V((1, width), F32)] * 4 + [V((1, 2 * half), F32)]
    scr += [D((1 + 2 * (half // width),)), D((2 * images,)), D((2 * images,))]
    scr += [V(t.shape, t.dtype) for t in (mixed, lse, qt, kv, kt, fi, nrm, pw)]
    scr += [D((8,)), V(send, BF), V((1, 2, 2, 2, 4) + blk, BF), V((1, 4, 4) + blk, BF), V((1, 2, 4) + blk, BF), V((1, 4) + blk, BF), V((1, 2) + blk, BF), V((1,) + blk, BF)]
    scr += [V((4, 2, 2, 4, 2) + blk, BF), V((4, 2, 4, 2) + blk, BF), V((4, 4, 2) + blk, BF), V((4, 2, 2) + blk, BF), V((4, 2) + blk, BF)]
    scr += [V((2,) + blk, F32), V((2,) + blk, BF), V((2,) + blk, BF), V(tok.shape, BF)]
    scr += [V((heads, keys, 2 * HEAD_DIM), F32), V((4, heads * HEAD_DIM, 256), BF), V((keys, cols), BF)]
    rowt = (64, width)
    scr += [V((2, 2, 4, 2) + rowt, BF), V((2, 4, 2) + rowt, BF), V((2, 2, 2) + rowt, BF), V((2, 2) + rowt, BF), V((2,) + rowt, BF), V((2,) + rowt, BF)]
    scr += [V((1, 2, 2, 2, 4) + pb, BF), V((4, 4) + pb, BF), V((2, 4) + pb, BF), V((4,) + pb, BF), V((3,) + pb, BF), V((24, width), F32), V((5, 16, width), F32)]
    for n in ((), (7,), (7,), (1, 10), (1, 10), (4, 9), (4, 9), (3,), (3,), (16,), (16,), (10,), (10,), (5,), (5,)):
        scr.append(D(n) if n else D)
    return pl.pallas_call(
        backward_kernel,
        out_shape=outs,
        in_specs=[VM] * 6 + [ANY] * 11,
        out_specs=[VM] * len(outs),
        scratch_shapes=scr,
        compiler_params=pltpu.CompilerParams(collective_id=2, has_side_effects=True, vmem_limit_bytes=63 << 20),
        name="dense_backward_reduce",
    )(tok, cot, cotx, mix, vec, hid, mx, ex, sh, mixed, lse, qt, kv, kt, fi, nrm, pw)


def backward_local_kernel(grad, mixed, lse, qt, kv, kt, out, dkv, dqt):
    _, _, c, _ = coords()
    heads, keys = kv.shape[0], kv.shape[1]
    wide = 2 * HEAD_DIM * heads
    dkv[...] = jnp.zeros_like(dkv)

    def step(s, carry):
        backward_step(s % heads, s // heads, c, grad, mixed, lse, qt, kv, kt, dkv, dqt)
        return carry

    lax.fori_loop(0, 4 * heads, step, 0)
    for g in range(8):
        rs = slice(g * 256, (g + 1) * 256)
        for h in range(heads):
            out[rs, 2 * h * HEAD_DIM : 2 * (h + 1) * HEAD_DIM] = dkv[h, rs, :].astype(BF)
        dq = dqt[(g // 4) * 2 + g % 2].astype(F32).T
        out[rs, wide:] = jnp.where((g // 2) % 2 == c, dq, 0.0).astype(BF)


def backward_local(grad, mixed, lse, qt, kv, kt):
    heads, keys = kv.shape[0], kv.shape[1]
    return pl.pallas_call(
        backward_local_kernel,
        out_shape=jax.ShapeDtypeStruct((keys, 3 * heads * HEAD_DIM), BF),
        in_specs=[VM] * 6,
        out_specs=VM,
        scratch_shapes=[pltpu.VMEM((heads, keys, 2 * HEAD_DIM), F32), pltpu.VMEM((4, heads * HEAD_DIM, 256), BF)],
        compiler_params=pltpu.CompilerParams(vmem_limit_bytes=50 << 20),
        name="attention_backward",
    )(grad, mixed, lse, qt, kv, kt)


def reduce_generic(gf, gp, gm, ge, gs, n_dev):
    every = ("dp", "ctx", "head")
    x, y, c, z = coords()
    flat = gf.reshape((1, -1) + gf.shape[-1:])
    both = jnp.concatenate([jnp.where(y == i, flat, jnp.zeros_like(flat)) for i in range(2)], axis=0)
    of = lax.psum_scatter(both.astype(F32), ("ctx", "head"), scatter_dimension=1, tiled=True)
    cols = gp.shape[-1]
    rows = gp.size // cols
    spread = lax.dynamic_update_slice_in_dim(jnp.zeros((rows, 4, cols), F32), gp.reshape(rows, 1, cols).astype(F32), z, 1)
    op = jnp.swapaxes(lax.psum_scatter(spread, every, scatter_dimension=0, tiled=True), 0, 1)
    rest = [
        lax.psum_scatter(g.reshape((n_dev, -1) + g.shape[-1:]).astype(F32), every, scatter_dimension=0, tiled=True)[0] for g in (gm, ge, gs)
    ]
    return [of, op] + rest


def layer_norm(token_rows, norm_gain, norm_shift):
    normed, inv_std = row_norm(token_rows)
    return (normed * norm_gain + norm_shift, normed, inv_std)


def norm_backward(grad_out, normed, inv_std, norm_gain):
    scaled = grad_out * norm_gain
    first_mean = jnp.mean(scaled, axis=-1, keepdims=True)
    second_mean = jnp.mean(scaled * normed, axis=-1, keepdims=True)
    return inv_std * (scaled - first_mean - normed * second_mean)


def gelu_parts(pre_act):
    cumulative = 0.5 * (1.0 + jax.scipy.special.erf(pre_act * (1.0 / math.sqrt(2.0))))
    density = jnp.exp(-0.5 * pre_act * pre_act) * (1.0 / math.sqrt(2.0 * math.pi))
    return pre_act * cumulative, cumulative + pre_act * density


def on_device(
    tokens,
    cotangent,
    lengths,
    attention_gain,
    attention_shift,
    packed_weight,
    query_bias,
    value_bias,
    mixer_weight,
    mixer_bias,
    feedforward_gain,
    feedforward_shift,
    expand_weight,
    expand_bias,
    shrink_weight,
    shrink_bias,
):
    images, shard_len, width = tokens.shape
    groups = lax.axis_size("head")
    heads = HEADS // groups
    part = heads * HEAD_DIM
    hidden = expand_weight.shape[1]
    rows = images * shard_len
    n_dev = lax.axis_size("dp") * lax.axis_size("ctx") * groups
    z = lax.axis_index("head")
    wr = packed_weight.shape[0]
    fr = shrink_weight.shape[0]

    tiled = wr % 8 == 0 and fr % 8 == 0 and lax.axis_size("dp") == 2
    slab = (lambda r, n: (r // 8, 8, n)) if tiled else (lambda r, n: (r, n))
    vecs = [attention_gain, attention_shift, query_bias, value_bias, mixer_bias, feedforward_gain, feedforward_shift, shrink_bias, expand_bias]
    mx, ex, sh = mixer_weight.reshape(slab(wr, width)), expand_weight.reshape(slab(wr, hidden)), shrink_weight.reshape(slab(fr, width))
    if tiled:
        mix, mixed_t, lse, fi, nrm, qt, kv, kt, full_packed, full_vecs, eb, mxo, exo, sho, cotx = forward_all(lengths, tokens, cotangent, packed_weight.reshape(slab(wr, 3 * width)), mx, ex, sh, vecs)
        hidden_bias = eb
    else:
        pk = jnp.stack([own_columns(packed_weight, g, part) for g in range(groups)])
        sv = jnp.stack([jnp.pad(v, (0, 128 - v.shape[0])) for v in vecs] + [jnp.zeros((128,), BF)] * 7)
        img, pko, mxo, exo, sho, svo = gather_generic(tokens, pk, mx, ex, sh, sv)
        full_packed = pko.reshape(width, 3 * part)
        svo = svo.reshape(n_dev, 16, 128).astype(F32)
        gain_one, shift_one, qb, vb, mb, gain_two, shift_two, sb = [svo[:, i, :wr].reshape(width) for i in range(8)]
        eb = svo[:, 8, :fr].reshape(hidden)
        own = lambda v: lax.dynamic_slice_in_dim(v, z * part, part)
        vb_own = own(vb).reshape(heads, 1, HEAD_DIM)
        bias = jnp.concatenate([jnp.concatenate([jnp.zeros_like(vb_own), vb_own], axis=1).reshape(2 * part), own(qb)])
        img = img.reshape(16, shard_len, width)
        mixed_t, lse, fi, nrm, qt, kv, kt = attention_forward(lengths, img, full_packed, gain_one[None], shift_one[None], bias[None])
        mix = exchange(mixed_t, 1)
    mix = mix.reshape(images, width, shard_len)
    full_mixer = mxo.reshape(width, width)
    full_expand = exo.reshape(width, -1)
    full_shrink = sho.reshape(-1, width)

    if tiled:
        ig, os_, oe, om, block_output, op, ov = backward_all(
            tokens, cotangent, cotx, mix, full_vecs, hidden_bias, full_mixer, full_expand, full_shrink, mixed_t, lse, qt, kv, kt, fi, nrm, full_packed
        )
        ig, os_, oe, om, block_output, op, *vec = hand_over([ig, os_, oe, om, block_output, op], ov, wr, fr)
        op = op.reshape(wr, 3 * width)
    else:
        token_rows = tokens.reshape(rows, width).astype(F32)
        mixed_rows = jnp.swapaxes(mix, 1, 2).reshape(rows, width)
        residual = token_rows + dot(mixed_rows, full_mixer) + mb
        second_out, second_normed, second_inv = layer_norm(residual, gain_two, shift_two)
        second_input = second_out.astype(BF)
        pre_act = dot(second_input, full_expand) + eb
        value, slope = gelu_parts(pre_act)
        activated = value.astype(BF)
        block_output = (residual + dot(activated, full_shrink) + sb).astype(BF)
        grad_in = cotangent.reshape(rows, width)
        grad_rows = grad_in.astype(F32)
        grad_shrink_b = jnp.sum(grad_rows, axis=0)
        grad_pre = jnp.einsum("rd,fd->rf", grad_in, full_shrink, preferred_element_type=F32) * slope
        grad_pre_bf = grad_pre.astype(BF)
        grad_expand_b = jnp.sum(grad_pre, axis=0)
        grad_second = jnp.einsum("rf,df->rd", grad_pre_bf, full_expand, preferred_element_type=F32)
        grad_gain_two = jnp.sum(grad_second * second_normed, axis=0)
        grad_shift_two = jnp.sum(grad_second, axis=0)
        grad_residual = grad_rows + norm_backward(grad_second, second_normed, second_inv, gain_two)
        grad_residual_bf = grad_residual.astype(BF)
        grad_mixer_b = jnp.sum(grad_residual, axis=0)
        grad_mixed = jnp.einsum("de,ire->idr", full_mixer, grad_residual_bf.reshape(images, shard_len, width), preferred_element_type=F32).astype(BF)
        grad_mixed = grad_mixed.reshape(images * groups, part, shard_len)
        grad_t = exchange(grad_mixed, 2)
        dqkv = backward_local(grad_t, mixed_t, lse, qt, kv, kt)
        grad_packed_w = jnp.einsum("rd,re->de", fi, dqkv, preferred_element_type=F32)
        grad_first_part = jnp.einsum("re,de->rd", dqkv, full_packed, preferred_element_type=F32)
        img_normed, _ = row_norm(img.reshape(16 * shard_len, width).astype(F32))
        dsum = jnp.sum(dqkv.astype(F32), axis=0)
        place = lambda v: lax.dynamic_update_slice_in_dim(jnp.zeros((width,), F32), v, z * part, 0)
        sums = [
            jnp.sum(grad_first_part * img_normed, axis=0),
            jnp.sum(grad_first_part, axis=0),
            place(dsum[2 * part :]),
            place(dsum[: 2 * part].reshape(heads, 2, HEAD_DIM)[:, 1].reshape(part)),
            grad_mixer_b,
            grad_gain_two,
            grad_shift_two,
            grad_shrink_b,
            grad_expand_b,
        ]
        vec = [lax.psum_scatter(t, ("dp", "ctx", "head"), scatter_dimension=0, tiled=True) for t in sums]
        of, op, om, oe, os_ = reduce_generic(
            grad_first_part.reshape(2, 2, groups, shard_len, width),
            grad_packed_w,
            jnp.einsum("rd,re->de", mixed_rows, grad_residual_bf, preferred_element_type=F32),
            jnp.einsum("rd,rf->df", second_input, grad_pre_bf, preferred_element_type=F32),
            jnp.einsum("rf,rd->fd", activated, grad_in, preferred_element_type=F32),
            n_dev,
        )
        op = op.reshape(groups, wr, 3 * part)
        okv = jnp.transpose(op[:, :, : 2 * part].reshape(groups, wr, heads, 2, HEAD_DIM), (1, 3, 0, 2, 4)).reshape(wr, 2 * width)
        op = jnp.concatenate([jnp.transpose(op[:, :, 2 * part :], (1, 0, 2)).reshape(wr, width), okv], axis=1)
        _, first_normed, first_inv = layer_norm(token_rows, gain_one, shift_one)
        ig = (grad_residual + norm_backward(of.reshape(rows, width), first_normed, first_inv, gain_one)).astype(BF)
    return (
        block_output.reshape(images, shard_len, width),
        ig.reshape(images, shard_len, width),
        vec[0],
        vec[1],
        op,
        vec[2],
        vec[3],
        om.reshape(wr, width),
        vec[4],
        vec[5],
        vec[6],
        oe.reshape(wr, hidden),
        vec[8],
        os_.reshape(fr, width),
        vec[7],
    )


def solution(mesh):
    every = ("dp", "ctx", "head")
    tok, vec, mat = P("dp", ("ctx", "head"), None), P(every), P(every, None)
    in_specs = (tok, tok, P("dp"), vec, vec, mat, vec, vec, mat, vec, vec, vec, mat, vec, mat, vec)
    out_specs = (tok, tok, vec, vec, mat, vec, vec, mat, vec, vec, vec, mat, vec, mat, vec)
    return jax.shard_map(on_device, mesh=mesh, in_specs=in_specs, out_specs=out_specs, check_vma=False)
```

```python
import functools
import math

import jax
import jax.numpy as jnp
from jax import lax
from jax.experimental import pallas as pl
from jax.experimental.pallas import tpu as pltpu
from jax.sharding import PartitionSpec as P

HEADS = 12
HEAD_DIM = 64
NORM_EPS = 1e-06
MASKED = -1e30
LOG2E = 1.4426950408889634
MESH = pl.DeviceIdType.MESH
ANY = pl.BlockSpec(memory_space=pl.ANY)
VM = pl.BlockSpec(memory_space=pltpu.VMEM)
SM = pl.BlockSpec(memory_space=pltpu.SMEM)
BF = jnp.bfloat16
F32 = jnp.float32
SPLIT = 2


def coords():
    ctx = lax.axis_index("ctx")
    return lax.axis_index("dp"), ctx // SPLIT, ctx % SPLIT, lax.axis_index("head")


def device(x, y, c, z):
    return (x, y * SPLIT + c, z)


def enter(targets):
    sem = pltpu.get_barrier_semaphore()
    for t in targets:
        pl.semaphore_signal(sem, inc=1, device_id=t, device_id_type=MESH)
    pl.semaphore_wait(sem, len(targets))


def rcopy(src, dst, ss, rs, to):
    return pltpu.make_async_remote_copy(src, dst, ss, rs, device_id=to, device_id_type=MESH)


def run_events(events):
    for _, fn in sorted(events, key=lambda e: e[0]):
        fn()


def partners(x, y, c, z):
    return dict(
        core=device(x, y, 1 - c, z),
        x=device(1 - x, y, c, z),
        y=device(x, 1 - y, c, z),
        z1=device(x, y, c, z ^ 1),
        z2=device(x, y, c, z ^ 2),
        z3=device(x, y, c, z ^ 3),
    )


def weight_gather(ev, co, to, src, out, sems, order, times):
    x, y, c, z = co
    lsem, zss, zrs, ass, ars, bss, brs, css, crs = sems
    a, b = order

    def spot(fa, fb):
        px = (1 - x if fa else x) if a == "x" else (1 - x if fb else x)
        py = (1 - y if fa else y) if a == "y" else (1 - y if fb else y)
        return px, py

    def at(fa, fb, k):
        return out(*spot(fa, fb), c, z ^ k)

    def group(fa, fb, cc):
        return out(*spot(fa, fb), cc, slice(None))

    F, T = False, True
    zsend = lambda i, k, ref, dst, name: rcopy(ref, dst, zss.at[i], zrs.at[k], to[name])
    asend = lambda k, ref: rcopy(ref, at(F, F, k), ass.at[k], ars.at[k], to[a])
    bsend = lambda fa, k, ref: rcopy(ref, at(fa, F, k), bss.at[int(fa), k], brs.at[int(fa), k], to[b])
    csend = lambda i, g: rcopy(g, g, css.at[i], crs.at[i], to["core"])
    local = lambda: pltpu.make_async_copy(src, at(F, F, 0), lsem)

    def begin():
        local().start()
        asend(0, src).start()
        bsend(F, 0, src).start()

    def z_begin():
        zsend(0, 0, src, at(F, F, 0), "z1").start()
        zsend(1, 1, src, at(F, F, 0), "z2").start()

    def z_land(k):
        d = at(F, F, k)
        zsend(k - 1, k - 1, d, d, "z1").wait_recv()
        if k == 2:
            zsend(2, 2, d, d, "z1").start()
        asend(k, d).start()
        bsend(F, k, d).start()

    def own_done():
        local().wait()
        csend(0, group(F, F, c)).start()

    def a_land(k):
        d = at(T, F, k)
        asend(k, d).wait_recv()
        bsend(T, k, d).start()
        if k == 3:
            csend(1, group(T, F, c)).start()

    def b_land(fa):
        for k in range(4):
            bsend(fa, k, at(fa, T, k)).wait_recv()
        csend(2 + int(fa), group(fa, T, c)).start()

    def last():
        d = at(F, F, 0)
        for i in range(3):
            zsend(i, 0, d, d, "z1").wait_send()
        for k in range(4):
            asend(k, d).wait_send()
            bsend(F, k, d).wait_send()
            bsend(T, k, d).wait_send()
        for i, (fa, fb) in enumerate(((F, F), (T, F), (F, T), (T, T))):
            csend(i, group(fa, fb, 1 - c)).wait()

    t_begin, t_z, t_zl, t_al, t_bl = times
    ev.append((t_begin, begin))
    ev.append((t_z, z_begin))
    for k in range(1, 4):
        ev.append((t_zl[k - 1], functools.partial(z_land, k)))
    ev.append((t_zl[2] + 0.3, own_done))
    for k in range(4):
        ev.append((t_al[k], functools.partial(a_land, k)))
    ev.append((t_bl[0], functools.partial(b_land, F)))
    ev.append((t_bl[1], functools.partial(b_land, T)))
    ev.append((1000.0, last))


def half_gather(ev, co, to, prepare, settle, own, view, sems, times):
    x, y, c, z = co
    zss, zrs, yss, yrs, css, crs = sems
    at = lambda k: view(y, c, z ^ k)
    zsend = lambda i, k, ref, dst, name: rcopy(ref, dst, zss.at[i], zrs.at[k], to[name])
    ysend = lambda k, ref: rcopy(ref, at(k), yss.at[k], yrs.at[k], to["y"])

    def csend(i):
        g = view(y if i == 0 else 1 - y, c, slice(None))
        return rcopy(g, g, css.at[i], crs.at[i], to["core"])

    def begin():
        prepare()
        ysend(0, own).start()

    def z_begin():
        zsend(0, 0, own, at(0), "z1").start()
        zsend(1, 1, own, at(0), "z2").start()

    def z_land(k):
        d = at(k)
        zsend(k - 1, k - 1, d, d, "z1").wait_recv()
        if k == 2:
            zsend(2, 2, d, d, "z1").start()
        ysend(k, d).start()
        if k == 3:
            settle()
            csend(0).start()

    def y_land():
        for k in range(4):
            d = view(1 - y, c, z ^ k)
            rcopy(d, d, yss.at[k], yrs.at[k], to["y"]).wait_recv()
        csend(1).start()

    def last():
        d = at(0)
        for i in range(3):
            zsend(i, 0, d, d, "z1").wait_send()
        for k in range(4):
            ysend(k, d).wait_send()
        for i in range(2):
            csend(i).wait()

    t_begin, t_z, t_zl, t_y = times
    ev.append((t_begin, begin))
    ev.append((t_z, z_begin))
    for k in range(1, 4):
        ev.append((t_zl[k - 1], functools.partial(z_land, k)))
    ev.append((t_y, y_land))
    ev.append((1000.5, last))


def small_gather(co, to, src, out, ls, ss, rs, spread):
    x, y, c, z = co
    own = src.at[z] if spread else src

    def begin():
        pltpu.make_async_copy(own, out.at[x, y, c, z], ls).start()
        for k in (1, 2, 3):
            rcopy(src.at[z ^ k] if spread else src, out.at[x, y, c, z], ss.at[k - 1], rs.at[k - 1], to["z%d" % k]).start()

    def step_y():
        pltpu.make_async_copy(own, out.at[x, y, c, z], ls).wait()
        for k in (1, 2, 3):
            d = out.at[x, y, c, z ^ k]
            rcopy(d, d, ss.at[k - 1], rs.at[k - 1], to["z1"]).wait()
        g = out.at[x, y, c]
        rcopy(g, g, ss.at[3], rs.at[3], to["y"]).start()

    def step_x():
        g = out.at[x, 1 - y, c]
        rcopy(g, g, ss.at[3], rs.at[3], to["y"]).wait()
        for yy in range(2):
            g = out.at[x, yy, c]
            rcopy(g, g, ss.at[4 + yy], rs.at[4 + yy], to["x"]).start()

    def step_c():
        for yy in range(2):
            g = out.at[1 - x, yy, c]
            rcopy(g, g, ss.at[4 + yy], rs.at[4 + yy], to["x"]).wait()
        for xx in range(2):
            for yy in range(2):
                g = out.at[xx, yy, c]
                rcopy(g, g, ss.at[6 + 2 * xx + yy], rs.at[6 + 2 * xx + yy], to["core"]).start()

    def last():
        for xx in range(2):
            for yy in range(2):
                g = out.at[xx, yy, 1 - c]
                rcopy(g, g, ss.at[6 + 2 * xx + yy], rs.at[6 + 2 * xx + yy], to["core"]).wait()

    return begin, step_y, step_x, step_c, last


def gather_generic(tok, pk, mx, ex, sh, sv):
    every = ("dp", "ctx", "head")
    images = lax.all_gather(tok, ("ctx", "head"), axis=1, tiled=True)
    img = lax.dynamic_index_in_dim(images, coords()[1], 0, keepdims=False)
    spread = lax.all_gather(pk, every, axis=1, tiled=True)
    pko = lax.dynamic_index_in_dim(spread, lax.axis_index("head"), 0, keepdims=False)
    return [img, pko] + [lax.all_gather(t, every, axis=0, tiled=True) for t in (mx, ex, sh, sv)]


def exchange_kernel(src, dst, ls, ss, rs):
    x, y, c, z = coords()
    others = [(dy, dz) for dy in range(2) for dz in range(4) if dy or dz]
    enter([device(x, y ^ dy, c, z ^ dz) for dy, dz in others])
    me = y * 4 + z
    mine = pltpu.make_async_copy(src.at[me], dst.at[me], ls)
    mine.start()
    copies = []
    for i, (dy, dz) in enumerate(others):
        ty, tz = y ^ dy, z ^ dz
        cp = rcopy(src.at[ty * 4 + tz], dst.at[me], ss.at[i], rs.at[i], device(x, ty, c, tz))
        cp.start()
        copies.append(cp)
    mine.wait()
    for cp in copies:
        cp.wait()


def exchange(src, cid):
    D = pltpu.SemaphoreType.DMA
    return pl.pallas_call(
        exchange_kernel,
        out_shape=jax.ShapeDtypeStruct(src.shape, src.dtype),
        in_specs=[ANY],
        out_specs=ANY,
        scratch_shapes=[D, D((7,)), D((7,))],
        compiler_params=pltpu.CompilerParams(collective_id=cid, has_side_effects=True),
        name="exchange_heads_%d" % cid,
    )(src)


def dot(a, b):
    return jnp.dot(a, b, preferred_element_type=F32)


def dot_nt(a, b):
    return lax.dot_general(a, b, (((1,), (1,)), ((), ())), preferred_element_type=F32)


def row_norm(rows):
    mean = jnp.mean(rows, axis=-1, keepdims=True)
    centred = rows - mean
    inv = lax.rsqrt(jnp.mean(centred * centred, axis=-1, keepdims=True) + NORM_EPS)
    return centred * inv, inv


def project(g, rows, length, gain, shift, bias, pw, fi, nrm, qt, kv, kt, vt):
    heads = kv.shape[0]
    hd, step = HEAD_DIM, 256
    wide = 2 * hd * heads
    normed, _ = row_norm(rows.astype(F32))
    first = (normed * gain + shift).astype(BF)
    off = pl.multiple_of(g * step, step)
    fi[pl.ds(off, step), :] = first
    nrm[pl.ds(off, step), :] = normed.astype(BF)
    kvq = (dot(first, pw[...]) + bias).astype(BF).astype(F32)
    flip = kvq.T
    ones = jnp.where(lax.broadcasted_iota(jnp.int32, (16, step), 0) == 0, 1.0, 0.0)
    pos = off + lax.broadcasted_iota(jnp.int32, (step, 2 * hd), 0)
    lane = lax.broadcasted_iota(jnp.int32, (step, 2 * hd), 1)
    extra = jnp.where(lane == 0, jnp.where(pos < length, 0.0, MASKED), jnp.where(lane < 4, 1.0, 0.0)).astype(BF)
    for h in range(heads):
        kt[h, g] = flip[2 * h * hd : (2 * h + 1) * hd].astype(BF)
        vt[h, g] = jnp.concatenate([flip[(2 * h + 1) * hd : (2 * h + 2) * hd], ones], axis=0).astype(BF)
        qt[g, h] = (flip[wide + h * hd : wide + (h + 1) * hd] * (1.0 / math.sqrt(hd))).astype(BF)
        kv[h, pl.ds(off, step), : 2 * hd] = kvq[:, 2 * h * hd : (2 * h + 2) * hd].astype(BF)
        kv[h, pl.ds(off, step), 2 * hd :] = extra


def attend(h, j, c, qt, kv, vt, mixed, lse):
    keys = kv.shape[1]
    hd, step, chunk = HEAD_DIM, 256, 512
    per = chunk // step
    row = lax.broadcasted_iota(jnp.int32, (16, step), 0)
    unit = jnp.where(row == 0, 1.0, 0.0).astype(BF)
    g = (j // 2) * 4 + c * 2 + j % 2
    sl = pl.ds(pl.multiple_of(h * hd, hd), hd)
    qa = jnp.concatenate([qt[g, h], jnp.zeros((hd, step), BF), unit, jnp.zeros((2 * hd - 16, step), BF)], axis=0)
    top = jnp.full((1, step), MASKED, F32)
    acc = jnp.zeros((hd + 16, step), F32)
    for kc in range(keys // chunk):
        s = dot(kv[h, kc * chunk : (kc + 1) * chunk, :], qa)
        new = jnp.maximum(top, jnp.max(s, axis=0, keepdims=True))
        pb = jnp.exp2((s - new) * LOG2E).astype(BF)
        scale = jnp.exp2((top - new) * LOG2E)
        part = dot(vt[h, kc * per], pb[:step])
        for i in range(1, per):
            part += dot(vt[h, kc * per + i], pb[i * step : (i + 1) * step])
        acc = acc * scale + part
        top = new
    total = acc[hd : hd + 1]
    out = acc[:hd] / total
    lse[j, h] = top + jnp.log(total)
    for i in range(2):
        mixed[2 * j + i, sl, :] = out[:, i * 128 : (i + 1) * 128].astype(BF)


def forward_kernel(lens, img, pw, gain, shift, bias, mixed, lse, fi, nrm, qt, kv, kt, vt):
    x, y, c, z = coords()
    heads, keys = kv.shape[0], kv.shape[1]
    length = lens[y]

    def rows_of(g, carry):
        rows = img[pl.ds(2 * g, 2)].reshape(256, img.shape[2])
        project(g, rows, length, gain[...], shift[...], bias[...], pw, fi, nrm, qt, kv, kt, vt)
        return carry

    def step(s, carry):
        attend(s % heads, s // heads, c, qt, kv, vt, mixed, lse)
        return carry

    lax.fori_loop(0, keys // 256, rows_of, 0)
    lax.fori_loop(0, 4 * heads, step, 0)


FT = dict(
    small=(0.0, 4.6, 12.3, 15.5, 18.4),
    tok=((0.1, 12.0, 12.1, 24.0), (4.8, 18.9, 19.0, 27.0)),
    mx=(5.5, 12.2, (24.2, 24.3, 29.0), (18.8, 33.0, 36.0, 40.0), (46.0, 50.5)),
    ex=(5.4, 34.0, (44.5, 44.6, 51.0), 57.0),
    sh=(5.3, 28.01, (38.5, 38.6, 46.5), 54.5),
    att=(30.0, 1.95),
)


def own_columns(rows, g, part):
    width = rows.shape[1] // 3
    at = lambda t, h: rows[:, t * width + g * part + h * HEAD_DIM : t * width + g * part + (h + 1) * HEAD_DIM]
    heads = part // HEAD_DIM
    return jnp.concatenate([at(t, h) for h in range(heads) for t in (1, 2)] + [at(0, h) for h in range(heads)], axis=1)


def forward_all_kernel(
    lens, tok, cot, pkw, mx, ex, sh, v0, v1, v2, v3, v4, v5, v6, v7, v8,
    mix, mixed_o, lse_o, fi_o, nrm_o, qt_o, kv_o, kt_o, pw_o, vec, hid, mxo, exo, sho, cotx,
    pk, sv, img, pwg, svg, mixed, lse, fi, nrm, qt, kv, kt, vt, pw, bias,
    ls, tys, tzs, tzr, tcs, tcr, ps, pr, vs, vr, xs, xr, xl, osem, xps, xpr, *wsems,
):
    co = coords()
    x, y, c, z = co
    to = partners(*co)
    zh = z // 2
    heads, keys = kv.shape[0], kv.shape[1]
    width = img.shape[4]
    n_dev = 32
    others = [(dy, dz) for dy in range(2) for dz in range(4) if dy or dz]
    part = heads * HEAD_DIM
    enter([to["core"], to["x"]] + [device(x, y ^ dy, c, z ^ dz) for dy, dz in others])
    length = lens[y]
    ev = []

    def arrange():
        raw = pkw[...].astype(F32).reshape(3 * 8, pkw.shape[2])
        for g in range(4):
            pk[g] = own_columns(raw, g, part).astype(BF).reshape(3, 8, 3 * part)
        vs_ = (v0, v1, v2, v3, v4, v5, v6, v7, v8)
        lines = [jnp.concatenate([v[...].astype(F32).reshape(1, -1), jnp.zeros((1, 128 - v.shape[-1]), F32)], axis=1) for v in vs_]
        sv[...] = jnp.concatenate(lines + [jnp.zeros((7, 128), F32)], axis=0).astype(BF)

    ev.append((-0.1, arrange))

    row = lambda r: y if r == 0 else 1 - y

    def tz(r, i, k, ref, dst, name):
        return rcopy(ref, dst, tzs.at[r, i], tzr.at[r, k], to[name])

    def tcore(r, k, ref):
        return rcopy(ref, img.at[row(r), c, z ^ k], tcs.at[r, k], tcr.at[r, k], to["core"])

    spread = lambda: rcopy(tok.at[1 - y], img.at[y, c, z], tys.at[0], tys.at[1], to["y"])
    keep = lambda: pltpu.make_async_copy(tok.at[y], img.at[y, c, z], ls.at[0])

    def t_begin(r):
        d = img.at[row(r), c, z]
        if r == 0:
            spread().start()
            keep().start()
            own = tok.at[y]
        else:
            rcopy(d, d, tys.at[0], tys.at[1], to["y"]).wait()
            own = d
        tz(r, 0, 0, own, d, "z1").start()
        tz(r, 1, 1, own, d, "z2").start()
        tcore(r, 0, own).start()

    def t_land(r, k):
        d = img.at[row(r), c, z ^ k]
        tz(r, k - 1, k - 1, d, d, "z1").wait_recv()
        if k == 2:
            tz(r, 2, 2, d, d, "z1").start()
        tcore(r, k, d).start()

    for r in range(2):
        t = FT["tok"][r]
        ev.append((t[0], functools.partial(t_begin, r)))
        for k in range(1, 4):
            ev.append((t[k], functools.partial(t_land, r, k)))

    def t_last():
        for r in range(2):
            d = img.at[row(r), c, z]
            for i in range(3):
                tz(r, i, 0, d, d, "z1").wait_send()
            for k in range(4):
                tcore(r, k, d).wait_send()

    ev.append((1001.0, t_last))

    steps_v = small_gather(co, to, sv, svg, ls.at[1], vs, vr, False)
    steps_p = small_gather(co, to, pk, pwg, ls.at[4], ps, pr, True)
    for t, fv, fp in zip(FT["small"], steps_v, steps_p):
        ev.append((t, fv))
        ev.append((t + 0.05, fp))

    def unpack():
        small = width // n_dev
        big = hid.shape[1] // n_dev
        part = heads * HEAD_DIM
        across = lambda n: lax.broadcasted_iota(jnp.int32, (1, n), 1)
        down = lambda n: lax.broadcasted_iota(jnp.int32, (n, 1), 0)
        hot = lambda m: jnp.where(m, 1.0, 0.0).astype(BF)
        col = across(width)
        val = dot(svg[...].reshape(n_dev * 16, 128), hot(col % small == down(128)))
        val = jnp.where(col // small == down(n_dev * 16) // 16, val, 0.0)
        val = jnp.sum(val.reshape(n_dev, 16, width), axis=0)
        vec[...] = val
        col = across(hid.shape[1])
        eight = svg[...].astype(F32).reshape(n_dev, 16, 128)[:, 8, :].astype(BF)
        line = dot(eight, hot(col % big == down(128)))
        hid[...] = jnp.sum(jnp.where(col // big == down(n_dev), line, 0.0), axis=0, keepdims=True)
        dst = across(3 * part)
        head, off = dst // (2 * HEAD_DIM), dst % (2 * HEAD_DIM)
        hv = jnp.where(jnp.logical_and(dst < 2 * part, off >= HEAD_DIM), z * part + head * HEAD_DIM + off - HEAD_DIM, -1)
        hq = jnp.where(dst >= 2 * part, z * part + dst - 2 * part, -1)
        rows = val.astype(BF)
        bq = dot(rows, hot(hq == down(width)))
        bv = dot(rows, hot(hv == down(width)))
        bias[...] = bq[2:3] + bv[3:4]

    def flatten():
        def body(i, carry):
            blk = pwg[i // 4, (i // 2) % 2, i % 2].astype(F32)
            n = blk.shape[0] * blk.shape[1] * blk.shape[2]
            pw[pl.ds(pl.multiple_of(i * n, n), n), :] = blk.reshape(n, blk.shape[3]).astype(BF)
            return carry

        lax.fori_loop(0, 8, body, 0)

    ev.append((FT["small"][4] + 0.1, unpack))
    ev.append((FT["small"][4] + 0.2, flatten))

    def project_group(r, mine, p):
        cc = c if mine else 1 - c
        zz = zh if p == 0 else 1 - zh
        if r == 0 and mine and p == 0:
            keep().wait()
        if not mine:
            for k in (2 * p, 2 * p + 1):
                d = img.at[row(r), cc, z ^ k]
                rcopy(d, d, tcs.at[r, k], tcr.at[r, k], to["core"]).wait_recv()
        g = row(r) * 4 + cc * 2 + zz
        rows = img[row(r), cc, pl.ds(2 * zz, 2)].reshape(256, width)
        project(g, rows, length, vec[0:1, :], vec[1:2, :], bias[...], pw, fi, nrm, qt, kv, kt, vt)

    t_ready = FT["small"][4] + 0.3
    for p in range(2):
        for r in range(2):
            for mine in (True, False):
                t = max(FT["tok"][r][1 if p == 0 else 3] + (0.3 if mine else 0.6), t_ready + 0.01 * (r * 2 + (not mine)))
                ev.append((t, functools.partial(project_group, r, mine, p)))

    weight_gather(ev, co, to, mx, lambda px, py, cc, zz: mxo.at[px, py, cc, zz], wsems[:9], "yx", FT["mx"])
    half = ex.shape[2] // 2
    cols = lambda xx: pl.ds(pl.multiple_of(xx * half, half), half)
    ex_view = lambda yy, cc, zz: exo.at[:, yy, cc, zz]
    sh_view = lambda yy, cc, zz: sho.at[yy, cc, zz]
    ex_own = lambda: pltpu.make_async_copy(ex.at[:, :, cols(x)], exo.at[x, y, c, z], ls.at[2])
    ex_swap = lambda: rcopy(ex.at[:, :, cols(1 - x)], exo.at[x, y, c, z], xps.at[0], xpr.at[0], to["x"])
    sh_own = lambda: pltpu.make_async_copy(sh, sho.at[y, c, z], ls.at[3])
    cot_swap = lambda: rcopy(cot, cotx, xps.at[1], xpr.at[1], to["x"])

    def swap():
        ex_own().start()
        ex_swap().start()
        cot_swap().start()

    def ex_ready():
        ex_own().wait()
        ex_swap().wait()

    ev.append((0.6, swap))
    ev.append((1003.0, lambda: cot_swap().wait()))
    half_gather(ev, co, to, ex_ready, lambda: None, ex_view(y, c, z), ex_view, wsems[9:15], FT["ex"])
    half_gather(ev, co, to, lambda: sh_own().start(), lambda: sh_own().wait(), sh, sh_view, wsems[15:21], FT["sh"])

    stored = [(fi, fi_o), (nrm, nrm_o), (qt, qt_o), (kv, kv_o), (kt, kt_o), (pw, pw_o), (mixed, mixed_o), (lse, lse_o)]
    store = lambda i: pltpu.make_async_copy(stored[i][0], stored[i][1], osem.at[i])

    def store_first():
        for i in range(6):
            store(i).start()

    t_att, t_step = FT["att"]
    steps = 4 * heads
    t_end = t_att + steps * t_step
    ev.append((t_att + 0.001, store_first))

    me = y * 4 + z

    def target(q):
        w = 3 - q
        return [(w // 2, 2 * (w % 2)), (w // 2, 2 * (w % 2) + 1)]

    def xcopy(dy, dz):
        i = dy * 4 + dz
        return rcopy(mixed.at[(y ^ dy) * 4 + (z ^ dz)], mix.at[me], xs.at[i], xr.at[i], device(x, y ^ dy, c, z ^ dz))

    mine_copy = lambda: pltpu.make_async_copy(mixed.at[me], mix.at[me], xl)

    def send_group(q):
        for dy, dz in target(q):
            if dy or dz:
                xcopy(dy, dz).start()
            else:
                mine_copy().start()

    for q in range(4):
        ev.append((t_att + (q + 1) * heads * t_step + 0.002, functools.partial(send_group, q)))

    def finish():
        store(6).start()
        store(7).start()
        for dy, dz in others:
            xcopy(dy, dz).wait()
        mine_copy().wait()

    ev.append((t_end + 3.8, finish))

    def drain():
        for i in range(8):
            store(i).wait()

    ev.append((1002.0, drain))

    ev.sort(key=lambda e: e[0])
    for t, fn in ev:
        if t < t_att:
            fn()

    def step(s, carry):
        for k in range(steps):
            here = [fn for t, fn in ev if t_att + k * t_step <= t < t_att + (k + 1) * t_step]
            if here:

                @pl.when(s == k)
                def _():
                    for fn in here:
                        fn()

        attend(s % heads, (3 - s // heads) ^ (2 * y + zh), c, qt, kv, vt, mixed, lse)
        return carry

    lax.fori_loop(0, steps, step, 0)
    for t, fn in ev:
        if t >= t_end:
            fn()


def forward_all(lens, tok, cot, pkw, mx, ex, sh, vecs):
    D, V, S = pltpu.SemaphoreType.DMA, pltpu.VMEM, jax.ShapeDtypeStruct
    shard, width = tok.shape[1], tok.shape[2]
    cols = pkw.shape[2] // 4
    pk_shape = (3, 8, cols)
    heads = cols // (3 * HEAD_DIM)
    keys = 16 * shard
    n = keys // 256
    lead = (2, SPLIT, SPLIT, 4)
    part = heads * HEAD_DIM
    hidden = ex.shape[2]
    outs = [
        S((8, part, shard), BF),
        S((8, part, shard), BF),
        S((4, heads, 1, 256), F32),
        S((keys, width), BF),
        S((keys, width), BF),
        S((n, heads, HEAD_DIM, 256), BF),
        S((heads, keys, 4 * HEAD_DIM), BF),
        S((heads, n, HEAD_DIM, 256), BF),
        S((width, cols), BF),
        S((16, width), F32),
        S((1, hidden), F32),
        S(lead + mx.shape, BF),
        S(lead + (3, 8, hidden // 2), BF),
        S(lead[1:] + sh.shape, BF),
        S(cot.shape, BF),
    ]
    wsem = [D, D((3,)), D((3,)), D((4,)), D((4,)), D((2, 4)), D((2, 4)), D((4,)), D((4,))]
    wsem += [D((3,)), D((3,)), D((4,)), D((4,)), D((2,)), D((2,))] * 2
    scr = [V((4,) + pk_shape, BF), V((16, 128), BF)]
    scr += [V((2, 2, 4) + tok.shape[1:], BF), V(lead + pk_shape, BF), V(lead + (16, 128), BF), V((8, part, shard), BF), V((4, heads, 1, 256), F32)]
    scr += [V((keys, width), BF), V((keys, width), BF), V((n, heads, HEAD_DIM, 256), BF), V((heads, keys, 4 * HEAD_DIM), BF)]
    scr += [V((heads, n, HEAD_DIM, 256), BF), V((heads, n, HEAD_DIM + 16, 256), BF), V((width, cols), BF), V((1, cols), F32)]
    scr += [D((5,)), D((2,)), D((2, 3)), D((2, 3)), D((2, 4)), D((2, 4)), D((10,)), D((10,)), D((10,)), D((10,)), D((8,)), D((8,)), D, D((8,)), D((2,)), D((2,))]
    return pl.pallas_call(
        forward_all_kernel,
        out_shape=outs,
        in_specs=[SM, ANY, ANY, VM, ANY, ANY, ANY] + [VM] * 9,
        out_specs=[ANY] * 9 + [VM] * 2 + [ANY] * 4,
        scratch_shapes=scr + wsem,
        compiler_params=pltpu.CompilerParams(collective_id=0, has_side_effects=True, vmem_limit_bytes=62 << 20),
        name="gather_attention_forward",
    )(lens, tok, cot, pkw, mx, ex, sh, *vecs)


def attention_forward(lens, img, pw, gain, shift, bias):
    heads = pw.shape[1] // (3 * HEAD_DIM)
    keys = img.shape[0] * img.shape[1]
    width = heads * HEAD_DIM
    n = keys // 256
    outs = [
        jax.ShapeDtypeStruct((8, width, 128), BF),
        jax.ShapeDtypeStruct((4, heads, 1, 256), F32),
        jax.ShapeDtypeStruct((keys, img.shape[2]), BF),
        jax.ShapeDtypeStruct((keys, img.shape[2]), BF),
        jax.ShapeDtypeStruct((n, heads, HEAD_DIM, 256), BF),
        jax.ShapeDtypeStruct((heads, keys, 4 * HEAD_DIM), BF),
        jax.ShapeDtypeStruct((heads, n, HEAD_DIM, 256), BF),
    ]
    return pl.pallas_call(
        forward_kernel,
        out_shape=outs,
        in_specs=[SM] + [VM] * 5,
        out_specs=[VM] * 7,
        scratch_shapes=[pltpu.VMEM((heads, n, HEAD_DIM + 16, 256), BF)],
        compiler_params=pltpu.CompilerParams(vmem_limit_bytes=50 << 20),
        name="attention_forward",
    )(lens, img, pw, gain, shift, bias)


def dot_tn(a, b):
    return lax.dot_general(a, b, (((0,), (0,)), ((), ())), preferred_element_type=F32)


def dense_body(
    tok, cot, cotx, mix, vec, hid, mx_h, ex_h, sh_h,
    base, upx, act, sin, cot2, gpre, gres, gresf, send, s4, s5, s6, s7, s8,
    mx, ex, sh, down_out, down_in, sems, ss, rs, then, early,
):
    co = coords()
    x = co[0]
    to = partners(*co)["x"]
    images, shard, width = tok.shape
    rows = images * shard
    half = ex.shape[1]
    n = half // width
    load = [pltpu.make_async_copy(mx_h, mx, sems.at[0])]
    for i in range(n):
        cols = slice(i * width, (i + 1) * width)
        load.append(pltpu.make_async_copy(ex_h.at[:, cols], ex.at[:, cols], sems.at[1 + i]))
        load.append(pltpu.make_async_copy(sh_h.at[cols, :], sh.at[cols, :], sems.at[1 + n + i]))
    for cp in load:
        cp.start()
    cin = cot[...].reshape(rows, width)
    cf = cin.astype(F32)
    s7[...] = jnp.sum(cf, axis=0, keepdims=True)
    cot2[:rows, :] = cin
    cot2[rows:, :] = cotx[...].reshape(rows, width)

    def sin_copy(i):
        return rcopy(sin.at[i * shard : (i + 1) * shard], sin.at[rows + i * shard : rows + (i + 1) * shard], ss.at[i], rs.at[i], to)

    def down_copy(i):
        return rcopy(down_out.at[i], down_in.at[i], ss.at[images + i], rs.at[images + i], to)

    load[0].wait()
    keep = []
    for i in range(images):
        res = tok[i].astype(F32) + dot_tn(mix[i], mx[...]) + vec[4:5, :]
        nr, iv = row_norm(res)
        sin[i * shard : (i + 1) * shard, :] = (nr * vec[5:6, :] + vec[6:7, :]).astype(BF)
        sin_copy(i).start()
        keep.append((res, nr, iv))
    residual, normed, inv = [jnp.concatenate(t, axis=0) for t in zip(*keep)]
    own = pl.ds(pl.multiple_of(x * half, half), half)
    s8[...] = jnp.zeros_like(s8)

    def chunks(lo, hi):
        up = jnp.zeros((hi - lo, width), F32)
        down = jnp.zeros((hi - lo, width), F32)
        second = sin[lo:hi, :]
        grad = cot2[lo:hi, :]
        for i in range(n):
            cols = slice(i * width, (i + 1) * width)
            if lo == 0:
                load[1 + 2 * i].wait()
                load[2 + 2 * i].wait()
            there = pl.ds(pl.multiple_of(x * half + i * width, width), width)
            pre = dot(second, ex[:, cols]) + hid[:, there]
            cum = 0.5 * (1.0 + lax.erf(pre * (1.0 / math.sqrt(2.0))))
            slope = cum + pre * (jnp.exp(-0.5 * pre * pre) * (1.0 / math.sqrt(2.0 * math.pi)))
            a = (pre * cum).astype(BF)
            act[lo:hi, cols] = a
            g = dot_nt(grad, sh[cols, :]) * slope
            s8[:, there] += jnp.sum(g, axis=0, keepdims=True)
            gb = g.astype(BF)
            gpre[lo:hi, cols] = gb
            up += dot(a, sh[cols, :])
            down += dot_nt(gb, ex[:, cols])
        return up, down

    up, down = chunks(0, rows)
    then()
    base[...] = (residual + up + vec[7:8, :]).reshape(images, shard, width)
    for i in range(images):
        sin_copy(i).wait()
        other_up, other_down = chunks(rows + i * shard, rows + (i + 1) * shard)
        down_out[i] = other_down.astype(BF)
        down_copy(i).start()
        upx[i] = other_up.astype(BF)
    early()
    rest = []
    for i in range(images):
        down_copy(i).wait()
        part = slice(i * shard, (i + 1) * shard)
        total = down[part] + down_in[i].astype(F32)
        nr = normed[part]
        scaled = total * vec[5:6, :]
        m1 = jnp.mean(scaled, axis=-1, keepdims=True)
        m2 = jnp.mean(scaled * nr, axis=-1, keepdims=True)
        gr = cf[part] + inv[part] * (scaled - m1 - nr * m2)
        gresf[i] = gr
        gb = gr.astype(BF)
        gres[part, :] = gb
        val = dot_nt(mx[...], gb).astype(BF)
        send[4 * i : 4 * (i + 1)] = val.reshape(4, width // 4, shard)
        sums = [jnp.sum(t, axis=0, keepdims=True) for t in (gr, total * nr, total)]
        rest.append(sums)
    for ref, a, b in zip((s4, s5, s6), *rest):
        ref[...] = a + b


def hand_over_kernel(*refs):
    n = 6
    src, vec, dst, outs = refs[:n], refs[n], refs[n + 1 : 2 * n + 1], refs[2 * n + 1 :]
    for i in range(n):
        dst[i][...] = src[i][...]
    for i, o in enumerate(outs):
        line = 16 if i == 8 else i
        o[...] = vec[line : line + 1, : o.shape[0]].reshape(o.shape[0])


def hand_over(arrays, vec, small, big):
    S = jax.ShapeDtypeStruct
    outs = [S(t.shape, t.dtype) for t in arrays] + [S((small,), F32)] * 8 + [S((big,), F32)]
    return pl.pallas_call(
        hand_over_kernel,
        out_shape=outs,
        in_specs=[VM] * 7,
        out_specs=[VM] * 15,
        name="hand_over",
    )(*arrays, vec)


def split3(value):
    hi = value.astype(BF)
    rest = value - hi.astype(F32)
    mid = rest.astype(BF)
    low = (rest - mid.astype(F32)).astype(BF)
    return hi, mid, low


def pick(value, hot):
    a, b, d = split3(value)
    return dot(a, hot) + dot(b, hot) + dot(d, hot)


def stacked_extra(lead, value, row):
    a, b, d = (t.astype(F32) for t in split3(value))
    out = jnp.where(row == 1, a, 0.0) + jnp.where(row == 2, b, 0.0) + jnp.where(row == 3, d, 0.0)
    return (jnp.where(row == 0, lead, 0.0) + out).astype(BF)


def backward_step(h, j, c, grad, mixed, lse, qt, kv, kt, dkv, dqt):
    keys = kv.shape[1]
    hd, step, chunk = HEAD_DIM, 256, 512
    per = chunk // step
    g = (j // 2) * 4 + c * 2 + j % 2
    sl = pl.ds(pl.multiple_of(h * hd, hd), hd)
    do = jnp.concatenate([grad[2 * j, sl, :], grad[2 * j + 1, sl, :]], axis=1)
    mx = jnp.concatenate([mixed[2 * j, sl, :], mixed[2 * j + 1, sl, :]], axis=1)
    delta = jnp.sum(do.astype(F32) * mx.astype(F32), axis=0, keepdims=True)
    row = lax.broadcasted_iota(jnp.int32, (16, step), 0)
    none = jnp.zeros((hd, step), BF)
    rest = jnp.zeros((2 * hd - 16, step), BF)
    qh = qt[g, h]
    qa = jnp.concatenate([qh, none, stacked_extra(1.0, -lse[j, h], row), rest], axis=0)
    da = jnp.concatenate([none, do, stacked_extra(0.0, -delta, row), rest], axis=0)
    qr = jnp.concatenate([qh, none], axis=0).astype(F32).T.astype(BF)
    dr = jnp.concatenate([none, do], axis=0).astype(F32).T.astype(BF)
    dq = jnp.zeros((hd, step), F32)
    for kc in range(keys // chunk):
        rows = slice(kc * chunk, (kc + 1) * chunk)
        block = kv[h, rows, :]
        p = jnp.exp2(dot(block, qa) * LOG2E)
        dp = dot(block, da)
        ds = (p * dp).astype(BF)
        dkv[h, rows, :] += dot(ds, qr) + dot(p.astype(BF), dr)
        for i in range(per):
            dq += dot(kt[h, kc * per + i], ds[i * step : (i + 1) * step])
    dqt[j, sl, :] = (dq * (1.0 / math.sqrt(hd))).astype(BF)


def add_into(dst, src, lead, n):
    def body(i, carry):
        dst[lead + (i,)] = dst[lead + (i,)] + src[i]
        return carry

    lax.fori_loop(0, n, body, 0)


def halving(co, to, G, u, bufs, ss, rs, order, finish):
    x, y, c, z = co
    zh, zl = z // 2, z % 2
    r0, r1, r2, r3, r4 = bufs
    a, b = order
    first = (lambda n: G.at[u, 1 - x, n, c]) if a == "x" else (lambda n: G.at[u, n, 1 - y, c])
    keep = (lambda n: (u, x, n, c)) if a == "x" else (lambda n: (u, n, y, c))
    second = G.at[u, x, 1 - y, c] if b == "y" else G.at[u, 1 - x, y, c]

    def cp0(i):
        return rcopy(G.at[u, i // 2, i % 2, 1 - c], r0.at[u, i], ss.at[u, i], rs.at[u, i], to["core"])

    def cp1(n):
        return rcopy(first(n), r1.at[u, n], ss.at[u, 4 + n], rs.at[u, 4 + n], to[a])

    cp2 = lambda: rcopy(second, r2.at[u], ss.at[u, 6], rs.at[u, 6], to[b])
    cp3 = lambda n: rcopy(G.at[u, x, y, c, 2 * n + 1 - zl], r3.at[u, n], ss.at[u, 7 + n], rs.at[u, 7 + n], to["z1"])
    cp4 = lambda: rcopy(G.at[u, x, y, c, 2 * (1 - zh) + zl], r4.at[u], ss.at[u, 9], rs.at[u, 9], to["z2"])

    def core_send():
        for i in range(4):
            cp0(i).start()

    def core_land():
        for i in range(4):
            cp0(i).wait()
            add_into(G, r0.at[u, i], (u, i // 2, i % 2, c), 4)

    def a_send():
        for n in range(2):
            cp1(n).start()

    def a_wait():
        for n in range(2):
            cp1(n).wait()

    def a_add():
        for n in range(2):
            add_into(G, r1.at[u, n], keep(n), 4)
        cp2().start()

    def b_land():
        cp2().wait()
        add_into(G, r2.at[u], (u, x, y, c), 4)
        for n in range(2):
            cp3(n).start()

    def z1_land():
        for n in range(2):
            cp3(n).wait()
            here = (u, x, y, c, 2 * n + zl)
            G[here] = G[here] + r3[u, n]
        cp4().start()

    def z2_land():
        cp4().wait()
        finish(G[u, x, y, c, z].astype(F32) + r4[u].astype(F32))

    return dict(core_send=core_send, core_land=core_land, a_send=a_send, a_wait=a_wait, a_add=a_add, b_land=b_land, z1_land=z1_land, z2_land=z2_land)


def half_sum(co, to, H, b, r0, r1, r3, r4, ss, rs, finish):
    x, y, c, z = co
    zh, zl = z // 2, z % 2
    cp0 = lambda i: rcopy(H.at[b, i, 1 - c], r0.at[b, i], ss.at[b, i], rs.at[b, i], to["core"])
    cp1 = lambda: rcopy(H.at[b, 1 - y, c], r1.at[b], ss.at[b, 2], rs.at[b, 2], to["y"])
    cp3 = lambda n: rcopy(H.at[b, y, c, 2 * n + 1 - zl], r3.at[b, n], ss.at[b, 3 + n], rs.at[b, 3 + n], to["z1"])
    cp4 = lambda: rcopy(H.at[b, y, c, 2 * (1 - zh) + zl], r4.at[b], ss.at[b, 5], rs.at[b, 5], to["z2"])

    def core_send():
        for i in range(2):
            cp0(i).start()

    def core_land():
        for i in range(2):
            cp0(i).wait()
            add_into(H, r0.at[b, i], (b, i, c), 4)

    def y_send():
        cp1().start()

    def y_land():
        cp1().wait()
        add_into(H, r1.at[b], (b, y, c), 4)
        for n in range(2):
            cp3(n).start()

    def z1_land():
        for n in range(2):
            cp3(n).wait()
            here = (b, y, c, 2 * n + zl)
            H[here] = H[here] + r3[b, n]
        cp4().start()

    def z2_land():
        cp4().wait()
        finish(H[b, y, c, z].astype(F32) + r4[b].astype(F32))

    return core_send, core_land, y_send, y_land, z1_land, z2_land


def half_sum_line(co, to, H, b, r0, r1, r3, r4, ss, rs, finish):
    x, y, c, z = co
    zh, zl = z // 2, z % 2
    cp0 = lambda i: rcopy(H.at[b, i, 1 - c], r0.at[b, i], ss.at[b, i], rs.at[b, i], to["core"])
    cp3 = lambda i, n: rcopy(H.at[b, i, c, 2 * n + 1 - zl], r1.at[b, 2 * i + n], ss.at[b, 2 + 2 * i + n], rs.at[b, 2 + 2 * i + n], to["z1"])
    cp4 = lambda i: rcopy(H.at[b, i, c, 2 * (1 - zh) + zl], r3.at[b, i], ss.at[b, 6 + i], rs.at[b, 6 + i], to["z2"])
    cp1 = lambda: rcopy(H.at[b, 1 - y, c, z], r4.at[b], ss.at[b, 8], rs.at[b, 8], to["y"])

    def core_send():
        for i in range(2):
            cp0(i).start()

    def core_land():
        for i in range(2):
            cp0(i).wait()
            add_into(H, r0.at[b, i], (b, i, c), 4)

    def z1_send():
        for i in range(2):
            for n in range(2):
                cp3(i, n).start()

    def z1_land():
        for i in range(2):
            for n in range(2):
                cp3(i, n).wait()
                here = (b, i, c, 2 * n + zl)
                H[here] = H[here] + r1[b, 2 * i + n]
        for i in range(2):
            cp4(i).start()

    def z2_land():
        for i in range(2):
            cp4(i).wait()
            here = (b, i, c, z)
            H[here] = H[here] + r3[b, i]
        cp1().start()

    def y_land():
        cp1().wait()
        finish(H[b, y, c, z].astype(F32) + r4[b].astype(F32))

    return core_send, core_land, z1_send, z1_land, z2_land, y_land


TIMES = dict(
    core=(0.95, 1.31, 1.4, 1.5, 2.6),
    send=(0.96, 1.32, 10.25, 1.51),
    y=(10.2, 16.0, 21.0, 15.5),
    z1=(19.5, 21.1, 29.0, 24.0),
    z2=(27.0, 31.5, 36.5, 30.0),
    mixer=(16.2, 24.5, 31.8, 38.0),
    att=(4.0, 1.6),
    walk=(0.1, 0.95, 3.0, 3.9),
    fold=(2.2, 5.0),
    half=(8.6, 13.5, 20.5, 26.5),
    full=(16.0, 21.5, 27.2, 35.0),
    last=(22.0, 27.4),
    packed=(5.2, 9.0, 14.5, 18.0, 33.0),
    vec=(8.4, 9.1, 14.6, 18.1, 26.0, 34.0),
)


def backward_kernel(
    tok, cot_in, cotx, mix, vec, hid, mx_h, ex_h, sh_h, mixed_h, lse_h, qt_h, kv_h, kt_h, fi_h, nrm_h, pw_h,
    out_in, out_s, out_e, out_m, out_b, out_p, out_v,
    mx, ex, sh, down_out, down_in, base, upx, act, sin, cot, gpre, gres, gresf, send, s4, s5, s6, s7, s8, wsem, dss, drs,
    mixed, lse, qt, kv, kt, fi, nrm, pw, lsem, grad, G, r0, r1, r2, r3, r4, H, h0, h1, h3, h4, F, xo, xe, ub,
    dkv, dqt, dall, GF, q0, q1, q2, q3, sq, GP, p0, p1, p2, p3, V, vr,
    els, ess, ers, gss, grs, hss, hrs, xss, xrs, qss, qrs, pss, prs, vss, vrs,
):
    co = coords()
    x, y, c, z = co
    to = partners(*co)
    zh, zl = z // 2, z % 2
    heads, keys = kv.shape[0], kv.shape[1]
    width = cot.shape[1]
    rows = gres.shape[0]
    gain = vec
    late = [(mixed_h, mixed), (lse_h, lse), (qt_h, qt), (kv_h, kv), (kt_h, kt), (fi_h, fi), (nrm_h, nrm), (pw_h, pw)]

    def local(i):
        return pltpu.make_async_copy(late[i][0], late[i][1], lsem.at[i])

    others = [(dy, dz) for dy in range(2) for dz in range(4) if dy or dz]
    enter([to["core"], to["x"]] + [device(x, y ^ dy, c, z ^ dz) for dy, dz in others])
    me = y * 4 + z

    def exch(i):
        dy, dz = others[i]
        return rcopy(send.at[(y ^ dy) * 4 + (z ^ dz)], grad.at[me], ess.at[i], ers.at[i], device(x, y ^ dy, c, z ^ dz))

    mine = pltpu.make_async_copy(send.at[me], grad.at[me], els)
    ev = []
    n_hid = 2 * act.shape[1] // width

    def shrink_all():
        span = act.shape[1] // 4

        def body(t, carry):
            val = dot_tn(act[:, pl.ds(pl.multiple_of(t * span, span), span)], cot[...]).astype(BF)
            val = val.reshape(4, 4, 3, 8, width)
            for zz in range(4):
                for i in range(4):
                    H[i // 2, t // 2, t % 2, zz, i % 2] = val[zz, i]
            return carry

        lax.fori_loop(0, 4, body, 0)

    def expand_one(q):
        for xx in range(2):
            val = dot_tn(sin[:, xx * width // 2 : (xx + 1) * width // 2], gpre[:, q * width : (q + 1) * width]).astype(BF)
            val = val.reshape(2, 2, 4, 3, 8, width)
            for i in range(16):
                H[2 + q, i // 8, (i // 4) % 2, i % 4, xx] = val[i // 8, (i // 4) % 2, i % 4]

    def mixer_one():
        half = rows // 2
        for t in range(2):
            sl = slice(t * width // 2, (t + 1) * width // 2)
            val = dot(mix[0, sl, :], gres[:half]) + dot(mix[1, sl, :], gres[half:])
            G[0, t] = val.astype(BF).reshape(2, 2, 4, 3, 8, width)

    def run(fns):
        for fn in fns:
            fn()

    def lanes(xx, q):
        return pl.ds(pl.multiple_of((xx * (n_hid // 2) + q) * width, width), width)

    swap = lambda q: rcopy(xo.at[q], xe.at[q], xss.at[q], xrs.at[q], to["x"])
    up_copy = lambda: rcopy(upx, ub, xss.at[2], xrs.at[2], to["x"])

    def done_s(b, val):
        for i in range(2):
            out_s[2 * b + i] = val[i]

    def done_e(q, val):
        F[...] = val
        out_e[:, :, lanes(x, q)] = F[x]
        xo[q] = F[1 - x].astype(BF)
        swap(q).start()

    def landed_e(q):
        swap(q).wait()
        out_e[:, :, lanes(1 - x, q)] = xe[q].astype(F32)

    def landed_up():
        up_copy().wait()
        for i in range(2):
            out_b[i] = (base[i] + ub[i].astype(F32)).astype(BF)

    ev.append((0.0, shrink_all))
    ev.append((0.6, functools.partial(expand_one, 0)))
    ev.append((0.8, functools.partial(expand_one, 1)))
    ev.append((1.05, mixer_one))
    ev.append((1.2, lambda: up_copy().start()))
    for b in range(4):
        fin = functools.partial(done_s, b) if b < 2 else functools.partial(done_e, b - 2)
        st = (half_sum if b < 3 else half_sum_line)(co, to, H, b, h0, h1, h3, h4, hss, hrs, fin)
        for t, fn in zip(((0.5, 0.51, 0.7, 0.9)[b], TIMES["core"][b], TIMES["send"][b], TIMES["y"][b], TIMES["z1"][b], TIMES["z2"][b]), st):
            ev.append((t, fn))
        if b >= 2:
            ev.append((TIMES["z2"][b] + 4.0, functools.partial(landed_e, b - 2)))
    ev.append((TIMES["z2"][3] + 4.1, landed_up))
    st = halving(co, to, G, 0, (r0, r1, r2, r3, r4), gss, grs, "xy", lambda val: out_m.__setitem__(Ellipsis, val))
    ev.append((1.1, st["core_send"]))
    ev.append((TIMES["core"][4], lambda: run([st["core_land"], st["a_send"]])))
    for t, names in zip(TIMES["mixer"], (("a_wait", "a_add"), ("b_land",), ("z1_land",), ("z2_land",))):
        ev.append((t, functools.partial(run, [st[k] for k in names])))

    def zero():
        def body(i, carry):
            for h in range(heads):
                dkv[h, pl.ds(pl.multiple_of(i * 256, 256), 256), :] = jnp.zeros((256, 2 * HEAD_DIM), F32)
            return carry

        lax.fori_loop(0, keys // 256, body, 0)

    def arrive(q):
        if q == 0:
            mine.wait()
            for i in range(5):
                local(i).wait()
        for i in range(7):
            if 2 * others[i][0] + others[i][1] // 2 == q:
                exch(i).wait()

    ev.append((1.3, zero))
    steps = 4 * heads
    t_att, t_step = TIMES["att"]
    t_end = t_att + t_step * steps
    for q in range(4):
        ev.append((t_att + heads * q * t_step + 0.001, functools.partial(arrive, q)))

    def begin():
        mine.start()
        for i in range(7):
            exch(i).start()
        V[...] = jnp.zeros_like(V)
        for i, ref in ((4, s4), (5, s5), (6, s6), (7, s7)):
            V[i : i + 1, :] = ref[...]
        for i in range(n_hid):
            V[8 + i : 9 + i, :] = s8[:, i * width : (i + 1) * width]

    ev.append((1.0, begin))

    def group(slot, mine_rows):
        cc = c if mine_rows else 1 - c
        yy = slot // 2
        g = yy * 4 + cc * 2 + slot % 2
        off = pl.multiple_of(g * 256, 256)
        rs_ = pl.ds(off, 256)
        wide = 2 * HEAD_DIM * heads
        dk = jnp.concatenate([dkv[h, rs_, :].astype(BF) for h in range(heads)], axis=1)
        gf = dot_nt(dk, pw[:, :wide])
        dall[rs_, :wide] = dk
        sums = jnp.sum(dk.astype(F32), axis=0, keepdims=True)
        V[16:17, :wide] += sums
        if mine_rows:
            dq = dqt[slot].astype(F32).T.astype(BF)
            gf += dot_nt(dq, pw[:, wide:])
            dall[rs_, wide:] = dq
            V[17:18, : dq.shape[1]] += jnp.sum(dq.astype(F32), axis=0, keepdims=True)
        else:
            dall[rs_, wide:] = jnp.zeros((256, heads * HEAD_DIM), BF)
        V[0:1, :] += jnp.sum(gf * nrm[rs_, :].astype(F32), axis=0, keepdims=True)
        V[1:2, :] += jnp.sum(gf, axis=0, keepdims=True)
        GF[yy, cc, pl.ds(2 * (slot % 2), 2)] = gf.astype(BF).reshape(2, 2, 64, width)

    def q_core(r):
        yy = rowof(r)
        return rcopy(GF.at[yy, 1 - c], q0.at[r], qss.at[r], qrs.at[r], to["core"])

    def q_z1(r, f, n):
        i = 2 + 4 * r + 2 * f + n
        return rcopy(GF.at[rowof(r), c, 2 * n + 1 - zl, f], q1.at[r, f, n], qss.at[i], qrs.at[i], to["z1"])

    def q_z2(r, f):
        i = 10 + 2 * r + f
        return rcopy(GF.at[rowof(r), c, 2 * (1 - zh) + zl, f], q2.at[r, f], qss.at[i], qrs.at[i], to["z2"])

    def q_y(f):
        return rcopy(sq.at[f], q3.at[f], qss.at[14 + f], qrs.at[14 + f], to["y"])

    def rowof(r):
        return 1 - y if r == 0 else y

    def walk(mine_rows, r):
        def body(i, carry):
            group(2 * rowof(r) + i, mine_rows)
            return carry

        lax.fori_loop(0, 2, body, 0)
        if not mine_rows:
            q_core(r).start()

    def q_sum(r):
        q_core(r).wait()
        yy = rowof(r)

        def body(i, carry):
            GF[yy, c, i // 2, i % 2] = GF[yy, c, i // 2, i % 2] + q0[r, i // 2, i % 2]
            return carry

        lax.fori_loop(0, 8, body, 0)
        if r == 0:
            q_send(0, 0)

    def q_send(r, f):
        for n in range(2):
            q_z1(r, f, n).start()

    chunks = [(r, f) for r in range(2) for f in range(2)]

    def q_half(i):
        r, f = chunks[i]
        for n in range(2):
            q_z1(r, f, n).wait()
        if i + 2 < 4:
            q_send(*chunks[i + 2])
        for n in range(2):
            here = (rowof(r), c, 2 * n + zl, f)
            GF[here] = GF[here] + q1[r, f, n]
        q_z2(r, f).start()

    def finish(img, f, total):
        rs_ = slice(64 * f, 64 * (f + 1))
        normed, inv = row_norm(tok[img, rs_].astype(F32))
        scaled = total * gain[0:1, :]
        m1 = jnp.mean(scaled, axis=-1, keepdims=True)
        m2 = jnp.mean(scaled * normed, axis=-1, keepdims=True)
        out_in[img, rs_] = (gresf[img, rs_] + inv * (scaled - m1 - normed * m2)).astype(BF)

    def q_full(i):
        r, f = chunks[i]
        q_z2(r, f).wait()
        total = GF[rowof(r), c, z, f].astype(F32) + q2[r, f].astype(F32)
        if r == 0:
            sq[f] = total.astype(BF)
            q_y(f).start()
        else:
            finish(y, f, total)

    def q_last(f):
        q_y(f).wait()
        finish(1 - y, f, q3[f].astype(F32))

    def late_rows():
        for i in range(5, 8):
            local(i).wait()

    ev.append((t_end + 0.05, late_rows))
    for i in range(4):
        ev.append((t_end + TIMES["walk"][i], functools.partial(walk, i % 2 == 1, i // 2)))
        ev.append((t_end + TIMES["half"][i], functools.partial(q_half, i)))
        ev.append((t_end + TIMES["full"][i], functools.partial(q_full, i)))
    for f in range(2):
        ev.append((t_end + TIMES["fold"][f], functools.partial(q_sum, f)))
        if f == 0:
            ev.append((t_end + TIMES["walk"][3] + 0.1, functools.partial(q_send, 0, 1)))
        ev.append((t_end + TIMES["last"][f], functools.partial(q_last, f)))

    def packed():
        val = dot_tn(fi[...], dall[...]).astype(BF)
        GP[0] = val.reshape(2, 2, 2, 4, 3, 8, val.shape[1])
        for i in range(4):
            p_core(i).start()

    def p_core(i):
        return rcopy(GP.at[0, i // 2, i % 2, 1 - c], p0.at[i], pss.at[i], prs.at[i], to["core"])

    def p_a(n):
        return rcopy(GP.at[0, 1 - x, n, c], p1.at[n], pss.at[4 + n], prs.at[4 + n], to["x"])

    p_b = lambda: rcopy(GP.at[0, x, 1 - y, c], p2, pss.at[6], prs.at[6], to["y"])
    p_z = lambda k: rcopy(GP.at[0, x, y, c, z ^ k], p3.at[k - 1], pss.at[6 + k], prs.at[6 + k], to["z%d" % k])

    def packed_core():
        for i in range(4):
            p_core(i).wait()
            add_into(GP, p0.at[i], (0, i // 2, i % 2, c), 4)
        for n in range(2):
            p_a(n).start()

    def packed_a():
        for n in range(2):
            p_a(n).wait()
            add_into(GP, p1.at[n], (0, x, n, c), 4)
        p_b().start()

    def packed_b():
        p_b().wait()
        add_into(GP, p2, (0, x, y, c), 4)
        for k in (1, 2, 3):
            p_z(k).start()

    def packed_z():
        GP[0, 1 - x, y, c, z] = GP[0, x, y, c, z]
        for k in (1, 2, 3):
            p_z(k).wait()
            GP[0, 1 - x, y, c, z ^ k] = p3[k - 1]
        part = heads * HEAD_DIM
        for g in range(4):
            val = GP[0, 1 - x, y, c, g].astype(F32)
            for h in range(heads):
                spots = ((1, 2 * h), (2, 2 * h + 1), (0, 2 * heads + h))
                for t, i in spots:
                    lo = t * width + g * part + h * HEAD_DIM
                    out_p[:, :, lo : lo + HEAD_DIM] = val[:, :, i * HEAD_DIM : (i + 1) * HEAD_DIM]

    def v_copy(i):
        return rcopy(V.at[0:16], vr.at[i], vss.at[i], vrs.at[i], to[("core", "x", "y", "z1", "z2")[i]])

    def vec_start():
        part = heads * HEAD_DIM
        wide = 2 * part
        src = lax.broadcasted_iota(jnp.int32, (wide, 1), 0)
        dst = lax.broadcasted_iota(jnp.int32, (1, width), 1)
        head, lane = src // (2 * HEAD_DIM), src % (2 * HEAD_DIM)
        to_v = jnp.where(lane >= HEAD_DIM, z * part + head * HEAD_DIM + lane - HEAD_DIM, -1)
        V[3:4, :] = pick(V[16:17, :wide], jnp.where(to_v == dst, 1.0, 0.0).astype(BF))
        V[2:3, :] = pick(V[17:18, :part], jnp.where(z * part + src[:part] == dst, 1.0, 0.0).astype(BF))
        v_copy(0).start()

    def vec_step(i):
        v_copy(i).wait()
        V[0:16, :] = V[0:16, :] + vr[i]
        if i < 4:
            v_copy(i + 1).start()
        else:
            n_dev = 32
            small = width // n_dev
            d = (x * 4 + y * 2 + c) * 4 + z
            src = lax.broadcasted_iota(jnp.int32, (width, 1), 0)
            dst = lax.broadcasted_iota(jnp.int32, (1, 128), 1)
            hot = jnp.where(dst < small, d * small + dst, -1) == src
            out_v[0:16, :] = pick(V[0:16, :], jnp.where(hot, 1.0, 0.0).astype(BF))
            big = n_hid * small
            hot = jnp.where(dst < big, (d % (n_dev // n_hid)) * big + dst, -1) == src
            line = lax.broadcasted_iota(jnp.int32, (16, 128), 0)
            val = pick(V[0:16, :], jnp.where(hot, 1.0, 0.0).astype(BF))
            val = jnp.where(line == 8 + d // (n_dev // n_hid), val, 0.0)
            out_v[16:17, :] = jnp.sum(val, axis=0, keepdims=True)

    for t, fn in zip(TIMES["packed"], (packed, packed_core, packed_a, packed_b, packed_z)):
        ev.append((t_end + t, fn))
    for t, fn in zip(TIMES["vec"], [vec_start] + [functools.partial(vec_step, i) for i in range(5)]):
        ev.append((t_end + t, fn))

    ev.sort(key=lambda e: e[0])
    dense_body(
        tok, cot_in, cotx, mix, vec, hid, mx_h, ex_h, sh_h,
        base, upx, act, sin, cot, gpre, gres, gresf, send, s4, s5, s6, s7, s8,
        mx, ex, sh, down_out, down_in, wsem, dss, drs,
        lambda: [local(i).start() for i in range(len(late))],
        lambda: [fn() for t, fn in ev if t < 1.0],
    )
    for t, fn in ev:
        if 1.0 <= t < t_att:
            fn()

    def step(s, carry):
        for k in range(steps):
            here = [fn for t, fn in ev if t_att + k * t_step <= t < t_att + (k + 1) * t_step]
            if here:

                @pl.when(s == k)
                def _():
                    for fn in here:
                        fn()

        backward_step(s % heads, (s // heads) ^ (2 * y + zh), c, grad, mixed, lse, qt, kv, kt, dkv, dqt)
        return carry

    lax.fori_loop(0, steps, step, 0)
    for t, fn in ev:
        if t >= t_end:
            fn()


def backward_all(tok, cot, cotx, mix, vec, hid, mx, ex, sh, mixed, lse, qt, kv, kt, fi, nrm, pw):
    D, V, S = pltpu.SemaphoreType.DMA, pltpu.VMEM, jax.ShapeDtypeStruct
    heads, keys = kv.shape[0], kv.shape[1]
    images, shard, width = tok.shape
    rows, half = images * shard, ex.shape[1]
    blk = (3, 8, width)
    cols = pw.shape[1]
    pb = (3, 8, cols)
    send = (4 * images, width // 4, shard)
    outs = [S(tok.shape, BF), S((4,) + blk, F32), S((3, 8, 2 * half), F32), S(blk, F32), S(tok.shape, BF), S((3, 8, 4 * cols), F32), S((24, 128), F32)]
    scr = [V(mx.shape, BF), V(ex.shape, BF), V(sh.shape, BF), V(tok.shape, BF), V(tok.shape, BF)]
    scr += [V(tok.shape, F32), V(tok.shape, BF), V((2 * rows, half), BF), V((2 * rows, width), BF), V((2 * rows, width), BF), V((2 * rows, half), BF)]
    scr += [V((rows, width), BF), V(tok.shape, F32), V(send, BF)] + [V((1, width), F32)] * 4 + [V((1, 2 * half), F32)]
    scr += [D((1 + 2 * (half // width),)), D((2 * images,)), D((2 * images,))]
    scr += [V(t.shape, t.dtype) for t in (mixed, lse, qt, kv, kt, fi, nrm, pw)]
    scr += [D((8,)), V(send, BF), V((1, 2, 2, 2, 4) + blk, BF), V((1, 4, 4) + blk, BF), V((1, 2, 4) + blk, BF), V((1, 4) + blk, BF), V((1, 2) + blk, BF), V((1,) + blk, BF)]
    scr += [V((4, 2, 2, 4, 2) + blk, BF), V((4, 2, 4, 2) + blk, BF), V((4, 4, 2) + blk, BF), V((4, 2, 2) + blk, BF), V((4, 2) + blk, BF)]
    scr += [V((2,) + blk, F32), V((2,) + blk, BF), V((2,) + blk, BF), V(tok.shape, BF)]
    scr += [V((heads, keys, 2 * HEAD_DIM), F32), V((4, heads * HEAD_DIM, 256), BF), V((keys, cols), BF)]
    rowt = (64, width)
    scr += [V((2, 2, 4, 2) + rowt, BF), V((2, 4, 2) + rowt, BF), V((2, 2, 2) + rowt, BF), V((2, 2) + rowt, BF), V((2,) + rowt, BF), V((2,) + rowt, BF)]
    scr += [V((1, 2, 2, 2, 4) + pb, BF), V((4, 4) + pb, BF), V((2, 4) + pb, BF), V((4,) + pb, BF), V((3,) + pb, BF), V((24, width), F32), V((5, 16, width), F32)]
    for n in ((), (7,), (7,), (1, 10), (1, 10), (4, 9), (4, 9), (3,), (3,), (16,), (16,), (10,), (10,), (5,), (5,)):
        scr.append(D(n) if n else D)
    return pl.pallas_call(
        backward_kernel,
        out_shape=outs,
        in_specs=[VM] * 6 + [ANY] * 11,
        out_specs=[VM] * len(outs),
        scratch_shapes=scr,
        compiler_params=pltpu.CompilerParams(collective_id=2, has_side_effects=True, vmem_limit_bytes=63 << 20),
        name="dense_backward_reduce",
    )(tok, cot, cotx, mix, vec, hid, mx, ex, sh, mixed, lse, qt, kv, kt, fi, nrm, pw)


def backward_local_kernel(grad, mixed, lse, qt, kv, kt, out, dkv, dqt):
    _, _, c, _ = coords()
    heads, keys = kv.shape[0], kv.shape[1]
    wide = 2 * HEAD_DIM * heads
    dkv[...] = jnp.zeros_like(dkv)

    def step(s, carry):
        backward_step(s % heads, s // heads, c, grad, mixed, lse, qt, kv, kt, dkv, dqt)
        return carry

    lax.fori_loop(0, 4 * heads, step, 0)
    for g in range(8):
        rs = slice(g * 256, (g + 1) * 256)
        for h in range(heads):
            out[rs, 2 * h * HEAD_DIM : 2 * (h + 1) * HEAD_DIM] = dkv[h, rs, :].astype(BF)
        dq = dqt[(g // 4) * 2 + g % 2].astype(F32).T
        out[rs, wide:] = jnp.where((g // 2) % 2 == c, dq, 0.0).astype(BF)


def backward_local(grad, mixed, lse, qt, kv, kt):
    heads, keys = kv.shape[0], kv.shape[1]
    return pl.pallas_call(
        backward_local_kernel,
        out_shape=jax.ShapeDtypeStruct((keys, 3 * heads * HEAD_DIM), BF),
        in_specs=[VM] * 6,
        out_specs=VM,
        scratch_shapes=[pltpu.VMEM((heads, keys, 2 * HEAD_DIM), F32), pltpu.VMEM((4, heads * HEAD_DIM, 256), BF)],
        compiler_params=pltpu.CompilerParams(vmem_limit_bytes=50 << 20),
        name="attention_backward",
    )(grad, mixed, lse, qt, kv, kt)


def reduce_generic(gf, gp, gm, ge, gs, n_dev):
    every = ("dp", "ctx", "head")
    x, y, c, z = coords()
    flat = gf.reshape((1, -1) + gf.shape[-1:])
    both = jnp.concatenate([jnp.where(y == i, flat, jnp.zeros_like(flat)) for i in range(2)], axis=0)
    of = lax.psum_scatter(both.astype(F32), ("ctx", "head"), scatter_dimension=1, tiled=True)
    cols = gp.shape[-1]
    rows = gp.size // cols
    spread = lax.dynamic_update_slice_in_dim(jnp.zeros((rows, 4, cols), F32), gp.reshape(rows, 1, cols).astype(F32), z, 1)
    op = jnp.swapaxes(lax.psum_scatter(spread, every, scatter_dimension=0, tiled=True), 0, 1)
    rest = [
        lax.psum_scatter(g.reshape((n_dev, -1) + g.shape[-1:]).astype(F32), every, scatter_dimension=0, tiled=True)[0] for g in (gm, ge, gs)
    ]
    return [of, op] + rest


def layer_norm(token_rows, norm_gain, norm_shift):
    normed, inv_std = row_norm(token_rows)
    return (normed * norm_gain + norm_shift, normed, inv_std)


def norm_backward(grad_out, normed, inv_std, norm_gain):
    scaled = grad_out * norm_gain
    first_mean = jnp.mean(scaled, axis=-1, keepdims=True)
    second_mean = jnp.mean(scaled * normed, axis=-1, keepdims=True)
    return inv_std * (scaled - first_mean - normed * second_mean)


def gelu_parts(pre_act):
    cumulative = 0.5 * (1.0 + jax.scipy.special.erf(pre_act * (1.0 / math.sqrt(2.0))))
    density = jnp.exp(-0.5 * pre_act * pre_act) * (1.0 / math.sqrt(2.0 * math.pi))
    return pre_act * cumulative, cumulative + pre_act * density


def on_device(
    tokens,
    cotangent,
    lengths,
    attention_gain,
    attention_shift,
    packed_weight,
    query_bias,
    value_bias,
    mixer_weight,
    mixer_bias,
    feedforward_gain,
    feedforward_shift,
    expand_weight,
    expand_bias,
    shrink_weight,
    shrink_bias,
):
    images, shard_len, width = tokens.shape
    groups = lax.axis_size("head")
    heads = HEADS // groups
    part = heads * HEAD_DIM
    hidden = expand_weight.shape[1]
    rows = images * shard_len
    n_dev = lax.axis_size("dp") * lax.axis_size("ctx") * groups
    z = lax.axis_index("head")
    wr = packed_weight.shape[0]
    fr = shrink_weight.shape[0]

    tiled = wr % 8 == 0 and fr % 8 == 0 and lax.axis_size("dp") == 2
    slab = (lambda r, n: (r // 8, 8, n)) if tiled else (lambda r, n: (r, n))
    vecs = [attention_gain, attention_shift, query_bias, value_bias, mixer_bias, feedforward_gain, feedforward_shift, shrink_bias, expand_bias]
    mx, ex, sh = mixer_weight.reshape(slab(wr, width)), expand_weight.reshape(slab(wr, hidden)), shrink_weight.reshape(slab(fr, width))
    if tiled:
        mix, mixed_t, lse, fi, nrm, qt, kv, kt, full_packed, full_vecs, eb, mxo, exo, sho, cotx = forward_all(lengths, tokens, cotangent, packed_weight.reshape(slab(wr, 3 * width)), mx, ex, sh, vecs)
        hidden_bias = eb
    else:
        pk = jnp.stack([own_columns(packed_weight, g, part) for g in range(groups)])
        sv = jnp.stack([jnp.pad(v, (0, 128 - v.shape[0])) for v in vecs] + [jnp.zeros((128,), BF)] * 7)
        img, pko, mxo, exo, sho, svo = gather_generic(tokens, pk, mx, ex, sh, sv)
        full_packed = pko.reshape(width, 3 * part)
        svo = svo.reshape(n_dev, 16, 128).astype(F32)
        gain_one, shift_one, qb, vb, mb, gain_two, shift_two, sb = [svo[:, i, :wr].reshape(width) for i in range(8)]
        eb = svo[:, 8, :fr].reshape(hidden)
        own = lambda v: lax.dynamic_slice_in_dim(v, z * part, part)
        vb_own = own(vb).reshape(heads, 1, HEAD_DIM)
        bias = jnp.concatenate([jnp.concatenate([jnp.zeros_like(vb_own), vb_own], axis=1).reshape(2 * part), own(qb)])
        img = img.reshape(16, shard_len, width)
        mixed_t, lse, fi, nrm, qt, kv, kt = attention_forward(lengths, img, full_packed, gain_one[None], shift_one[None], bias[None])
        mix = exchange(mixed_t, 1)
    mix = mix.reshape(images, width, shard_len)
    full_mixer = mxo.reshape(width, width)
    full_expand = exo.reshape(width, -1)
    full_shrink = sho.reshape(-1, width)

    if tiled:
        ig, os_, oe, om, block_output, op, ov = backward_all(
            tokens, cotangent, cotx, mix, full_vecs, hidden_bias, full_mixer, full_expand, full_shrink, mixed_t, lse, qt, kv, kt, fi, nrm, full_packed
        )
        ig, os_, oe, om, block_output, op, *vec = hand_over([ig, os_, oe, om, block_output, op], ov, wr, fr)
        op = op.reshape(wr, 3 * width)
    else:
        token_rows = tokens.reshape(rows, width).astype(F32)
        mixed_rows = jnp.swapaxes(mix, 1, 2).reshape(rows, width)
        residual = token_rows + dot(mixed_rows, full_mixer) + mb
        second_out, second_normed, second_inv = layer_norm(residual, gain_two, shift_two)
        second_input = second_out.astype(BF)
        pre_act = dot(second_input, full_expand) + eb
        value, slope = gelu_parts(pre_act)
        activated = value.astype(BF)
        block_output = (residual + dot(activated, full_shrink) + sb).astype(BF)
        grad_in = cotangent.reshape(rows, width)
        grad_rows = grad_in.astype(F32)
        grad_shrink_b = jnp.sum(grad_rows, axis=0)
        grad_pre = jnp.einsum("rd,fd->rf", grad_in, full_shrink, preferred_element_type=F32) * slope
        grad_pre_bf = grad_pre.astype(BF)
        grad_expand_b = jnp.sum(grad_pre, axis=0)
        grad_second = jnp.einsum("rf,df->rd", grad_pre_bf, full_expand, preferred_element_type=F32)
        grad_gain_two = jnp.sum(grad_second * second_normed, axis=0)
        grad_shift_two = jnp.sum(grad_second, axis=0)
        grad_residual = grad_rows + norm_backward(grad_second, second_normed, second_inv, gain_two)
        grad_residual_bf = grad_residual.astype(BF)
        grad_mixer_b = jnp.sum(grad_residual, axis=0)
        grad_mixed = jnp.einsum("de,ire->idr", full_mixer, grad_residual_bf.reshape(images, shard_len, width), preferred_element_type=F32).astype(BF)
        grad_mixed = grad_mixed.reshape(images * groups, part, shard_len)
        grad_t = exchange(grad_mixed, 2)
        dqkv = backward_local(grad_t, mixed_t, lse, qt, kv, kt)
        grad_packed_w = jnp.einsum("rd,re->de", fi, dqkv, preferred_element_type=F32)
        grad_first_part = jnp.einsum("re,de->rd", dqkv, full_packed, preferred_element_type=F32)
        img_normed, _ = row_norm(img.reshape(16 * shard_len, width).astype(F32))
        dsum = jnp.sum(dqkv.astype(F32), axis=0)
        place = lambda v: lax.dynamic_update_slice_in_dim(jnp.zeros((width,), F32), v, z * part, 0)
        sums = [
            jnp.sum(grad_first_part * img_normed, axis=0),
            jnp.sum(grad_first_part, axis=0),
            place(dsum[2 * part :]),
            place(dsum[: 2 * part].reshape(heads, 2, HEAD_DIM)[:, 1].reshape(part)),
            grad_mixer_b,
            grad_gain_two,
            grad_shift_two,
            grad_shrink_b,
            grad_expand_b,
        ]
        vec = [lax.psum_scatter(t, ("dp", "ctx", "head"), scatter_dimension=0, tiled=True) for t in sums]
        of, op, om, oe, os_ = reduce_generic(
            grad_first_part.reshape(2, 2, groups, shard_len, width),
            grad_packed_w,
            jnp.einsum("rd,re->de", mixed_rows, grad_residual_bf, preferred_element_type=F32),
            jnp.einsum("rd,rf->df", second_input, grad_pre_bf, preferred_element_type=F32),
            jnp.einsum("rf,rd->fd", activated, grad_in, preferred_element_type=F32),
            n_dev,
        )
        op = op.reshape(groups, wr, 3 * part)
        okv = jnp.transpose(op[:, :, : 2 * part].reshape(groups, wr, heads, 2, HEAD_DIM), (1, 3, 0, 2, 4)).reshape(wr, 2 * width)
        op = jnp.concatenate([jnp.transpose(op[:, :, 2 * part :], (1, 0, 2)).reshape(wr, width), okv], axis=1)
        _, first_normed, first_inv = layer_norm(token_rows, gain_one, shift_one)
        ig = (grad_residual + norm_backward(of.reshape(rows, width), first_normed, first_inv, gain_one)).astype(BF)
    return (
        block_output.reshape(images, shard_len, width),
        ig.reshape(images, shard_len, width),
        vec[0],
        vec[1],
        op,
        vec[2],
        vec[3],
        om.reshape(wr, width),
        vec[4],
        vec[5],
        vec[6],
        oe.reshape(wr, hidden),
        vec[8],
        os_.reshape(fr, width),
        vec[7],
    )


def solution(mesh):
    every = ("dp", "ctx", "head")
    tok, vec, mat = P("dp", ("ctx", "head"), None), P(every), P(every, None)
    in_specs = (tok, tok, P("dp"), vec, vec, mat, vec, vec, mat, vec, vec, vec, mat, vec, mat, vec)
    out_specs = (tok, tok, vec, vec, mat, vec, vec, mat, vec, vec, vec, mat, vec, mat, vec)
    return jax.shard_map(on_device, mesh=mesh, in_specs=in_specs, out_specs=out_specs, check_vma=False)
```

```python
import functools
import math

import jax
import jax.numpy as jnp
from jax import lax
from jax.experimental import pallas as pl
from jax.experimental.pallas import tpu as pltpu
from jax.sharding import PartitionSpec as P

HEADS = 12
HEAD_DIM = 64
NORM_EPS = 1e-06
MASKED = -1e30
LOG2E = 1.4426950408889634
MESH = pl.DeviceIdType.MESH
ANY = pl.BlockSpec(memory_space=pl.ANY)
VM = pl.BlockSpec(memory_space=pltpu.VMEM)
SM = pl.BlockSpec(memory_space=pltpu.SMEM)
BF = jnp.bfloat16
F32 = jnp.float32
SPLIT = 2


def coords():
    ctx = lax.axis_index("ctx")
    return lax.axis_index("dp"), ctx // SPLIT, ctx % SPLIT, lax.axis_index("head")


def device(x, y, c, z):
    return (x, y * SPLIT + c, z)


def enter(targets):
    sem = pltpu.get_barrier_semaphore()
    for t in targets:
        pl.semaphore_signal(sem, inc=1, device_id=t, device_id_type=MESH)
    pl.semaphore_wait(sem, len(targets))


def rcopy(src, dst, ss, rs, to):
    return pltpu.make_async_remote_copy(src, dst, ss, rs, device_id=to, device_id_type=MESH)


def run_events(events):
    for _, fn in sorted(events, key=lambda e: e[0]):
        fn()


def partners(x, y, c, z):
    return dict(
        core=device(x, y, 1 - c, z),
        x=device(1 - x, y, c, z),
        y=device(x, 1 - y, c, z),
        z1=device(x, y, c, z ^ 1),
        z2=device(x, y, c, z ^ 2),
        z3=device(x, y, c, z ^ 3),
    )


def weight_gather(ev, co, to, src, out, sems, order, times):
    x, y, c, z = co
    lsem, zss, zrs, ass, ars, bss, brs, css, crs = sems
    a, b = order

    def spot(fa, fb):
        px = (1 - x if fa else x) if a == "x" else (1 - x if fb else x)
        py = (1 - y if fa else y) if a == "y" else (1 - y if fb else y)
        return px, py

    def at(fa, fb, k):
        return out(*spot(fa, fb), c, z ^ k)

    def group(fa, fb, cc):
        return out(*spot(fa, fb), cc, slice(None))

    F, T = False, True
    zsend = lambda i, k, ref, dst, name: rcopy(ref, dst, zss.at[i], zrs.at[k], to[name])
    asend = lambda k, ref: rcopy(ref, at(F, F, k), ass.at[k], ars.at[k], to[a])
    bsend = lambda fa, k, ref: rcopy(ref, at(fa, F, k), bss.at[int(fa), k], brs.at[int(fa), k], to[b])
    csend = lambda i, g: rcopy(g, g, css.at[i], crs.at[i], to["core"])
    local = lambda: pltpu.make_async_copy(src, at(F, F, 0), lsem)

    def begin():
        local().start()
        asend(0, src).start()
        bsend(F, 0, src).start()

    def z_begin():
        zsend(0, 0, src, at(F, F, 0), "z1").start()
        zsend(1, 1, src, at(F, F, 0), "z2").start()

    def z_land(k):
        d = at(F, F, k)
        zsend(k - 1, k - 1, d, d, "z1").wait_recv()
        if k == 2:
            zsend(2, 2, d, d, "z1").start()
        asend(k, d).start()
        bsend(F, k, d).start()

    def own_done():
        local().wait()
        csend(0, group(F, F, c)).start()

    def a_land(k):
        d = at(T, F, k)
        asend(k, d).wait_recv()
        bsend(T, k, d).start()
        if k == 3:
            csend(1, group(T, F, c)).start()

    def b_land(fa):
        for k in range(4):
            bsend(fa, k, at(fa, T, k)).wait_recv()
        csend(2 + int(fa), group(fa, T, c)).start()

    def last():
        d = at(F, F, 0)
        for i in range(3):
            zsend(i, 0, d, d, "z1").wait_send()
        for k in range(4):
            asend(k, d).wait_send()
            bsend(F, k, d).wait_send()
            bsend(T, k, d).wait_send()
        for i, (fa, fb) in enumerate(((F, F), (T, F), (F, T), (T, T))):
            csend(i, group(fa, fb, 1 - c)).wait()

    t_begin, t_z, t_zl, t_al, t_bl = times
    ev.append((t_begin, begin))
    ev.append((t_z, z_begin))
    for k in range(1, 4):
        ev.append((t_zl[k - 1], functools.partial(z_land, k)))
    ev.append((t_zl[2] + 0.3, own_done))
    for k in range(4):
        ev.append((t_al[k], functools.partial(a_land, k)))
    ev.append((t_bl[0], functools.partial(b_land, F)))
    ev.append((t_bl[1], functools.partial(b_land, T)))
    ev.append((1000.0, last))


def half_gather(ev, co, to, prepare, settle, own, view, sems, times):
    x, y, c, z = co
    zss, zrs, yss, yrs, css, crs = sems
    at = lambda k: view(y, c, z ^ k)
    zsend = lambda i, k, ref, dst, name: rcopy(ref, dst, zss.at[i], zrs.at[k], to[name])
    ysend = lambda k, ref: rcopy(ref, at(k), yss.at[k], yrs.at[k], to["y"])

    def csend(i):
        g = view(y if i == 0 else 1 - y, c, slice(None))
        return rcopy(g, g, css.at[i], crs.at[i], to["core"])

    def begin():
        prepare()
        ysend(0, own).start()

    def z_begin():
        zsend(0, 0, own, at(0), "z1").start()
        zsend(1, 1, own, at(0), "z2").start()

    def z_land(k):
        d = at(k)
        zsend(k - 1, k - 1, d, d, "z1").wait_recv()
        if k == 2:
            zsend(2, 2, d, d, "z1").start()
        ysend(k, d).start()
        if k == 3:
            settle()
            csend(0).start()

    def y_land():
        for k in range(4):
            d = view(1 - y, c, z ^ k)
            rcopy(d, d, yss.at[k], yrs.at[k], to["y"]).wait_recv()
        csend(1).start()

    def last():
        d = at(0)
        for i in range(3):
            zsend(i, 0, d, d, "z1").wait_send()
        for k in range(4):
            ysend(k, d).wait_send()
        for i in range(2):
            csend(i).wait()

    t_begin, t_z, t_zl, t_y = times
    ev.append((t_begin, begin))
    ev.append((t_z, z_begin))
    for k in range(1, 4):
        ev.append((t_zl[k - 1], functools.partial(z_land, k)))
    ev.append((t_y, y_land))
    ev.append((1000.5, last))


def small_gather(co, to, src, out, ls, ss, rs, spread):
    x, y, c, z = co
    own = src.at[z] if spread else src

    def begin():
        pltpu.make_async_copy(own, out.at[x, y, c, z], ls).start()
        for k in (1, 2, 3):
            rcopy(src.at[z ^ k] if spread else src, out.at[x, y, c, z], ss.at[k - 1], rs.at[k - 1], to["z%d" % k]).start()

    def step_y():
        pltpu.make_async_copy(own, out.at[x, y, c, z], ls).wait()
        for k in (1, 2, 3):
            d = out.at[x, y, c, z ^ k]
            rcopy(d, d, ss.at[k - 1], rs.at[k - 1], to["z1"]).wait()
        g = out.at[x, y, c]
        rcopy(g, g, ss.at[3], rs.at[3], to["y"]).start()

    def step_x():
        g = out.at[x, 1 - y, c]
        rcopy(g, g, ss.at[3], rs.at[3], to["y"]).wait()
        for yy in range(2):
            g = out.at[x, yy, c]
            rcopy(g, g, ss.at[4 + yy], rs.at[4 + yy], to["x"]).start()

    def step_c():
        for yy in range(2):
            g = out.at[1 - x, yy, c]
            rcopy(g, g, ss.at[4 + yy], rs.at[4 + yy], to["x"]).wait()
        for xx in range(2):
            for yy in range(2):
                g = out.at[xx, yy, c]
                rcopy(g, g, ss.at[6 + 2 * xx + yy], rs.at[6 + 2 * xx + yy], to["core"]).start()

    def last():
        for xx in range(2):
            for yy in range(2):
                g = out.at[xx, yy, 1 - c]
                rcopy(g, g, ss.at[6 + 2 * xx + yy], rs.at[6 + 2 * xx + yy], to["core"]).wait()

    return begin, step_y, step_x, step_c, last


def gather_generic(tok, pk, mx, ex, sh, sv):
    every = ("dp", "ctx", "head")
    images = lax.all_gather(tok, ("ctx", "head"), axis=1, tiled=True)
    img = lax.dynamic_index_in_dim(images, coords()[1], 0, keepdims=False)
    spread = lax.all_gather(pk, every, axis=1, tiled=True)
    pko = lax.dynamic_index_in_dim(spread, lax.axis_index("head"), 0, keepdims=False)
    return [img, pko] + [lax.all_gather(t, every, axis=0, tiled=True) for t in (mx, ex, sh, sv)]


def exchange_kernel(src, dst, ls, ss, rs):
    x, y, c, z = coords()
    others = [(dy, dz) for dy in range(2) for dz in range(4) if dy or dz]
    enter([device(x, y ^ dy, c, z ^ dz) for dy, dz in others])
    me = y * 4 + z
    mine = pltpu.make_async_copy(src.at[me], dst.at[me], ls)
    mine.start()
    copies = []
    for i, (dy, dz) in enumerate(others):
        ty, tz = y ^ dy, z ^ dz
        cp = rcopy(src.at[ty * 4 + tz], dst.at[me], ss.at[i], rs.at[i], device(x, ty, c, tz))
        cp.start()
        copies.append(cp)
    mine.wait()
    for cp in copies:
        cp.wait()


def exchange(src, cid):
    D = pltpu.SemaphoreType.DMA
    return pl.pallas_call(
        exchange_kernel,
        out_shape=jax.ShapeDtypeStruct(src.shape, src.dtype),
        in_specs=[ANY],
        out_specs=ANY,
        scratch_shapes=[D, D((7,)), D((7,))],
        compiler_params=pltpu.CompilerParams(collective_id=cid, has_side_effects=True),
        name="exchange_heads_%d" % cid,
    )(src)


def dot(a, b):
    return jnp.dot(a, b, preferred_element_type=F32)


def dot_nt(a, b):
    return lax.dot_general(a, b, (((1,), (1,)), ((), ())), preferred_element_type=F32)


def row_norm(rows):
    mean = jnp.mean(rows, axis=-1, keepdims=True)
    centred = rows - mean
    inv = lax.rsqrt(jnp.mean(centred * centred, axis=-1, keepdims=True) + NORM_EPS)
    return centred * inv, inv


def project(g, rows, length, gain, shift, bias, pw, fi, nrm, qt, kv, kt, vt):
    heads = kv.shape[0]
    hd, step = HEAD_DIM, 256
    wide = 2 * hd * heads
    normed, _ = row_norm(rows.astype(F32))
    first = (normed * gain + shift).astype(BF)
    off = pl.multiple_of(g * step, step)
    fi[pl.ds(off, step), :] = first
    nrm[pl.ds(off, step), :] = normed.astype(BF)
    kvq = (dot(first, pw[...]) + bias).astype(BF).astype(F32)
    flip = kvq.T
    ones = jnp.where(lax.broadcasted_iota(jnp.int32, (16, step), 0) == 0, 1.0, 0.0)
    pos = off + lax.broadcasted_iota(jnp.int32, (step, 2 * hd), 0)
    lane = lax.broadcasted_iota(jnp.int32, (step, 2 * hd), 1)
    extra = jnp.where(lane == 0, jnp.where(pos < length, 0.0, MASKED), jnp.where(lane < 4, 1.0, 0.0)).astype(BF)
    for h in range(heads):
        kt[h, g] = flip[2 * h * hd : (2 * h + 1) * hd].astype(BF)
        vt[h, g] = jnp.concatenate([flip[(2 * h + 1) * hd : (2 * h + 2) * hd], ones], axis=0).astype(BF)
        qt[g, h] = (flip[wide + h * hd : wide + (h + 1) * hd] * (1.0 / math.sqrt(hd))).astype(BF)
        kv[h, pl.ds(off, step), : 2 * hd] = kvq[:, 2 * h * hd : (2 * h + 2) * hd].astype(BF)
        kv[h, pl.ds(off, step), 2 * hd :] = extra


def attend(h, j, c, qt, kv, vt, mixed, lse):
    keys = kv.shape[1]
    hd, step, chunk = HEAD_DIM, 256, 512
    per = chunk // step
    row = lax.broadcasted_iota(jnp.int32, (16, step), 0)
    unit = jnp.where(row == 0, 1.0, 0.0).astype(BF)
    g = (j // 2) * 4 + c * 2 + j % 2
    sl = pl.ds(pl.multiple_of(h * hd, hd), hd)
    qa = jnp.concatenate([qt[g, h], jnp.zeros((hd, step), BF), unit, jnp.zeros((2 * hd - 16, step), BF)], axis=0)
    top = jnp.full((1, step), MASKED, F32)
    acc = jnp.zeros((hd + 16, step), F32)
    for kc in range(keys // chunk):
        s = dot(kv[h, kc * chunk : (kc + 1) * chunk, :], qa)
        new = jnp.maximum(top, jnp.max(s, axis=0, keepdims=True))
        pb = jnp.exp2((s - new) * LOG2E).astype(BF)
        scale = jnp.exp2((top - new) * LOG2E)
        part = dot(vt[h, kc * per], pb[:step])
        for i in range(1, per):
            part += dot(vt[h, kc * per + i], pb[i * step : (i + 1) * step])
        acc = acc * scale + part
        top = new
    total = acc[hd : hd + 1]
    out = acc[:hd] / total
    lse[j, h] = top + jnp.log(total)
    for i in range(2):
        mixed[2 * j + i, sl, :] = out[:, i * 128 : (i + 1) * 128].astype(BF)


def forward_kernel(lens, img, pw, gain, shift, bias, mixed, lse, fi, nrm, qt, kv, kt, vt):
    x, y, c, z = coords()
    heads, keys = kv.shape[0], kv.shape[1]
    length = lens[y]

    def rows_of(g, carry):
        rows = img[pl.ds(2 * g, 2)].reshape(256, img.shape[2])
        project(g, rows, length, gain[...], shift[...], bias[...], pw, fi, nrm, qt, kv, kt, vt)
        return carry

    def step(s, carry):
        attend(s % heads, s // heads, c, qt, kv, vt, mixed, lse)
        return carry

    lax.fori_loop(0, keys // 256, rows_of, 0)
    lax.fori_loop(0, 4 * heads, step, 0)


FT = dict(
    small=(0.0, 4.6, 12.3, 15.5, 18.4),
    tok=((0.1, 12.0, 12.1, 24.0), (4.8, 18.9, 19.0, 27.0)),
    mx=(5.5, 12.2, (24.2, 24.3, 29.0), (18.8, 33.0, 36.0, 40.0), (46.0, 50.5)),
    ex=(5.4, 34.0, (44.5, 44.6, 51.0), 57.0),
    sh=(5.3, 28.01, (38.5, 38.6, 46.5), 54.5),
    att=(30.0, 1.95),
)


def own_columns(rows, g, part):
    width = rows.shape[1] // 3
    at = lambda t, h: rows[:, t * width + g * part + h * HEAD_DIM : t * width + g * part + (h + 1) * HEAD_DIM]
    heads = part // HEAD_DIM
    return jnp.concatenate([at(t, h) for h in range(heads) for t in (1, 2)] + [at(0, h) for h in range(heads)], axis=1)


def forward_all_kernel(
    lens, tok, cot, pkw, mx, ex, sh, v0, v1, v2, v3, v4, v5, v6, v7, v8,
    mix, mixed_o, lse_o, fi_o, nrm_o, qt_o, kv_o, kt_o, pw_o, vec, hid, mxo, exo, sho, cotx,
    pk, sv, img, pwg, svg, mixed, lse, fi, nrm, qt, kv, kt, vt, pw, bias,
    ls, tys, tzs, tzr, tcs, tcr, ps, pr, vs, vr, xs, xr, xl, osem, xps, xpr, *wsems,
):
    co = coords()
    x, y, c, z = co
    to = partners(*co)
    zh = z // 2
    heads, keys = kv.shape[0], kv.shape[1]
    width = img.shape[4]
    n_dev = 32
    others = [(dy, dz) for dy in range(2) for dz in range(4) if dy or dz]
    part = heads * HEAD_DIM
    enter([to["core"], to["x"]] + [device(x, y ^ dy, c, z ^ dz) for dy, dz in others])
    length = lens[y]
    ev = []

    def arrange():
        raw = pkw[...].astype(F32).reshape(3 * 8, pkw.shape[2])
        for g in range(4):
            pk[g] = own_columns(raw, g, part).astype(BF).reshape(3, 8, 3 * part)
        vs_ = (v0, v1, v2, v3, v4, v5, v6, v7, v8)
        lines = [jnp.concatenate([v[...].astype(F32).reshape(1, -1), jnp.zeros((1, 128 - v.shape[-1]), F32)], axis=1) for v in vs_]
        sv[...] = jnp.concatenate(lines + [jnp.zeros((7, 128), F32)], axis=0).astype(BF)

    ev.append((-0.1, arrange))

    row = lambda r: y if r == 0 else 1 - y

    def tz(r, i, k, ref, dst, name):
        return rcopy(ref, dst, tzs.at[r, i], tzr.at[r, k], to[name])

    def tcore(r, k, ref):
        return rcopy(ref, img.at[row(r), c, z ^ k], tcs.at[r, k], tcr.at[r, k], to["core"])

    spread = lambda: rcopy(tok.at[1 - y], img.at[y, c, z], tys.at[0], tys.at[1], to["y"])
    keep = lambda: pltpu.make_async_copy(tok.at[y], img.at[y, c, z], ls.at[0])

    def t_begin(r):
        d = img.at[row(r), c, z]
        if r == 0:
            spread().start()
            keep().start()
            own = tok.at[y]
        else:
            rcopy(d, d, tys.at[0], tys.at[1], to["y"]).wait()
            own = d
        tz(r, 0, 0, own, d, "z1").start()
        tz(r, 1, 1, own, d, "z2").start()
        tcore(r, 0, own).start()

    def t_land(r, k):
        d = img.at[row(r), c, z ^ k]
        tz(r, k - 1, k - 1, d, d, "z1").wait_recv()
        if k == 2:
            tz(r, 2, 2, d, d, "z1").start()
        tcore(r, k, d).start()

    for r in range(2):
        t = FT["tok"][r]
        ev.append((t[0], functools.partial(t_begin, r)))
        for k in range(1, 4):
            ev.append((t[k], functools.partial(t_land, r, k)))

    def t_last():
        for r in range(2):
            d = img.at[row(r), c, z]
            for i in range(3):
                tz(r, i, 0, d, d, "z1").wait_send()
            for k in range(4):
                tcore(r, k, d).wait_send()

    ev.append((1001.0, t_last))

    steps_v = small_gather(co, to, sv, svg, ls.at[1], vs, vr, False)
    steps_p = small_gather(co, to, pk, pwg, ls.at[4], ps, pr, True)
    for t, fv, fp in zip(FT["small"], steps_v, steps_p):
        ev.append((t, fv))
        ev.append((t + 0.05, fp))

    def unpack():
        small = width // n_dev
        big = hid.shape[1] // n_dev
        part = heads * HEAD_DIM
        across = lambda n: lax.broadcasted_iota(jnp.int32, (1, n), 1)
        down = lambda n: lax.broadcasted_iota(jnp.int32, (n, 1), 0)
        hot = lambda m: jnp.where(m, 1.0, 0.0).astype(BF)
        col = across(width)
        val = dot(svg[...].reshape(n_dev * 16, 128), hot(col % small == down(128)))
        val = jnp.where(col // small == down(n_dev * 16) // 16, val, 0.0)
        val = jnp.sum(val.reshape(n_dev, 16, width), axis=0)
        vec[...] = val
        col = across(hid.shape[1])
        eight = svg[...].astype(F32).reshape(n_dev, 16, 128)[:, 8, :].astype(BF)
        line = dot(eight, hot(col % big == down(128)))
        hid[...] = jnp.sum(jnp.where(col // big == down(n_dev), line, 0.0), axis=0, keepdims=True)
        dst = across(3 * part)
        head, off = dst // (2 * HEAD_DIM), dst % (2 * HEAD_DIM)
        hv = jnp.where(jnp.logical_and(dst < 2 * part, off >= HEAD_DIM), z * part + head * HEAD_DIM + off - HEAD_DIM, -1)
        hq = jnp.where(dst >= 2 * part, z * part + dst - 2 * part, -1)
        rows = val.astype(BF)
        bq = dot(rows, hot(hq == down(width)))
        bv = dot(rows, hot(hv == down(width)))
        bias[...] = bq[2:3] + bv[3:4]

    def flatten():
        def body(i, carry):
            blk = pwg[i // 4, (i // 2) % 2, i % 2].astype(F32)
            n = blk.shape[0] * blk.shape[1] * blk.shape[2]
            pw[pl.ds(pl.multiple_of(i * n, n), n), :] = blk.reshape(n, blk.shape[3]).astype(BF)
            return carry

        lax.fori_loop(0, 8, body, 0)

    ev.append((FT["small"][4] + 0.1, unpack))
    ev.append((FT["small"][4] + 0.2, flatten))

    def project_group(r, mine, p):
        cc = c if mine else 1 - c
        zz = zh if p == 0 else 1 - zh
        if r == 0 and mine and p == 0:
            keep().wait()
        if not mine:
            for k in (2 * p, 2 * p + 1):
                d = img.at[row(r), cc, z ^ k]
                rcopy(d, d, tcs.at[r, k], tcr.at[r, k], to["core"]).wait_recv()
        g = row(r) * 4 + cc * 2 + zz
        rows = img[row(r), cc, pl.ds(2 * zz, 2)].reshape(256, width)
        project(g, rows, length, vec[0:1, :], vec[1:2, :], bias[...], pw, fi, nrm, qt, kv, kt, vt)

    t_ready = FT["small"][4] + 0.3
    for p in range(2):
        for r in range(2):
            for mine in (True, False):
                t = max(FT["tok"][r][1 if p == 0 else 3] + (0.3 if mine else 0.6), t_ready + 0.01 * (r * 2 + (not mine)))
                ev.append((t, functools.partial(project_group, r, mine, p)))

    weight_gather(ev, co, to, mx, lambda px, py, cc, zz: mxo.at[px, py, cc, zz], wsems[:9], "yx", FT["mx"])
    half = ex.shape[2] // 2
    cols = lambda xx: pl.ds(pl.multiple_of(xx * half, half), half)
    ex_view = lambda yy, cc, zz: exo.at[:, yy, cc, zz]
    sh_view = lambda yy, cc, zz: sho.at[yy, cc, zz]
    ex_own = lambda: pltpu.make_async_copy(ex.at[:, :, cols(x)], exo.at[x, y, c, z], ls.at[2])
    ex_swap = lambda: rcopy(ex.at[:, :, cols(1 - x)], exo.at[x, y, c, z], xps.at[0], xpr.at[0], to["x"])
    sh_own = lambda: pltpu.make_async_copy(sh, sho.at[y, c, z], ls.at[3])
    cot_swap = lambda: rcopy(cot, cotx, xps.at[1], xpr.at[1], to["x"])

    def swap():
        ex_own().start()
        ex_swap().start()
        cot_swap().start()

    def ex_ready():
        ex_own().wait()
        ex_swap().wait()

    ev.append((0.6, swap))
    ev.append((1003.0, lambda: cot_swap().wait()))
    half_gather(ev, co, to, ex_ready, lambda: None, ex_view(y, c, z), ex_view, wsems[9:15], FT["ex"])
    half_gather(ev, co, to, lambda: sh_own().start(), lambda: sh_own().wait(), sh, sh_view, wsems[15:21], FT["sh"])

    stored = [(fi, fi_o), (nrm, nrm_o), (qt, qt_o), (kv, kv_o), (kt, kt_o), (pw, pw_o), (mixed, mixed_o), (lse, lse_o)]
    store = lambda i: pltpu.make_async_copy(stored[i][0], stored[i][1], osem.at[i])

    def store_first():
        for i in range(6):
            store(i).start()

    t_att, t_step = FT["att"]
    steps = 4 * heads
    t_end = t_att + steps * t_step
    ev.append((t_att + 0.001, store_first))

    me = y * 4 + z

    def target(q):
        w = 3 - q
        return [(w // 2, 2 * (w % 2)), (w // 2, 2 * (w % 2) + 1)]

    def xcopy(dy, dz):
        i = dy * 4 + dz
        return rcopy(mixed.at[(y ^ dy) * 4 + (z ^ dz)], mix.at[me], xs.at[i], xr.at[i], device(x, y ^ dy, c, z ^ dz))

    mine_copy = lambda: pltpu.make_async_copy(mixed.at[me], mix.at[me], xl)

    def send_group(q):
        for dy, dz in target(q):
            if dy or dz:
                xcopy(dy, dz).start()
            else:
                mine_copy().start()

    for q in range(4):
        ev.append((t_att + (q + 1) * heads * t_step + 0.002, functools.partial(send_group, q)))

    def finish():
        store(6).start()
        store(7).start()
        for dy, dz in others:
            xcopy(dy, dz).wait()
        mine_copy().wait()

    ev.append((t_end + 3.8, finish))

    def drain():
        for i in range(8):
            store(i).wait()

    ev.append((1002.0, drain))

    ev.sort(key=lambda e: e[0])
    for t, fn in ev:
        if t < t_att:
            fn()

    def step(s, carry):
        for k in range(steps):
            here = [fn for t, fn in ev if t_att + k * t_step <= t < t_att + (k + 1) * t_step]
            if here:

                @pl.when(s == k)
                def _():
                    for fn in here:
                        fn()

        attend(s % heads, (3 - s // heads) ^ (2 * y + zh), c, qt, kv, vt, mixed, lse)
        return carry

    lax.fori_loop(0, steps, step, 0)
    for t, fn in ev:
        if t >= t_end:
            fn()


def forward_all(lens, tok, cot, pkw, mx, ex, sh, vecs):
    D, V, S = pltpu.SemaphoreType.DMA, pltpu.VMEM, jax.ShapeDtypeStruct
    shard, width = tok.shape[1], tok.shape[2]
    cols = pkw.shape[2] // 4
    pk_shape = (3, 8, cols)
    heads = cols // (3 * HEAD_DIM)
    keys = 16 * shard
    n = keys // 256
    lead = (2, SPLIT, SPLIT, 4)
    part = heads * HEAD_DIM
    hidden = ex.shape[2]
    outs = [
        S((8, part, shard), BF),
        S((8, part, shard), BF),
        S((4, heads, 1, 256), F32),
        S((keys, width), BF),
        S((keys, width), BF),
        S((n, heads, HEAD_DIM, 256), BF),
        S((heads, keys, 4 * HEAD_DIM), BF),
        S((heads, n, HEAD_DIM, 256), BF),
        S((width, cols), BF),
        S((16, width), F32),
        S((1, hidden), F32),
        S(lead + mx.shape, BF),
        S(lead + (3, 8, hidden // 2), BF),
        S(lead[1:] + sh.shape, BF),
        S(cot.shape, BF),
    ]
    wsem = [D, D((3,)), D((3,)), D((4,)), D((4,)), D((2, 4)), D((2, 4)), D((4,)), D((4,))]
    wsem += [D((3,)), D((3,)), D((4,)), D((4,)), D((2,)), D((2,))] * 2
    scr = [V((4,) + pk_shape, BF), V((16, 128), BF)]
    scr += [V((2, 2, 4) + tok.shape[1:], BF), V(lead + pk_shape, BF), V(lead + (16, 128), BF), V((8, part, shard), BF), V((4, heads, 1, 256), F32)]
    scr += [V((keys, width), BF), V((keys, width), BF), V((n, heads, HEAD_DIM, 256), BF), V((heads, keys, 4 * HEAD_DIM), BF)]
    scr += [V((heads, n, HEAD_DIM, 256), BF), V((heads, n, HEAD_DIM + 16, 256), BF), V((width, cols), BF), V((1, cols), F32)]
    scr += [D((5,)), D((2,)), D((2, 3)), D((2, 3)), D((2, 4)), D((2, 4)), D((10,)), D((10,)), D((10,)), D((10,)), D((8,)), D((8,)), D, D((8,)), D((2,)), D((2,))]
    return pl.pallas_call(
        forward_all_kernel,
        out_shape=outs,
        in_specs=[SM, ANY, ANY, VM, ANY, ANY, ANY] + [VM] * 9,
        out_specs=[ANY] * 9 + [VM] * 2 + [ANY] * 4,
        scratch_shapes=scr + wsem,
        compiler_params=pltpu.CompilerParams(collective_id=0, has_side_effects=True, vmem_limit_bytes=62 << 20),
        name="gather_attention_forward",
    )(lens, tok, cot, pkw, mx, ex, sh, *vecs)


def attention_forward(lens, img, pw, gain, shift, bias):
    heads = pw.shape[1] // (3 * HEAD_DIM)
    keys = img.shape[0] * img.shape[1]
    width = heads * HEAD_DIM
    n = keys // 256
    outs = [
        jax.ShapeDtypeStruct((8, width, 128), BF),
        jax.ShapeDtypeStruct((4, heads, 1, 256), F32),
        jax.ShapeDtypeStruct((keys, img.shape[2]), BF),
        jax.ShapeDtypeStruct((keys, img.shape[2]), BF),
        jax.ShapeDtypeStruct((n, heads, HEAD_DIM, 256), BF),
        jax.ShapeDtypeStruct((heads, keys, 4 * HEAD_DIM), BF),
        jax.ShapeDtypeStruct((heads, n, HEAD_DIM, 256), BF),
    ]
    return pl.pallas_call(
        forward_kernel,
        out_shape=outs,
        in_specs=[SM] + [VM] * 5,
        out_specs=[VM] * 7,
        scratch_shapes=[pltpu.VMEM((heads, n, HEAD_DIM + 16, 256), BF)],
        compiler_params=pltpu.CompilerParams(vmem_limit_bytes=50 << 20),
        name="attention_forward",
    )(lens, img, pw, gain, shift, bias)


def dot_tn(a, b):
    return lax.dot_general(a, b, (((0,), (0,)), ((), ())), preferred_element_type=F32)


def dense_body(
    tok, cot, cotx, mix, vec, hid, mx_h, ex_h, sh_h,
    base, upx, act, sin, cot2, gpre, gres, gresf, send, s4, s5, s6, s7, s8,
    mx, ex, sh, down_out, down_in, sems, ss, rs, then, early,
):
    co = coords()
    x = co[0]
    to = partners(*co)["x"]
    images, shard, width = tok.shape
    rows = images * shard
    half = ex.shape[1]
    n = half // width
    load = [pltpu.make_async_copy(mx_h, mx, sems.at[0])]
    for i in range(n):
        cols = slice(i * width, (i + 1) * width)
        load.append(pltpu.make_async_copy(ex_h.at[:, cols], ex.at[:, cols], sems.at[1 + i]))
        load.append(pltpu.make_async_copy(sh_h.at[cols, :], sh.at[cols, :], sems.at[1 + n + i]))
    for cp in load:
        cp.start()
    cin = cot[...].reshape(rows, width)
    cf = cin.astype(F32)
    s7[...] = jnp.sum(cf, axis=0, keepdims=True)
    cot2[:rows, :] = cin
    cot2[rows:, :] = cotx[...].reshape(rows, width)

    def sin_copy(i):
        return rcopy(sin.at[i * shard : (i + 1) * shard], sin.at[rows + i * shard : rows + (i + 1) * shard], ss.at[i], rs.at[i], to)

    def down_copy(i):
        return rcopy(down_out.at[i], down_in.at[i], ss.at[images + i], rs.at[images + i], to)

    load[0].wait()
    keep = []
    for i in range(images):
        res = tok[i].astype(F32) + dot_tn(mix[i], mx[...]) + vec[4:5, :]
        nr, iv = row_norm(res)
        sin[i * shard : (i + 1) * shard, :] = (nr * vec[5:6, :] + vec[6:7, :]).astype(BF)
        sin_copy(i).start()
        keep.append((res, nr, iv))
    residual, normed, inv = [jnp.concatenate(t, axis=0) for t in zip(*keep)]
    own = pl.ds(pl.multiple_of(x * half, half), half)
    s8[...] = jnp.zeros_like(s8)

    def chunks(lo, hi):
        up = jnp.zeros((hi - lo, width), F32)
        down = jnp.zeros((hi - lo, width), F32)
        second = sin[lo:hi, :]
        grad = cot2[lo:hi, :]
        for i in range(n):
            cols = slice(i * width, (i + 1) * width)
            if lo == 0:
                load[1 + 2 * i].wait()
                load[2 + 2 * i].wait()
            there = pl.ds(pl.multiple_of(x * half + i * width, width), width)
            pre = dot(second, ex[:, cols]) + hid[:, there]
            cum = 0.5 * (1.0 + lax.erf(pre * (1.0 / math.sqrt(2.0))))
            slope = cum + pre * (jnp.exp(-0.5 * pre * pre) * (1.0 / math.sqrt(2.0 * math.pi)))
            a = (pre * cum).astype(BF)
            act[lo:hi, cols] = a
            g = dot_nt(grad, sh[cols, :]) * slope
            s8[:, there] += jnp.sum(g, axis=0, keepdims=True)
            gb = g.astype(BF)
            gpre[lo:hi, cols] = gb
            up += dot(a, sh[cols, :])
            down += dot_nt(gb, ex[:, cols])
        return up, down

    up, down = chunks(0, rows)
    then()
    base[...] = (residual + up + vec[7:8, :]).reshape(images, shard, width)
    for i in range(images):
        sin_copy(i).wait()
        other_up, other_down = chunks(rows + i * shard, rows + (i + 1) * shard)
        down_out[i] = other_down.astype(BF)
        down_copy(i).start()
        upx[i] = other_up.astype(BF)
    early()
    rest = []
    for i in range(images):
        down_copy(i).wait()
        part = slice(i * shard, (i + 1) * shard)
        total = down[part] + down_in[i].astype(F32)
        nr = normed[part]
        scaled = total * vec[5:6, :]
        m1 = jnp.mean(scaled, axis=-1, keepdims=True)
        m2 = jnp.mean(scaled * nr, axis=-1, keepdims=True)
        gr = cf[part] + inv[part] * (scaled - m1 - nr * m2)
        gresf[i] = gr
        gb = gr.astype(BF)
        gres[part, :] = gb
        val = dot_nt(mx[...], gb).astype(BF)
        send[4 * i : 4 * (i + 1)] = val.reshape(4, width // 4, shard)
        sums = [jnp.sum(t, axis=0, keepdims=True) for t in (gr, total * nr, total)]
        rest.append(sums)
    for ref, a, b in zip((s4, s5, s6), *rest):
        ref[...] = a + b


def hand_over_kernel(*refs):
    n = 6
    src, vec, dst, outs = refs[:n], refs[n], refs[n + 1 : 2 * n + 1], refs[2 * n + 1 :]
    for i in range(n):
        dst[i][...] = src[i][...]
    for i, o in enumerate(outs):
        line = 16 if i == 8 else i
        o[...] = vec[line : line + 1, : o.shape[0]].reshape(o.shape[0])


def hand_over(arrays, vec, small, big):
    S = jax.ShapeDtypeStruct
    outs = [S(t.shape, t.dtype) for t in arrays] + [S((small,), F32)] * 8 + [S((big,), F32)]
    return pl.pallas_call(
        hand_over_kernel,
        out_shape=outs,
        in_specs=[VM] * 7,
        out_specs=[VM] * 15,
        name="hand_over",
    )(*arrays, vec)


def split3(value):
    hi = value.astype(BF)
    rest = value - hi.astype(F32)
    mid = rest.astype(BF)
    low = (rest - mid.astype(F32)).astype(BF)
    return hi, mid, low


def pick(value, hot):
    a, b, d = split3(value)
    return dot(a, hot) + dot(b, hot) + dot(d, hot)


def stacked_extra(lead, value, row):
    a, b, d = (t.astype(F32) for t in split3(value))
    out = jnp.where(row == 1, a, 0.0) + jnp.where(row == 2, b, 0.0) + jnp.where(row == 3, d, 0.0)
    return (jnp.where(row == 0, lead, 0.0) + out).astype(BF)


def backward_step(h, j, c, grad, mixed, lse, qt, kv, kt, dkv, dqt):
    keys = kv.shape[1]
    hd, step, chunk = HEAD_DIM, 256, 512
    per = chunk // step
    g = (j // 2) * 4 + c * 2 + j % 2
    sl = pl.ds(pl.multiple_of(h * hd, hd), hd)
    do = jnp.concatenate([grad[2 * j, sl, :], grad[2 * j + 1, sl, :]], axis=1)
    mx = jnp.concatenate([mixed[2 * j, sl, :], mixed[2 * j + 1, sl, :]], axis=1)
    delta = jnp.sum(do.astype(F32) * mx.astype(F32), axis=0, keepdims=True)
    row = lax.broadcasted_iota(jnp.int32, (16, step), 0)
    none = jnp.zeros((hd, step), BF)
    rest = jnp.zeros((2 * hd - 16, step), BF)
    qh = qt[g, h]
    qa = jnp.concatenate([qh, none, stacked_extra(1.0, -lse[j, h], row), rest], axis=0)
    da = jnp.concatenate([none, do, stacked_extra(0.0, -delta, row), rest], axis=0)
    qr = jnp.concatenate([qh, none], axis=0).astype(F32).T.astype(BF)
    dr = jnp.concatenate([none, do], axis=0).astype(F32).T.astype(BF)
    dq = jnp.zeros((hd, step), F32)
    for kc in range(keys // chunk):
        rows = slice(kc * chunk, (kc + 1) * chunk)
        block = kv[h, rows, :]
        p = jnp.exp2(dot(block, qa) * LOG2E)
        dp = dot(block, da)
        ds = (p * dp).astype(BF)
        dkv[h, rows, :] += dot(ds, qr) + dot(p.astype(BF), dr)
        for i in range(per):
            dq += dot(kt[h, kc * per + i], ds[i * step : (i + 1) * step])
    dqt[j, sl, :] = (dq * (1.0 / math.sqrt(hd))).astype(BF)


def add_into(dst, src, lead, n):
    def body(i, carry):
        dst[lead + (i,)] = dst[lead + (i,)] + src[i]
        return carry

    lax.fori_loop(0, n, body, 0)


def halving(co, to, G, u, bufs, ss, rs, order, finish):
    x, y, c, z = co
    zh, zl = z // 2, z % 2
    r0, r1, r2, r3, r4 = bufs
    a, b = order
    first = (lambda n: G.at[u, 1 - x, n, c]) if a == "x" else (lambda n: G.at[u, n, 1 - y, c])
    keep = (lambda n: (u, x, n, c)) if a == "x" else (lambda n: (u, n, y, c))
    second = G.at[u, x, 1 - y, c] if b == "y" else G.at[u, 1 - x, y, c]

    def cp0(i):
        return rcopy(G.at[u, i // 2, i % 2, 1 - c], r0.at[u, i], ss.at[u, i], rs.at[u, i], to["core"])

    def cp1(n):
        return rcopy(first(n), r1.at[u, n], ss.at[u, 4 + n], rs.at[u, 4 + n], to[a])

    cp2 = lambda: rcopy(second, r2.at[u], ss.at[u, 6], rs.at[u, 6], to[b])
    cp3 = lambda n: rcopy(G.at[u, x, y, c, 2 * n + 1 - zl], r3.at[u, n], ss.at[u, 7 + n], rs.at[u, 7 + n], to["z1"])
    cp4 = lambda: rcopy(G.at[u, x, y, c, 2 * (1 - zh) + zl], r4.at[u], ss.at[u, 9], rs.at[u, 9], to["z2"])

    def core_send():
        for i in range(4):
            cp0(i).start()

    def core_land():
        for i in range(4):
            cp0(i).wait()
            add_into(G, r0.at[u, i], (u, i // 2, i % 2, c), 4)

    def a_send():
        for n in range(2):
            cp1(n).start()

    def a_wait():
        for n in range(2):
            cp1(n).wait()

    def a_add():
        for n in range(2):
            add_into(G, r1.at[u, n], keep(n), 4)
        cp2().start()

    def b_land():
        cp2().wait()
        add_into(G, r2.at[u], (u, x, y, c), 4)
        for n in range(2):
            cp3(n).start()

    def z1_land():
        for n in range(2):
            cp3(n).wait()
            here = (u, x, y, c, 2 * n + zl)
            G[here] = G[here] + r3[u, n]
        cp4().start()

    def z2_land():
        cp4().wait()
        finish(G[u, x, y, c, z].astype(F32) + r4[u].astype(F32))

    return dict(core_send=core_send, core_land=core_land, a_send=a_send, a_wait=a_wait, a_add=a_add, b_land=b_land, z1_land=z1_land, z2_land=z2_land)


def half_sum(co, to, H, b, r0, r1, r3, r4, ss, rs, finish):
    x, y, c, z = co
    zh, zl = z // 2, z % 2
    cp0 = lambda i: rcopy(H.at[b, i, 1 - c], r0.at[b, i], ss.at[b, i], rs.at[b, i], to["core"])
    cp1 = lambda: rcopy(H.at[b, 1 - y, c], r1.at[b], ss.at[b, 2], rs.at[b, 2], to["y"])
    cp3 = lambda n: rcopy(H.at[b, y, c, 2 * n + 1 - zl], r3.at[b, n], ss.at[b, 3 + n], rs.at[b, 3 + n], to["z1"])
    cp4 = lambda: rcopy(H.at[b, y, c, 2 * (1 - zh) + zl], r4.at[b], ss.at[b, 5], rs.at[b, 5], to["z2"])

    def core_send():
        for i in range(2):
            cp0(i).start()

    def core_land():
        for i in range(2):
            cp0(i).wait()
            add_into(H, r0.at[b, i], (b, i, c), 4)

    def y_send():
        cp1().start()

    def y_land():
        cp1().wait()
        add_into(H, r1.at[b], (b, y, c), 4)
        for n in range(2):
            cp3(n).start()

    def z1_land():
        for n in range(2):
            cp3(n).wait()
            here = (b, y, c, 2 * n + zl)
            H[here] = H[here] + r3[b, n]
        cp4().start()

    def z2_land():
        cp4().wait()
        finish(H[b, y, c, z].astype(F32) + r4[b].astype(F32))

    return core_send, core_land, y_send, y_land, z1_land, z2_land


def half_sum_line(co, to, H, b, r0, r1, r3, r4, ss, rs, finish):
    x, y, c, z = co
    zh, zl = z // 2, z % 2
    cp0 = lambda i: rcopy(H.at[b, i, 1 - c], r0.at[b, i], ss.at[b, i], rs.at[b, i], to["core"])
    cp3 = lambda i, n: rcopy(H.at[b, i, c, 2 * n + 1 - zl], r1.at[b, 2 * i + n], ss.at[b, 2 + 2 * i + n], rs.at[b, 2 + 2 * i + n], to["z1"])
    cp4 = lambda i: rcopy(H.at[b, i, c, 2 * (1 - zh) + zl], r3.at[b, i], ss.at[b, 6 + i], rs.at[b, 6 + i], to["z2"])
    cp1 = lambda: rcopy(H.at[b, 1 - y, c, z], r4.at[b], ss.at[b, 8], rs.at[b, 8], to["y"])

    def core_send():
        for i in range(2):
            cp0(i).start()

    def core_land():
        for i in range(2):
            cp0(i).wait()
            add_into(H, r0.at[b, i], (b, i, c), 4)

    def z1_send():
        for i in range(2):
            for n in range(2):
                cp3(i, n).start()

    def z1_land():
        for i in range(2):
            for n in range(2):
                cp3(i, n).wait()
                here = (b, i, c, 2 * n + zl)
                H[here] = H[here] + r1[b, 2 * i + n]
        for i in range(2):
            cp4(i).start()

    def z2_land():
        for i in range(2):
            cp4(i).wait()
            here = (b, i, c, z)
            H[here] = H[here] + r3[b, i]
        cp1().start()

    def y_land():
        cp1().wait()
        finish(H[b, y, c, z].astype(F32) + r4[b].astype(F32))

    return core_send, core_land, z1_send, z1_land, z2_land, y_land


TIMES = dict(
    core=(0.95, 1.31, 1.4, 1.5, 2.6),
    send=(0.96, 1.32, 10.25, 1.51),
    y=(10.2, 16.0, 21.0, 15.5),
    z1=(19.5, 21.1, 28.25, 24.0),
    z2=(27.0, 31.5, 36.5, 30.0),
    mixer=(16.2, 24.5, 28.3, 38.0),
    att=(4.0, 1.6),
    walk=(0.1, 0.95, 3.0, 3.9),
    fold=(2.2, 5.0),
    half=(8.6, 13.5, 20.5, 26.5),
    full=(16.0, 21.5, 27.2, 35.0),
    last=(22.0, 27.4),
    packed=(5.2, 9.0, 14.5, 18.0, 33.0),
    vec=(8.4, 9.1, 14.6, 18.1, 26.0, 34.0),
)


def backward_kernel(
    tok, cot_in, cotx, mix, vec, hid, mx_h, ex_h, sh_h, mixed_h, lse_h, qt_h, kv_h, kt_h, fi_h, nrm_h, pw_h,
    out_in, out_s, out_e, out_m, out_b, out_p, out_v,
    mx, ex, sh, down_out, down_in, base, upx, act, sin, cot, gpre, gres, gresf, send, s4, s5, s6, s7, s8, wsem, dss, drs,
    mixed, lse, qt, kv, kt, fi, nrm, pw, lsem, grad, G, r0, r1, r2, r3, r4, H, h0, h1, h3, h4, F, xo, xe, ub,
    dkv, dqt, dall, GF, q0, q1, q2, q3, sq, GP, p0, p1, p2, p3, V, vr,
    els, ess, ers, gss, grs, hss, hrs, xss, xrs, qss, qrs, pss, prs, vss, vrs,
):
    co = coords()
    x, y, c, z = co
    to = partners(*co)
    zh, zl = z // 2, z % 2
    heads, keys = kv.shape[0], kv.shape[1]
    width = cot.shape[1]
    rows = gres.shape[0]
    gain = vec
    late = [(mixed_h, mixed), (lse_h, lse), (qt_h, qt), (kv_h, kv), (kt_h, kt), (fi_h, fi), (nrm_h, nrm), (pw_h, pw)]

    def local(i):
        return pltpu.make_async_copy(late[i][0], late[i][1], lsem.at[i])

    others = [(dy, dz) for dy in range(2) for dz in range(4) if dy or dz]
    enter([to["core"], to["x"]] + [device(x, y ^ dy, c, z ^ dz) for dy, dz in others])
    me = y * 4 + z

    def exch(i):
        dy, dz = others[i]
        return rcopy(send.at[(y ^ dy) * 4 + (z ^ dz)], grad.at[me], ess.at[i], ers.at[i], device(x, y ^ dy, c, z ^ dz))

    mine = pltpu.make_async_copy(send.at[me], grad.at[me], els)
    ev = []
    n_hid = 2 * act.shape[1] // width

    def shrink_all():
        span = act.shape[1] // 4

        def body(t, carry):
            val = dot_tn(act[:, pl.ds(pl.multiple_of(t * span, span), span)], cot[...]).astype(BF)
            val = val.reshape(4, 4, 3, 8, width)
            for zz in range(4):
                for i in range(4):
                    H[i // 2, t // 2, t % 2, zz, i % 2] = val[zz, i]
            return carry

        lax.fori_loop(0, 4, body, 0)

    def expand_one(q):
        for xx in range(2):
            val = dot_tn(sin[:, xx * width // 2 : (xx + 1) * width // 2], gpre[:, q * width : (q + 1) * width]).astype(BF)
            val = val.reshape(2, 2, 4, 3, 8, width)
            for i in range(16):
                H[2 + q, i // 8, (i // 4) % 2, i % 4, xx] = val[i // 8, (i // 4) % 2, i % 4]

    def mixer_one():
        half = rows // 2
        for t in range(2):
            sl = slice(t * width // 2, (t + 1) * width // 2)
            val = dot(mix[0, sl, :], gres[:half]) + dot(mix[1, sl, :], gres[half:])
            G[0, t] = val.astype(BF).reshape(2, 2, 4, 3, 8, width)

    def run(fns):
        for fn in fns:
            fn()

    def lanes(xx, q):
        return pl.ds(pl.multiple_of((xx * (n_hid // 2) + q) * width, width), width)

    swap = lambda q: rcopy(xo.at[q], xe.at[q], xss.at[q], xrs.at[q], to["x"])
    up_copy = lambda: rcopy(upx, ub, xss.at[2], xrs.at[2], to["x"])

    def done_s(b, val):
        for i in range(2):
            out_s[2 * b + i] = val[i]

    def done_e(q, val):
        F[...] = val
        out_e[:, :, lanes(x, q)] = F[x]
        xo[q] = F[1 - x].astype(BF)
        swap(q).start()

    def landed_e(q):
        swap(q).wait()
        out_e[:, :, lanes(1 - x, q)] = xe[q].astype(F32)

    def landed_up():
        up_copy().wait()
        for i in range(2):
            out_b[i] = (base[i] + ub[i].astype(F32)).astype(BF)

    ev.append((0.0, shrink_all))
    ev.append((0.6, functools.partial(expand_one, 0)))
    ev.append((0.8, functools.partial(expand_one, 1)))
    ev.append((1.05, mixer_one))
    ev.append((1.2, lambda: up_copy().start()))
    for b in range(4):
        fin = functools.partial(done_s, b) if b < 2 else functools.partial(done_e, b - 2)
        st = (half_sum if b < 3 else half_sum_line)(co, to, H, b, h0, h1, h3, h4, hss, hrs, fin)
        for t, fn in zip(((0.5, 0.51, 0.7, 0.9)[b], TIMES["core"][b], TIMES["send"][b], TIMES["y"][b], TIMES["z1"][b], TIMES["z2"][b]), st):
            ev.append((t, fn))
        if b >= 2:
            ev.append((TIMES["z2"][b] + 4.0, functools.partial(landed_e, b - 2)))
    ev.append((TIMES["z2"][3] + 4.1, landed_up))
    st = halving(co, to, G, 0, (r0, r1, r2, r3, r4), gss, grs, "xy", lambda val: out_m.__setitem__(Ellipsis, val))
    ev.append((1.1, st["core_send"]))
    ev.append((TIMES["core"][4], lambda: run([st["core_land"], st["a_send"]])))
    for t, names in zip(TIMES["mixer"], (("a_wait", "a_add"), ("b_land",), ("z1_land",), ("z2_land",))):
        ev.append((t, functools.partial(run, [st[k] for k in names])))

    def zero():
        def body(i, carry):
            for h in range(heads):
                dkv[h, pl.ds(pl.multiple_of(i * 256, 256), 256), :] = jnp.zeros((256, 2 * HEAD_DIM), F32)
            return carry

        lax.fori_loop(0, keys // 256, body, 0)

    def arrive(q):
        if q == 0:
            mine.wait()
            for i in range(5):
                local(i).wait()
        for i in range(7):
            if 2 * others[i][0] + others[i][1] // 2 == q:
                exch(i).wait()

    ev.append((1.3, zero))
    steps = 4 * heads
    t_att, t_step = TIMES["att"]
    t_end = t_att + t_step * steps
    for q in range(4):
        ev.append((t_att + heads * q * t_step + 0.001, functools.partial(arrive, q)))

    def begin():
        mine.start()
        for i in range(7):
            exch(i).start()
        V[...] = jnp.zeros_like(V)
        for i, ref in ((4, s4), (5, s5), (6, s6), (7, s7)):
            V[i : i + 1, :] = ref[...]
        for i in range(n_hid):
            V[8 + i : 9 + i, :] = s8[:, i * width : (i + 1) * width]

    ev.append((1.0, begin))

    def group(slot, mine_rows):
        cc = c if mine_rows else 1 - c
        yy = slot // 2
        g = yy * 4 + cc * 2 + slot % 2
        off = pl.multiple_of(g * 256, 256)
        rs_ = pl.ds(off, 256)
        wide = 2 * HEAD_DIM * heads
        dk = jnp.concatenate([dkv[h, rs_, :].astype(BF) for h in range(heads)], axis=1)
        gf = dot_nt(dk, pw[:, :wide])
        dall[rs_, :wide] = dk
        sums = jnp.sum(dk.astype(F32), axis=0, keepdims=True)
        V[16:17, :wide] += sums
        if mine_rows:
            dq = dqt[slot].astype(F32).T.astype(BF)
            gf += dot_nt(dq, pw[:, wide:])
            dall[rs_, wide:] = dq
            V[17:18, : dq.shape[1]] += jnp.sum(dq.astype(F32), axis=0, keepdims=True)
        else:
            dall[rs_, wide:] = jnp.zeros((256, heads * HEAD_DIM), BF)
        V[0:1, :] += jnp.sum(gf * nrm[rs_, :].astype(F32), axis=0, keepdims=True)
        V[1:2, :] += jnp.sum(gf, axis=0, keepdims=True)
        GF[yy, cc, pl.ds(2 * (slot % 2), 2)] = gf.astype(BF).reshape(2, 2, 64, width)

    def q_core(r):
        yy = rowof(r)
        return rcopy(GF.at[yy, 1 - c], q0.at[r], qss.at[r], qrs.at[r], to["core"])

    def q_z1(r, f, n):
        i = 2 + 4 * r + 2 * f + n
        return rcopy(GF.at[rowof(r), c, 2 * n + 1 - zl, f], q1.at[r, f, n], qss.at[i], qrs.at[i], to["z1"])

    def q_z2(r, f):
        i = 10 + 2 * r + f
        return rcopy(GF.at[rowof(r), c, 2 * (1 - zh) + zl, f], q2.at[r, f], qss.at[i], qrs.at[i], to["z2"])

    def q_y(f):
        return rcopy(sq.at[f], q3.at[f], qss.at[14 + f], qrs.at[14 + f], to["y"])

    def rowof(r):
        return 1 - y if r == 0 else y

    def walk(mine_rows, r):
        def body(i, carry):
            group(2 * rowof(r) + i, mine_rows)
            return carry

        lax.fori_loop(0, 2, body, 0)
        if not mine_rows:
            q_core(r).start()

    def q_sum(r):
        q_core(r).wait()
        yy = rowof(r)

        def body(i, carry):
            GF[yy, c, i // 2, i % 2] = GF[yy, c, i // 2, i % 2] + q0[r, i // 2, i % 2]
            return carry

        lax.fori_loop(0, 8, body, 0)
        if r == 0:
            q_send(0, 0)

    def q_send(r, f):
        for n in range(2):
            q_z1(r, f, n).start()

    chunks = [(r, f) for r in range(2) for f in range(2)]

    def q_half(i):
        r, f = chunks[i]
        for n in range(2):
            q_z1(r, f, n).wait()
        if i + 2 < 4:
            q_send(*chunks[i + 2])
        for n in range(2):
            here = (rowof(r), c, 2 * n + zl, f)
            GF[here] = GF[here] + q1[r, f, n]
        q_z2(r, f).start()

    def finish(img, f, total):
        rs_ = slice(64 * f, 64 * (f + 1))
        normed, inv = row_norm(tok[img, rs_].astype(F32))
        scaled = total * gain[0:1, :]
        m1 = jnp.mean(scaled, axis=-1, keepdims=True)
        m2 = jnp.mean(scaled * normed, axis=-1, keepdims=True)
        out_in[img, rs_] = (gresf[img, rs_] + inv * (scaled - m1 - normed * m2)).astype(BF)

    def q_full(i):
        r, f = chunks[i]
        q_z2(r, f).wait()
        total = GF[rowof(r), c, z, f].astype(F32) + q2[r, f].astype(F32)
        if r == 0:
            sq[f] = total.astype(BF)
            q_y(f).start()
        else:
            finish(y, f, total)

    def q_last(f):
        q_y(f).wait()
        finish(1 - y, f, q3[f].astype(F32))

    def late_rows():
        for i in range(5, 8):
            local(i).wait()

    ev.append((t_end + 0.05, late_rows))
    for i in range(4):
        ev.append((t_end + TIMES["walk"][i], functools.partial(walk, i % 2 == 1, i // 2)))
        ev.append((t_end + TIMES["half"][i], functools.partial(q_half, i)))
        ev.append((t_end + TIMES["full"][i], functools.partial(q_full, i)))
    for f in range(2):
        ev.append((t_end + TIMES["fold"][f], functools.partial(q_sum, f)))
        if f == 0:
            ev.append((t_end + TIMES["walk"][3] + 0.1, functools.partial(q_send, 0, 1)))
        ev.append((t_end + TIMES["last"][f], functools.partial(q_last, f)))

    def packed():
        val = dot_tn(fi[...], dall[...]).astype(BF)
        GP[0] = val.reshape(2, 2, 2, 4, 3, 8, val.shape[1])
        for i in range(4):
            p_core(i).start()

    def p_core(i):
        return rcopy(GP.at[0, i // 2, i % 2, 1 - c], p0.at[i], pss.at[i], prs.at[i], to["core"])

    def p_a(n):
        return rcopy(GP.at[0, 1 - x, n, c], p1.at[n], pss.at[4 + n], prs.at[4 + n], to["x"])

    p_b = lambda: rcopy(GP.at[0, x, 1 - y, c], p2, pss.at[6], prs.at[6], to["y"])
    p_z = lambda k: rcopy(GP.at[0, x, y, c, z ^ k], p3.at[k - 1], pss.at[6 + k], prs.at[6 + k], to["z%d" % k])

    def packed_core():
        for i in range(4):
            p_core(i).wait()
            add_into(GP, p0.at[i], (0, i // 2, i % 2, c), 4)
        for n in range(2):
            p_a(n).start()

    def packed_a():
        for n in range(2):
            p_a(n).wait()
            add_into(GP, p1.at[n], (0, x, n, c), 4)
        p_b().start()

    def packed_b():
        p_b().wait()
        add_into(GP, p2, (0, x, y, c), 4)
        for k in (1, 2, 3):
            p_z(k).start()

    def packed_z():
        GP[0, 1 - x, y, c, z] = GP[0, x, y, c, z]
        for k in (1, 2, 3):
            p_z(k).wait()
            GP[0, 1 - x, y, c, z ^ k] = p3[k - 1]
        part = heads * HEAD_DIM
        for g in range(4):
            val = GP[0, 1 - x, y, c, g].astype(F32)
            for h in range(heads):
                spots = ((1, 2 * h), (2, 2 * h + 1), (0, 2 * heads + h))
                for t, i in spots:
                    lo = t * width + g * part + h * HEAD_DIM
                    out_p[:, :, lo : lo + HEAD_DIM] = val[:, :, i * HEAD_DIM : (i + 1) * HEAD_DIM]

    def v_copy(i):
        return rcopy(V.at[0:16], vr.at[i], vss.at[i], vrs.at[i], to[("core", "x", "y", "z1", "z2")[i]])

    def vec_start():
        part = heads * HEAD_DIM
        wide = 2 * part
        src = lax.broadcasted_iota(jnp.int32, (wide, 1), 0)
        dst = lax.broadcasted_iota(jnp.int32, (1, width), 1)
        head, lane = src // (2 * HEAD_DIM), src % (2 * HEAD_DIM)
        to_v = jnp.where(lane >= HEAD_DIM, z * part + head * HEAD_DIM + lane - HEAD_DIM, -1)
        V[3:4, :] = pick(V[16:17, :wide], jnp.where(to_v == dst, 1.0, 0.0).astype(BF))
        V[2:3, :] = pick(V[17:18, :part], jnp.where(z * part + src[:part] == dst, 1.0, 0.0).astype(BF))
        v_copy(0).start()

    def vec_step(i):
        v_copy(i).wait()
        V[0:16, :] = V[0:16, :] + vr[i]
        if i < 4:
            v_copy(i + 1).start()
        else:
            n_dev = 32
            small = width // n_dev
            d = (x * 4 + y * 2 + c) * 4 + z
            src = lax.broadcasted_iota(jnp.int32, (width, 1), 0)
            dst = lax.broadcasted_iota(jnp.int32, (1, 128), 1)
            hot = jnp.where(dst < small, d * small + dst, -1) == src
            out_v[0:16, :] = pick(V[0:16, :], jnp.where(hot, 1.0, 0.0).astype(BF))
            big = n_hid * small
            hot = jnp.where(dst < big, (d % (n_dev // n_hid)) * big + dst, -1) == src
            line = lax.broadcasted_iota(jnp.int32, (16, 128), 0)
            val = pick(V[0:16, :], jnp.where(hot, 1.0, 0.0).astype(BF))
            val = jnp.where(line == 8 + d // (n_dev // n_hid), val, 0.0)
            out_v[16:17, :] = jnp.sum(val, axis=0, keepdims=True)

    for t, fn in zip(TIMES["packed"], (packed, packed_core, packed_a, packed_b, packed_z)):
        ev.append((t_end + t, fn))
    for t, fn in zip(TIMES["vec"], [vec_start] + [functools.partial(vec_step, i) for i in range(5)]):
        ev.append((t_end + t, fn))

    ev.sort(key=lambda e: e[0])
    dense_body(
        tok, cot_in, cotx, mix, vec, hid, mx_h, ex_h, sh_h,
        base, upx, act, sin, cot, gpre, gres, gresf, send, s4, s5, s6, s7, s8,
        mx, ex, sh, down_out, down_in, wsem, dss, drs,
        lambda: [local(i).start() for i in range(len(late))],
        lambda: [fn() for t, fn in ev if t < 1.0],
    )
    for t, fn in ev:
        if 1.0 <= t < t_att:
            fn()

    def step(s, carry):
        for k in range(steps):
            here = [fn for t, fn in ev if t_att + k * t_step <= t < t_att + (k + 1) * t_step]
            if here:

                @pl.when(s == k)
                def _():
                    for fn in here:
                        fn()

        backward_step(s % heads, (s // heads) ^ (2 * y + zh), c, grad, mixed, lse, qt, kv, kt, dkv, dqt)
        return carry

    lax.fori_loop(0, steps, step, 0)
    for t, fn in ev:
        if t >= t_end:
            fn()


def backward_all(tok, cot, cotx, mix, vec, hid, mx, ex, sh, mixed, lse, qt, kv, kt, fi, nrm, pw):
    D, V, S = pltpu.SemaphoreType.DMA, pltpu.VMEM, jax.ShapeDtypeStruct
    heads, keys = kv.shape[0], kv.shape[1]
    images, shard, width = tok.shape
    rows, half = images * shard, ex.shape[1]
    blk = (3, 8, width)
    cols = pw.shape[1]
    pb = (3, 8, cols)
    send = (4 * images, width // 4, shard)
    outs = [S(tok.shape, BF), S((4,) + blk, F32), S((3, 8, 2 * half), F32), S(blk, F32), S(tok.shape, BF), S((3, 8, 4 * cols), F32), S((24, 128), F32)]
    scr = [V(mx.shape, BF), V(ex.shape, BF), V(sh.shape, BF), V(tok.shape, BF), V(tok.shape, BF)]
    scr += [V(tok.shape, F32), V(tok.shape, BF), V((2 * rows, half), BF), V((2 * rows, width), BF), V((2 * rows, width), BF), V((2 * rows, half), BF)]
    scr += [V((rows, width), BF), V(tok.shape, F32), V(send, BF)] + [V((1, width), F32)] * 4 + [V((1, 2 * half), F32)]
    scr += [D((1 + 2 * (half // width),)), D((2 * images,)), D((2 * images,))]
    scr += [V(t.shape, t.dtype) for t in (mixed, lse, qt, kv, kt, fi, nrm, pw)]
    scr += [D((8,)), V(send, BF), V((1, 2, 2, 2, 4) + blk, BF), V((1, 4, 4) + blk, BF), V((1, 2, 4) + blk, BF), V((1, 4) + blk, BF), V((1, 2) + blk, BF), V((1,) + blk, BF)]
    scr += [V((4, 2, 2, 4, 2) + blk, BF), V((4, 2, 4, 2) + blk, BF), V((4, 4, 2) + blk, BF), V((4, 2, 2) + blk, BF), V((4, 2) + blk, BF)]
    scr += [V((2,) + blk, F32), V((2,) + blk, BF), V((2,) + blk, BF), V(tok.shape, BF)]
    scr += [V((heads, keys, 2 * HEAD_DIM), F32), V((4, heads * HEAD_DIM, 256), BF), V((keys, cols), BF)]
    rowt = (64, width)
    scr += [V((2, 2, 4, 2) + rowt, BF), V((2, 4, 2) + rowt, BF), V((2, 2, 2) + rowt, BF), V((2, 2) + rowt, BF), V((2,) + rowt, BF), V((2,) + rowt, BF)]
    scr += [V((1, 2, 2, 2, 4) + pb, BF), V((4, 4) + pb, BF), V((2, 4) + pb, BF), V((4,) + pb, BF), V((3,) + pb, BF), V((24, width), F32), V((5, 16, width), F32)]
    for n in ((), (7,), (7,), (1, 10), (1, 10), (4, 9), (4, 9), (3,), (3,), (16,), (16,), (10,), (10,), (5,), (5,)):
        scr.append(D(n) if n else D)
    return pl.pallas_call(
        backward_kernel,
        out_shape=outs,
        in_specs=[VM] * 6 + [ANY] * 11,
        out_specs=[VM] * len(outs),
        scratch_shapes=scr,
        compiler_params=pltpu.CompilerParams(collective_id=2, has_side_effects=True, vmem_limit_bytes=63 << 20),
        name="dense_backward_reduce",
    )(tok, cot, cotx, mix, vec, hid, mx, ex, sh, mixed, lse, qt, kv, kt, fi, nrm, pw)


def backward_local_kernel(grad, mixed, lse, qt, kv, kt, out, dkv, dqt):
    _, _, c, _ = coords()
    heads, keys = kv.shape[0], kv.shape[1]
    wide = 2 * HEAD_DIM * heads
    dkv[...] = jnp.zeros_like(dkv)

    def step(s, carry):
        backward_step(s % heads, s // heads, c, grad, mixed, lse, qt, kv, kt, dkv, dqt)
        return carry

    lax.fori_loop(0, 4 * heads, step, 0)
    for g in range(8):
        rs = slice(g * 256, (g + 1) * 256)
        for h in range(heads):
            out[rs, 2 * h * HEAD_DIM : 2 * (h + 1) * HEAD_DIM] = dkv[h, rs, :].astype(BF)
        dq = dqt[(g // 4) * 2 + g % 2].astype(F32).T
        out[rs, wide:] = jnp.where((g // 2) % 2 == c, dq, 0.0).astype(BF)


def backward_local(grad, mixed, lse, qt, kv, kt):
    heads, keys = kv.shape[0], kv.shape[1]
    return pl.pallas_call(
        backward_local_kernel,
        out_shape=jax.ShapeDtypeStruct((keys, 3 * heads * HEAD_DIM), BF),
        in_specs=[VM] * 6,
        out_specs=VM,
        scratch_shapes=[pltpu.VMEM((heads, keys, 2 * HEAD_DIM), F32), pltpu.VMEM((4, heads * HEAD_DIM, 256), BF)],
        compiler_params=pltpu.CompilerParams(vmem_limit_bytes=50 << 20),
        name="attention_backward",
    )(grad, mixed, lse, qt, kv, kt)


def reduce_generic(gf, gp, gm, ge, gs, n_dev):
    every = ("dp", "ctx", "head")
    x, y, c, z = coords()
    flat = gf.reshape((1, -1) + gf.shape[-1:])
    both = jnp.concatenate([jnp.where(y == i, flat, jnp.zeros_like(flat)) for i in range(2)], axis=0)
    of = lax.psum_scatter(both.astype(F32), ("ctx", "head"), scatter_dimension=1, tiled=True)
    cols = gp.shape[-1]
    rows = gp.size // cols
    spread = lax.dynamic_update_slice_in_dim(jnp.zeros((rows, 4, cols), F32), gp.reshape(rows, 1, cols).astype(F32), z, 1)
    op = jnp.swapaxes(lax.psum_scatter(spread, every, scatter_dimension=0, tiled=True), 0, 1)
    rest = [
        lax.psum_scatter(g.reshape((n_dev, -1) + g.shape[-1:]).astype(F32), every, scatter_dimension=0, tiled=True)[0] for g in (gm, ge, gs)
    ]
    return [of, op] + rest


def layer_norm(token_rows, norm_gain, norm_shift):
    normed, inv_std = row_norm(token_rows)
    return (normed * norm_gain + norm_shift, normed, inv_std)


def norm_backward(grad_out, normed, inv_std, norm_gain):
    scaled = grad_out * norm_gain
    first_mean = jnp.mean(scaled, axis=-1, keepdims=True)
    second_mean = jnp.mean(scaled * normed, axis=-1, keepdims=True)
    return inv_std * (scaled - first_mean - normed * second_mean)


def gelu_parts(pre_act):
    cumulative = 0.5 * (1.0 + jax.scipy.special.erf(pre_act * (1.0 / math.sqrt(2.0))))
    density = jnp.exp(-0.5 * pre_act * pre_act) * (1.0 / math.sqrt(2.0 * math.pi))
    return pre_act * cumulative, cumulative + pre_act * density


def on_device(
    tokens,
    cotangent,
    lengths,
    attention_gain,
    attention_shift,
    packed_weight,
    query_bias,
    value_bias,
    mixer_weight,
    mixer_bias,
    feedforward_gain,
    feedforward_shift,
    expand_weight,
    expand_bias,
    shrink_weight,
    shrink_bias,
):
    images, shard_len, width = tokens.shape
    groups = lax.axis_size("head")
    heads = HEADS // groups
    part = heads * HEAD_DIM
    hidden = expand_weight.shape[1]
    rows = images * shard_len
    n_dev = lax.axis_size("dp") * lax.axis_size("ctx") * groups
    z = lax.axis_index("head")
    wr = packed_weight.shape[0]
    fr = shrink_weight.shape[0]

    tiled = wr % 8 == 0 and fr % 8 == 0 and lax.axis_size("dp") == 2
    slab = (lambda r, n: (r // 8, 8, n)) if tiled else (lambda r, n: (r, n))
    vecs = [attention_gain, attention_shift, query_bias, value_bias, mixer_bias, feedforward_gain, feedforward_shift, shrink_bias, expand_bias]
    mx, ex, sh = mixer_weight.reshape(slab(wr, width)), expand_weight.reshape(slab(wr, hidden)), shrink_weight.reshape(slab(fr, width))
    if tiled:
        mix, mixed_t, lse, fi, nrm, qt, kv, kt, full_packed, full_vecs, eb, mxo, exo, sho, cotx = forward_all(lengths, tokens, cotangent, packed_weight.reshape(slab(wr, 3 * width)), mx, ex, sh, vecs)
        hidden_bias = eb
    else:
        pk = jnp.stack([own_columns(packed_weight, g, part) for g in range(groups)])
        sv = jnp.stack([jnp.pad(v, (0, 128 - v.shape[0])) for v in vecs] + [jnp.zeros((128,), BF)] * 7)
        img, pko, mxo, exo, sho, svo = gather_generic(tokens, pk, mx, ex, sh, sv)
        full_packed = pko.reshape(width, 3 * part)
        svo = svo.reshape(n_dev, 16, 128).astype(F32)
        gain_one, shift_one, qb, vb, mb, gain_two, shift_two, sb = [svo[:, i, :wr].reshape(width) for i in range(8)]
        eb = svo[:, 8, :fr].reshape(hidden)
        own = lambda v: lax.dynamic_slice_in_dim(v, z * part, part)
        vb_own = own(vb).reshape(heads, 1, HEAD_DIM)
        bias = jnp.concatenate([jnp.concatenate([jnp.zeros_like(vb_own), vb_own], axis=1).reshape(2 * part), own(qb)])
        img = img.reshape(16, shard_len, width)
        mixed_t, lse, fi, nrm, qt, kv, kt = attention_forward(lengths, img, full_packed, gain_one[None], shift_one[None], bias[None])
        mix = exchange(mixed_t, 1)
    mix = mix.reshape(images, width, shard_len)
    full_mixer = mxo.reshape(width, width)
    full_expand = exo.reshape(width, -1)
    full_shrink = sho.reshape(-1, width)

    if tiled:
        ig, os_, oe, om, block_output, op, ov = backward_all(
            tokens, cotangent, cotx, mix, full_vecs, hidden_bias, full_mixer, full_expand, full_shrink, mixed_t, lse, qt, kv, kt, fi, nrm, full_packed
        )
        ig, os_, oe, om, block_output, op, *vec = hand_over([ig, os_, oe, om, block_output, op], ov, wr, fr)
        op = op.reshape(wr, 3 * width)
    else:
        token_rows = tokens.reshape(rows, width).astype(F32)
        mixed_rows = jnp.swapaxes(mix, 1, 2).reshape(rows, width)
        residual = token_rows + dot(mixed_rows, full_mixer) + mb
        second_out, second_normed, second_inv = layer_norm(residual, gain_two, shift_two)
        second_input = second_out.astype(BF)
        pre_act = dot(second_input, full_expand) + eb
        value, slope = gelu_parts(pre_act)
        activated = value.astype(BF)
        block_output = (residual + dot(activated, full_shrink) + sb).astype(BF)
        grad_in = cotangent.reshape(rows, width)
        grad_rows = grad_in.astype(F32)
        grad_shrink_b = jnp.sum(grad_rows, axis=0)
        grad_pre = jnp.einsum("rd,fd->rf", grad_in, full_shrink, preferred_element_type=F32) * slope
        grad_pre_bf = grad_pre.astype(BF)
        grad_expand_b = jnp.sum(grad_pre, axis=0)
        grad_second = jnp.einsum("rf,df->rd", grad_pre_bf, full_expand, preferred_element_type=F32)
        grad_gain_two = jnp.sum(grad_second * second_normed, axis=0)
        grad_shift_two = jnp.sum(grad_second, axis=0)
        grad_residual = grad_rows + norm_backward(grad_second, second_normed, second_inv, gain_two)
        grad_residual_bf = grad_residual.astype(BF)
        grad_mixer_b = jnp.sum(grad_residual, axis=0)
        grad_mixed = jnp.einsum("de,ire->idr", full_mixer, grad_residual_bf.reshape(images, shard_len, width), preferred_element_type=F32).astype(BF)
        grad_mixed = grad_mixed.reshape(images * groups, part, shard_len)
        grad_t = exchange(grad_mixed, 2)
        dqkv = backward_local(grad_t, mixed_t, lse, qt, kv, kt)
        grad_packed_w = jnp.einsum("rd,re->de", fi, dqkv, preferred_element_type=F32)
        grad_first_part = jnp.einsum("re,de->rd", dqkv, full_packed, preferred_element_type=F32)
        img_normed, _ = row_norm(img.reshape(16 * shard_len, width).astype(F32))
        dsum = jnp.sum(dqkv.astype(F32), axis=0)
        place = lambda v: lax.dynamic_update_slice_in_dim(jnp.zeros((width,), F32), v, z * part, 0)
        sums = [
            jnp.sum(grad_first_part * img_normed, axis=0),
            jnp.sum(grad_first_part, axis=0),
            place(dsum[2 * part :]),
            place(dsum[: 2 * part].reshape(heads, 2, HEAD_DIM)[:, 1].reshape(part)),
            grad_mixer_b,
            grad_gain_two,
            grad_shift_two,
            grad_shrink_b,
            grad_expand_b,
        ]
        vec = [lax.psum_scatter(t, ("dp", "ctx", "head"), scatter_dimension=0, tiled=True) for t in sums]
        of, op, om, oe, os_ = reduce_generic(
            grad_first_part.reshape(2, 2, groups, shard_len, width),
            grad_packed_w,
            jnp.einsum("rd,re->de", mixed_rows, grad_residual_bf, preferred_element_type=F32),
            jnp.einsum("rd,rf->df", second_input, grad_pre_bf, preferred_element_type=F32),
            jnp.einsum("rf,rd->fd", activated, grad_in, preferred_element_type=F32),
            n_dev,
        )
        op = op.reshape(groups, wr, 3 * part)
        okv = jnp.transpose(op[:, :, : 2 * part].reshape(groups, wr, heads, 2, HEAD_DIM), (1, 3, 0, 2, 4)).reshape(wr, 2 * width)
        op = jnp.concatenate([jnp.transpose(op[:, :, 2 * part :], (1, 0, 2)).reshape(wr, width), okv], axis=1)
        _, first_normed, first_inv = layer_norm(token_rows, gain_one, shift_one)
        ig = (grad_residual + norm_backward(of.reshape(rows, width), first_normed, first_inv, gain_one)).astype(BF)
    return (
        block_output.reshape(images, shard_len, width),
        ig.reshape(images, shard_len, width),
        vec[0],
        vec[1],
        op,
        vec[2],
        vec[3],
        om.reshape(wr, width),
        vec[4],
        vec[5],
        vec[6],
        oe.reshape(wr, hidden),
        vec[8],
        os_.reshape(fr, width),
        vec[7],
    )


def solution(mesh):
    every = ("dp", "ctx", "head")
    tok, vec, mat = P("dp", ("ctx", "head"), None), P(every), P(every, None)
    in_specs = (tok, tok, P("dp"), vec, vec, mat, vec, vec, mat, vec, vec, vec, mat, vec, mat, vec)
    out_specs = (tok, tok, vec, vec, mat, vec, vec, mat, vec, vec, vec, mat, vec, mat, vec)
    return jax.shard_map(on_device, mesh=mesh, in_specs=in_specs, out_specs=out_specs, check_vma=False)
```
